32 devices in a mesh: dp: 8 (over y, x, core), fsdp: 4 (over z).
Axes of the slice: x: 2, y: 2, z: 4, core: 2. Of those that a mesh axis runs over, the one named last changes fastest.
Arguments:
- tokens: bfloat16 [32, 256, 1152], P(('dp', 'fsdp')), may hold values from -6 to 6
- condition: bfloat16 [32, 1152], P(('dp', 'fsdp')), may hold values from -6 to 6
- grid_sizes: int32 [32, 2], P(('dp', 'fsdp')), may hold values from 12 to 20, as said below
- w_ada: bfloat16 [1152, 6912], P('fsdp'), may hold values from -0.1875 to 0.1875
- w_qkv: bfloat16 [1152, 3456], P('fsdp'), may hold values from -0.1875 to 0.1875
- w_out: bfloat16 [1152, 1152], P('fsdp'), may hold values from -1 to 1
- w_up: bfloat16 [1152, 4608], P('fsdp'), may hold values from -0.1875 to 0.1875
- w_down: bfloat16 [4608, 1152], P('fsdp'), may hold values from -0.09375 to 0.09375
- b_ada: bfloat16 [6912], P('fsdp'), may hold values from -3 to 3
- b_qv: bfloat16 [2304], P('fsdp'), may hold values from -3 to 3
- b_out: bfloat16 [1152], P('fsdp'), may hold values from -3 to 3
- b_up: bfloat16 [4608], P('fsdp'), may hold values from -3 to 3
- b_down: bfloat16 [1152], P('fsdp'), may hold values from -3 to 3
- cotangent: bfloat16 [32, 256, 1152], P(('dp', 'fsdp')), may hold values from -6 to 6
Outputs:
- output: bfloat16 [32, 256, 1152], P(('dp', 'fsdp'))
- grad_tokens: bfloat16 [32, 256, 1152], P(('dp', 'fsdp'))
- grad_condition: float32 [32, 1152], P(('dp', 'fsdp'))
- grad_w_ada: float32 [1152, 6912], P('fsdp', 'dp')
- grad_w_qkv: float32 [1152, 3456], P('fsdp', 'dp')
- grad_w_out: float32 [1152, 1152], P('fsdp', 'dp')
- grad_w_up: float32 [1152, 4608], P('fsdp', 'dp')
- grad_w_down: float32 [4608, 1152], P('fsdp', 'dp')
- grad_b_ada: float32 [6912], P('fsdp')
- grad_b_qv: float32 [2304], P('fsdp')
- grad_b_out: float32 [1152], P('fsdp')
- grad_b_up: float32 [4608], P('fsdp')
- grad_b_down: float32 [1152], P('fsdp')
The draws below stay inside these ranges and needn't reach their ends.
Inputs may be any that keep to these rules, and one draw needn't show every extreme that they name: `grid_sizes`: each image grid has 12 to 20 rows and columns and at most 256 tokens; image 0 has 12 rows and 20 columns, and image 1 has 20 rows and 12 columns.
All inputs are finite; a program needn't handle non-finite values.
Results may differ from the reference program's by a relative error of at most 0.015.
The reference program's roundings to bfloat16 on the way count: a program that leaves them out, or rounds other values in their place, can miss the bound.
Values may be sent and summed in bfloat16 or wider, within the bound.
No kernel may reach another device: no remote copies, remote signals or barrier semaphores. Data moves between devices by JAX's collectives and lax.ppermute only.
A program may use at most 256 MiB of HBM per device.

```python
import math
import jax
import jax.numpy as jnp
from jax import lax

HEAD_DIM = 72
D = 1152
FF = 4608
SLOTS = 256
GRID_MIN = 12
GRID_MAX = 20
IMG_DEV = 1
IMAGES = 32


def draw_grid_sizes(key, part):
    first_key, second_key = jax.random.split(jax.random.fold_in(key, 17))
    heights = jax.random.randint(first_key, (IMAGES,), GRID_MIN, GRID_MAX + 1)
    widest = jnp.minimum(GRID_MAX, SLOTS // heights)
    spread = jax.random.randint(second_key, (IMAGES,), 0, 1 << 20)
    widths = GRID_MIN + spread % (widest - GRID_MIN + 1)
    heights = heights.at[0].set(GRID_MIN).at[1].set(GRID_MAX)
    widths = widths.at[0].set(GRID_MAX).at[1].set(GRID_MIN)
    return jnp.stack([heights, widths], axis=1).astype(jnp.int32)


def block_scale(rng, shape, cuts, least, high):
    gain, own = 1.0, jax.random.fold_in(rng, 6)
    for dim, parts in cuts:
        steps = jnp.exp(jax.random.uniform(jax.random.fold_in(own, dim), (parts,), jnp.float32, least / len(cuts), high / len(cuts)))
        gain = gain * jnp.repeat(steps, shape[dim] // parts).reshape([-1 if axis == dim else 1 for axis in range(len(shape))])
    return gain


def bell_draw(stream_key, dims, deviation, most, shards=(), held_as=jnp.bfloat16):
    loudness = block_scale(stream_key, dims, shards, -0.22, 0.18) if shards else 1.0
    values = jax.random.normal(stream_key, dims, jnp.float32) * deviation * loudness
    return jnp.minimum(jnp.maximum(values, -most), most).astype(held_as)


def setup_inputs(seed: int = 0) -> dict:
    key_list = jax.random.split(jax.random.key(seed), 15)
    tokens = bell_draw(key_list[0], (IMAGES, SLOTS, D), 1.0, 6.0, ((0, 32),))
    condition = bell_draw(key_list[1], (IMAGES, D), 1.0, 6.0, ((0, 32),))
    grid_sizes = draw_grid_sizes(jax.random.fold_in(key_list[14], 71), 0)
    w_ada = bell_draw(key_list[3], (D, 6 * D), D ** -0.5, 0.1875, ((0, 4),))
    w_qkv = bell_draw(key_list[4], (D, 3 * D), D ** -0.5, 0.1875, ((0, 4),))
    w_out = bell_draw(key_list[5], (D, D), (D // 32) ** -0.5, 1.0, ((0, 4),))
    w_up = bell_draw(key_list[6], (D, FF), D ** -0.5, 0.1875, ((0, 4),))
    w_down = bell_draw(key_list[7], (FF, D), FF ** -0.5, 0.09375, ((0, 4),))
    b_ada = bell_draw(key_list[8], (6 * D,), 0.5, 3.0, ((0, 4),))
    b_qv = bell_draw(key_list[9], (2 * D,), 0.5, 3.0, ((0, 4),))
    b_out = bell_draw(key_list[10], (D,), 0.5, 3.0, ((0, 4),))
    b_up = bell_draw(key_list[11], (FF,), 0.5, 3.0, ((0, 4),))
    b_down = bell_draw(key_list[12], (D,), 0.5, 3.0, ((0, 4),))
    cotangent = bell_draw(key_list[13], (IMAGES, SLOTS, D), 1.0, 6.0, ((0, 32),))
    return {"tokens": tokens, "condition": condition, "grid_sizes": grid_sizes, "w_ada": w_ada, "w_qkv": w_qkv, "w_out": w_out, "w_up": w_up, "w_down": w_down, "b_ada": b_ada, "b_qv": b_qv, "b_out": b_out, "b_up": b_up, "b_down": b_down, "cotangent": cotangent}


@jax.custom_vjp
def low(v):
    return lax.optimization_barrier(v.astype(jnp.bfloat16)).astype(jnp.float32)

@jax.custom_vjp
def low_back(v):
    return v

def low_keep(v):
    return (low(v), None)

def low_pass(kept, grad):
    return (grad,)

def back_keep(v):
    return (v, None)

def back_low(kept, grad):
    return (low(grad),)
low.defvjp(low_keep, low_pass)
low_back.defvjp(back_keep, back_low)
exact_mode = lax.Precision.HIGHEST
epsilon = 1e-06
masked_value = -1e+30
gelu_root = math.sqrt(2.0 / math.pi)

def layer_norm(values_in):
    centred = values_in - lax.optimization_barrier(jnp.mean(values_in, axis=-1, keepdims=True))
    spread = lax.optimization_barrier(jnp.mean(centred * centred, axis=-1, keepdims=True))
    return centred * lax.rsqrt(spread + epsilon)

def gelu_tanh(pre_act):
    return 0.5 * pre_act * (1.0 + jnp.tanh(gelu_root * (pre_act + 0.044715 * pre_act * pre_act * pre_act)))

def project(left, right):
    return jnp.einsum('isd,de->ise', left, right, precision=exact_mode)

def forward(tokens_wide, cond_wide, live_rows, w_ada, w_qkv, w_out, w_up, w_down, b_ada, b_qv, b_out, b_up, b_down):
    width = w_out.shape[0]
    images = tokens_wide.shape[0]
    slots = tokens_wide.shape[1]
    heads = width // HEAD_DIM
    cond_act = low(cond_wide * jax.nn.sigmoid(cond_wide))
    modulation = low_back(jnp.dot(cond_act, w_ada, precision=exact_mode) + b_ada)
    portions = jnp.split(modulation, 6, axis=1)
    shift_one, scale_one, gate_one, shift_two, scale_two, gate_two = [portion[:, None, :] for portion in portions]
    normed = low(layer_norm(tokens_wide) * (1.0 + scale_one) + shift_one)
    projected = project(normed, w_qkv)
    queries = low_back(low(projected[..., :width] + b_qv[:width])).reshape(images, slots, heads, HEAD_DIM)
    key_part = low_back(low(projected[..., width:2 * width])).reshape(images, slots, heads, HEAD_DIM)
    values = low_back(low(projected[..., 2 * width:] + b_qv[width:])).reshape(images, slots, heads, HEAD_DIM)
    raw = low_back(jnp.einsum('iqhe,ikhe->ihqk', queries, key_part, precision=exact_mode) * HEAD_DIM ** (-0.5))
    scores = jnp.where(live_rows[:, None, None, :] > 0, raw, masked_value)
    highest = lax.optimization_barrier(jnp.max(scores, axis=-1, keepdims=True))
    lse = highest + jnp.log(lax.optimization_barrier(jnp.sum(jnp.exp(scores - highest), axis=-1, keepdims=True)))
    probs = low(jnp.exp(scores - lse))
    attended = jnp.einsum('ihqk,ikhe->iqhe', probs, values, precision=exact_mode).reshape(images, slots, width)
    attended = low_back(low(attended))
    attn_out = low_back(project(attended, w_out) + b_out)
    middle = tokens_wide + gate_one * attn_out
    normed_two = low(layer_norm(middle) * (1.0 + scale_two) + shift_two)
    pre_act = low_back(project(normed_two, w_up) + b_up)
    activated = low(gelu_tanh(pre_act))
    mlp_out = low_back(project(activated, w_down) + b_down)
    return live_rows[:, :, None] * (middle + gate_two * mlp_out)

def reference(tokens, condition, grid_sizes, w_ada, w_qkv, w_out, w_up, w_down, b_ada, b_qv, b_out, b_up, b_down, cotangent):
    group_size = 4 * IMG_DEV
    group_count = IMAGES // group_size
    live_rows = (jnp.arange(SLOTS)[None, :] < (grid_sizes[:, 0] * grid_sizes[:, 1])[:, None]).astype(jnp.float32)
    params = tuple((weight.astype(jnp.float32) for weight in (w_ada, w_qkv, w_out, w_up, w_down, b_ada, b_qv, b_out, b_up, b_down)))

    def regroup(array):
        return array.reshape((group_count, group_size) + array.shape[1:])

    def flatten(array):
        return array.reshape((IMAGES,) + array.shape[2:])

    def one_group(running, inputs):
        tokens_part, cond_part, live_part, cot_part = inputs

        def local_forward(tokens_wide, cond_wide, *weights):
            return forward(tokens_wide, cond_wide, live_part, *weights)
        result, pullback = jax.vjp(local_forward, tokens_part.astype(jnp.float32), cond_part.astype(jnp.float32), *params)
        gradients = pullback(cot_part.astype(jnp.float32))
        running = tuple((summed + gradient for summed, gradient in zip(running, gradients[2:])))
        return (running, (result.astype(jnp.bfloat16), gradients[0].astype(jnp.bfloat16), gradients[1]))
    start = tuple((jnp.zeros_like(weight) for weight in params))
    totals, stacked = lax.scan(one_group, start, (regroup(tokens), regroup(condition), regroup(live_rows), regroup(cotangent)))
    return (flatten(stacked[0]), flatten(stacked[1]), flatten(stacked[2]), totals[0], totals[1], totals[2], totals[3], totals[4], totals[5], totals[6], totals[7], totals[8], totals[9])
```

```python
import math

import jax
import jax.numpy as jnp
from jax import lax
from jax.experimental import pallas as pl
from jax.experimental.pallas import tpu as pltpu
from jax.sharding import PartitionSpec as P

HEAD_DIM = 72
BOX = 8

epsilon = 1e-06
masked_value = -1e30
gelu_root = math.sqrt(2.0 / math.pi)
f32 = jnp.float32
bf16 = jnp.bfloat16


def norm_parts(values_in):
    centred = values_in - jnp.mean(values_in, axis=-1, keepdims=True)
    spread = jnp.mean(centred * centred, axis=-1, keepdims=True)
    rate = lax.rsqrt(spread + epsilon)
    return centred * rate, rate


def norm_back(normal, rate, grad):
    mean_grad = jnp.mean(grad, axis=-1, keepdims=True)
    mean_both = jnp.mean(grad * normal, axis=-1, keepdims=True)
    return rate * (grad - mean_grad - normal * mean_both)


def gelu_tanh(pre_act):
    return (
        0.5
        * pre_act
        * (1.0 + jnp.tanh(gelu_root * (pre_act + 0.044715 * pre_act * pre_act * pre_act)))
    )


def after(value, other):
    return lax.optimization_barrier((value, other))[0]


def pick(array, index, axis=0):
    return lax.dynamic_index_in_dim(array, index, axis, keepdims=False)


def make_body(dp, fs):
    groups = dp // BOX

    def box_send(x, bits):
        return lax.ppermute(x, "dp", [(i, i ^ bits) for i in range(dp)])

    def ring_send(x, hops):
        return lax.ppermute(x, "fsdp", [(i, (i + hops) % fs) for i in range(fs)])

    def group_send(x, hops):
        return lax.ppermute(x, "dp", [(i, (i + hops * BOX) % dp) for i in range(dp)])

    def ring_gather(x):
        return [x] + [ring_send(x, k) for k in range(1, fs)]

    def ring_sorted(blocks, z):
        back = jnp.stack(blocks[::-1] + blocks[::-1])
        return lax.dynamic_slice_in_dim(back, fs - 1 - z, fs, 0)

    def box_gather_rows(x):
        half = x.shape[0] // 2
        along_x = box_send(x, 2)
        along_y = box_send(x, 4)
        far_top = box_send(along_x[:half], 4)
        far_low = box_send(along_y[half:], 2)
        mine = jnp.concatenate([x, along_x, along_y, far_top, far_low], axis=0)
        return jnp.concatenate([mine, box_send(mine, 1)], axis=0)

    def box_exchange(blocks, place):
        pairs = blocks.reshape((BOX // 2, 2) + blocks.shape[1:])
        core = lax.rem(place, 2)
        chip = lax.div(place, 2)
        kept = pick(pairs, core, 1)
        got = box_send(pick(pairs, 1 - core, 1), 1)
        first, second = [pick(kept, chip)], [pick(got, chip)]
        for k in range(1, BOX // 2):
            both = jnp.stack([pick(kept, chip ^ k), pick(got, chip ^ k)])
            both = box_send(both, 2 * k)
            first.append(both[0])
            second.append(both[1])
        return jnp.concatenate(first + second, axis=-1)

    def gather_small(x):
        for bits in (1, 2, 4):
            x = jnp.concatenate([x, box_send(x, bits)], axis=0)
        if groups > 1:
            x = jnp.concatenate([x] + [group_send(x, k) for k in range(1, groups)], axis=0)
        return x

    def sum_small(x, z):
        total = pick(x, z)
        for k in range(1, fs):
            total = total + ring_send(pick(x, lax.rem(z + k, fs)), k)
        for bits in (1, 2, 4):
            total = total + box_send(total, bits)
        part = total
        for k in range(1, groups):
            total = total + group_send(part, k)
        return total

    def ring_sum(x, z):
        total = pick(x, z)
        for k in range(1, fs):
            sent = pick(x, lax.rem(z + k, fs)).astype(bf16)
            total = total + ring_send(sent, k).astype(f32)
        return total

    def group_sum(x, group):
        total = pick(x, group)
        for k in range(1, groups):
            total = total + group_send(pick(x, lax.rem(group + k, groups)), k)
        return total

    def spread_shard(quarter):
        pieces = []
        held = quarter
        for k in range(1, fs):
            held = ring_send(held, 1)
            other = box_send(held, 2 if k % 2 else 4)
            pieces.append((k, 0, held))
            pieces.append((k, 1, other))
            pieces.append((k, 2, box_send(held, 1)))
            pieces.append((k, 3, box_send(other, 1)))
        return pieces

    def assemble(where, owns, pieces):
        n_own = len(owns)
        widths = [own.shape[-1] for own in owns]
        starts = [sum(widths[:i]) for i in range(n_own)]
        lead, width = pieces[0][2].shape[0], sum(widths)
        n_copies = n_own * (1 + len(pieces))

        def kernel(where_ref, *refs):
            own_refs = refs[:n_own]
            piece_refs = refs[n_own : n_own + len(pieces)]
            out_refs = refs[n_own + len(pieces) : -1]
            sems = refs[-1]
            copies = []
            for i in range(n_own):
                target = out_refs[i].at[where_ref[0]]
                copies.append((own_refs[i], target))
                for (k, kind, unused), piece in zip(pieces, piece_refs):
                    source = piece.at[:, :, pl.ds(starts[i], widths[i])]
                    target = out_refs[i].at[where_ref[k], where_ref[fs + kind]]
                    copies.append((source, target))
            started = [
                pltpu.make_async_copy(source, target, sems.at[j])
                for j, (source, target) in enumerate(copies)
            ]
            for copy in started:
                copy.start()
            for copy in started:
                copy.wait()

        any_spec = pl.BlockSpec(memory_space=pl.ANY)
        outs = pl.pallas_call(
            kernel,
            out_shape=[
                jax.ShapeDtypeStruct((fs, 4, lead, 8, each), bf16) for each in widths
            ],
            in_specs=[pl.BlockSpec(memory_space=pltpu.SMEM)]
            + [any_spec] * (n_own + len(pieces)),
            out_specs=[any_spec] * n_own,
            scratch_shapes=[pltpu.SemaphoreType.DMA((n_copies,))],
            cost_estimate=pl.CostEstimate(
                flops=0, transcendentals=0, bytes_accessed=fs * 4 * lead * 8 * width * 4
            ),
        )(
            where,
            *[own.reshape(4, lead, 8, own.shape[-1]) for own in owns],
            *[piece for unused, unused_kind, piece in pieces],
        )
        return [out.reshape(fs * 4 * lead * 8, out.shape[-1]) for out in outs]

    def body(
        tokens,
        condition,
        grid_sizes,
        w_ada,
        w_qkv,
        w_out,
        w_up,
        w_down,
        b_ada,
        b_qv,
        b_out,
        b_up,
        b_down,
        cotangent,
    ):
        slots, width = tokens.shape[1:]
        heads = width // HEAD_DIM
        hidden = w_up.shape[1]
        rank = lax.axis_index("dp")
        z = lax.axis_index("fsdp")
        place = lax.rem(rank, BOX)
        group = lax.div(rank, BOX)
        core = place & 1
        side = ((place >> 1) ^ (place >> 2)) & 1
        near = 2 * side + core
        far = 2 * (1 - side) + core
        where = jnp.stack(
            [lax.rem(z - k + fs, fs) for k in range(fs)] + [near, far, near ^ 1, far ^ 1]
        ).astype(jnp.int32)

        def quarter_of(shard):
            rows, cols = shard.shape
            return pick(shard.reshape(4, rows // 32, 8, cols), near)

        first_quarter = jnp.concatenate([quarter_of(w_qkv), quarter_of(w_out)], axis=-1)
        first_pieces = spread_shard(first_quarter)
        up_pieces = spread_shard(after(quarter_of(w_up), first_pieces[-4][2]))
        down_pieces = spread_shard(after(quarter_of(w_down), up_pieces[-4][2]))

        cond_wide = condition[0].astype(f32)
        gate = jax.nn.sigmoid(cond_wide)
        cond_act = (cond_wide * gate).astype(bf16)
        small = jnp.concatenate([cond_act, b_ada, b_qv, b_out, b_up, b_down])
        small_all = ring_gather(small)
        rows_z = width // fs
        conds = jnp.stack(
            [lax.dynamic_slice_in_dim(each, z * rows_z, rows_z, 0) for each in small_all]
        )
        biases = ring_sorted(small_all, z).astype(f32)
        ends = [width]
        for bias in (b_ada, b_qv, b_out, b_up, b_down):
            ends.append(ends[-1] + bias.shape[0])
        bias_ada, bias_qv, bias_out, bias_up, bias_down = [
            biases[:, ends[i] : ends[i + 1]].reshape(-1) for i in range(5)
        ]
        partial = jnp.dot(conds, w_ada, preferred_element_type=f32)
        modulation = partial[0] + bias_ada
        for k in range(1, fs):
            modulation = modulation + ring_send(partial[k], fs - k)
        shift_one, scale_one, gate_one, shift_two, scale_two, gate_two = [
            modulation[i * width : (i + 1) * width][None, :] for i in range(6)
        ]
        conds_all = gather_small(conds)

        live = grid_sizes[0, 0] * grid_sizes[0, 1]
        live_rows = (lax.broadcasted_iota(jnp.int32, (slots, 1), 0) < live).astype(f32)
        live_keys = lax.broadcasted_iota(jnp.int32, (1, 1, slots), 2) < live
        tokens_wide = tokens[0].astype(f32)
        norm_one, rate_one = norm_parts(tokens_wide)
        normed = (norm_one * (1.0 + scale_one) + shift_one).astype(bf16)
        upstream = live_rows * cotangent[0].astype(f32)
        d_mlp = (gate_two * upstream).astype(bf16)
        normed_box = box_gather_rows(normed)
        d_mlp_box = box_gather_rows(d_mlp)

        qkv_full, out_full = assemble(where, [w_qkv, w_out], first_pieces)
        projected = jnp.dot(normed, qkv_full, preferred_element_type=f32)
        queries = (projected[:, :width] + bias_qv[:width]).astype(bf16)
        key_part = projected[:, width : 2 * width].astype(bf16)
        values = (projected[:, 2 * width :] + bias_qv[width:]).astype(bf16)
        queries = queries.reshape(slots, heads, HEAD_DIM)
        key_part = key_part.reshape(slots, heads, HEAD_DIM)
        values = values.reshape(slots, heads, HEAD_DIM)
        raw = jnp.einsum("qhe,khe->hqk", queries, key_part, preferred_element_type=f32)
        scores = jnp.where(live_keys, raw * HEAD_DIM ** (-0.5), masked_value)
        highest = jnp.max(scores, axis=-1, keepdims=True)
        lse = highest + jnp.log(jnp.sum(jnp.exp(scores - highest), axis=-1, keepdims=True))
        probs = jnp.exp(scores - lse)
        probs_low = probs.astype(bf16)
        attended = jnp.einsum("hqk,khe->qhe", probs_low, values, preferred_element_type=f32)
        attended = attended.reshape(slots, width).astype(bf16)
        attn_out = jnp.dot(attended, out_full, preferred_element_type=f32) + bias_out
        middle = tokens_wide + gate_one * attn_out
        norm_two, rate_two = norm_parts(middle)
        normed_two = (norm_two * (1.0 + scale_two) + shift_two).astype(bf16)
        attended_box = box_gather_rows(attended)
        normed_two_box = box_gather_rows(normed_two)

        (up_full,) = assemble(where, [w_up], up_pieces)
        pre_act = jnp.dot(normed_two, up_full, preferred_element_type=f32) + bias_up
        activated = gelu_tanh(pre_act).astype(bf16)
        act_blocks = activated.T.reshape(fs, BOX, hidden // fs // BOX, slots)
        act_blocks = act_blocks.transpose(1, 0, 2, 3).reshape(BOX, hidden // BOX, slots)
        act_box = box_exchange(act_blocks, place)
        (down_full,) = assemble(where, [w_down], down_pieces)
        mlp_out = jnp.dot(activated, down_full, preferred_element_type=f32) + bias_down
        output = (live_rows * (middle + gate_two * mlp_out)).astype(bf16)

        def column_blocks(grad_t):
            n = grad_t.shape[0] // dp
            blocks = grad_t.reshape(groups, BOX, n, slots).transpose(1, 0, 2, 3)
            return blocks.reshape(BOX, groups * n, slots)

        def weight_grad(left_box, right_box):
            grad = lax.dot_general(
                left_box, right_box, (((0,), (1,)), ((), ())), preferred_element_type=f32
            )
            rows, cols = grad.shape
            grad = ring_sum(grad.reshape(fs, rows // fs, cols), z)
            grad = grad.reshape(rows // fs, groups, cols // groups)
            return group_sum(grad.transpose(1, 0, 2), group)

        d_gate_two = jnp.sum(upstream * mlp_out, axis=0)
        grad_down = jnp.dot(act_box, d_mlp_box, preferred_element_type=f32)
        grad_down = ring_sum(grad_down.reshape(fs, hidden // fs // BOX, width), z)
        grad_down = grad_down.reshape(hidden // fs // BOX, groups, width // groups)
        grad_down = group_sum(grad_down.transpose(1, 0, 2), group)
        down_rows = hidden // fs // BOX
        down_blocks = grad_down.reshape(down_rows, BOX, width // dp).transpose(1, 0, 2)
        down_parts = [pick(down_blocks, place)] + [
            box_send(pick(down_blocks, place ^ k), k) for k in range(1, BOX)
        ]
        down_order = jnp.stack([place ^ k for k in range(BOX)])
        grad_w_down = jnp.stack(down_parts)[down_order].reshape(BOX * down_rows, width // dp)

        d_act = lax.dot_general(
            d_mlp, down_full, (((1,), (1,)), ((), ())), preferred_element_type=f32
        )
        unused_gelu, gelu_pull = jax.vjp(gelu_tanh, pre_act)
        d_pre = gelu_pull(d_act)[0].astype(bf16)
        d_pre_box = box_exchange(column_blocks(d_pre.T), place)
        grad_w_up = weight_grad(normed_two_box, d_pre_box)
        d_normed_two = lax.dot_general(
            d_pre, up_full, (((1,), (1,)), ((), ())), preferred_element_type=f32
        )
        d_shift_two = jnp.sum(d_normed_two, axis=0)
        d_scale_two = jnp.sum(d_normed_two * norm_two, axis=0)
        d_middle = upstream + norm_back(norm_two, rate_two, d_normed_two * (1.0 + scale_two))
        d_gate_one = jnp.sum(d_middle * attn_out, axis=0)
        d_attn = (gate_one * d_middle).astype(bf16)
        d_attn_box = box_exchange(column_blocks(d_attn.T), place)
        grad_w_out = weight_grad(attended_box, d_attn_box)

        d_mod_early = jnp.concatenate([d_gate_one, d_shift_two, d_scale_two, d_gate_two])
        d_mod_early = jnp.stack(ring_gather(d_mod_early.astype(bf16)))
        d_mod_early_all = gather_small(d_mod_early)

        def shards(vector):
            return vector.reshape(fs, -1)

        bias_early = jnp.concatenate(
            [
                shards(jnp.sum(d_attn.astype(f32), axis=0)),
                shards(jnp.sum(d_pre.astype(f32), axis=0)),
                shards(jnp.sum(d_mlp.astype(f32), axis=0)),
            ],
            axis=1,
        )
        bias_early = sum_small(bias_early, z)
        grad_b_out = bias_early[: width // fs]
        grad_b_up = bias_early[width // fs : (width + hidden) // fs]
        grad_b_down = bias_early[(width + hidden) // fs :]

        d_attended = lax.dot_general(
            d_attn, out_full, (((1,), (1,)), ((), ())), preferred_element_type=f32
        )
        d_attended = d_attended.astype(bf16).reshape(slots, heads, HEAD_DIM)
        d_probs = jnp.einsum("qhe,khe->hqk", d_attended, values, preferred_element_type=f32)
        d_values = jnp.einsum(
            "hqk,qhe->khe", probs_low, d_attended, preferred_element_type=f32
        ).astype(bf16)
        row_inner = jnp.sum(probs * d_probs, axis=-1, keepdims=True)
        d_scores = (probs * (d_probs - row_inner)).astype(bf16)
        d_queries = (
            jnp.einsum("hqk,khe->qhe", d_scores, key_part, preferred_element_type=f32)
            * HEAD_DIM ** (-0.5)
        ).astype(bf16)
        d_keys = (
            jnp.einsum("hqk,qhe->khe", d_scores, queries, preferred_element_type=f32)
            * HEAD_DIM ** (-0.5)
        ).astype(bf16)
        d_projected = jnp.concatenate(
            [
                d_queries.reshape(slots, width),
                d_keys.reshape(slots, width),
                d_values.reshape(slots, width),
            ],
            axis=1,
        )
        d_projected_box = box_exchange(column_blocks(d_projected.T), place)
        grad_w_qkv = weight_grad(normed_box, d_projected_box)
        sums = jnp.sum(d_projected.astype(f32), axis=0)
        grad_b_qv = sum_small(
            shards(jnp.concatenate([sums[:width], sums[2 * width :]])), z
        )
        d_normed = lax.dot_general(
            d_projected, qkv_full, (((1,), (1,)), ((), ())), preferred_element_type=f32
        )
        d_shift_one = jnp.sum(d_normed, axis=0)
        d_scale_one = jnp.sum(d_normed * norm_one, axis=0)
        grad_tokens = d_middle + norm_back(norm_one, rate_one, d_normed * (1.0 + scale_one))

        d_mod_late = jnp.concatenate([d_shift_one, d_scale_one]).astype(bf16)
        d_mod_late = jnp.stack(ring_gather(d_mod_late))
        d_mod_all = jnp.concatenate([gather_small(d_mod_late), d_mod_early_all], axis=1)
        d_mod_near = jnp.concatenate([d_mod_late, d_mod_early], axis=1)
        ada_cols = w_ada.shape[1] // dp
        d_mod_cols = pick(d_mod_all.reshape(-1, dp, ada_cols), rank, 1)
        grad_w_ada = lax.dot_general(
            conds_all, d_mod_cols, (((0,), (0,)), ((), ())), preferred_element_type=f32
        )
        sums_ada = jnp.sum(d_mod_all.astype(f32), axis=0)
        grad_b_ada = pick(shards(sums_ada), z)
        d_conds = lax.dot_general(
            d_mod_near, w_ada, (((1,), (1,)), ((), ())), preferred_element_type=f32
        )
        cond_parts = [d_conds[0]] + [ring_send(d_conds[k], fs - k) for k in range(1, fs)]
        twice = jnp.stack(cond_parts + cond_parts)
        d_cond_act = lax.dynamic_slice_in_dim(twice, lax.rem(fs - z, fs), fs, 0).reshape(-1)
        grad_condition = d_cond_act * gate * (1.0 + cond_wide * (1.0 - gate))
        return (
            output[None],
            grad_tokens.astype(bf16)[None],
            grad_condition[None],
            grad_w_ada,
            grad_w_qkv,
            grad_w_out,
            grad_w_up,
            grad_w_down,
            grad_b_ada,
            grad_b_qv,
            grad_b_out,
            grad_b_up,
            grad_b_down,
        )

    return body


def solution(mesh):
    return jax.shard_map(
        make_body(mesh.shape["dp"], mesh.shape["fsdp"]),
        mesh=mesh,
        in_specs=(
            P(("dp", "fsdp"), None, None),
            P(("dp", "fsdp"), None),
            P(("dp", "fsdp"), None),
            P("fsdp", None),
            P("fsdp", None),
            P("fsdp", None),
            P("fsdp", None),
            P("fsdp", None),
            P("fsdp"),
            P("fsdp"),
            P("fsdp"),
            P("fsdp"),
            P("fsdp"),
            P(("dp", "fsdp"), None, None),
        ),
        out_specs=(
            P(("dp", "fsdp"), None, None),
            P(("dp", "fsdp"), None, None),
            P(("dp", "fsdp"), None),
            P("fsdp", "dp"),
            P("fsdp", "dp"),
            P("fsdp", "dp"),
            P("fsdp", "dp"),
            P("fsdp", "dp"),
            P("fsdp"),
            P("fsdp"),
            P("fsdp"),
            P("fsdp"),
            P("fsdp"),
        ),
        check_vma=False,
    )
```

```python
import math

import jax
import jax.numpy as jnp
from jax import lax
from jax.experimental import pallas as pl
from jax.experimental.pallas import tpu as pltpu
from jax.sharding import PartitionSpec as P

HEAD_DIM = 72
BOX = 8

epsilon = 1e-06
masked_value = -1e30
gelu_root = math.sqrt(2.0 / math.pi)
f32 = jnp.float32
bf16 = jnp.bfloat16


def norm_parts(values_in):
    centred = values_in - jnp.mean(values_in, axis=-1, keepdims=True)
    spread = jnp.mean(centred * centred, axis=-1, keepdims=True)
    rate = lax.rsqrt(spread + epsilon)
    return centred * rate, rate


def norm_back(normal, rate, grad):
    mean_grad = jnp.mean(grad, axis=-1, keepdims=True)
    mean_both = jnp.mean(grad * normal, axis=-1, keepdims=True)
    return rate * (grad - mean_grad - normal * mean_both)


def gelu_tanh(pre_act):
    return (
        0.5
        * pre_act
        * (1.0 + jnp.tanh(gelu_root * (pre_act + 0.044715 * pre_act * pre_act * pre_act)))
    )


def after(value, other):
    return lax.optimization_barrier((value, other))[0]


def gated(values):
    return lax.optimization_barrier(values)


def pick(array, index, axis=0):
    return lax.dynamic_index_in_dim(array, index, axis, keepdims=False)


def make_body(dp, fs):
    groups = dp // BOX

    def box_send(x, bits):
        return lax.ppermute(x, "dp", [(i, i ^ bits) for i in range(dp)])

    def side_send(x):
        return lax.ppermute(x, "dp", [(i, i ^ (4 if i & 1 else 2)) for i in range(dp)])

    def ring_send(x, hops):
        return lax.ppermute(x, "fsdp", [(i, (i + hops) % fs) for i in range(fs)])

    def group_send(x, hops):
        return lax.ppermute(x, "dp", [(i, (i + hops * BOX) % dp) for i in range(dp)])

    def ring_gather(x):
        return [x] + [ring_send(x, k) for k in range(1, fs)]

    def ring_sorted(blocks, z):
        back = jnp.stack(blocks[::-1] + blocks[::-1])
        return lax.dynamic_slice_in_dim(back, fs - 1 - z, fs, 0)

    def chip_near(x):
        return box_send(x, 2), box_send(x, 4)

    def chip_far(near):
        half = near[0].shape[0] // 2
        return box_send(near[0][:half], 4), box_send(near[1][half:], 2)

    def chip_exchange(blocks, chip):
        return [pick(blocks, chip)] + [
            box_send(pick(blocks, chip ^ k), 2 * k) for k in range(1, BOX // 2)
        ]

    def ring_sum(x, z):
        total = pick(x, z)
        for k in range(1, fs):
            sent = pick(x, lax.rem(z + k, fs)).astype(bf16)
            total = total + ring_send(sent, k).astype(f32)
        return total

    def group_sum(x, group):
        total = pick(x, group)
        for k in range(1, groups):
            total = total + group_send(pick(x, lax.rem(group + k, groups)), k)
        return total

    def assemble(where, owns, pieces):
        arrays = []
        for piece, unused in (each for kind in pieces for each in kind):
            if not any(piece is array for array in arrays):
                arrays.append(piece)
        position = {id(array): i for i, array in enumerate(arrays)}
        plan = [[(position[id(piece)], index) for piece, index in kind] for kind in pieces]
        n_own, n_arrays, n_kinds = len(owns), len(arrays), len(pieces)
        widths = [own.shape[-1] for own in owns]
        starts = [sum(widths[:i]) for i in range(n_own)]
        lead, width = arrays[0].shape[-3], sum(widths)

        def kernel(where_ref, *refs):
            own_refs = refs[:n_own]
            array_refs = refs[n_own : n_own + n_arrays]
            out_refs = refs[n_own + n_arrays : -1]
            sems = refs[-1]
            step = pl.program_id(0)

            def run(copies):
                started = [
                    pltpu.make_async_copy(source, target, sems.at[j])
                    for j, (source, target) in enumerate(copies)
                ]
                for copy in started:
                    copy.start()
                for copy in started:
                    copy.wait()

            @pl.when(step == 0)
            def own_rows():
                run([(own_refs[i], out_refs[i].at[0]) for i in range(n_own)])

            for block in range(1, fs):

                @pl.when(step == block)
                def other_rows(block=block):
                    copies = []
                    for kind in range(n_kinds):
                        which, index = plan[kind][block - 1]
                        source = array_refs[which]
                        source = source if index is None else source.at[index]
                        for i in range(n_own):
                            part = source.at[:, :, pl.ds(starts[i], widths[i])]
                            copies.append((part, out_refs[i].at[0, where_ref[fs + kind]]))
                    run(copies)

        any_spec = pl.BlockSpec(memory_space=pl.ANY)
        outs = pl.pallas_call(
            kernel,
            out_shape=[
                jax.ShapeDtypeStruct((fs, 4, lead, 8, each), bf16) for each in widths
            ],
            grid_spec=pltpu.PrefetchScalarGridSpec(
                num_scalar_prefetch=1,
                grid=(fs,),
                in_specs=[any_spec] * (n_own + n_arrays),
                out_specs=[
                    pl.BlockSpec(
                        (1, 4, lead, 8, each), lambda k, where_ref: (where_ref[k], 0, 0, 0, 0)
                    )
                    for each in widths
                ],
                scratch_shapes=[pltpu.SemaphoreType.DMA((n_own * n_kinds,))],
            ),
            cost_estimate=pl.CostEstimate(
                flops=0, transcendentals=0, bytes_accessed=fs * 4 * lead * 8 * width * 4
            ),
            compiler_params=pltpu.CompilerParams(vmem_limit_bytes=24 << 20),
        )(where, *[own.reshape(4, lead, 8, own.shape[-1]) for own in owns], *arrays)
        return [out.reshape(fs * 4 * lead * 8, out.shape[-1]) for out in outs]

    def assemble_wide(where, owns, mine, got):
        n_own, n_pieces = len(owns), len(mine)
        widths = [own.shape[-1] for own in owns]
        width = sum(widths)
        part = mine[0].shape[-1]
        lead = owns[0].shape[0] // 32
        split = mine[3].shape[0]

        def col_plan(core):
            plan, first = [], 0
            low, high = (0, part) if core == 0 else (part, width)
            offset = 0 if core == 0 else width - part
            for i, each in enumerate(widths):
                start, end = max(low, first), min(high, first + each)
                if start < end:
                    plan.append((start - offset, i, start - first, end - start))
                first += each
            return plan

        def row_plan(block):
            base = (block - 1) * lead
            plan = [(i, base, i, 0, lead) for i in range(3)]
            top = min(max(split - base, 0), lead)
            if top:
                plan.append((3, base, 3, 0, top))
            if top < lead:
                plan.append((4, base + top - split, 3, top, lead - top))
            return plan

        def kernel(where_ref, *refs):
            own_refs = refs[:n_own]
            sets = (refs[n_own : n_own + n_pieces], refs[n_own + n_pieces : n_own + 2 * n_pieces])
            out_refs = refs[n_own + 2 * n_pieces : -1]
            sems = refs[-1]
            step = pl.program_id(0)

            def run(copies):
                started = [
                    pltpu.make_async_copy(source, target, sems.at[j])
                    for j, (source, target) in enumerate(copies)
                ]
                for copy in started:
                    copy.start()
                for copy in started:
                    copy.wait()

            @pl.when(step == 0)
            def own_rows():
                run([(own_refs[i], out_refs[i].at[0]) for i in range(n_own)])

            for block in range(1, fs):
                for core in range(2):

                    @pl.when((step == block) & (where_ref[fs] == core))
                    def other_rows(block=block, core=core):
                        copies = []
                        for side, piece_refs in enumerate(sets):
                            for piece, first, slot, row, rows in row_plan(block):
                                for col, i, target_col, cols in col_plan(core ^ side):
                                    source = piece_refs[piece].at[
                                        first : first + rows, :, col : col + cols
                                    ]
                                    target = out_refs[i].at[
                                        0,
                                        where_ref[fs + 1 + slot],
                                        row : row + rows,
                                        :,
                                        target_col : target_col + cols,
                                    ]
                                    copies.append((source, target))
                        run(copies)

        n_sems = max(
            n_own,
            max(
                len(row_plan(block)) * (len(col_plan(0)) + len(col_plan(1)))
                for block in range(1, fs)
            ),
        )
        any_spec = pl.BlockSpec(memory_space=pl.ANY)
        outs = pl.pallas_call(
            kernel,
            out_shape=[
                jax.ShapeDtypeStruct((fs, 4, lead, 8, each), bf16) for each in widths
            ],
            grid_spec=pltpu.PrefetchScalarGridSpec(
                num_scalar_prefetch=1,
                grid=(fs,),
                in_specs=[any_spec] * (n_own + 2 * n_pieces),
                out_specs=[
                    pl.BlockSpec(
                        (1, 4, lead, 8, each), lambda k, where_ref: (where_ref[k], 0, 0, 0, 0)
                    )
                    for each in widths
                ],
                scratch_shapes=[pltpu.SemaphoreType.DMA((n_sems,))],
            ),
            cost_estimate=pl.CostEstimate(
                flops=0, transcendentals=0, bytes_accessed=fs * 4 * lead * 8 * width * 4
            ),
            compiler_params=pltpu.CompilerParams(vmem_limit_bytes=24 << 20),
        )(where, *[own.reshape(4, lead, 8, own.shape[-1]) for own in owns], *mine, *got)
        return [out.reshape(fs * 4 * lead * 8, out.shape[-1]) for out in outs]

    def column_grad(where, lefts, rights):
        slots, n = rights[0].shape[1], rights[0].shape[0] // 2
        width = lefts[0].shape[1]
        tile = width // 3
        half = slots // 2

        def kernel(where_ref, x0, x1, x2, x3, x4, y0, y1, y2, y3, keep_ref, send_ref):
            core = where_ref[0]
            for out_ref, first in ((keep_ref, core * n), (send_ref, (1 - core) * n)):
                rows = pl.ds(pl.multiple_of(first, 16), n)
                total = None
                for x, y, cols in (
                    (x0, y0, slice(None)),
                    (x1, y1, slice(None)),
                    (x2, y2, slice(None)),
                    (x3, y3, slice(0, half)),
                    (x4, y3, slice(half, slots)),
                ):
                    part = jnp.dot(y[rows, cols], x[...], preferred_element_type=f32)
                    total = part if total is None else total + part
                out_ref[...] = total

        left_specs = [
            pl.BlockSpec((left.shape[0], tile), lambda i, where_ref: (0, i)) for left in lefts
        ]
        right_spec = pl.BlockSpec((2 * n, slots), lambda i, where_ref: (0, 0))
        out_spec = pl.BlockSpec((n, tile), lambda i, where_ref: (0, i))
        return pl.pallas_call(
            kernel,
            out_shape=[jax.ShapeDtypeStruct((n, width), f32)] * 2,
            grid_spec=pltpu.PrefetchScalarGridSpec(
                num_scalar_prefetch=1,
                grid=(width // tile,),
                in_specs=left_specs + [right_spec] * 4,
                out_specs=[out_spec] * 2,
            ),
            cost_estimate=pl.CostEstimate(
                flops=16 * slots * width * n,
                transcendentals=0,
                bytes_accessed=8 * slots * (width + 2 * n) + 8 * width * n,
            ),
            compiler_params=pltpu.CompilerParams(vmem_limit_bytes=32 << 20),
        )(where, *lefts, *rights)

    def split_grad(where, keep, got):
        n, width = keep.shape
        rows = width // fs
        padded = -(-n // 128) * 128

        def kernel(where_ref, keep_ref, got_ref, own_ref, *rest):
            send_refs, turned = rest[:-1], rest[-1]
            for first in range(0, width, 128):
                total = keep_ref[:, first : first + 128] + got_ref[:, first : first + 128]
                if padded > n:
                    total = jnp.concatenate([total, jnp.zeros((padded - n, 128), f32)], axis=0)
                turned[first : first + 128, :] = total.T[:, :n]
            z = where_ref[0]
            own_ref[...] = turned[pl.ds(pl.multiple_of(z * rows, 16), rows), :]
            for k, send_ref in enumerate(send_refs):
                target = lax.rem(z + k + 1, fs)
                block = turned[pl.ds(pl.multiple_of(target * rows, 16), rows), :]
                send_ref[...] = block.astype(bf16)

        whole = pl.BlockSpec(memory_space=pltpu.VMEM)
        return pl.pallas_call(
            kernel,
            out_shape=[jax.ShapeDtypeStruct((rows, n), f32)]
            + [jax.ShapeDtypeStruct((rows, n), bf16)] * (fs - 1),
            in_specs=[pl.BlockSpec(memory_space=pltpu.SMEM), whole, whole],
            out_specs=[whole] * fs,
            scratch_shapes=[pltpu.VMEM((width, n), f32)],
            cost_estimate=pl.CostEstimate(
                flops=width * n, transcendentals=0, bytes_accessed=11 * width * n
            ),
            compiler_params=pltpu.CompilerParams(vmem_limit_bytes=32 << 20),
        )(where, keep, got)

    def row_grad(where, lefts, rights):
        rows = lefts[0].shape[0] // fs
        slots, n = lefts[0].shape[1], rows // 2
        width = rights[0].shape[1]
        half = slots // 2

        def kernel(where_ref, x0, x1, x2, x3, y0, y1, y2, y3, y4, keep_ref, send_ref):
            core = where_ref[0]
            for out_ref, first in ((keep_ref, core * n), (send_ref, (1 - core) * n)):
                lines = pl.ds(pl.multiple_of(first, 16), n)
                total = None
                for x, y, cols in (
                    (x0, y0, slice(None)),
                    (x1, y1, slice(None)),
                    (x2, y2, slice(None)),
                    (x3, y3, slice(0, half)),
                    (x3, y4, slice(half, slots)),
                ):
                    part = jnp.dot(x[lines, cols], y[...], preferred_element_type=f32)
                    total = part if total is None else total + part
                out_ref[0] = total

        left_spec = pl.BlockSpec((rows, slots), lambda i, where_ref: (i, 0))
        right_specs = [
            pl.BlockSpec((right.shape[0], width), lambda i, where_ref: (0, 0))
            for right in rights
        ]
        out_spec = pl.BlockSpec((1, n, width), lambda i, where_ref: (i, 0, 0))
        return pl.pallas_call(
            kernel,
            out_shape=[jax.ShapeDtypeStruct((fs, n, width), f32)] * 2,
            grid_spec=pltpu.PrefetchScalarGridSpec(
                num_scalar_prefetch=1,
                grid=(fs,),
                in_specs=[left_spec] * 4 + right_specs,
                out_specs=[out_spec] * 2,
            ),
            cost_estimate=pl.CostEstimate(
                flops=8 * slots * width * rows * fs,
                transcendentals=0,
                bytes_accessed=8 * slots * (width + rows * fs) + 4 * width * rows * fs,
            ),
            compiler_params=pltpu.CompilerParams(vmem_limit_bytes=32 << 20),
        )(where, *lefts, *rights)

    def body(
        tokens,
        condition,
        grid_sizes,
        w_ada,
        w_qkv,
        w_out,
        w_up,
        w_down,
        b_ada,
        b_qv,
        b_out,
        b_up,
        b_down,
        cotangent,
    ):
        slots, width = tokens.shape[1:]
        heads = width // HEAD_DIM
        hidden = w_up.shape[1]
        rank = lax.axis_index("dp")
        z = lax.axis_index("fsdp")
        place = lax.rem(rank, BOX)
        group = lax.div(rank, BOX)
        core = place & 1
        chip = place >> 1
        side = (chip ^ (chip >> 1)) & 1
        near = 2 * side + core
        far = 2 * (1 - side) + core
        where = jnp.stack(
            [lax.rem(z - k + fs, fs) for k in range(fs)] + [near, far, near ^ 1, far ^ 1]
        ).astype(jnp.int32)
        where_core = core.reshape(1).astype(jnp.int32)
        where_wide = jnp.stack(
            [lax.rem(z - k + fs, fs) for k in range(fs)] + [core] + [chip ^ k for k in range(4)]
        ).astype(jnp.int32)

        cond_wide = condition[0].astype(f32)
        gate = jax.nn.sigmoid(cond_wide)
        cond_act = (cond_wide * gate).astype(bf16)
        row = max(width, b_ada.shape[0])
        small = jnp.stack(
            [
                jnp.pad(each, (0, row - each.shape[0]))
                for each in (cond_act, b_ada, b_qv, b_out, b_up, b_down)
            ]
        )

        def quarter_of(shard):
            rows, cols = shard.shape
            return pick(shard.reshape(4, rows // 32, 8, cols), near)

        def ring_on(held, count):
            helds = []
            for unused in range(count):
                held = ring_send(held, 1)
                helds.append(held)
            return helds

        last = fs - 1
        small_all = ring_gather(small)
        raw = jnp.concatenate([tokens[0], cotangent[0]], axis=1)
        raw_near = chip_near(raw)
        qkv_helds = ring_on(quarter_of(w_qkv), 1)
        def chip_rows_of(shard):
            rows, cols = shard.shape
            return pick(shard.reshape(4, rows // 32, 8, cols), chip)

        mid_rows = jnp.concatenate([chip_rows_of(w_out), chip_rows_of(w_up)], axis=-1)
        mid_width = mid_rows.shape[-1]
        mid_part = -(-mid_width // 256) * 128
        mid_start = jnp.where(core == 0, 0, mid_width - mid_part)
        mid_eighth = lax.dynamic_slice_in_dim(mid_rows, mid_start, mid_part, 2)
        down_quarter = quarter_of(w_down)
        small_all = gated(small_all)

        rows_z = width // fs
        conds = jnp.stack(
            [lax.dynamic_slice_in_dim(each[0], z * rows_z, rows_z, 0) for each in small_all]
        )
        partial = jnp.dot(conds, w_ada, preferred_element_type=f32)
        partials = [partial[0]] + [ring_send(partial[k], fs - k) for k in range(1, fs)]
        qkv_helds += ring_on(qkv_helds[-1], fs - 3)
        tokens_wide = tokens[0].astype(f32)
        norm_one, rate_one = norm_parts(tokens_wide)
        small_all, partials, qkv_helds, raw_near, norm_one, rate_one = gated(
            (small_all, partials, qkv_helds, raw_near, norm_one, rate_one)
        )

        biases = ring_sorted(small_all, z).astype(f32)
        bias_ada, bias_qv, bias_out, bias_up, bias_down = [
            biases[:, i + 1, : each.shape[0]].reshape(-1)
            for i, each in enumerate((b_ada, b_qv, b_out, b_up, b_down))
        ]
        modulation = sum(partials[1:], partials[0] + bias_ada)
        shift_one, scale_one, gate_one, shift_two, scale_two, gate_two = [
            modulation[i * width : (i + 1) * width][None, :] for i in range(6)
        ]
        live = grid_sizes[0, 0] * grid_sizes[0, 1]
        head = jnp.concatenate(
            [shift_one, scale_one, gate_two, jnp.broadcast_to(live.astype(f32), (1, width))]
        )
        heads_got = [box_send(head, bits) for bits in (2, 4, 6)]
        raw_far = chip_far(raw_near)
        qkv_helds += ring_on(qkv_helds[-1], 1)
        live_rows = (lax.broadcasted_iota(jnp.int32, (slots, 1), 0) < live).astype(f32)
        live_keys = lax.broadcasted_iota(jnp.int32, (1, 1, slots), 2) < live
        normed = (norm_one * (1.0 + scale_one) + shift_one).astype(bf16)
        upstream = live_rows * cotangent[0].astype(f32)
        d_mlp = (gate_two * upstream).astype(bf16)
        heads_got, raw_far, qkv_helds, normed, d_mlp = gated(
            (heads_got, raw_far, qkv_helds, normed, d_mlp)
        )

        qkv_mine = jnp.stack(qkv_helds)
        qkv_other = side_send(qkv_mine)
        qkv_mine_got = box_send(qkv_mine, 1)
        mid_helds = ring_on(after(mid_eighth, qkv_mine), fs - 2)

        def head_of(raw_rows, first, got):
            shift, scale, gate_last = got[0:1], got[1:2], got[2:3]
            rows = lax.broadcasted_iota(jnp.int32, (raw_rows.shape[0], 1), 0) + first
            normal = norm_parts(raw_rows[:, :width].astype(f32))[0]
            alive = (rows < got[3, 0].astype(jnp.int32)).astype(f32)
            upstream_rows = alive * raw_rows[:, width:].astype(f32)
            return (
                (normal * (1.0 + scale) + shift).astype(bf16),
                (gate_last * upstream_rows).astype(bf16),
            )

        half = slots // 2
        normed_box, d_mlp_box = [normed], [d_mlp]
        for raw_rows, first, got in zip(
            raw_near + raw_far, (0, 0, 0, half), heads_got + heads_got[2:]
        ):
            one, two = head_of(raw_rows, first, got)
            normed_box.append(one)
            d_mlp_box.append(two)
        normed, qkv_mine, qkv_other, qkv_mine_got, mid_helds, normed_box, d_mlp_box = gated(
            (normed, qkv_mine, qkv_other, qkv_mine_got, mid_helds, normed_box, d_mlp_box)
        )

        def in_order(array):
            return [(array, k) for k in range(last)]

        qkv_other_got = box_send(qkv_other, 1)
        mid_helds += ring_on(mid_helds[-1], 1)
        mid_mine = jnp.concatenate(mid_helds)
        mid_near = chip_near(mid_mine)
        down_helds = ring_on(after(down_quarter, mid_mine), 1)
        (qkv_full,) = assemble(
            where,
            [w_qkv],
            [in_order(each) for each in (qkv_mine, qkv_other, qkv_mine_got, qkv_other_got)],
        )
        projected = jnp.dot(normed, qkv_full, preferred_element_type=f32)
        queries = (projected[:, :width] + bias_qv[:width]).astype(bf16)
        key_part = projected[:, width : 2 * width].astype(bf16)
        values = (projected[:, 2 * width :] + bias_qv[width:]).astype(bf16)
        queries = queries.reshape(slots, heads, HEAD_DIM)
        key_part = key_part.reshape(slots, heads, HEAD_DIM)
        values = values.reshape(slots, heads, HEAD_DIM)
        scores = jnp.einsum("qhe,khe->hqk", queries, key_part, preferred_element_type=f32)
        scores = jnp.where(live_keys, scores * HEAD_DIM ** (-0.5), masked_value)
        highest = jnp.max(scores, axis=-1, keepdims=True)
        lse = highest + jnp.log(jnp.sum(jnp.exp(scores - highest), axis=-1, keepdims=True))
        probs = jnp.exp(scores - lse)
        probs_low = probs.astype(bf16)
        attended = jnp.einsum("hqk,khe->qhe", probs_low, values, preferred_element_type=f32)
        attended = attended.reshape(slots, width).astype(bf16)
        attended, mid_mine, mid_near, down_helds = gated(
            (attended, mid_mine, mid_near, down_helds)
        )

        mid_far = chip_far(mid_near)
        mid_got = [box_send(each, 1) for each in (mid_mine, *mid_near)]
        down_helds += ring_on(down_helds[-1], 1)
        attended, mid_far, mid_got, down_helds = gated((attended, mid_far, mid_got, down_helds))

        mid_got += [box_send(each, 1) for each in mid_far]
        down_others = [side_send(each) for each in down_helds]
        down_helds += ring_on(down_helds[-1], fs - 3)
        attended_near = chip_near(attended)
        attended_far = chip_far(attended_near)
        out_full, up_full = assemble_wide(
            where_wide, [w_out, w_up], (mid_mine, *mid_near, *mid_far), mid_got
        )
        attn_out = jnp.dot(attended, out_full, preferred_element_type=f32) + bias_out
        middle = tokens_wide + gate_one * attn_out
        norm_two, rate_two = norm_parts(middle)
        normed_two = (norm_two * (1.0 + scale_two) + shift_two).astype(bf16)
        pre_act = jnp.dot(normed_two, up_full, preferred_element_type=f32) + bias_up
        activated = gelu_tanh(pre_act).astype(bf16)
        act_blocks = activated.T.reshape(fs, BOX // 2, 2 * hidden // fs // BOX, slots)
        act_blocks = act_blocks.transpose(1, 0, 2, 3).reshape(BOX // 2, -1, slots)
        down_helds, down_others, attended_far, act_blocks, normed_two = gated(
            (down_helds, down_others, attended_far, act_blocks, normed_two)
        )
        attended_box = [attended, *attended_near, *attended_far]

        down_others.append(side_send(down_helds[-1]))
        down_mine = jnp.stack(down_helds)
        down_mine_got = box_send(down_mine, 1)
        down_early = jnp.stack(down_others[:-1])
        down_early_got = box_send(down_early, 1)
        down_others, down_mine, down_mine_got, down_early_got, act_blocks = gated(
            (down_others, down_mine, down_mine_got, down_early_got, act_blocks)
        )

        down_last_got = box_send(down_others[-1], 1)
        act_box = chip_exchange(act_blocks, chip)
        (down_full,) = assemble(
            where,
            [w_down],
            [
                in_order(down_mine),
                [(each, None) for each in down_others],
                in_order(down_mine_got),
                [(down_early_got, k) for k in range(last - 1)] + [(down_last_got, None)],
            ],
        )
        d_act = lax.dot_general(
            d_mlp, down_full, (((1,), (1,)), ((), ())), preferred_element_type=f32
        )
        unused_gelu, gelu_pull = jax.vjp(gelu_tanh, pre_act)
        d_pre = gelu_pull(d_act)[0].astype(bf16)

        def column_blocks(grad_t):
            n = grad_t.shape[0] // dp
            blocks = grad_t.reshape(groups, BOX, n, slots).transpose(1, 0, 2, 3)
            return blocks.reshape(BOX // 2, 2 * groups * n, slots)

        d_pre_blocks = column_blocks(d_pre.T)
        d_pre, d_pre_blocks, act_box, normed_two = gated(
            (d_pre, d_pre_blocks, act_box, normed_two)
        )

        d_pre_box = chip_exchange(d_pre_blocks, chip)
        normed_two_near = chip_near(normed_two)
        keep_down, send_down = row_grad(where_core, act_box, d_mlp_box)
        got_down = box_send(send_down, 1)
        d_normed_two = lax.dot_general(
            d_pre, up_full, (((1,), (1,)), ((), ())), preferred_element_type=f32
        )
        d_shift_two = jnp.sum(d_normed_two, axis=0)
        d_scale_two = jnp.sum(d_normed_two * norm_two, axis=0)
        d_middle = upstream + norm_back(norm_two, rate_two, d_normed_two * (1.0 + scale_two))
        d_gate_one = jnp.sum(d_middle * attn_out, axis=0)
        d_attn = (gate_one * d_middle).astype(bf16)
        d_attn_blocks = column_blocks(d_attn.T)
        d_attended = lax.dot_general(
            d_attn, out_full, (((1,), (1,)), ((), ())), preferred_element_type=f32
        )
        d_attended = d_attended.astype(bf16).reshape(slots, heads, HEAD_DIM)
        d_probs = jnp.einsum("qhe,khe->hqk", d_attended, values, preferred_element_type=f32)
        d_values = jnp.einsum(
            "hqk,qhe->khe", probs_low, d_attended, preferred_element_type=f32
        ).astype(bf16)
        row_inner = jnp.sum(probs * d_probs, axis=-1, keepdims=True)
        d_scores = (probs * (d_probs - row_inner)).astype(bf16)
        d_queries = (
            jnp.einsum("hqk,khe->qhe", d_scores, key_part, preferred_element_type=f32)
            * HEAD_DIM ** (-0.5)
        ).astype(bf16)
        d_keys = (
            jnp.einsum("hqk,qhe->khe", d_scores, queries, preferred_element_type=f32)
            * HEAD_DIM ** (-0.5)
        ).astype(bf16)
        d_projected = jnp.concatenate(
            [
                d_queries.reshape(slots, width),
                d_keys.reshape(slots, width),
                d_values.reshape(slots, width),
            ],
            axis=1,
        )
        d_projected_blocks = column_blocks(d_projected.T)
        (
            d_projected,
            d_projected_blocks,
            d_attn_blocks,
            d_pre_box,
            normed_two_near,
            keep_down,
            got_down,
            activated,
        ) = gated(
            (
                d_projected,
                d_projected_blocks,
                d_attn_blocks,
                d_pre_box,
                normed_two_near,
                keep_down,
                got_down,
                activated,
            )
        )

        d_projected_box = chip_exchange(d_projected_blocks, chip)
        normed_two_far = chip_far(normed_two_near)
        normed_two_box = [normed_two, *normed_two_near, *normed_two_far]
        d_attn_box = chip_exchange(d_attn_blocks, chip)
        d_normed = lax.dot_general(
            d_projected, qkv_full, (((1,), (1,)), ((), ())), preferred_element_type=f32
        )
        d_shift_one = jnp.sum(d_normed, axis=0)
        d_scale_one = jnp.sum(d_normed * norm_one, axis=0)
        grad_tokens = d_middle + norm_back(norm_one, rate_one, d_normed * (1.0 + scale_one))
        mlp_out = jnp.dot(activated, down_full, preferred_element_type=f32) + bias_down
        output = (live_rows * (middle + gate_two * mlp_out)).astype(bf16)
        d_gate_two = jnp.sum(upstream * mlp_out, axis=0)

        def weight_grad(lefts, rights):
            keep, send = column_grad(where_core, lefts, rights)
            grad, *sends = split_grad(where[:1], keep, box_send(send, 1))
            for k, sent in enumerate(sends):
                grad = grad + ring_send(sent, k + 1).astype(f32)
            rows, cols = grad.shape
            grad = grad.reshape(rows, groups, cols // groups)
            return group_sum(grad.transpose(1, 0, 2), group)

        grad_down = ring_sum(keep_down + got_down, z)
        down_rows = grad_down.shape[0]
        grad_down = grad_down.reshape(down_rows, groups, width // groups)
        grad_down = group_sum(grad_down.transpose(1, 0, 2), group)
        down_blocks = grad_down.reshape(down_rows, BOX, width // dp).transpose(1, 0, 2)
        if groups == 1:
            parts = lax.all_to_all(down_blocks, "dp", 0, 0, tiled=True)
        else:
            parts = [pick(down_blocks, place)] + [
                box_send(pick(down_blocks, place ^ k), k) for k in range(1, BOX)
            ]
            parts = jnp.stack(parts)
            parts = jnp.stack([pick(parts, place ^ k) for k in range(BOX)])
        grad_w_down = parts.reshape(BOX * down_rows, width // dp)
        grad_w_up = weight_grad(normed_two_box, d_pre_box)
        grad_w_out = weight_grad(attended_box, d_attn_box)
        grad_w_qkv = weight_grad(normed_box, d_projected_box)

        def row_sum(array):
            return jnp.sum(array.astype(f32), axis=0)

        d_mod = [d_shift_one, d_scale_one, d_gate_one, d_shift_two, d_scale_two, d_gate_two]
        images = jnp.stack(d_mod + [cond_act.astype(f32), cond_act.astype(f32)]).astype(bf16)
        total = [
            row_sum(d_projected[:, :width]),
            row_sum(d_projected[:, 2 * width :]),
            row_sum(d_attn),
            row_sum(d_mlp),
            row_sum(d_pre),
        ]
        total = jnp.concatenate([each.reshape(-1, width) for each in total])
        images_near = jnp.stack(ring_gather(images))
        totals = ring_gather(total)
        total = sum(totals[1:], totals[0])
        images = images_near
        for bits in (1, 2, 4):
            images = jnp.concatenate([images, box_send(images, bits)])
            total = total + box_send(total, bits)
        images_box, total_box = images, total
        for k in range(1, groups):
            images = jnp.concatenate([images, group_send(images_box, k)])
            total = total + group_send(total_box, k)
        conds_all = lax.dynamic_slice_in_dim(images[:, 6], z * rows_z, rows_z, 1)
        d_mod_all = images[:, :6]
        ada_cols = 6 * width // dp
        grad_w_ada = lax.dot_general(
            conds_all,
            lax.dynamic_slice_in_dim(
                d_mod_all.reshape(dp * fs, 6 * width), rank * ada_cols, ada_cols, 1
            ),
            (((0,), (0,)), ((), ())),
            preferred_element_type=f32,
        )
        d_conds = lax.dot_general(
            images_near[:, :6].reshape(fs, 6 * width),
            w_ada,
            (((1,), (1,)), ((), ())),
            preferred_element_type=f32,
        )
        cond_parts = [d_conds[0]] + [ring_send(d_conds[k], fs - k) for k in range(1, fs)]
        twice = jnp.stack(cond_parts + cond_parts)
        d_cond_act = lax.dynamic_slice_in_dim(twice, lax.rem(fs - z, fs), fs, 0).reshape(-1)
        grad_condition = d_cond_act * gate * (1.0 + cond_wide * (1.0 - gate))

        def shard_of(rows):
            return pick(rows.reshape(fs, -1), z)

        grads_bias = [
            shard_of(jnp.sum(d_mod_all.astype(f32), axis=0)),
            shard_of(total[:2]),
            shard_of(total[2]),
            shard_of(total[4:]),
            shard_of(total[3]),
        ]
        return (
            output[None],
            grad_tokens.astype(bf16)[None],
            grad_condition[None],
            grad_w_ada,
            grad_w_qkv,
            grad_w_out,
            grad_w_up,
            grad_w_down,
            *grads_bias,
        )

    return body


def solution(mesh):
    return jax.shard_map(
        make_body(mesh.shape["dp"], mesh.shape["fsdp"]),
        mesh=mesh,
        in_specs=(
            P(("dp", "fsdp"), None, None),
            P(("dp", "fsdp"), None),
            P(("dp", "fsdp"), None),
            P("fsdp", None),
            P("fsdp", None),
            P("fsdp", None),
            P("fsdp", None),
            P("fsdp", None),
            P("fsdp"),
            P("fsdp"),
            P("fsdp"),
            P("fsdp"),
            P("fsdp"),
            P(("dp", "fsdp"), None, None),
        ),
        out_specs=(
            P(("dp", "fsdp"), None, None),
            P(("dp", "fsdp"), None, None),
            P(("dp", "fsdp"), None),
            P("fsdp", "dp"),
            P("fsdp", "dp"),
            P("fsdp", "dp"),
            P("fsdp", "dp"),
            P("fsdp", "dp"),
            P("fsdp"),
            P("fsdp"),
            P("fsdp"),
            P("fsdp"),
            P("fsdp"),
        ),
        check_vma=False,
    )
```

```python
import math

import jax
import jax.numpy as jnp
from jax import lax
from jax.experimental import pallas as pl
from jax.experimental.pallas import tpu as pltpu
from jax.sharding import PartitionSpec as P

HEAD_DIM = 72
BOX = 8

epsilon = 1e-06
masked_value = -1e30
gelu_root = math.sqrt(2.0 / math.pi)
f32 = jnp.float32
bf16 = jnp.bfloat16


def norm_parts(values_in):
    centred = values_in - jnp.mean(values_in, axis=-1, keepdims=True)
    spread = jnp.mean(centred * centred, axis=-1, keepdims=True)
    rate = lax.rsqrt(spread + epsilon)
    return centred * rate, rate


def norm_back(normal, rate, grad):
    mean_grad = jnp.mean(grad, axis=-1, keepdims=True)
    mean_both = jnp.mean(grad * normal, axis=-1, keepdims=True)
    return rate * (grad - mean_grad - normal * mean_both)


def gelu_tanh(pre_act):
    return (
        0.5
        * pre_act
        * (1.0 + jnp.tanh(gelu_root * (pre_act + 0.044715 * pre_act * pre_act * pre_act)))
    )


def after(value, other):
    return lax.optimization_barrier((value, other))[0]


def gated(values):
    return lax.optimization_barrier(values)


def pick(array, index, axis=0):
    return lax.dynamic_index_in_dim(array, index, axis, keepdims=False)


def make_body(dp, fs):
    groups = dp // BOX

    def box_send(x, bits):
        return lax.ppermute(x, "dp", [(i, i ^ bits) for i in range(dp)])

    def side_send(x):
        return lax.ppermute(x, "dp", [(i, i ^ (4 if i & 1 else 2)) for i in range(dp)])

    def ring_send(x, hops):
        return lax.ppermute(x, "fsdp", [(i, (i + hops) % fs) for i in range(fs)])

    def group_send(x, hops):
        return lax.ppermute(x, "dp", [(i, (i + hops * BOX) % dp) for i in range(dp)])

    def ring_gather(x):
        return [x] + [ring_send(x, k) for k in range(1, fs)]

    def ring_sorted(blocks, z):
        back = jnp.stack(blocks[::-1] + blocks[::-1])
        return lax.dynamic_slice_in_dim(back, fs - 1 - z, fs, 0)

    def chip_near(x):
        return box_send(x, 2), box_send(x, 4)

    def chip_far(near):
        half = near[0].shape[0] // 2
        return box_send(near[0][:half], 4), box_send(near[1][half:], 2)

    def chip_exchange(blocks, chip):
        return [pick(blocks, chip)] + [
            box_send(pick(blocks, chip ^ k), 2 * k) for k in range(1, BOX // 2)
        ]

    def ring_sum(x, z):
        total = pick(x, z)
        for k in range(1, fs):
            sent = pick(x, lax.rem(z + k, fs)).astype(bf16)
            total = total + ring_send(sent, k).astype(f32)
        return total

    def group_sum(x, group):
        total = pick(x, group)
        for k in range(1, groups):
            total = total + group_send(pick(x, lax.rem(group + k, groups)), k)
        return total

    def cost(microseconds):
        return pl.CostEstimate(
            flops=int(microseconds * 5e8),
            transcendentals=0,
            bytes_accessed=int(microseconds * 1.6e6),
        )

    vmem = pl.BlockSpec(memory_space=pltpu.VMEM)
    smem = pl.BlockSpec(memory_space=pltpu.SMEM)

    def params(mebibytes):
        return pltpu.CompilerParams(vmem_limit_bytes=mebibytes << 20)

    def chunks(rows, step, work):
        def one(i, unused):
            work(pl.ds(pl.multiple_of(i * step, step), step), i * step)
            return unused

        lax.fori_loop(0, rows // step, one, 0)

    def alive_rows(first, rows, live):
        return ((lax.broadcasted_iota(jnp.int32, (rows, 1), 0) + first) < live).astype(f32)

    def modulation_parts(conds, w_ada, bias_ada, extra):
        images = conds.shape[0]
        parts, width = bias_ada.shape

        def kernel(cond_ref, w_ref, bias_ref, extra_ref, *out_refs):
            for part in range(parts):
                cols = slice(part * width, (part + 1) * width)
                product = jnp.dot(cond_ref[...], w_ref[:, cols], preferred_element_type=f32)
                product = product + bias_ref[part : part + 1, :]
                for image, out_ref in enumerate(out_refs):
                    out_ref[part : part + 1, :] = product[image : image + 1, :]
            for out_ref in out_refs:
                out_ref[parts:, :] = extra_ref[...]

        rows = parts + extra.shape[0]
        return pl.pallas_call(
            kernel,
            out_shape=[jax.ShapeDtypeStruct((rows, width), f32)] * images,
            in_specs=[vmem] * 4,
            out_specs=[vmem] * images,
            cost_estimate=cost(4),
            compiler_params=params(60),
        )(conds, w_ada, bias_ada, extra)

    def modulation_rows(partials, live):
        rows, width = partials[0].shape

        def kernel(live_ref, *refs):
            mods_ref, head_ref = refs[-2:]
            total = refs[0][...]
            for ref in refs[1:-2]:
                total = total + ref[...]
            mods_ref[...] = total
            head_ref[...] = jnp.full(head_ref.shape, live_ref[0].astype(f32))
            head_ref[0:2, :] = total[0:2, :]
            head_ref[2:3, :] = total[5:6, :]

        return pl.pallas_call(
            kernel,
            out_shape=[jax.ShapeDtypeStruct((rows, width), f32)] * 2,
            in_specs=[smem] + [vmem] * len(partials),
            out_specs=[vmem] * 2,
            cost_estimate=cost(1),
            compiler_params=params(60),
        )(live, *partials)

    def other_heads(raws, firsts, heads):
        n = len(raws)
        width = raws[0].shape[1] // 2

        def kernel(*refs):
            raw_refs, head_refs = refs[:n], refs[n : 2 * n]
            normed_refs, d_mlp_refs = refs[2 * n : 3 * n], refs[3 * n :]
            for raw, head, normed, d_mlp, first in zip(
                raw_refs, head_refs, normed_refs, d_mlp_refs, firsts
            ):
                live = head[3, 0].astype(jnp.int32)

                def work(rows, start):
                    normal = norm_parts(raw[rows, :width].astype(f32))[0]
                    normed[rows, :] = (
                        normal * (1.0 + head[1:2, :]) + head[0:1, :]
                    ).astype(bf16)
                    count = normal.shape[0]
                    up_rows = alive_rows(start + first, count, live) * raw[
                        rows, width:
                    ].astype(f32)
                    d_mlp[rows, :] = (head[2:3, :] * up_rows).astype(bf16)

                chunks(raw.shape[0], 32, work)

        outs = pl.pallas_call(
            kernel,
            out_shape=[jax.ShapeDtypeStruct((raw.shape[0], width), bf16) for raw in raws] * 2,
            in_specs=[vmem] * (2 * n),
            out_specs=[vmem] * (2 * n),
            cost_estimate=cost(8),
            compiler_params=params(60),
        )(*raws, *heads)
        return outs[:n], outs[n:]

    def piece_plan(pieces):
        arrays = []
        for piece, unused in (each for kind in pieces for each in kind):
            if not any(piece is array for array in arrays):
                arrays.append(piece)
        position = {id(array): i for i, array in enumerate(arrays)}
        plan = [[(position[id(piece)], index) for piece, index in kind] for kind in pieces]
        return arrays, plan

    def piece_copies(where_ref, own_ref, array_refs, plan, whole_ref):
        copies = [(own_ref, whole_ref.at[where_ref[0]])]
        for kind, blocks in enumerate(plan):
            for k, (which, index) in enumerate(blocks):
                source = array_refs[which] if index is None else array_refs[which].at[index]
                copies.append((source, whole_ref.at[where_ref[k + 1], where_ref[fs + kind]]))
        return copies

    def wide_copies(core, where_ref, own_refs, sets, whole_refs):
        widths = [ref.shape[-1] for ref in own_refs]
        width, part = sum(widths), sets[0][0].shape[-1]
        lead, split = whole_refs[0].shape[2], sets[0][3].shape[0]
        copies = [(own, whole.at[where_ref[0]]) for own, whole in zip(own_refs, whole_refs)]
        for side, piece_refs in enumerate(sets):
            low, high = (0, part) if core ^ side == 0 else (part, width)
            offset = 0 if core ^ side == 0 else width - part
            for block in range(1, fs):
                base = (block - 1) * lead
                top = min(max(split - base, 0), lead)
                rows = [(i, base, i, 0, lead) for i in range(3)]
                if top:
                    rows.append((3, base, 3, 0, top))
                if top < lead:
                    rows.append((4, base + top - split, 3, top, lead - top))
                for piece, first, slot, row, count in rows:
                    start = 0
                    for i, each in enumerate(widths):
                        left, right = max(low, start), min(high, start + each)
                        if left < right:
                            source = piece_refs[piece].at[
                                first : first + count, :, left - offset : right - offset
                            ]
                            target = whole_refs[i].at[
                                where_ref[block],
                                where_ref[fs + 1 + slot],
                                row : row + count,
                                :,
                                left - start : right - start,
                            ]
                            copies.append((source, target))
                        start += each
        return copies

    def copy_all(copies, sems):
        return [
            pltpu.make_async_copy(source, target, sems.at[j])
            for j, (source, target) in enumerate(copies)
        ]

    def start_all(copies):
        for copy in copies:
            copy.start()

    def wait_all(copies):
        for copy in copies:
            copy.wait()

    def in_blocks(shard):
        rows, cols = shard.shape
        return shard.reshape(4, rows // 32, 8, cols)

    any_spec = pl.BlockSpec(memory_space=pl.ANY)

    def projection(where, normed, own, pieces, biases):
        slots, width = normed.shape
        arrays, plan = piece_plan(pieces)
        own = in_blocks(own)
        shape = (fs,) + own.shape

        def kernel(where_ref, normed_ref, bias_ref, own_ref, *refs):
            array_refs = refs[: len(arrays)]
            turned_ref, whole_ref, scratch, sems, out_sem = refs[len(arrays) :]
            copies = copy_all(
                piece_copies(where_ref, own_ref, array_refs, plan, scratch), sems
            )
            start_all(copies)
            wait_all(copies)
            out = pltpu.make_async_copy(scratch, whole_ref, out_sem)
            out.start()
            w_ref = scratch.reshape(width, 3 * width)
            for part in range(3):
                cols = slice(part * width, (part + 1) * width)
                proj = jnp.dot(normed_ref[...], w_ref[:, cols], preferred_element_type=f32)
                if part != 1:
                    proj = proj + bias_ref[part // 2 : part // 2 + 1, :]
                turned_ref[cols, :] = proj.astype(bf16).astype(f32).T
            out.wait()

        turned, whole = pl.pallas_call(
            kernel,
            out_shape=[
                jax.ShapeDtypeStruct((3 * width, slots), f32),
                jax.ShapeDtypeStruct(shape, bf16),
            ],
            in_specs=[smem, vmem, vmem, any_spec] + [any_spec] * len(arrays),
            out_specs=[vmem, any_spec],
            scratch_shapes=[
                pltpu.VMEM(shape, bf16),
                pltpu.SemaphoreType.DMA((1 + 4 * (fs - 1),)),
                pltpu.SemaphoreType.DMA,
            ],
            cost_estimate=cost(11),
            compiler_params=params(60),
        )(where, normed, biases, own, *arrays)
        return turned, whole.reshape(width, 3 * width)

    def attention(turned, live):
        slots = turned.shape[1]
        width = turned.shape[0] // 3
        count = width // HEAD_DIM
        scale = HEAD_DIM ** (-0.5)

        def kernel(live_ref, turned_ref, attended_ref, out_turned):
            live_keys = lax.broadcasted_iota(jnp.int32, (1, slots), 1) < live_ref[0]

            def head(h, unused):
                def rows(part):
                    first = pl.multiple_of(part * width + h * HEAD_DIM, 8)
                    return turned_ref[pl.ds(first, HEAD_DIM), :].astype(bf16)

                scores = lax.dot_general(
                    rows(0), rows(1), (((0,), (0,)), ((), ())), preferred_element_type=f32
                )
                scores = jnp.where(live_keys, scores * scale, masked_value)
                highest = jnp.max(scores, axis=-1, keepdims=True)
                total = jnp.sum(jnp.exp(scores - highest), axis=-1, keepdims=True)
                probs = jnp.exp(scores - (highest + jnp.log(total)))
                out = lax.dot_general(
                    rows(2),
                    probs.astype(bf16),
                    (((1,), (1,)), ((), ())),
                    preferred_element_type=f32,
                )
                out_turned[pl.ds(pl.multiple_of(h * HEAD_DIM, 8), HEAD_DIM), :] = out
                return unused

            lax.fori_loop(0, count, head, 0)
            attended_ref[...] = out_turned[...].T.astype(bf16)

        return pl.pallas_call(
            kernel,
            out_shape=jax.ShapeDtypeStruct((slots, width), bf16),
            in_specs=[smem, vmem],
            out_specs=vmem,
            scratch_shapes=[pltpu.VMEM((width, slots), f32)],
            cost_estimate=cost(11),
            compiler_params=params(60),
        )(live, turned)

    def attention_back(turned, d_turned, live):
        width, slots = d_turned.shape
        count = width // HEAD_DIM
        scale = HEAD_DIM ** (-0.5)

        def kernel(live_ref, turned_ref, d_ref, out_ref, total_ref):
            live_keys = lax.broadcasted_iota(jnp.int32, (1, slots), 1) < live_ref[0]

            def head(h, unused):
                def place(part):
                    return pl.ds(pl.multiple_of(part * width + h * HEAD_DIM, 8), HEAD_DIM)

                query = turned_ref[place(0), :].astype(bf16)
                key_part = turned_ref[place(1), :].astype(bf16)
                value = turned_ref[place(2), :].astype(bf16)
                d_out = d_ref[place(0), :].astype(bf16)
                both_first = (((0,), (0,)), ((), ()))
                scores = lax.dot_general(
                    query, key_part, both_first, preferred_element_type=f32
                )
                scores = jnp.where(live_keys, scores * scale, masked_value)
                highest = jnp.max(scores, axis=-1, keepdims=True)
                total = jnp.sum(jnp.exp(scores - highest), axis=-1, keepdims=True)
                probs = jnp.exp(scores - (highest + jnp.log(total)))
                d_probs = lax.dot_general(
                    d_out, value, both_first, preferred_element_type=f32
                )
                inner = jnp.sum(probs * d_probs, axis=-1, keepdims=True)
                d_scores = (probs * (d_probs - inner)).astype(bf16)
                total_ref[place(2), :] = jnp.dot(
                    d_out, probs.astype(bf16), preferred_element_type=f32
                )
                total_ref[place(0), :] = scale * lax.dot_general(
                    key_part, d_scores, (((1,), (1,)), ((), ())), preferred_element_type=f32
                )
                total_ref[place(1), :] = scale * jnp.dot(
                    query, d_scores, preferred_element_type=f32
                )
                return unused

            lax.fori_loop(0, count, head, 0)
            out_ref[...] = total_ref[...].astype(bf16)

        return pl.pallas_call(
            kernel,
            out_shape=jax.ShapeDtypeStruct((3 * width, slots), bf16),
            in_specs=[smem, vmem, vmem],
            out_specs=vmem,
            scratch_shapes=[pltpu.VMEM((3 * width, slots), f32)],
            cost_estimate=cost(12),
            compiler_params=params(60),
        )(live, turned, d_turned)

    def middle_forward(where, attended, tokens_own, owns, sets, bias_out, bias_up, mods):
        slots, width = attended.shape
        owns = [in_blocks(own) for own in owns]
        hidden = owns[1].shape[-1]
        tile = hidden // fs
        quarter = tile // 4
        shapes = [(fs,) + own.shape for own in owns]
        n_pieces = len(sets[0])
        n_copies = 2 + 2 * 15 * (fs - 1)

        def kernel(where_ref, attended_ref, tokens_ref, bias_out_ref, bias_up_ref, mods_ref, *refs):
            own_refs = refs[:2]
            set_refs = (refs[2 : 2 + n_pieces], refs[2 + n_pieces : 2 + 2 * n_pieces])
            (
                attn_ref,
                normed_ref,
                pre_ref,
                act_ref,
                turned_ref,
                whole_out,
                whole_up,
                scratch_out,
                scratch_up,
                sems,
                out_sems,
            ) = refs[2 + 2 * n_pieces :]
            step = pl.program_id(0)
            scratches, wholes = (scratch_out, scratch_up), (whole_out, whole_up)

            def outs():
                return [
                    pltpu.make_async_copy(scratch, whole, out_sems.at[i])
                    for i, (scratch, whole) in enumerate(zip(scratches, wholes))
                ]

            @pl.when(step == 0)
            def first():
                for core in range(2):

                    @pl.when(where_ref[fs] == core)
                    def gather(core=core):
                        copies = copy_all(
                            wide_copies(core, where_ref, own_refs, set_refs, scratches), sems
                        )
                        start_all(copies)
                        wait_all(copies)

                start_all(outs())
                attn_ref[...] = (
                    jnp.dot(
                        attended_ref[...],
                        scratch_out.reshape(width, width)[...],
                        preferred_element_type=f32,
                    )
                    + bias_out_ref[...]
                )

                def work(rows, unused):
                    middle = tokens_ref[rows, :].astype(f32) + mods_ref[2:3, :] * attn_ref[rows, :]
                    normal = norm_parts(middle)[0]
                    normed_ref[rows, :] = (
                        normal * (1.0 + mods_ref[4:5, :]) + mods_ref[3:4, :]
                    ).astype(bf16)

                chunks(slots, 32, work)

            cols = pl.ds(pl.multiple_of(step * tile, 128), tile)
            pre_ref[...] = (
                jnp.dot(
                    normed_ref[...],
                    scratch_up.reshape(width, hidden)[:, cols],
                    preferred_element_type=f32,
                )
                + bias_up_ref[0]
            )

            def work(rows, unused):
                act_ref[rows, :] = gelu_tanh(pre_ref[rows, :]).astype(bf16)

            chunks(slots, 32, work)
            for chip in range(4):
                cols = slice(chip * quarter, (chip + 1) * quarter)
                turned_ref[chip, :, :] = act_ref[:, cols].astype(f32).T.astype(bf16)

            @pl.when(step == fs - 1)
            def last():
                wait_all(outs())

        def whole(shape):
            return pl.BlockSpec(shape, lambda j, where_ref: (0,) * len(shape))

        *results, whole_out, whole_up = pl.pallas_call(
            kernel,
            out_shape=[
                jax.ShapeDtypeStruct((slots, width), f32),
                jax.ShapeDtypeStruct((slots, width), bf16),
                jax.ShapeDtypeStruct((slots, hidden), f32),
                jax.ShapeDtypeStruct((slots, hidden), bf16),
                jax.ShapeDtypeStruct((4, fs * quarter, slots), bf16),
            ]
            + [jax.ShapeDtypeStruct(shape, bf16) for shape in shapes],
            grid_spec=pltpu.PrefetchScalarGridSpec(
                num_scalar_prefetch=1,
                grid=(fs,),
                in_specs=[
                    whole((slots, width)),
                    whole((slots, width)),
                    whole((1, width)),
                    pl.BlockSpec((1, 1, tile), lambda j, where_ref: (j, 0, 0)),
                    whole(mods.shape),
                ]
                + [any_spec] * (2 + 2 * n_pieces),
                out_specs=[
                    whole((slots, width)),
                    whole((slots, width)),
                    pl.BlockSpec((slots, tile), lambda j, where_ref: (0, j)),
                    pl.BlockSpec((slots, tile), lambda j, where_ref: (0, j)),
                    pl.BlockSpec((4, quarter, slots), lambda j, where_ref: (0, j, 0)),
                    any_spec,
                    any_spec,
                ],
                scratch_shapes=[pltpu.VMEM(shape, bf16) for shape in shapes]
                + [pltpu.SemaphoreType.DMA((n_copies,)), pltpu.SemaphoreType.DMA((2,))],
            ),
            cost_estimate=cost(20),
            compiler_params=params(60),
        )(
            where,
            attended,
            tokens_own,
            bias_out.reshape(1, width),
            bias_up.reshape(fs, 1, tile),
            mods,
            *owns,
            *sets[0],
            *sets[1],
        )
        return (
            *results,
            whole_out.reshape(width, width),
            whole_up.reshape(width, hidden),
        )

    def hidden_back(where, d_mlp, own, pieces, pre_act):
        slots, width = d_mlp.shape
        hidden = pre_act.shape[1]
        tile = hidden // fs
        arrays, plan = piece_plan(pieces)
        own = in_blocks(own)
        shape = (fs,) + own.shape

        def kernel(where_ref, d_mlp_ref, pre_ref, own_ref, *refs):
            array_refs = refs[: len(arrays)]
            (
                d_pre_ref,
                turned_ref,
                sum_ref,
                whole_ref,
                d_act_ref,
                scratch,
                sems,
                out_sem,
            ) = refs[len(arrays) :]
            step = pl.program_id(0)

            def out():
                return pltpu.make_async_copy(scratch, whole_ref, out_sem)

            @pl.when(step == 0)
            def first():
                copies = copy_all(
                    piece_copies(where_ref, own_ref, array_refs, plan, scratch), sems
                )
                start_all(copies)
                wait_all(copies)
                out().start()

            d_act_ref[...] = lax.dot_general(
                d_mlp_ref[...],
                scratch.at[step].reshape(tile, width)[...],
                (((1,), (1,)), ((), ())),
                preferred_element_type=f32,
            )

            def work(rows, unused):
                pre = pre_ref[rows, :]
                square = pre * pre
                bend = jnp.tanh(gelu_root * (pre + 0.044715 * square * pre))
                slope = 0.5 * (1.0 + bend) + 0.5 * pre * (1.0 - bend * bend) * gelu_root * (
                    1.0 + 3.0 * 0.044715 * square
                )
                d_pre = (d_act_ref[rows, :] * slope).astype(bf16)
                d_pre_ref[rows, :] = d_pre
                d_act_ref[rows, :] = d_pre.astype(f32)

            chunks(slots, 32, work)
            sum_ref[0] = jnp.sum(d_act_ref[...], axis=0, keepdims=True)
            turned_ref[...] = d_act_ref[...].T.astype(bf16)

            @pl.when(step == fs - 1)
            def last():
                out().wait()

        *results, whole = pl.pallas_call(
            kernel,
            out_shape=[
                jax.ShapeDtypeStruct((slots, hidden), bf16),
                jax.ShapeDtypeStruct((hidden, slots), bf16),
                jax.ShapeDtypeStruct((fs, 1, tile), f32),
                jax.ShapeDtypeStruct(shape, bf16),
            ],
            grid_spec=pltpu.PrefetchScalarGridSpec(
                num_scalar_prefetch=1,
                grid=(fs,),
                in_specs=[
                    pl.BlockSpec((slots, width), lambda j, where_ref: (0, 0)),
                    pl.BlockSpec((slots, tile), lambda j, where_ref: (0, j)),
                    any_spec,
                ]
                + [any_spec] * len(arrays),
                out_specs=[
                    pl.BlockSpec((slots, tile), lambda j, where_ref: (0, j)),
                    pl.BlockSpec((tile, slots), lambda j, where_ref: (j, 0)),
                    pl.BlockSpec((1, 1, tile), lambda j, where_ref: (j, 0, 0)),
                    any_spec,
                ],
                scratch_shapes=[
                    pltpu.VMEM((slots, tile), f32),
                    pltpu.VMEM(shape, bf16),
                    pltpu.SemaphoreType.DMA((1 + 4 * (fs - 1),)),
                    pltpu.SemaphoreType.DMA,
                ],
            ),
            cost_estimate=cost(15),
            compiler_params=params(60),
        )(where, d_mlp, pre_act, own, *arrays)
        return (*results, whole.reshape(hidden, width))

    def middle_back(d_pre, up_full, out_full, attn_out, tokens_own, cotangent_own, mods, live):
        slots, hidden = d_pre.shape
        width = attn_out.shape[1]
        tile = hidden // fs

        def kernel(
            live_ref,
            d_pre_ref,
            up_ref,
            out_ref,
            attn_ref,
            tokens_ref,
            cot_ref,
            mods_ref,
            d_middle_ref,
            d_attn_turned_ref,
            d_attended_turned_ref,
            sums_ref,
            total,
            d_attn_ref,
        ):
            step = pl.program_id(0)
            part = lax.dot_general(
                d_pre_ref[...],
                up_ref[...],
                (((1,), (1,)), ((), ())),
                preferred_element_type=f32,
            )

            @pl.when(step == 0)
            def start():
                total[...] = part

            @pl.when(step > 0)
            def add():
                total[...] += part

            @pl.when(step == fs - 1)
            def finish():
                sums_ref[...] = jnp.zeros_like(sums_ref)

                def work(rows, first):
                    grad = total[rows, :]
                    attn = attn_ref[rows, :]
                    middle = tokens_ref[rows, :].astype(f32) + mods_ref[2:3, :] * attn
                    normal, rate = norm_parts(middle)
                    alive = alive_rows(first, grad.shape[0], live_ref[0])
                    d_middle = alive * cot_ref[rows, :].astype(f32) + norm_back(
                        normal, rate, grad * (1.0 + mods_ref[4:5, :])
                    )
                    d_middle_ref[rows, :] = d_middle
                    d_attn = (mods_ref[2:3, :] * d_middle).astype(bf16)
                    d_attn_ref[rows, :] = d_attn
                    for i, each in enumerate(
                        (d_middle * attn, grad, grad * normal, d_attn.astype(f32))
                    ):
                        sums_ref[i : i + 1, :] += jnp.sum(each, axis=0, keepdims=True)

                chunks(slots, 32, work)
                d_attn_turned_ref[...] = d_attn_ref[...].astype(f32).T.astype(bf16)
                d_attended = lax.dot_general(
                    d_attn_ref[...],
                    out_ref[...],
                    (((1,), (1,)), ((), ())),
                    preferred_element_type=f32,
                )
                d_attended_turned_ref[...] = d_attended.astype(bf16).astype(f32).T

        def whole(shape):
            return pl.BlockSpec(shape, lambda j, live_ref: (0,) * len(shape))

        return pl.pallas_call(
            kernel,
            out_shape=[
                jax.ShapeDtypeStruct((slots, width), f32),
                jax.ShapeDtypeStruct((width, slots), bf16),
                jax.ShapeDtypeStruct((width, slots), f32),
                jax.ShapeDtypeStruct((8, width), f32),
            ],
            grid_spec=pltpu.PrefetchScalarGridSpec(
                num_scalar_prefetch=1,
                grid=(fs,),
                in_specs=[
                    pl.BlockSpec((slots, tile), lambda j, live_ref: (0, j)),
                    pl.BlockSpec((width, tile), lambda j, live_ref: (0, j)),
                    whole((width, width)),
                    whole((slots, width)),
                    whole((slots, width)),
                    whole((slots, width)),
                    whole(mods.shape),
                ],
                out_specs=[
                    whole((slots, width)),
                    whole((width, slots)),
                    whole((width, slots)),
                    whole((8, width)),
                ],
                scratch_shapes=[
                    pltpu.VMEM((slots, width), f32),
                    pltpu.VMEM((slots, width), bf16),
                ],
            ),
            cost_estimate=cost(12),
            compiler_params=params(60),
        )(live, d_pre, up_full, out_full, attn_out, tokens_own, cotangent_own, mods)

    def first_back(d_turned, qkv_full, tokens_own, d_middle, mods):
        slots, width = d_middle.shape

        def kernel(d_ref, w_ref, tokens_ref, d_middle_ref, mods_ref, grad_ref, sums_ref, total):
            sums_ref[...] = jnp.zeros_like(sums_ref)
            for part in range(3):
                cols = slice(part * width, (part + 1) * width)
                d_part = d_ref[cols, :].astype(f32).T
                if part != 1:
                    row = 2 + part // 2
                    sums_ref[row : row + 1, :] = jnp.sum(d_part, axis=0, keepdims=True)
                product = lax.dot_general(
                    d_part.astype(bf16),
                    w_ref[:, cols],
                    (((1,), (1,)), ((), ())),
                    preferred_element_type=f32,
                )
                if part == 0:
                    total[...] = product
                else:
                    total[...] += product

            def work(rows, unused):
                grad = total[rows, :]
                normal, rate = norm_parts(tokens_ref[rows, :].astype(f32))
                sums_ref[0:1, :] += jnp.sum(grad, axis=0, keepdims=True)
                sums_ref[1:2, :] += jnp.sum(grad * normal, axis=0, keepdims=True)
                grad_ref[rows, :] = (
                    d_middle_ref[rows, :]
                    + norm_back(normal, rate, grad * (1.0 + mods_ref[1:2, :]))
                ).astype(bf16)

            chunks(slots, 32, work)

        return pl.pallas_call(
            kernel,
            out_shape=[
                jax.ShapeDtypeStruct((slots, width), bf16),
                jax.ShapeDtypeStruct((8, width), f32),
            ],
            in_specs=[vmem] * 5,
            out_specs=[vmem] * 2,
            scratch_shapes=[pltpu.VMEM((slots, width), f32)],
            cost_estimate=cost(9),
            compiler_params=params(60),
        )(d_turned, qkv_full, tokens_own, d_middle, mods)

    def output_rows(
        activated, down_full, bias_down, tokens_own, attn_out, cotangent_own, d_mlp, mods, live
    ):
        slots, hidden = activated.shape
        width = attn_out.shape[1]
        tile = hidden // fs

        def kernel(
            live_ref,
            act_ref,
            down_ref,
            bias_ref,
            tokens_ref,
            attn_ref,
            cot_ref,
            d_mlp_ref,
            mods_ref,
            out_ref,
            sums_ref,
            total,
        ):
            step = pl.program_id(0)
            part = jnp.dot(act_ref[...], down_ref[...], preferred_element_type=f32)

            @pl.when(step == 0)
            def start():
                total[...] = part

            @pl.when(step > 0)
            def add():
                total[...] += part

            @pl.when(step == fs - 1)
            def finish():
                sums_ref[...] = jnp.zeros_like(sums_ref)

                def work(rows, first):
                    mlp_out = total[rows, :] + bias_ref[...]
                    middle = (
                        tokens_ref[rows, :].astype(f32) + mods_ref[2:3, :] * attn_ref[rows, :]
                    )
                    alive = alive_rows(first, mlp_out.shape[0], live_ref[0])
                    out_ref[rows, :] = (alive * (middle + mods_ref[5:6, :] * mlp_out)).astype(bf16)
                    d_gate = alive * cot_ref[rows, :].astype(f32) * mlp_out
                    sums_ref[0:1, :] += jnp.sum(d_gate, axis=0, keepdims=True)
                    sums_ref[1:2, :] += jnp.sum(
                        d_mlp_ref[rows, :].astype(f32), axis=0, keepdims=True
                    )

                chunks(slots, 32, work)

        def whole(shape):
            return pl.BlockSpec(shape, lambda j, live_ref: (0,) * len(shape))

        return pl.pallas_call(
            kernel,
            out_shape=[
                jax.ShapeDtypeStruct((slots, width), bf16),
                jax.ShapeDtypeStruct((8, width), f32),
            ],
            grid_spec=pltpu.PrefetchScalarGridSpec(
                num_scalar_prefetch=1,
                grid=(fs,),
                in_specs=[
                    pl.BlockSpec((slots, tile), lambda j, live_ref: (0, j)),
                    pl.BlockSpec((tile, width), lambda j, live_ref: (j, 0)),
                    whole((1, width)),
                    whole((slots, width)),
                    whole((slots, width)),
                    whole((slots, width)),
                    whole((slots, width)),
                    whole(mods.shape),
                ],
                out_specs=[whole((slots, width)), whole((8, width))],
                scratch_shapes=[pltpu.VMEM((slots, width), f32)],
            ),
            cost_estimate=cost(6),
            compiler_params=params(60),
        )(
            live,
            activated,
            down_full,
            bias_down.reshape(1, width),
            tokens_own,
            attn_out,
            cotangent_own,
            d_mlp,
            mods,
        )

    def column_grad(where, lefts, rights, start, stop):
        slots, n = rights[0].shape[1], (stop - start) // 2
        right_rows = rights[0].shape[0]
        width = lefts[0].shape[1]
        tile = width // 3
        half = slots // 2

        def kernel(where_ref, x0, x1, x2, x3, x4, y0, y1, y2, y3, keep_ref, send_ref):
            core = where_ref[0]
            for out_ref, first in ((keep_ref, core * n), (send_ref, (1 - core) * n)):
                rows = pl.ds(pl.multiple_of(start + first, 16), n)
                total = None
                for x, y, cols in (
                    (x0, y0, slice(None)),
                    (x1, y1, slice(None)),
                    (x2, y2, slice(None)),
                    (x3, y3, slice(0, half)),
                    (x4, y3, slice(half, slots)),
                ):
                    part = jnp.dot(y[rows, cols], x[...], preferred_element_type=f32)
                    total = part if total is None else total + part
                out_ref[...] = total

        left_specs = [
            pl.BlockSpec((left.shape[0], tile), lambda i, where_ref: (0, i)) for left in lefts
        ]
        right_spec = pl.BlockSpec((right_rows, slots), lambda i, where_ref: (0, 0))
        out_spec = pl.BlockSpec((n, tile), lambda i, where_ref: (0, i))
        return pl.pallas_call(
            kernel,
            out_shape=[jax.ShapeDtypeStruct((n, width), f32)] * 2,
            grid_spec=pltpu.PrefetchScalarGridSpec(
                num_scalar_prefetch=1,
                grid=(width // tile,),
                in_specs=left_specs + [right_spec] * 4,
                out_specs=[out_spec] * 2,
            ),
            cost_estimate=cost(7),
            compiler_params=params(60),
        )(where, *lefts, *rights)

    def split_grad(where, keep, got):
        n, width = keep.shape
        rows = width // fs
        padded = -(-n // 128) * 128

        def kernel(where_ref, keep_ref, got_ref, own_ref, *rest):
            send_refs, turned = rest[:-1], rest[-1]
            for first in range(0, width, 128):
                total = keep_ref[:, first : first + 128] + got_ref[:, first : first + 128]
                if padded > n:
                    total = jnp.concatenate([total, jnp.zeros((padded - n, 128), f32)], axis=0)
                turned[first : first + 128, :] = total.T[:, :n]
            z = where_ref[0]
            own_ref[...] = turned[pl.ds(pl.multiple_of(z * rows, 16), rows), :]
            for k, send_ref in enumerate(send_refs):
                target = lax.rem(z + k + 1, fs)
                block = turned[pl.ds(pl.multiple_of(target * rows, 16), rows), :]
                send_ref[...] = block.astype(bf16)

        whole = pl.BlockSpec(memory_space=pltpu.VMEM)
        return pl.pallas_call(
            kernel,
            out_shape=[jax.ShapeDtypeStruct((rows, n), f32)]
            + [jax.ShapeDtypeStruct((rows, n), bf16)] * (fs - 1),
            in_specs=[pl.BlockSpec(memory_space=pltpu.SMEM), whole, whole],
            out_specs=[whole] * fs,
            scratch_shapes=[pltpu.VMEM((width, n), f32)],
            cost_estimate=cost(4),
            compiler_params=params(60),
        )(where, keep, got)

    def split_rows(where, keep, got):
        count, rows, width = keep.shape

        def kernel(where_ref, keep_ref, got_ref, own_ref, *send_refs):
            z = where_ref[0]
            own_ref[...] = keep_ref[z] + got_ref[z]
            for k, send_ref in enumerate(send_refs):
                target = lax.rem(z + k + 1, count)
                send_ref[...] = (keep_ref[target] + got_ref[target]).astype(bf16)

        return pl.pallas_call(
            kernel,
            out_shape=[jax.ShapeDtypeStruct((rows, width), f32)]
            + [jax.ShapeDtypeStruct((rows, width), bf16)] * (count - 1),
            in_specs=[smem, vmem, vmem],
            out_specs=[vmem] * count,
            cost_estimate=cost(3),
            compiler_params=params(60),
        )(where, keep, got)

    def down_columns(parts):
        rows, width = parts[0].shape
        cols = width // BOX

        def kernel(*refs):
            total = refs[0][...]
            for ref in refs[1:-1]:
                total = total + ref[...].astype(f32)
            for block in range(BOX):
                refs[-1][block] = total[:, block * cols : (block + 1) * cols]

        return pl.pallas_call(
            kernel,
            out_shape=jax.ShapeDtypeStruct((BOX, rows, cols), f32),
            in_specs=[vmem] * len(parts),
            out_specs=vmem,
            cost_estimate=cost(2),
            compiler_params=params(60),
        )(*parts)

    def row_grad(where, lefts, rights):
        rows = lefts[0].shape[0] // fs
        slots, n = lefts[0].shape[1], rows // 2
        width = rights[0].shape[1]
        half = slots // 2

        def kernel(where_ref, x0, x1, x2, x3, y0, y1, y2, y3, y4, keep_ref, send_ref):
            core = where_ref[0]
            for out_ref, first in ((keep_ref, core * n), (send_ref, (1 - core) * n)):
                lines = pl.ds(pl.multiple_of(first, 16), n)
                total = None
                for x, y, cols in (
                    (x0, y0, slice(None)),
                    (x1, y1, slice(None)),
                    (x2, y2, slice(None)),
                    (x3, y3, slice(0, half)),
                    (x3, y4, slice(half, slots)),
                ):
                    part = jnp.dot(x[lines, cols], y[...], preferred_element_type=f32)
                    total = part if total is None else total + part
                out_ref[0] = total

        left_spec = pl.BlockSpec((rows, slots), lambda i, where_ref: (i, 0))
        right_specs = [
            pl.BlockSpec((right.shape[0], width), lambda i, where_ref: (0, 0))
            for right in rights
        ]
        out_spec = pl.BlockSpec((1, n, width), lambda i, where_ref: (i, 0, 0))
        return pl.pallas_call(
            kernel,
            out_shape=[jax.ShapeDtypeStruct((fs, n, width), f32)] * 2,
            grid_spec=pltpu.PrefetchScalarGridSpec(
                num_scalar_prefetch=1,
                grid=(fs,),
                in_specs=[left_spec] * 4 + right_specs,
                out_specs=[out_spec] * 2,
            ),
            cost_estimate=cost(6),
            compiler_params=params(60),
        )(where, *lefts, *rights)

    def body(
        tokens,
        condition,
        grid_sizes,
        w_ada,
        w_qkv,
        w_out,
        w_up,
        w_down,
        b_ada,
        b_qv,
        b_out,
        b_up,
        b_down,
        cotangent,
    ):
        slots, width = tokens.shape[1:]
        heads = width // HEAD_DIM
        hidden = w_up.shape[1]
        rank = lax.axis_index("dp")
        z = lax.axis_index("fsdp")
        place = lax.rem(rank, BOX)
        group = lax.div(rank, BOX)
        core = place & 1
        chip = place >> 1
        side = (chip ^ (chip >> 1)) & 1
        near = 2 * side + core
        far = 2 * (1 - side) + core
        where = jnp.stack(
            [lax.rem(z - k + fs, fs) for k in range(fs)] + [near, far, near ^ 1, far ^ 1]
        ).astype(jnp.int32)
        where_core = core.reshape(1).astype(jnp.int32)
        where_wide = jnp.stack(
            [lax.rem(z - k + fs, fs) for k in range(fs)] + [core] + [chip ^ k for k in range(4)]
        ).astype(jnp.int32)

        cond_wide = condition.astype(f32)
        gate = jax.nn.sigmoid(cond_wide)
        cond_act = (cond_wide * gate).astype(bf16)

        def quarter_of(shard):
            return pick(in_blocks(shard), near)

        cond_rows = ring_gather(cond_act)
        raw = jnp.concatenate([tokens[0], cotangent[0]], axis=1)
        raw_near = chip_near(raw)
        qkv_helds = [ring_send(quarter_of(w_qkv), 1)]
        mid_rows = jnp.concatenate(
            [pick(in_blocks(w_out), chip), pick(in_blocks(w_up), chip)], axis=-1
        )
        mid_width = mid_rows.shape[-1]
        mid_part = -(-mid_width // 256) * 128
        mid_start = jnp.where(core == 0, 0, mid_width - mid_part)
        mid_eighth = lax.dynamic_slice_in_dim(mid_rows, mid_start, mid_part, 2)
        down_quarter = quarter_of(w_down)
        ada_shard = b_ada.shape[0]
        bias_ada = lax.dynamic_update_slice_in_dim(
            jnp.zeros((fs * ada_shard,), f32), b_ada.astype(f32), z * ada_shard, 0
        ).reshape(6, width)
        small = jnp.concatenate([b_qv, b_out, b_down, b_up]).astype(f32).reshape(-1, width)
        cond_rows, bias_ada, small, mid_eighth, down_quarter = gated(
            (cond_rows, bias_ada, small, mid_eighth, down_quarter)
        )

        rows_z = width // fs
        conds = jnp.concatenate(cond_rows)
        conds_z = lax.dynamic_slice_in_dim(conds, z * rows_z, rows_z, 1)
        partials = modulation_parts(conds_z, w_ada, bias_ada, small)
        partials = [partials[0]] + [ring_send(partials[k], fs - k) for k in range(1, fs)]
        qkv_helds.append(ring_send(qkv_helds[-1], 1))
        partials, qkv_helds, raw_near = gated((partials, qkv_helds, raw_near))

        live = (grid_sizes[0, 0] * grid_sizes[0, 1]).reshape(1)
        mods, head = modulation_rows(partials, live)
        heads_got = [box_send(head, bits) for bits in (2, 4, 6)]
        raw_far = chip_far(raw_near)
        qkv_helds.append(ring_send(qkv_helds[-1], 1))
        mods, head, heads_got, raw_far, qkv_helds = gated(
            (mods, head, heads_got, raw_far, qkv_helds)
        )

        qkv_mine = jnp.stack(qkv_helds)
        qkv_other = side_send(qkv_mine)
        qkv_mine_got = box_send(qkv_mine, 1)
        qkv_other_got = box_send(qkv_other, 1)
        mid_helds = [ring_send(after(mid_eighth, qkv_mine), 1)]
        mid_helds.append(ring_send(mid_helds[-1], 1))
        (normed,), (d_mlp,) = other_heads((raw,), (0,), (head,))
        bias_rows = [each[6:].reshape(-1) for each in partials]
        bias_rows = jnp.stack(bias_rows + bias_rows)
        biases = lax.dynamic_slice_in_dim(bias_rows, lax.rem(fs - z, fs), fs, 0)
        ends = [0]
        for bias in (b_qv, b_out, b_down, b_up):
            ends.append(ends[-1] + bias.shape[0])
        bias_qv, bias_out, bias_down, bias_up = [
            biases[:, ends[i] : ends[i + 1]].reshape(-1) for i in range(4)
        ]
        (
            qkv_mine,
            qkv_other,
            qkv_mine_got,
            qkv_other_got,
            mid_helds,
            normed,
            d_mlp,
            bias_qv,
            bias_out,
            bias_down,
            bias_up,
        ) = gated(
            (
                qkv_mine,
                qkv_other,
                qkv_mine_got,
                qkv_other_got,
                mid_helds,
                normed,
                d_mlp,
                bias_qv,
                bias_out,
                bias_down,
                bias_up,
            )
        )

        last = fs - 1

        def in_order(array):
            return [(array, k) for k in range(last)]

        mid_helds.append(ring_send(mid_helds[-1], 1))
        turned, qkv_full = projection(
            where,
            normed,
            w_qkv,
            [in_order(each) for each in (qkv_mine, qkv_other, qkv_mine_got, qkv_other_got)],
            bias_qv.reshape(2, width),
        )
        turned, qkv_full, mid_helds = gated((turned, qkv_full, mid_helds))

        mid_mine = jnp.concatenate(mid_helds)
        mid_near = chip_near(mid_mine)
        mid_got = [box_send(mid_mine, 1)]
        down_helds = [ring_send(after(down_quarter, mid_mine), 1)]
        attended = attention(turned, live)
        normed_box, d_mlp_box = other_heads(
            (*raw_near, *raw_far), (0, 0, 0, slots // 2), (*heads_got, heads_got[2])
        )
        normed_box, d_mlp_box = [normed, *normed_box], [d_mlp, *d_mlp_box]
        attended, mid_mine, mid_near, mid_got, down_helds, normed_box, d_mlp_box = gated(
            (attended, mid_mine, mid_near, mid_got, down_helds, normed_box, d_mlp_box)
        )

        mid_far = chip_far(mid_near)
        mid_got += [box_send(each, 1) for each in mid_near]
        down_helds.append(ring_send(down_helds[-1], 1))
        attended, mid_far, mid_got, down_helds = gated((attended, mid_far, mid_got, down_helds))

        mid_got += [box_send(each, 1) for each in mid_far]
        down_helds.append(ring_send(down_helds[-1], 1))
        down_others = [side_send(each) for each in down_helds[:-1]]
        attended_near = chip_near(attended)
        attn_out, normed_two, pre_act, activated, act_blocks, out_full, up_full = middle_forward(
            where_wide,
            attended,
            tokens[0],
            [w_out, w_up],
            ((mid_mine, *mid_near, *mid_far), mid_got),
            bias_out,
            bias_up,
            mods,
        )
        attended_near, down_helds, down_others, act_blocks, normed_two = gated(
            (attended_near, down_helds, down_others, act_blocks, normed_two)
        )

        down_others.append(side_send(down_helds[-1]))
        down_helds_got = [box_send(each, 1) for each in down_helds]
        down_others_got = [box_send(each, 1) for each in down_others]
        act_blocks, down_helds, down_others, down_helds_got, down_others_got = gated(
            (act_blocks, down_helds, down_others, down_helds_got, down_others_got)
        )

        act_box = chip_exchange(act_blocks, chip)
        normed_two_near = chip_near(normed_two)
        d_pre, d_pre_turned, d_pre_sums, down_full = hidden_back(
            where,
            d_mlp,
            w_down,
            [
                [(each, None) for each in kind]
                for kind in (down_helds, down_others, down_helds_got, down_others_got)
            ],
            pre_act,
        )

        def column_blocks(grad_t):
            n = grad_t.shape[0] // dp
            blocks = grad_t.reshape(groups, BOX, n, slots).transpose(1, 0, 2, 3)
            return blocks.reshape(BOX // 2, 2 * groups * n, slots)

        d_pre_blocks = column_blocks(d_pre_turned)
        d_pre, d_pre_blocks, act_box, normed_two_near = gated(
            (d_pre, d_pre_blocks, act_box, normed_two_near)
        )

        d_pre_box = chip_exchange(d_pre_blocks, chip)
        keep_down, send_down = row_grad(where_core, act_box, d_mlp_box)
        got_down = box_send(send_down, 1)
        d_middle, d_attn_turned, d_attended_turned, middle_sums = middle_back(
            d_pre, up_full, out_full, attn_out, tokens[0], cotangent[0], mods, live
        )
        d_attn_blocks = column_blocks(d_attn_turned)
        d_projected = attention_back(turned, d_attended_turned, live)
        d_projected_blocks = column_blocks(d_projected)
        d_projected, d_projected_blocks, d_attn_blocks, d_pre_box, got_down = gated(
            (d_projected, d_projected_blocks, d_attn_blocks, d_pre_box, got_down)
        )

        def after_core(grad_parts):
            grad, *sends = split_grad(where[:1], *grad_parts)
            return [grad] + [ring_send(sent, k + 1) for k, sent in enumerate(sends)]

        def own_block_cols(parts):
            grad = sum((each.astype(f32) for each in parts[1:]), parts[0])
            rows, cols = grad.shape
            grad = grad.reshape(rows, groups, cols // groups)
            return group_sum(grad.transpose(1, 0, 2), group)

        last_blocks = jnp.concatenate([d_projected_blocks, d_attn_blocks], axis=1)
        last_box = chip_exchange(last_blocks, chip)
        normed_two_far = chip_far(normed_two_near)
        attended_far = chip_far(attended_near)
        attended_box = [attended, *attended_near, *attended_far]
        normed_two_box = [normed_two, *normed_two_near, *normed_two_far]
        keep_up, send_up = column_grad(
            where_core, normed_two_box, d_pre_box, 0, d_pre_box[0].shape[0]
        )
        got_up = box_send(send_up, 1)
        down_parts = split_rows(where[:1], keep_down, got_down)
        down_parts = [down_parts[0]] + [
            ring_send(sent, k + 1) for k, sent in enumerate(down_parts[1:])
        ]
        grad_tokens, first_sums = first_back(d_projected, qkv_full, tokens[0], d_middle, mods)
        last_box, attended_box, down_parts, first_sums, keep_up, got_up = gated(
            (last_box, attended_box, down_parts, first_sums, keep_up, got_up)
        )

        cut = d_projected_blocks.shape[1]
        keep_qkv, send_qkv = column_grad(where_core, normed_box, last_box, 0, cut)
        got_qkv = box_send(send_qkv, 1)
        keep_out, send_out = column_grad(
            where_core, attended_box, last_box, cut, last_box[0].shape[0]
        )
        got_out = box_send(send_out, 1)
        up_parts = after_core((keep_up, got_up))
        output, output_sums = output_rows(
            activated,
            down_full,
            bias_down,
            tokens[0],
            attn_out,
            cotangent[0],
            d_mlp,
            mods,
            live,
        )
        d_mod = jnp.concatenate([first_sums[0:2], middle_sums[0:3], output_sums[0:1]])
        cond_row = cond_act.astype(f32)
        images = jnp.concatenate([d_mod, cond_row, cond_row]).astype(bf16)
        total = jnp.concatenate(
            [
                first_sums[2:4],
                middle_sums[3:4],
                output_sums[1:2],
                d_pre_sums.reshape(hidden // width, width),
            ]
        )
        images_near = jnp.stack(ring_gather(images))
        totals = ring_gather(total)
        got_qkv, got_out, up_parts, images_near, totals = gated(
            (got_qkv, got_out, up_parts, images_near, totals)
        )

        qkv_parts = after_core((keep_qkv, got_qkv))
        out_parts = after_core((keep_out, got_out))
        down_rows = down_parts[0].shape[0]
        if groups == 1:
            down_blocks = down_columns(down_parts)
            parts = lax.all_to_all(down_blocks, "dp", 0, 0, tiled=True)
        else:
            grad_down = own_block_cols(down_parts)
            down_blocks = grad_down.reshape(down_rows, BOX, width // dp).transpose(1, 0, 2)
            parts = [pick(down_blocks, place)] + [
                box_send(pick(down_blocks, place ^ k), k) for k in range(1, BOX)
            ]
            parts = jnp.stack(parts)
            parts = jnp.stack([pick(parts, place ^ k) for k in range(BOX)])
        grad_w_down = parts.reshape(BOX * down_rows, width // dp)
        grad_w_up = own_block_cols(up_parts)
        grad_w_out = own_block_cols(out_parts)
        grad_w_qkv = own_block_cols(qkv_parts)

        images, total = images_near, sum(totals[1:], totals[0])
        for bits in (1, 2, 4):
            images = jnp.concatenate([images, box_send(images, bits)])
            total = total + box_send(total, bits)
        images_box, total_box = images, total
        for k in range(1, groups):
            images = jnp.concatenate([images, group_send(images_box, k)])
            total = total + group_send(total_box, k)
        conds_all = lax.dynamic_slice_in_dim(images[:, 6], z * rows_z, rows_z, 1)
        d_mod_all = images[:, :6]
        ada_cols = 6 * width // dp
        grad_w_ada = lax.dot_general(
            conds_all,
            lax.dynamic_slice_in_dim(
                d_mod_all.reshape(dp * fs, 6 * width), rank * ada_cols, ada_cols, 1
            ),
            (((0,), (0,)), ((), ())),
            preferred_element_type=f32,
        )
        d_conds = lax.dot_general(
            images_near[:, :6].reshape(fs, 6 * width),
            w_ada,
            (((1,), (1,)), ((), ())),
            preferred_element_type=f32,
        )
        cond_parts = [d_conds[0]] + [ring_send(d_conds[k], fs - k) for k in range(1, fs)]
        twice = jnp.stack(cond_parts + cond_parts)
        d_cond_act = lax.dynamic_slice_in_dim(twice, lax.rem(fs - z, fs), fs, 0).reshape(-1)
        grad_condition = d_cond_act[None] * gate * (1.0 + cond_wide * (1.0 - gate))

        def shard_of(rows):
            return pick(rows.reshape(fs, -1), z)

        grads_bias = [
            shard_of(jnp.sum(d_mod_all.astype(f32), axis=0)),
            shard_of(total[:2]),
            shard_of(total[2]),
            shard_of(total[4:]),
            shard_of(total[3]),
        ]
        return (
            output[None],
            grad_tokens[None],
            grad_condition,
            grad_w_ada,
            grad_w_qkv,
            grad_w_out,
            grad_w_up,
            grad_w_down,
            *grads_bias,
        )

    return body


def solution(mesh):
    return jax.shard_map(
        make_body(mesh.shape["dp"], mesh.shape["fsdp"]),
        mesh=mesh,
        in_specs=(
            P(("dp", "fsdp"), None, None),
            P(("dp", "fsdp"), None),
            P(("dp", "fsdp"), None),
            P("fsdp", None),
            P("fsdp", None),
            P("fsdp", None),
            P("fsdp", None),
            P("fsdp", None),
            P("fsdp"),
            P("fsdp"),
            P("fsdp"),
            P("fsdp"),
            P("fsdp"),
            P(("dp", "fsdp"), None, None),
        ),
        out_specs=(
            P(("dp", "fsdp"), None, None),
            P(("dp", "fsdp"), None, None),
            P(("dp", "fsdp"), None),
            P("fsdp", "dp"),
            P("fsdp", "dp"),
            P("fsdp", "dp"),
            P("fsdp", "dp"),
            P("fsdp", "dp"),
            P("fsdp"),
            P("fsdp"),
            P("fsdp"),
            P("fsdp"),
            P("fsdp"),
        ),
        check_vma=False,
    )
```

```python
import math

import jax
import jax.numpy as jnp
from jax import lax
from jax.experimental import pallas as pl
from jax.experimental.pallas import tpu as pltpu
from jax.sharding import PartitionSpec as P

HEAD_DIM = 72
BOX = 8

epsilon = 1e-06
masked_value = -1e30
gelu_root = math.sqrt(2.0 / math.pi)
f32 = jnp.float32
bf16 = jnp.bfloat16


def norm_parts(values_in):
    centred = values_in - jnp.mean(values_in, axis=-1, keepdims=True)
    spread = jnp.mean(centred * centred, axis=-1, keepdims=True)
    rate = lax.rsqrt(spread + epsilon)
    return centred * rate, rate


def norm_back(normal, rate, grad):
    mean_grad = jnp.mean(grad, axis=-1, keepdims=True)
    mean_both = jnp.mean(grad * normal, axis=-1, keepdims=True)
    return rate * (grad - mean_grad - normal * mean_both)


def gelu_tanh(pre_act):
    return (
        0.5
        * pre_act
        * (1.0 + jnp.tanh(gelu_root * (pre_act + 0.044715 * pre_act * pre_act * pre_act)))
    )


def after(value, other):
    return lax.optimization_barrier((value, other))[0]


def gated(values):
    return lax.optimization_barrier(values)


def pick(array, index, axis=0):
    return lax.dynamic_index_in_dim(array, index, axis, keepdims=False)


def make_body(dp, fs):
    groups = dp // BOX

    def box_send(x, bits):
        return lax.ppermute(x, "dp", [(i, i ^ bits) for i in range(dp)])

    def side_send(x):
        return lax.ppermute(x, "dp", [(i, i ^ (4 if i & 1 else 2)) for i in range(dp)])

    def ring_send(x, hops):
        return lax.ppermute(x, "fsdp", [(i, (i + hops) % fs) for i in range(fs)])

    def group_send(x, hops):
        return lax.ppermute(x, "dp", [(i, (i + hops * BOX) % dp) for i in range(dp)])

    def ring_gather(x):
        return [x] + [ring_send(x, k) for k in range(1, fs)]

    def ring_sorted(blocks, z):
        back = jnp.stack(blocks[::-1] + blocks[::-1])
        return lax.dynamic_slice_in_dim(back, fs - 1 - z, fs, 0)

    def chip_near(x):
        return box_send(x, 2), box_send(x, 4)

    def chip_far(near):
        half = near[0].shape[0] // 2
        return box_send(near[0][:half], 4), box_send(near[1][half:], 2)

    def chip_exchange(blocks):
        return [blocks[0]] + [box_send(blocks[k], 2 * k) for k in range(1, BOX // 2)]

    def ring_sum(x, z):
        total = pick(x, z)
        for k in range(1, fs):
            sent = pick(x, lax.rem(z + k, fs)).astype(bf16)
            total = total + ring_send(sent, k).astype(f32)
        return total

    def group_sum(x, group):
        total = pick(x, group)
        for k in range(1, groups):
            total = total + group_send(pick(x, lax.rem(group + k, groups)), k)
        return total

    def cost(microseconds):
        return pl.CostEstimate(
            flops=int(microseconds * 1e8),
            transcendentals=0,
            bytes_accessed=int(microseconds * 3.2e5),
        )

    vmem = pl.BlockSpec(memory_space=pltpu.VMEM)
    smem = pl.BlockSpec(memory_space=pltpu.SMEM)

    def params(mebibytes):
        return pltpu.CompilerParams(vmem_limit_bytes=mebibytes << 20)

    def chunks(rows, step, work):
        def one(i, unused):
            work(pl.ds(pl.multiple_of(i * step, step), step), i * step)
            return unused

        lax.fori_loop(0, rows // step, one, 0)

    def alive_rows(first, rows, live):
        return ((lax.broadcasted_iota(jnp.int32, (rows, 1), 0) + first) < live).astype(f32)

    def modulation_parts(conds, w_ada, bias_ada, extra):
        images = conds.shape[0]
        parts, width = bias_ada.shape

        def kernel(cond_ref, w_ref, bias_ref, extra_ref, *out_refs):
            for part in range(parts):
                cols = slice(part * width, (part + 1) * width)
                product = jnp.dot(cond_ref[...], w_ref[:, cols], preferred_element_type=f32)
                product = product + bias_ref[part : part + 1, :]
                for image, out_ref in enumerate(out_refs):
                    out_ref[part : part + 1, :] = product[image : image + 1, :]
            for out_ref in out_refs:
                out_ref[parts:, :] = extra_ref[...]

        rows = parts + extra.shape[0]
        return pl.pallas_call(
            kernel,
            out_shape=[jax.ShapeDtypeStruct((rows, width), f32)] * images,
            in_specs=[vmem] * 4,
            out_specs=[vmem] * images,
            cost_estimate=cost(4),
            compiler_params=params(60),
        )(conds, w_ada, bias_ada, extra)

    def modulation_rows(partials, live):
        rows, width = partials[0].shape

        def kernel(live_ref, *refs):
            mods_ref, head_ref = refs[-2:]
            total = refs[0][...]
            for ref in refs[1:-2]:
                total = total + ref[...]
            mods_ref[...] = total
            head_ref[...] = jnp.full(head_ref.shape, live_ref[0].astype(f32))
            head_ref[0:2, :] = total[0:2, :]
            head_ref[2:3, :] = total[5:6, :]

        return pl.pallas_call(
            kernel,
            out_shape=[jax.ShapeDtypeStruct((rows, width), f32)] * 2,
            in_specs=[smem] + [vmem] * len(partials),
            out_specs=[vmem] * 2,
            cost_estimate=cost(1),
            compiler_params=params(60),
        )(live, *partials)

    def other_heads(raws, firsts, heads):
        n = len(raws)
        width = raws[0].shape[1] // 2

        def kernel(*refs):
            raw_refs, head_refs = refs[:n], refs[n : 2 * n]
            normed_refs, d_mlp_refs = refs[2 * n : 3 * n], refs[3 * n :]
            for raw, head, normed, d_mlp, first in zip(
                raw_refs, head_refs, normed_refs, d_mlp_refs, firsts
            ):
                live = head[3, 0].astype(jnp.int32)

                def work(rows, start):
                    normal = norm_parts(raw[rows, :width].astype(f32))[0]
                    normed[rows, :] = (
                        normal * (1.0 + head[1:2, :]) + head[0:1, :]
                    ).astype(bf16)
                    count = normal.shape[0]
                    up_rows = alive_rows(start + first, count, live) * raw[
                        rows, width:
                    ].astype(f32)
                    d_mlp[rows, :] = (head[2:3, :] * up_rows).astype(bf16)

                chunks(raw.shape[0], 32, work)

        outs = pl.pallas_call(
            kernel,
            out_shape=[jax.ShapeDtypeStruct((raw.shape[0], width), bf16) for raw in raws] * 2,
            in_specs=[vmem] * (2 * n),
            out_specs=[vmem] * (2 * n),
            cost_estimate=cost(8),
            compiler_params=params(60),
        )(*raws, *heads)
        return outs[:n], outs[n:]

    def piece_plan(pieces):
        arrays = []
        for piece, unused in (each for kind in pieces for each in kind):
            if not any(piece is array for array in arrays):
                arrays.append(piece)
        position = {id(array): i for i, array in enumerate(arrays)}
        plan = [[(position[id(piece)], index) for piece, index in kind] for kind in pieces]
        return arrays, plan

    def piece_copies(where_ref, own_ref, array_refs, plan, whole_ref):
        copies = [(own_ref, whole_ref.at[where_ref[0]])]
        for kind, blocks in enumerate(plan):
            for k, (which, index) in enumerate(blocks):
                source = array_refs[which] if index is None else array_refs[which].at[index]
                copies.append((source, whole_ref.at[where_ref[k + 1], where_ref[fs + kind]]))
        return copies

    def wide_copies(core, where_ref, own_refs, sets, whole_refs):
        widths = [ref.shape[-1] for ref in own_refs]
        width, part = sum(widths), sets[0][0].shape[-1]
        lead, split = whole_refs[0].shape[2], sets[0][3].shape[0]
        copies = [(own, whole.at[where_ref[0]]) for own, whole in zip(own_refs, whole_refs)]
        for side, piece_refs in enumerate(sets):
            low, high = (0, part) if core ^ side == 0 else (part, width)
            offset = 0 if core ^ side == 0 else width - part
            for block in range(1, fs):
                base = (block - 1) * lead
                top = min(max(split - base, 0), lead)
                rows = [(i, base, i, 0, lead) for i in range(3)]
                if top:
                    rows.append((3, base, 3, 0, top))
                if top < lead:
                    rows.append((4, base + top - split, 3, top, lead - top))
                for piece, first, slot, row, count in rows:
                    start = 0
                    for i, each in enumerate(widths):
                        left, right = max(low, start), min(high, start + each)
                        if left < right:
                            source = piece_refs[piece].at[
                                first : first + count, :, left - offset : right - offset
                            ]
                            target = whole_refs[i].at[
                                where_ref[block],
                                where_ref[fs + 1 + slot],
                                row : row + count,
                                :,
                                left - start : right - start,
                            ]
                            copies.append((source, target))
                        start += each
        return copies

    def copy_all(copies, sems):
        return [
            pltpu.make_async_copy(source, target, sems.at[j])
            for j, (source, target) in enumerate(copies)
        ]

    def start_all(copies):
        for copy in copies:
            copy.start()

    def wait_all(copies):
        for copy in copies:
            copy.wait()

    def in_blocks(shard):
        rows, cols = shard.shape
        return shard.reshape(4, rows // 32, 8, cols)

    any_spec = pl.BlockSpec(memory_space=pl.ANY)

    def projection(where, normed, own, pieces, biases):
        slots, width = normed.shape
        arrays, plan = piece_plan(pieces)
        own = in_blocks(own)
        shape = (fs,) + own.shape

        def kernel(where_ref, normed_ref, bias_ref, own_ref, *refs):
            array_refs = refs[: len(arrays)]
            turned_ref, whole_ref, scratch, sems, out_sem = refs[len(arrays) :]
            copies = copy_all(
                piece_copies(where_ref, own_ref, array_refs, plan, scratch), sems
            )
            start_all(copies)
            wait_all(copies)
            out = pltpu.make_async_copy(scratch, whole_ref, out_sem)
            out.start()
            w_ref = scratch.reshape(width, 3 * width)
            for part in range(3):
                cols = slice(part * width, (part + 1) * width)
                proj = jnp.dot(normed_ref[...], w_ref[:, cols], preferred_element_type=f32)
                if part != 1:
                    proj = proj + bias_ref[part // 2 : part // 2 + 1, :]
                turned_ref[cols, :] = proj.astype(bf16).astype(f32).T
            out.wait()

        turned, whole = pl.pallas_call(
            kernel,
            out_shape=[
                jax.ShapeDtypeStruct((3 * width, slots), f32),
                jax.ShapeDtypeStruct(shape, bf16),
            ],
            in_specs=[smem, vmem, vmem, any_spec] + [any_spec] * len(arrays),
            out_specs=[vmem, any_spec],
            scratch_shapes=[
                pltpu.VMEM(shape, bf16),
                pltpu.SemaphoreType.DMA((1 + 4 * (fs - 1),)),
                pltpu.SemaphoreType.DMA,
            ],
            cost_estimate=cost(11),
            compiler_params=params(60),
        )(where, normed, biases, own, *arrays)
        return turned, whole.reshape(width, 3 * width)

    def attention(turned, live):
        slots = turned.shape[1]
        width = turned.shape[0] // 3
        count = width // HEAD_DIM
        heads_at_once = 2 if count % 2 == 0 else 1
        scale = HEAD_DIM ** (-0.5)

        def kernel(live_ref, turned_ref, attended_ref, out_turned):
            live_keys = lax.broadcasted_iota(jnp.int32, (1, slots), 1) < live_ref[0]

            def head(h):
                def rows(part):
                    first = pl.multiple_of(part * width + h * HEAD_DIM, 8)
                    return turned_ref[pl.ds(first, HEAD_DIM), :].astype(bf16)

                scores = lax.dot_general(
                    rows(0), rows(1), (((0,), (0,)), ((), ())), preferred_element_type=f32
                )
                scores = jnp.where(live_keys, scores * scale, masked_value)
                highest = jnp.max(scores, axis=-1, keepdims=True)
                total = jnp.sum(jnp.exp(scores - highest), axis=-1, keepdims=True)
                probs = jnp.exp(scores - (highest + jnp.log(total)))
                return lax.dot_general(
                    rows(2),
                    probs.astype(bf16),
                    (((1,), (1,)), ((), ())),
                    preferred_element_type=f32,
                )

            def some_heads(i, unused):
                outs = [head(i * heads_at_once + j) for j in range(heads_at_once)]
                for j, out in enumerate(outs):
                    first = pl.multiple_of((i * heads_at_once + j) * HEAD_DIM, 8)
                    out_turned[pl.ds(first, HEAD_DIM), :] = out
                return unused

            lax.fori_loop(0, count // heads_at_once, some_heads, 0)
            attended_ref[...] = out_turned[...].T.astype(bf16)

        return pl.pallas_call(
            kernel,
            out_shape=jax.ShapeDtypeStruct((slots, width), bf16),
            in_specs=[smem, vmem],
            out_specs=vmem,
            scratch_shapes=[pltpu.VMEM((width, slots), f32)],
            cost_estimate=cost(11),
            compiler_params=params(60),
        )(live, turned)

    def attention_back(turned, d_turned, d_attn_turned, live, where_chip):
        width, slots = d_turned.shape
        parts = (3 * width // 4, width // 4)
        count = width // HEAD_DIM
        heads_at_once = 2 if count % 2 == 0 else 1
        scale = HEAD_DIM ** (-0.5)

        def kernel(live_ref, chip_ref, turned_ref, d_ref, d_attn_ref, out_ref, *rest):
            block_refs, total_ref = rest[:-1], rest[-1]
            live_keys = lax.broadcasted_iota(jnp.int32, (1, slots), 1) < live_ref[0]

            def place_of(h, part):
                return pl.ds(pl.multiple_of(part * width + h * HEAD_DIM, 8), HEAD_DIM)

            def head(h):
                def place(part):
                    return place_of(h, part)

                query = turned_ref[place(0), :].astype(bf16)
                key_part = turned_ref[place(1), :].astype(bf16)
                value = turned_ref[place(2), :].astype(bf16)
                d_out = d_ref[place(0), :].astype(bf16)
                both_first = (((0,), (0,)), ((), ()))
                scores = lax.dot_general(
                    query, key_part, both_first, preferred_element_type=f32
                )
                scores = jnp.where(live_keys, scores * scale, masked_value)
                highest = jnp.max(scores, axis=-1, keepdims=True)
                total = jnp.sum(jnp.exp(scores - highest), axis=-1, keepdims=True)
                probs = jnp.exp(scores - (highest + jnp.log(total)))
                d_probs = lax.dot_general(
                    d_out, value, both_first, preferred_element_type=f32
                )
                inner = jnp.sum(probs * d_probs, axis=-1, keepdims=True)
                d_scores = (probs * (d_probs - inner)).astype(bf16)
                d_value = jnp.dot(d_out, probs.astype(bf16), preferred_element_type=f32)
                d_query = scale * lax.dot_general(
                    key_part, d_scores, (((1,), (1,)), ((), ())), preferred_element_type=f32
                )
                d_key = scale * jnp.dot(query, d_scores, preferred_element_type=f32)
                return d_query, d_key, d_value

            def some_heads(i, unused):
                outs = [head(i * heads_at_once + j) for j in range(heads_at_once)]
                for j, parts in enumerate(outs):
                    for part, out in enumerate(parts):
                        total_ref[place_of(i * heads_at_once + j, part), :] = out
                return unused

            lax.fori_loop(0, count // heads_at_once, some_heads, 0)
            out_ref[...] = total_ref[...].astype(bf16)
            for k, block in enumerate(block_refs):
                first = pl.multiple_of(chip_ref[k] * parts[0], 16)
                block[: parts[0], :] = total_ref[pl.ds(first, parts[0]), :].astype(bf16)
                first = pl.multiple_of(chip_ref[k] * parts[1], 16)
                block[parts[0] :, :] = d_attn_ref[pl.ds(first, parts[1]), :]

        n_blocks = 4 if groups == 1 else 0
        return pl.pallas_call(
            kernel,
            out_shape=[jax.ShapeDtypeStruct((3 * width, slots), bf16)]
            + [jax.ShapeDtypeStruct((width, slots), bf16)] * n_blocks,
            in_specs=[smem, smem, vmem, vmem, vmem],
            out_specs=[vmem] * (1 + n_blocks),
            scratch_shapes=[pltpu.VMEM((3 * width, slots), f32)],
            cost_estimate=cost(12),
            compiler_params=params(60),
        )(live, where_chip, turned, d_turned, d_attn_turned)

    def middle_forward(where, attended, tokens_own, owns, sets, bias_out, bias_up, mods):
        slots, width = attended.shape
        owns = [in_blocks(own) for own in owns]
        hidden = owns[1].shape[-1]
        tile = hidden // fs
        quarter = tile // 4
        shapes = [(fs,) + own.shape for own in owns]
        n_pieces = len(sets[0])
        n_copies = 2 + 2 * 15 * (fs - 1)

        def kernel(where_ref, attended_ref, tokens_ref, bias_out_ref, bias_up_ref, mods_ref, *refs):
            own_refs = refs[:2]
            set_refs = (refs[2 : 2 + n_pieces], refs[2 + n_pieces : 2 + 2 * n_pieces])
            (
                attn_ref,
                normed_ref,
                pre_ref,
                act_ref,
                block0,
                block1,
                block2,
                block3,
                whole_out,
                whole_up,
                scratch_out,
                scratch_up,
                turned,
                sems,
                out_sems,
            ) = refs[2 + 2 * n_pieces :]
            step = pl.program_id(0)
            scratches, wholes = (scratch_out, scratch_up), (whole_out, whole_up)

            def outs():
                return [
                    pltpu.make_async_copy(scratch, whole, out_sems.at[i])
                    for i, (scratch, whole) in enumerate(zip(scratches, wholes))
                ]

            @pl.when(step == 0)
            def first():
                for core in range(2):

                    @pl.when(where_ref[fs] == core)
                    def gather(core=core):
                        copies = copy_all(
                            wide_copies(core, where_ref, own_refs, set_refs, scratches), sems
                        )
                        start_all(copies)
                        wait_all(copies)

                start_all(outs())
                attn_ref[...] = (
                    jnp.dot(
                        attended_ref[...],
                        scratch_out.reshape(width, width)[...],
                        preferred_element_type=f32,
                    )
                    + bias_out_ref[...]
                )

                def work(rows, unused):
                    middle = tokens_ref[rows, :].astype(f32) + mods_ref[2:3, :] * attn_ref[rows, :]
                    normal = norm_parts(middle)[0]
                    normed_ref[rows, :] = (
                        normal * (1.0 + mods_ref[4:5, :]) + mods_ref[3:4, :]
                    ).astype(bf16)

                chunks(slots, 32, work)

            cols = pl.ds(pl.multiple_of(step * tile, 128), tile)
            pre_ref[...] = (
                jnp.dot(
                    normed_ref[...],
                    scratch_up.reshape(width, hidden)[:, cols],
                    preferred_element_type=f32,
                )
                + bias_up_ref[0]
            )

            def work(rows, unused):
                act_ref[rows, :] = gelu_tanh(pre_ref[rows, :]).astype(bf16)

            chunks(slots, 32, work)
            turned[...] = act_ref[...].astype(f32).T
            for k, block in enumerate((block0, block1, block2, block3)):
                first = pl.multiple_of(where_ref[fs + 1 + k] * quarter, 16)
                block[...] = turned[pl.ds(first, quarter), :].astype(bf16)

            @pl.when(step == fs - 1)
            def last():
                wait_all(outs())

        def whole(shape):
            return pl.BlockSpec(shape, lambda j, where_ref: (0,) * len(shape))

        *results, whole_out, whole_up = pl.pallas_call(
            kernel,
            out_shape=[
                jax.ShapeDtypeStruct((slots, width), f32),
                jax.ShapeDtypeStruct((slots, width), bf16),
                jax.ShapeDtypeStruct((slots, hidden), f32),
                jax.ShapeDtypeStruct((slots, hidden), bf16),
            ]
            + [jax.ShapeDtypeStruct((fs * quarter, slots), bf16)] * 4
            + [jax.ShapeDtypeStruct(shape, bf16) for shape in shapes],
            grid_spec=pltpu.PrefetchScalarGridSpec(
                num_scalar_prefetch=1,
                grid=(fs,),
                in_specs=[
                    whole((slots, width)),
                    whole((slots, width)),
                    whole((1, width)),
                    pl.BlockSpec((1, 1, tile), lambda j, where_ref: (j, 0, 0)),
                    whole(mods.shape),
                ]
                + [any_spec] * (2 + 2 * n_pieces),
                out_specs=[
                    whole((slots, width)),
                    whole((slots, width)),
                    pl.BlockSpec((slots, tile), lambda j, where_ref: (0, j)),
                    pl.BlockSpec((slots, tile), lambda j, where_ref: (0, j)),
                ]
                + [pl.BlockSpec((quarter, slots), lambda j, where_ref: (j, 0))] * 4
                + [any_spec, any_spec],
                scratch_shapes=[pltpu.VMEM(shape, bf16) for shape in shapes]
                + [
                    pltpu.VMEM((tile, slots), f32),
                    pltpu.SemaphoreType.DMA((n_copies,)),
                    pltpu.SemaphoreType.DMA((2,)),
                ],
            ),
            cost_estimate=cost(20),
            compiler_params=params(60),
        )(
            where,
            attended,
            tokens_own,
            bias_out.reshape(1, width),
            bias_up.reshape(fs, 1, tile),
            mods,
            *owns,
            *sets[0],
            *sets[1],
        )
        return (
            *results,
            whole_out.reshape(width, width),
            whole_up.reshape(width, hidden),
        )

    def hidden_back(where, d_mlp, own, pieces, pre_act):
        slots, width = d_mlp.shape
        hidden = pre_act.shape[1]
        tile = hidden // fs
        if groups == 1:
            turned_shapes = [jax.ShapeDtypeStruct((tile, slots), bf16)] * 4
            turned_specs = [pl.BlockSpec((tile, slots), lambda j, where_ref: (0, 0))] * 4
        else:
            turned_shapes = [jax.ShapeDtypeStruct((hidden, slots), bf16)]
            turned_specs = [pl.BlockSpec((tile, slots), lambda j, where_ref: (j, 0))]
        arrays, plan = piece_plan(pieces)
        own = in_blocks(own)
        shape = (fs,) + own.shape

        def kernel(where_ref, d_mlp_ref, pre_ref, own_ref, *refs):
            array_refs = refs[: len(arrays)]
            d_pre_ref, *turned_refs, sum_ref, whole_ref = refs[len(arrays) : -4]
            d_act_ref, scratch, sems, out_sem = refs[-4:]
            step = pl.program_id(0)

            def out():
                return pltpu.make_async_copy(scratch, whole_ref, out_sem)

            @pl.when(step == 0)
            def first():
                copies = copy_all(
                    piece_copies(where_ref, own_ref, array_refs, plan, scratch), sems
                )
                start_all(copies)
                wait_all(copies)
                out().start()

            d_act_ref[...] = lax.dot_general(
                d_mlp_ref[...],
                scratch.at[step].reshape(tile, width)[...],
                (((1,), (1,)), ((), ())),
                preferred_element_type=f32,
            )

            def work(rows, unused):
                pre = pre_ref[rows, :]
                square = pre * pre
                bend = jnp.tanh(gelu_root * (pre + 0.044715 * square * pre))
                slope = 0.5 * (1.0 + bend) + 0.5 * pre * (1.0 - bend * bend) * gelu_root * (
                    1.0 + 3.0 * 0.044715 * square
                )
                d_pre = (d_act_ref[rows, :] * slope).astype(bf16)
                d_pre_ref[rows, :] = d_pre
                d_act_ref[rows, :] = d_pre.astype(f32)

            chunks(slots, 32, work)
            sum_ref[0] = jnp.sum(d_act_ref[...], axis=0, keepdims=True)
            if groups == 1:
                for k, turned_ref in enumerate(turned_refs):

                    @pl.when(step == where_ref[fs + 4 + k])
                    def block(turned_ref=turned_ref):
                        turned_ref[...] = d_act_ref[...].T.astype(bf16)
            else:
                turned_refs[0][...] = d_act_ref[...].T.astype(bf16)

            @pl.when(step == fs - 1)
            def last():
                out().wait()

        *results, whole = pl.pallas_call(
            kernel,
            out_shape=[
                jax.ShapeDtypeStruct((slots, hidden), bf16),
                *turned_shapes,
                jax.ShapeDtypeStruct((fs, 1, tile), f32),
                jax.ShapeDtypeStruct(shape, bf16),
            ],
            grid_spec=pltpu.PrefetchScalarGridSpec(
                num_scalar_prefetch=1,
                grid=(fs,),
                in_specs=[
                    pl.BlockSpec((slots, width), lambda j, where_ref: (0, 0)),
                    pl.BlockSpec((slots, tile), lambda j, where_ref: (0, j)),
                    any_spec,
                ]
                + [any_spec] * len(arrays),
                out_specs=[
                    pl.BlockSpec((slots, tile), lambda j, where_ref: (0, j)),
                    *turned_specs,
                    pl.BlockSpec((1, 1, tile), lambda j, where_ref: (j, 0, 0)),
                    any_spec,
                ],
                scratch_shapes=[
                    pltpu.VMEM((slots, tile), f32),
                    pltpu.VMEM(shape, bf16),
                    pltpu.SemaphoreType.DMA((1 + 4 * (fs - 1),)),
                    pltpu.SemaphoreType.DMA,
                ],
            ),
            cost_estimate=cost(15),
            compiler_params=params(60),
        )(where, d_mlp, pre_act, own, *arrays)
        return (*results, whole.reshape(hidden, width))

    def middle_back(d_pre, up_full, out_full, attn_out, tokens_own, cotangent_own, mods, live):
        slots, hidden = d_pre.shape
        width = attn_out.shape[1]
        tile = hidden // fs

        def kernel(
            live_ref,
            d_pre_ref,
            up_ref,
            out_ref,
            attn_ref,
            tokens_ref,
            cot_ref,
            mods_ref,
            d_middle_ref,
            d_attn_turned_ref,
            d_attended_turned_ref,
            sums_ref,
            total,
            d_attn_ref,
        ):
            step = pl.program_id(0)
            part = lax.dot_general(
                d_pre_ref[...],
                up_ref[...],
                (((1,), (1,)), ((), ())),
                preferred_element_type=f32,
            )

            @pl.when(step == 0)
            def start():
                total[...] = part

            @pl.when(step > 0)
            def add():
                total[...] += part

            @pl.when(step == fs - 1)
            def finish():
                sums_ref[...] = jnp.zeros_like(sums_ref)

                def work(rows, first):
                    grad = total[rows, :]
                    attn = attn_ref[rows, :]
                    middle = tokens_ref[rows, :].astype(f32) + mods_ref[2:3, :] * attn
                    normal, rate = norm_parts(middle)
                    alive = alive_rows(first, grad.shape[0], live_ref[0])
                    d_middle = alive * cot_ref[rows, :].astype(f32) + norm_back(
                        normal, rate, grad * (1.0 + mods_ref[4:5, :])
                    )
                    d_middle_ref[rows, :] = d_middle
                    d_attn = (mods_ref[2:3, :] * d_middle).astype(bf16)
                    d_attn_ref[rows, :] = d_attn
                    for i, each in enumerate(
                        (d_middle * attn, grad, grad * normal, d_attn.astype(f32))
                    ):
                        sums_ref[i : i + 1, :] += jnp.sum(each, axis=0, keepdims=True)

                chunks(slots, 32, work)
                d_attn_turned_ref[...] = d_attn_ref[...].astype(f32).T.astype(bf16)
                d_attended = lax.dot_general(
                    d_attn_ref[...],
                    out_ref[...],
                    (((1,), (1,)), ((), ())),
                    preferred_element_type=f32,
                )
                d_attended_turned_ref[...] = d_attended.astype(bf16).astype(f32).T

        def whole(shape):
            return pl.BlockSpec(shape, lambda j, live_ref: (0,) * len(shape))

        return pl.pallas_call(
            kernel,
            out_shape=[
                jax.ShapeDtypeStruct((slots, width), f32),
                jax.ShapeDtypeStruct((width, slots), bf16),
                jax.ShapeDtypeStruct((width, slots), f32),
                jax.ShapeDtypeStruct((8, width), f32),
            ],
            grid_spec=pltpu.PrefetchScalarGridSpec(
                num_scalar_prefetch=1,
                grid=(fs,),
                in_specs=[
                    pl.BlockSpec((slots, tile), lambda j, live_ref: (0, j)),
                    pl.BlockSpec((width, tile), lambda j, live_ref: (0, j)),
                    whole((width, width)),
                    whole((slots, width)),
                    whole((slots, width)),
                    whole((slots, width)),
                    whole(mods.shape),
                ],
                out_specs=[
                    whole((slots, width)),
                    whole((width, slots)),
                    whole((width, slots)),
                    whole((8, width)),
                ],
                scratch_shapes=[
                    pltpu.VMEM((slots, width), f32),
                    pltpu.VMEM((slots, width), bf16),
                ],
            ),
            cost_estimate=cost(12),
            compiler_params=params(60),
        )(live, d_pre, up_full, out_full, attn_out, tokens_own, cotangent_own, mods)

    def first_back(d_turned, qkv_full, tokens_own, d_middle, mods):
        slots, width = d_middle.shape

        def kernel(d_ref, w_ref, tokens_ref, d_middle_ref, mods_ref, grad_ref, sums_ref, total):
            sums_ref[...] = jnp.zeros_like(sums_ref)
            for part in range(3):
                cols = slice(part * width, (part + 1) * width)
                d_part = d_ref[cols, :].astype(f32).T
                if part != 1:
                    row = 2 + part // 2
                    sums_ref[row : row + 1, :] = jnp.sum(d_part, axis=0, keepdims=True)
                product = lax.dot_general(
                    d_part.astype(bf16),
                    w_ref[:, cols],
                    (((1,), (1,)), ((), ())),
                    preferred_element_type=f32,
                )
                if part == 0:
                    total[...] = product
                else:
                    total[...] += product

            def work(rows, unused):
                grad = total[rows, :]
                normal, rate = norm_parts(tokens_ref[rows, :].astype(f32))
                sums_ref[0:1, :] += jnp.sum(grad, axis=0, keepdims=True)
                sums_ref[1:2, :] += jnp.sum(grad * normal, axis=0, keepdims=True)
                grad_ref[rows, :] = (
                    d_middle_ref[rows, :]
                    + norm_back(normal, rate, grad * (1.0 + mods_ref[1:2, :]))
                ).astype(bf16)

            chunks(slots, 32, work)

        return pl.pallas_call(
            kernel,
            out_shape=[
                jax.ShapeDtypeStruct((slots, width), bf16),
                jax.ShapeDtypeStruct((8, width), f32),
            ],
            in_specs=[vmem] * 5,
            out_specs=[vmem] * 2,
            scratch_shapes=[pltpu.VMEM((slots, width), f32)],
            cost_estimate=cost(9),
            compiler_params=params(60),
        )(d_turned, qkv_full, tokens_own, d_middle, mods)

    def output_rows(
        activated, down_full, bias_down, tokens_own, attn_out, cotangent_own, d_mlp, mods, live
    ):
        slots, hidden = activated.shape
        width = attn_out.shape[1]
        tile = hidden // fs

        def kernel(
            live_ref,
            act_ref,
            down_ref,
            bias_ref,
            tokens_ref,
            attn_ref,
            cot_ref,
            d_mlp_ref,
            mods_ref,
            out_ref,
            sums_ref,
            total,
        ):
            step = pl.program_id(0)
            part = jnp.dot(act_ref[...], down_ref[...], preferred_element_type=f32)

            @pl.when(step == 0)
            def start():
                total[...] = part

            @pl.when(step > 0)
            def add():
                total[...] += part

            @pl.when(step == fs - 1)
            def finish():
                sums_ref[...] = jnp.zeros_like(sums_ref)

                def work(rows, first):
                    mlp_out = total[rows, :] + bias_ref[...]
                    middle = (
                        tokens_ref[rows, :].astype(f32) + mods_ref[2:3, :] * attn_ref[rows, :]
                    )
                    alive = alive_rows(first, mlp_out.shape[0], live_ref[0])
                    out_ref[rows, :] = (alive * (middle + mods_ref[5:6, :] * mlp_out)).astype(bf16)
                    d_gate = alive * cot_ref[rows, :].astype(f32) * mlp_out
                    sums_ref[0:1, :] += jnp.sum(d_gate, axis=0, keepdims=True)
                    sums_ref[1:2, :] += jnp.sum(
                        d_mlp_ref[rows, :].astype(f32), axis=0, keepdims=True
                    )

                chunks(slots, 32, work)

        def whole(shape):
            return pl.BlockSpec(shape, lambda j, live_ref: (0,) * len(shape))

        return pl.pallas_call(
            kernel,
            out_shape=[
                jax.ShapeDtypeStruct((slots, width), bf16),
                jax.ShapeDtypeStruct((8, width), f32),
            ],
            grid_spec=pltpu.PrefetchScalarGridSpec(
                num_scalar_prefetch=1,
                grid=(fs,),
                in_specs=[
                    pl.BlockSpec((slots, tile), lambda j, live_ref: (0, j)),
                    pl.BlockSpec((tile, width), lambda j, live_ref: (j, 0)),
                    whole((1, width)),
                    whole((slots, width)),
                    whole((slots, width)),
                    whole((slots, width)),
                    whole((slots, width)),
                    whole(mods.shape),
                ],
                out_specs=[whole((slots, width)), whole((8, width))],
                scratch_shapes=[pltpu.VMEM((slots, width), f32)],
            ),
            cost_estimate=cost(6),
            compiler_params=params(60),
        )(
            live,
            activated,
            down_full,
            bias_down.reshape(1, width),
            tokens_own,
            attn_out,
            cotangent_own,
            d_mlp,
            mods,
        )

    def column_grad(where, items, rights):
        slots = rights[0].shape[1]
        width = items[0][0][0].shape[1]
        tile = width // 3
        half = slots // 2
        counts = [(stop - start) // 2 for unused, start, stop in items]
        n_out = sum(counts)
        lefts = [left for box, unused, unused_stop in items for left in box]

        def kernel(where_ref, *refs):
            core = where_ref[0]
            y0, y1, y2, y3, keep_ref, send_ref = refs[len(lefts) :]
            for i, (unused, start, unused_stop) in enumerate(items):
                x0, x1, x2, x3, x4 = refs[5 * i : 5 * i + 5]
                n = counts[i]
                below = sum(counts[:i])
                for out_ref, first in ((keep_ref, core * n), (send_ref, (1 - core) * n)):
                    rows = pl.ds(pl.multiple_of(start + first, 16), n)
                    total = None
                    for x, y, cols in (
                        (x0, y0, slice(None)),
                        (x1, y1, slice(None)),
                        (x2, y2, slice(None)),
                        (x3, y3, slice(0, half)),
                        (x4, y3, slice(half, slots)),
                    ):
                        part = jnp.dot(y[rows, cols], x[...], preferred_element_type=f32)
                        total = part if total is None else total + part
                    out_ref[below : below + n, :] = total

        left_specs = [
            pl.BlockSpec((left.shape[0], tile), lambda i, where_ref: (0, i)) for left in lefts
        ]
        right_spec = pl.BlockSpec(rights[0].shape, lambda i, where_ref: (0, 0))
        out_spec = pl.BlockSpec((n_out, tile), lambda i, where_ref: (0, i))
        return pl.pallas_call(
            kernel,
            out_shape=[jax.ShapeDtypeStruct((n_out, width), f32)] * 2,
            grid_spec=pltpu.PrefetchScalarGridSpec(
                num_scalar_prefetch=1,
                grid=(width // tile,),
                in_specs=left_specs + [right_spec] * 4,
                out_specs=[out_spec] * 2,
            ),
            cost_estimate=cost(8),
            compiler_params=params(60),
        )(where, *lefts, *rights)

    def sums_message(first_sums, middle_sums, output_sums, d_pre_sums, cond_act):
        width = cond_act.shape[1]
        extra = d_pre_sums.shape[0]

        def kernel(first_ref, middle_ref, output_ref, d_pre_ref, cond_ref, out_ref):
            out_ref[0:2, :] = first_ref[0:2, :].astype(bf16).astype(f32)
            out_ref[2:5, :] = middle_ref[0:3, :].astype(bf16).astype(f32)
            out_ref[5:6, :] = output_ref[0:1, :].astype(bf16).astype(f32)
            for row in (6, 7):
                out_ref[row : row + 1, :] = cond_ref[...].astype(f32)
            out_ref[8:10, :] = first_ref[2:4, :]
            out_ref[10:11, :] = middle_ref[3:4, :]
            out_ref[11:12, :] = output_ref[1:2, :]
            out_ref[12:, :] = d_pre_ref[...]

        return pl.pallas_call(
            kernel,
            out_shape=jax.ShapeDtypeStruct((12 + extra, width), f32),
            in_specs=[vmem] * 5,
            out_specs=vmem,
            cost_estimate=cost(1),
            compiler_params=params(60),
        )(first_sums, middle_sums, output_sums, d_pre_sums, cond_act)

    def column_total(pairs):
        width = pairs[0][0].shape[1]
        n = sum(keep.shape[0] for keep, unused in pairs)
        padded = -(-n // 128) * 128

        def kernel(*refs):
            for first in range(0, width, 128):
                cols = slice(first, first + 128)
                totals = [
                    refs[2 * i][:, cols] + refs[2 * i + 1][:, cols] for i in range(len(pairs))
                ]
                if padded > n:
                    totals.append(jnp.zeros((padded - n, 128), f32))
                total = jnp.concatenate(totals, axis=0) if len(totals) > 1 else totals[0]
                refs[-1][cols, :] = total.T.astype(bf16)

        return pl.pallas_call(
            kernel,
            out_shape=jax.ShapeDtypeStruct((width, padded), bf16),
            in_specs=[vmem] * (2 * len(pairs)),
            out_specs=vmem,
            cost_estimate=cost(4),
            compiler_params=params(60),
        )(*[each for pair in pairs for each in pair])

    def row_total(keep, got):
        def kernel(keep_ref, got_ref, out_ref):
            out_ref[...] = (keep_ref[...] + got_ref[...]).astype(bf16)

        total = pl.pallas_call(
            kernel,
            out_shape=jax.ShapeDtypeStruct(keep.shape, bf16),
            in_specs=[vmem] * 2,
            out_specs=vmem,
            cost_estimate=cost(3),
            compiler_params=params(60),
        )(keep, got)
        return total.reshape(-1, keep.shape[2])

    def fsdp_sum(x):
        return lax.psum_scatter(x, "fsdp", scatter_dimension=0, tiled=True)

    def row_grad(where, lefts, rights):
        rows = lefts[0].shape[0] // fs
        slots, n = lefts[0].shape[1], rows // 2
        width = rights[0].shape[1]
        half = slots // 2

        def kernel(where_ref, x0, x1, x2, x3, y0, y1, y2, y3, y4, keep_ref, send_ref):
            core = where_ref[0]
            for out_ref, first in ((keep_ref, core * n), (send_ref, (1 - core) * n)):
                lines = pl.ds(pl.multiple_of(first, 16), n)
                total = None
                for x, y, cols in (
                    (x0, y0, slice(None)),
                    (x1, y1, slice(None)),
                    (x2, y2, slice(None)),
                    (x3, y3, slice(0, half)),
                    (x3, y4, slice(half, slots)),
                ):
                    part = jnp.dot(x[lines, cols], y[...], preferred_element_type=f32)
                    total = part if total is None else total + part
                out_ref[0] = total

        left_spec = pl.BlockSpec((rows, slots), lambda i, where_ref: (i, 0))
        right_specs = [
            pl.BlockSpec((right.shape[0], width), lambda i, where_ref: (0, 0))
            for right in rights
        ]
        out_spec = pl.BlockSpec((1, n, width), lambda i, where_ref: (i, 0, 0))
        return pl.pallas_call(
            kernel,
            out_shape=[jax.ShapeDtypeStruct((fs, n, width), f32)] * 2,
            grid_spec=pltpu.PrefetchScalarGridSpec(
                num_scalar_prefetch=1,
                grid=(fs,),
                in_specs=[left_spec] * 4 + right_specs,
                out_specs=[out_spec] * 2,
            ),
            cost_estimate=cost(6),
            compiler_params=params(60),
        )(where, *lefts, *rights)

    def body(
        tokens,
        condition,
        grid_sizes,
        w_ada,
        w_qkv,
        w_out,
        w_up,
        w_down,
        b_ada,
        b_qv,
        b_out,
        b_up,
        b_down,
        cotangent,
    ):
        slots, width = tokens.shape[1:]
        heads = width // HEAD_DIM
        hidden = w_up.shape[1]
        rank = lax.axis_index("dp")
        z = lax.axis_index("fsdp")
        place = lax.rem(rank, BOX)
        group = lax.div(rank, BOX)
        core = place & 1
        chip = place >> 1
        side = (chip ^ (chip >> 1)) & 1
        near = 2 * side + core
        far = 2 * (1 - side) + core
        where = jnp.stack(
            [lax.rem(z - k + fs, fs) for k in range(fs)]
            + [near, far, near ^ 1, far ^ 1]
            + [chip ^ k for k in range(4)]
        ).astype(jnp.int32)
        where_core = core.reshape(1).astype(jnp.int32)
        where_wide = jnp.stack(
            [lax.rem(z - k + fs, fs) for k in range(fs)] + [core] + [chip ^ k for k in range(4)]
        ).astype(jnp.int32)

        cond_wide = condition.astype(f32)
        gate = jax.nn.sigmoid(cond_wide)
        cond_act = (cond_wide * gate).astype(bf16)

        def quarter_of(shard):
            return pick(in_blocks(shard), near)

        qkv_quarter = quarter_of(w_qkv)
        cond_rows = ring_gather(after(cond_act, qkv_quarter))
        raw = jnp.concatenate([tokens[0], cotangent[0]], axis=1)
        qkv_helds = [ring_send(qkv_quarter, 1)]
        mid_rows = jnp.concatenate(
            [pick(in_blocks(w_out), chip), pick(in_blocks(w_up), chip)], axis=-1
        )
        mid_width = mid_rows.shape[-1]
        mid_part = -(-mid_width // 256) * 128
        mid_start = jnp.where(core == 0, 0, mid_width - mid_part)
        mid_eighth = lax.dynamic_slice_in_dim(mid_rows, mid_start, mid_part, 2)
        down_quarter = quarter_of(w_down)
        ada_shard = b_ada.shape[0]
        bias_ada = lax.dynamic_update_slice_in_dim(
            jnp.zeros((fs * ada_shard,), f32), b_ada.astype(f32), z * ada_shard, 0
        ).reshape(6, width)
        small = jnp.concatenate([b_qv, b_out, b_down, b_up]).astype(f32).reshape(-1, width)
        cond_rows, qkv_helds, bias_ada, small, mid_eighth, down_quarter = gated(
            (cond_rows, qkv_helds, bias_ada, small, mid_eighth, down_quarter)
        )

        rows_z = width // fs
        conds = jnp.concatenate(cond_rows)
        conds_z = lax.dynamic_slice_in_dim(conds, z * rows_z, rows_z, 1)
        partials = modulation_parts(conds_z, w_ada, bias_ada, small)
        partials = [partials[0]] + [ring_send(partials[k], fs - k) for k in range(1, fs)]
        raw_near = chip_near(after(raw, conds_z))
        qkv_helds.append(ring_send(qkv_helds[-1], 1))
        partials, qkv_helds = gated((partials, qkv_helds))

        live = (grid_sizes[0, 0] * grid_sizes[0, 1]).reshape(1)
        mods, head = modulation_rows(partials, live)
        (normed,), (d_mlp,) = other_heads((raw,), (0,), (head,))
        qkv_helds.append(ring_send(qkv_helds[-1], 1))
        mods, head, normed, d_mlp, raw_near, qkv_helds = gated(
            (mods, head, normed, d_mlp, raw_near, qkv_helds)
        )

        qkv_mine = jnp.stack(qkv_helds)
        qkv_other = side_send(qkv_mine)
        qkv_mine_got = box_send(qkv_mine, 1)
        mid_helds = [ring_send(after(mid_eighth, qkv_mine), 1)]
        bias_rows = [each[6:].reshape(-1) for each in partials]
        bias_rows = jnp.stack(bias_rows + bias_rows)
        biases = lax.dynamic_slice_in_dim(bias_rows, lax.rem(fs - z, fs), fs, 0)
        ends = [0]
        for bias in (b_qv, b_out, b_down, b_up):
            ends.append(ends[-1] + bias.shape[0])
        biases = [biases[:, ends[i] : ends[i + 1]].reshape(-1) for i in range(4)]
        qkv_mine, qkv_other, qkv_mine_got, mid_helds, biases = gated(
            (qkv_mine, qkv_other, qkv_mine_got, mid_helds, biases)
        )
        bias_qv, bias_out, bias_down, bias_up = biases

        last = fs - 1

        def in_order(array):
            return [(array, k) for k in range(last)]

        qkv_other_got = box_send(qkv_other, 1)
        raw_far = chip_far([after(each, qkv_other) for each in raw_near])
        mid_helds.append(ring_send(mid_helds[-1], 1))
        turned, qkv_full = projection(
            where,
            normed,
            w_qkv,
            [in_order(each) for each in (qkv_mine, qkv_other, qkv_mine_got, qkv_other_got)],
            bias_qv.reshape(2, width),
        )
        turned, qkv_full, mid_helds, raw_far = gated((turned, qkv_full, mid_helds, raw_far))

        heads_got = [box_send(after(head, turned), bits) for bits in (2, 4, 6)]
        mid_helds.append(ring_send(mid_helds[-1], 1))
        attended = attention(turned, live)
        attended, mid_helds, heads_got = gated((attended, mid_helds, heads_got))

        mid_mine = jnp.concatenate(mid_helds)
        mid_near = chip_near(mid_mine)
        mid_got = [box_send(mid_mine, 1)]
        down_helds = [ring_send(after(down_quarter, mid_mine), 1)]
        down_helds.append(ring_send(down_helds[-1], 1))
        normed_box, d_mlp_box = other_heads(
            (*raw_near, *raw_far), (0, 0, 0, slots // 2), (*heads_got, heads_got[2])
        )
        normed_box, d_mlp_box = [normed, *normed_box], [d_mlp, *d_mlp_box]
        attended, mid_mine, mid_near, mid_got, down_helds, normed_box, d_mlp_box = gated(
            (attended, mid_mine, mid_near, mid_got, down_helds, normed_box, d_mlp_box)
        )

        mid_far = chip_far(mid_near)
        mid_got += [box_send(each, 1) for each in mid_near]
        down_helds.append(ring_send(down_helds[-1], 1))
        attended, mid_far, mid_got, down_helds = gated((attended, mid_far, mid_got, down_helds))

        mid_got += [box_send(each, 1) for each in mid_far]
        down_others = [side_send(each) for each in down_helds]
        attn_out, normed_two, pre_act, activated, *act_blocks, out_full, up_full = middle_forward(
            where_wide,
            attended,
            tokens[0],
            [w_out, w_up],
            ((mid_mine, *mid_near, *mid_far), mid_got),
            bias_out,
            bias_up,
            mods,
        )
        down_helds, down_others, act_blocks, normed_two = gated(
            (down_helds, down_others, act_blocks, normed_two)
        )

        down_got = [[box_send(each, 1) for each in kind] for kind in (down_helds, down_others)]
        act_blocks, down_got = gated((act_blocks, down_got))

        act_box = chip_exchange(act_blocks)
        d_pre, *d_pre_turned, d_pre_sums, down_full = hidden_back(
            where,
            d_mlp,
            w_down,
            [[(each, None) for each in kind] for kind in (down_helds, down_others, *down_got)],
            pre_act,
        )

        def column_blocks(grad_t):
            n = grad_t.shape[0] // dp
            blocks = grad_t.reshape(groups, BOX, n, slots).transpose(1, 0, 2, 3)
            blocks = blocks.reshape(BOX // 2, 2 * groups * n, slots)
            return [pick(blocks, chip ^ k) for k in range(BOX // 2)]

        d_pre_blocks = d_pre_turned if groups == 1 else column_blocks(d_pre_turned[0])
        output, output_sums = output_rows(
            activated,
            down_full,
            bias_down,
            tokens[0],
            attn_out,
            cotangent[0],
            d_mlp,
            mods,
            live,
        )
        d_pre, d_pre_blocks, act_box, normed_two, output_sums = gated(
            (d_pre, d_pre_blocks, act_box, normed_two, output_sums)
        )

        d_pre_box = chip_exchange(d_pre_blocks)
        keep_down, send_down = row_grad(where_core, act_box, d_mlp_box)
        d_middle, d_attn_turned, d_attended_turned, middle_sums = middle_back(
            d_pre, up_full, out_full, attn_out, tokens[0], cotangent[0], mods, live
        )
        d_attended_turned, d_attn_turned, d_pre_box, keep_down, send_down, normed_two = gated(
            (d_attended_turned, d_attn_turned, d_pre_box, keep_down, send_down, normed_two)
        )

        normed_two_near = chip_near(normed_two)
        total_down = row_total(keep_down, box_send(send_down, 1))
        d_projected, *last_blocks = attention_back(
            turned, d_attended_turned, d_attn_turned, live, where[fs + 4 :]
        )
        if groups > 1:
            last_blocks = [
                jnp.concatenate(pair)
                for pair in zip(column_blocks(d_projected), column_blocks(d_attn_turned))
            ]
        normed_two_far = chip_far([after(each, d_projected) for each in normed_two_near])
        normed_two_box = [normed_two, *normed_two_near, *normed_two_far]
        d_projected, last_blocks, normed_two_box, total_down = gated(
            (d_projected, last_blocks, normed_two_box, total_down)
        )
        grad_down = fsdp_sum(total_down)

        last_box = chip_exchange(last_blocks)
        grad_tokens, first_sums = first_back(d_projected, qkv_full, tokens[0], d_middle, mods)
        keep_up, send_up = column_grad(
            after(where_core, first_sums), [(normed_two_box, 0, d_pre_box[0].shape[0])], d_pre_box
        )
        last_box, first_sums, keep_up, send_up = gated((last_box, first_sums, keep_up, send_up))

        total_up = column_total([(keep_up, box_send(send_up, 1))])
        attended_near = chip_near(attended)
        cut = 3 * last_box[0].shape[0] // 4
        keep_qkv, send_qkv = column_grad(where_core, [(normed_box, 0, cut)], last_box)
        attended_far = chip_far([after(each, (keep_qkv, total_up)) for each in attended_near])
        attended_box = [attended, *attended_near, *attended_far]
        message = sums_message(
            first_sums, middle_sums, output_sums, d_pre_sums.reshape(-1, width), cond_act
        )
        messages = ring_gather(message)
        total_up, keep_qkv, send_qkv, messages, attended_box = gated(
            (total_up, keep_qkv, send_qkv, messages, attended_box)
        )
        grad_up = fsdp_sum(total_up)

        got_qkv = box_send(send_qkv, 1)
        keep_out, send_out = column_grad(
            where_core, [(attended_box, cut, last_box[0].shape[0])], last_box
        )
        got_out = box_send(send_out, 1)
        grad_last = fsdp_sum(column_total([(keep_qkv, got_qkv), (keep_out, got_out)]))
        images_near = jnp.stack([each[:8] for each in messages]).astype(bf16)
        totals = [each[8:] for each in messages]

        def over_groups(grad):
            rows, cols = grad.shape
            return group_sum(grad.reshape(rows, groups, -1).transpose(1, 0, 2), group)

        cut_cols, last_cols = cut // 2, last_box[0].shape[0] // 2
        grad_w_up = over_groups(grad_up[:, : d_pre_box[0].shape[0] // 2].astype(f32))
        grad_w_qkv = over_groups(grad_last[:, :cut_cols].astype(f32))
        grad_w_out = over_groups(grad_last[:, cut_cols:last_cols].astype(f32))

        images, total = images_near, sum(totals[1:], totals[0])
        for bits in (1, 2, 4):
            images = jnp.concatenate([images, box_send(images, bits)])
            total = total + box_send(total, bits)
        images_box, total_box = images, total
        for k in range(1, groups):
            images = jnp.concatenate([images, group_send(images_box, k)])
            total = total + group_send(total_box, k)
        grad_down = over_groups(after(grad_down, got_qkv).astype(f32))
        down_rows = grad_down.shape[0]
        down_blocks = grad_down.reshape(down_rows, BOX, -1).transpose(1, 0, 2)
        if groups == 1:
            parts = lax.all_to_all(down_blocks, "dp", 0, 0, tiled=True)
        else:
            parts = [pick(down_blocks, place)] + [
                box_send(pick(down_blocks, place ^ k), k) for k in range(1, BOX)
            ]
            parts = jnp.stack(parts)
            parts = jnp.stack([pick(parts, place ^ k) for k in range(BOX)])
        grad_w_down = parts.reshape(BOX * down_rows, width // dp)
        conds_all = lax.dynamic_slice_in_dim(images[:, 6], z * rows_z, rows_z, 1)
        d_mod_all = images[:, :6]
        ada_cols = 6 * width // dp
        grad_w_ada = lax.dot_general(
            conds_all,
            lax.dynamic_slice_in_dim(
                d_mod_all.reshape(dp * fs, 6 * width), rank * ada_cols, ada_cols, 1
            ),
            (((0,), (0,)), ((), ())),
            preferred_element_type=f32,
        )
        d_conds = lax.dot_general(
            images_near[:, :6].reshape(fs, 6 * width),
            w_ada,
            (((1,), (1,)), ((), ())),
            preferred_element_type=f32,
        )
        cond_parts = [d_conds[0]] + [ring_send(d_conds[k], fs - k) for k in range(1, fs)]
        twice = jnp.stack(cond_parts + cond_parts)
        d_cond_act = lax.dynamic_slice_in_dim(twice, lax.rem(fs - z, fs), fs, 0).reshape(-1)
        grad_condition = d_cond_act[None] * gate * (1.0 + cond_wide * (1.0 - gate))

        def shard_of(rows):
            return pick(rows.reshape(fs, -1), z)

        grads_bias = [
            shard_of(jnp.sum(d_mod_all.astype(f32), axis=0)),
            shard_of(total[:2]),
            shard_of(total[2]),
            shard_of(total[4:]),
            shard_of(total[3]),
        ]
        return (
            output[None],
            grad_tokens[None],
            grad_condition,
            grad_w_ada,
            grad_w_qkv,
            grad_w_out,
            grad_w_up,
            grad_w_down,
            *grads_bias,
        )

    return body


def solution(mesh):
    return jax.shard_map(
        make_body(mesh.shape["dp"], mesh.shape["fsdp"]),
        mesh=mesh,
        in_specs=(
            P(("dp", "fsdp"), None, None),
            P(("dp", "fsdp"), None),
            P(("dp", "fsdp"), None),
            P("fsdp", None),
            P("fsdp", None),
            P("fsdp", None),
            P("fsdp", None),
            P("fsdp", None),
            P("fsdp"),
            P("fsdp"),
            P("fsdp"),
            P("fsdp"),
            P("fsdp"),
            P(("dp", "fsdp"), None, None),
        ),
        out_specs=(
            P(("dp", "fsdp"), None, None),
            P(("dp", "fsdp"), None, None),
            P(("dp", "fsdp"), None),
            P("fsdp", "dp"),
            P("fsdp", "dp"),
            P("fsdp", "dp"),
            P("fsdp", "dp"),
            P("fsdp", "dp"),
            P("fsdp"),
            P("fsdp"),
            P("fsdp"),
            P("fsdp"),
            P("fsdp"),
        ),
        check_vma=False,
    )
```

```python
import math

import jax
import jax.numpy as jnp
from jax import lax
from jax.experimental import pallas as pl
from jax.experimental.pallas import tpu as pltpu
from jax.sharding import PartitionSpec as P

HEAD_DIM = 72
BOX = 8

epsilon = 1e-06
masked_value = -1e30
gelu_root = math.sqrt(2.0 / math.pi)
f32 = jnp.float32
bf16 = jnp.bfloat16


def norm_parts(values_in):
    centred = values_in - jnp.mean(values_in, axis=-1, keepdims=True)
    spread = jnp.mean(centred * centred, axis=-1, keepdims=True)
    rate = lax.rsqrt(spread + epsilon)
    return centred * rate, rate


def norm_back(normal, rate, grad):
    mean_grad = jnp.mean(grad, axis=-1, keepdims=True)
    mean_both = jnp.mean(grad * normal, axis=-1, keepdims=True)
    return rate * (grad - mean_grad - normal * mean_both)


def gelu_tanh(pre_act):
    return (
        0.5
        * pre_act
        * (1.0 + jnp.tanh(gelu_root * (pre_act + 0.044715 * pre_act * pre_act * pre_act)))
    )


def after(value, other):
    return lax.optimization_barrier((value, other))[0]


def gated(values):
    return lax.optimization_barrier(values)


def pick(array, index, axis=0):
    return lax.dynamic_index_in_dim(array, index, axis, keepdims=False)


def make_body(dp, fs):
    groups = dp // BOX

    def box_send(x, bits):
        return lax.ppermute(x, "dp", [(i, i ^ bits) for i in range(dp)])

    def side_send(x):
        return lax.ppermute(x, "dp", [(i, i ^ (4 if i & 1 else 2)) for i in range(dp)])

    def ring_send(x, hops):
        return lax.ppermute(x, "fsdp", [(i, (i + hops) % fs) for i in range(fs)])

    def group_send(x, hops):
        return lax.ppermute(x, "dp", [(i, (i + hops * BOX) % dp) for i in range(dp)])

    def ring_gather(x):
        return [x] + [ring_send(x, k) for k in range(1, fs)]

    def ring_sorted(blocks, z):
        back = jnp.stack(blocks[::-1] + blocks[::-1])
        return lax.dynamic_slice_in_dim(back, fs - 1 - z, fs, 0)

    def chip_near(x):
        return box_send(x, 2), box_send(x, 4)

    def chip_far(near):
        half = near[0].shape[0] // 2
        return box_send(near[0][:half], 4), box_send(near[1][half:], 2)

    def chip_exchange(blocks):
        return [blocks[0]] + [box_send(blocks[k], 2 * k) for k in range(1, BOX // 2)]

    def ring_sum(x, z):
        total = pick(x, z)
        for k in range(1, fs):
            sent = pick(x, lax.rem(z + k, fs)).astype(bf16)
            total = total + ring_send(sent, k).astype(f32)
        return total

    def group_sum(x, group):
        total = pick(x, group)
        for k in range(1, groups):
            total = total + group_send(pick(x, lax.rem(group + k, groups)), k)
        return total

    def cost(microseconds):
        return pl.CostEstimate(
            flops=int(microseconds * 1e8),
            transcendentals=0,
            bytes_accessed=int(microseconds * 3.2e5),
        )

    vmem = pl.BlockSpec(memory_space=pltpu.VMEM)
    smem = pl.BlockSpec(memory_space=pltpu.SMEM)

    def params(mebibytes):
        return pltpu.CompilerParams(vmem_limit_bytes=mebibytes << 20)

    def chunks(rows, step, work):
        def one(i, unused):
            work(pl.ds(pl.multiple_of(i * step, step), step), i * step)
            return unused

        lax.fori_loop(0, rows // step, one, 0)

    def alive_rows(first, rows, live):
        return ((lax.broadcasted_iota(jnp.int32, (rows, 1), 0) + first) < live).astype(f32)

    def modulation_parts(conds, w_ada, bias_ada, extra):
        images = conds.shape[0]
        parts, width = bias_ada.shape

        def kernel(cond_ref, w_ref, bias_ref, extra_ref, *out_refs):
            for part in range(parts):
                cols = slice(part * width, (part + 1) * width)
                product = jnp.dot(cond_ref[...], w_ref[:, cols], preferred_element_type=f32)
                product = product + bias_ref[part : part + 1, :]
                for image, out_ref in enumerate(out_refs):
                    out_ref[part : part + 1, :] = product[image : image + 1, :]
            for out_ref in out_refs:
                out_ref[parts:, :] = extra_ref[...]

        rows = parts + extra.shape[0]
        return pl.pallas_call(
            kernel,
            out_shape=[jax.ShapeDtypeStruct((rows, width), f32)] * images,
            in_specs=[vmem] * 4,
            out_specs=[vmem] * images,
            cost_estimate=cost(4),
            compiler_params=params(60),
        )(conds, w_ada, bias_ada, extra)

    def modulation_rows(partials, live):
        rows, width = partials[0].shape

        def kernel(live_ref, *refs):
            mods_ref, head_ref = refs[-2:]
            total = refs[0][...]
            for ref in refs[1:-2]:
                total = total + ref[...]
            mods_ref[...] = total
            head_ref[...] = jnp.full(head_ref.shape, live_ref[0].astype(f32))
            head_ref[0:2, :] = total[0:2, :]
            head_ref[2:3, :] = total[5:6, :]

        return pl.pallas_call(
            kernel,
            out_shape=[jax.ShapeDtypeStruct((rows, width), f32)] * 2,
            in_specs=[smem] + [vmem] * len(partials),
            out_specs=[vmem] * 2,
            cost_estimate=cost(1),
            compiler_params=params(60),
        )(live, *partials)

    def other_heads(raws, firsts, heads):
        n = len(raws)
        width = raws[0].shape[1] // 2

        def kernel(*refs):
            raw_refs, head_refs = refs[:n], refs[n : 2 * n]
            normed_refs, d_mlp_refs = refs[2 * n : 3 * n], refs[3 * n :]
            for raw, head, normed, d_mlp, first in zip(
                raw_refs, head_refs, normed_refs, d_mlp_refs, firsts
            ):
                live = head[3, 0].astype(jnp.int32)

                def work(rows, start):
                    normal = norm_parts(raw[rows, :width].astype(f32))[0]
                    normed[rows, :] = (
                        normal * (1.0 + head[1:2, :]) + head[0:1, :]
                    ).astype(bf16)
                    count = normal.shape[0]
                    up_rows = alive_rows(start + first, count, live) * raw[
                        rows, width:
                    ].astype(f32)
                    d_mlp[rows, :] = (head[2:3, :] * up_rows).astype(bf16)

                chunks(raw.shape[0], 32, work)

        outs = pl.pallas_call(
            kernel,
            out_shape=[jax.ShapeDtypeStruct((raw.shape[0], width), bf16) for raw in raws] * 2,
            in_specs=[vmem] * (2 * n),
            out_specs=[vmem] * (2 * n),
            cost_estimate=cost(8),
            compiler_params=params(60),
        )(*raws, *heads)
        return outs[:n], outs[n:]

    def piece_plan(pieces):
        arrays = []
        for piece, unused in (each for kind in pieces for each in kind):
            if not any(piece is array for array in arrays):
                arrays.append(piece)
        position = {id(array): i for i, array in enumerate(arrays)}
        plan = [[(position[id(piece)], index) for piece, index in kind] for kind in pieces]
        return arrays, plan

    def piece_copies(where_ref, own_ref, array_refs, plan, whole_ref):
        copies = [(own_ref, whole_ref.at[where_ref[0]])]
        for kind, blocks in enumerate(plan):
            for k, (which, index) in enumerate(blocks):
                source = array_refs[which] if index is None else array_refs[which].at[index]
                copies.append((source, whole_ref.at[where_ref[k + 1], where_ref[fs + kind]]))
        return copies

    def wide_copies(core, where_ref, own_refs, sets, whole_refs):
        widths = [ref.shape[-1] for ref in own_refs]
        width, part = sum(widths), sets[0][0].shape[-1]
        lead, split = whole_refs[0].shape[2], sets[0][3].shape[0]
        copies = [(own, whole.at[where_ref[0]]) for own, whole in zip(own_refs, whole_refs)]
        for side, piece_refs in enumerate(sets):
            low, high = (0, part) if core ^ side == 0 else (part, width)
            offset = 0 if core ^ side == 0 else width - part
            for block in range(1, fs):
                base = (block - 1) * lead
                top = min(max(split - base, 0), lead)
                rows = [(i, base, i, 0, lead) for i in range(3)]
                if top:
                    rows.append((3, base, 3, 0, top))
                if top < lead:
                    rows.append((4, base + top - split, 3, top, lead - top))
                for piece, first, slot, row, count in rows:
                    start = 0
                    for i, each in enumerate(widths):
                        left, right = max(low, start), min(high, start + each)
                        if left < right:
                            source = piece_refs[piece].at[
                                first : first + count, :, left - offset : right - offset
                            ]
                            target = whole_refs[i].at[
                                where_ref[block],
                                where_ref[fs + 1 + slot],
                                row : row + count,
                                :,
                                left - start : right - start,
                            ]
                            copies.append((source, target))
                        start += each
        return copies

    def copy_all(copies, sems):
        return [
            pltpu.make_async_copy(source, target, sems.at[j])
            for j, (source, target) in enumerate(copies)
        ]

    def start_all(copies):
        for copy in copies:
            copy.start()

    def wait_all(copies):
        for copy in copies:
            copy.wait()

    def in_blocks(shard):
        rows, cols = shard.shape
        return shard.reshape(4, rows // 32, 8, cols)

    any_spec = pl.BlockSpec(memory_space=pl.ANY)

    def projection(where, normed, own, pieces, biases):
        slots, width = normed.shape
        arrays, plan = piece_plan(pieces)
        own = in_blocks(own)
        shape = (fs,) + own.shape

        def kernel(where_ref, normed_ref, bias_ref, own_ref, *refs):
            array_refs = refs[: len(arrays)]
            turned_ref, whole_ref, scratch, sems, out_sem = refs[len(arrays) :]
            copies = copy_all(
                piece_copies(where_ref, own_ref, array_refs, plan, scratch), sems
            )
            start_all(copies)
            wait_all(copies)
            out = pltpu.make_async_copy(scratch, whole_ref, out_sem)
            out.start()
            w_ref = scratch.reshape(width, 3 * width)
            for part in range(3):
                cols = slice(part * width, (part + 1) * width)
                proj = jnp.dot(normed_ref[...], w_ref[:, cols], preferred_element_type=f32)
                if part != 1:
                    proj = proj + bias_ref[part // 2 : part // 2 + 1, :]
                turned_ref[cols, :] = proj.astype(bf16).astype(f32).T
            out.wait()

        turned, whole = pl.pallas_call(
            kernel,
            out_shape=[
                jax.ShapeDtypeStruct((3 * width, slots), f32),
                jax.ShapeDtypeStruct(shape, bf16),
            ],
            in_specs=[smem, vmem, vmem, any_spec] + [any_spec] * len(arrays),
            out_specs=[vmem, any_spec],
            scratch_shapes=[
                pltpu.VMEM(shape, bf16),
                pltpu.SemaphoreType.DMA((1 + 4 * (fs - 1),)),
                pltpu.SemaphoreType.DMA,
            ],
            cost_estimate=cost(11),
            compiler_params=params(60),
        )(where, normed, biases, own, *arrays)
        return turned, whole.reshape(width, 3 * width)

    def attention(turned, live):
        slots = turned.shape[1]
        width = turned.shape[0] // 3
        count = width // HEAD_DIM
        heads_at_once = 2 if count % 2 == 0 else 1
        scale = HEAD_DIM ** (-0.5)

        def kernel(live_ref, turned_ref, attended_ref, out_turned):
            live_keys = lax.broadcasted_iota(jnp.int32, (1, slots), 1) < live_ref[0]

            def head(h):
                def rows(part):
                    first = pl.multiple_of(part * width + h * HEAD_DIM, 8)
                    return turned_ref[pl.ds(first, HEAD_DIM), :].astype(bf16)

                scores = lax.dot_general(
                    rows(0), rows(1), (((0,), (0,)), ((), ())), preferred_element_type=f32
                )
                scores = jnp.where(live_keys, scores * scale, masked_value)
                highest = jnp.max(scores, axis=-1, keepdims=True)
                total = jnp.sum(jnp.exp(scores - highest), axis=-1, keepdims=True)
                probs = jnp.exp(scores - (highest + jnp.log(total)))
                return lax.dot_general(
                    rows(2),
                    probs.astype(bf16),
                    (((1,), (1,)), ((), ())),
                    preferred_element_type=f32,
                )

            def some_heads(i, unused):
                outs = [head(i * heads_at_once + j) for j in range(heads_at_once)]
                for j, out in enumerate(outs):
                    first = pl.multiple_of((i * heads_at_once + j) * HEAD_DIM, 8)
                    out_turned[pl.ds(first, HEAD_DIM), :] = out
                return unused

            lax.fori_loop(0, count // heads_at_once, some_heads, 0)
            attended_ref[...] = out_turned[...].T.astype(bf16)

        return pl.pallas_call(
            kernel,
            out_shape=jax.ShapeDtypeStruct((slots, width), bf16),
            in_specs=[smem, vmem],
            out_specs=vmem,
            scratch_shapes=[pltpu.VMEM((width, slots), f32)],
            cost_estimate=cost(11),
            compiler_params=params(60),
        )(live, turned)

    def attention_back(turned, d_turned, live, where_chip):
        width, slots = d_turned.shape
        part = 3 * width // 4
        count = width // HEAD_DIM
        heads_at_once = 1
        scale = HEAD_DIM ** (-0.5)

        def kernel(live_ref, chip_ref, turned_ref, d_ref, out_ref, *rest):
            block_refs, total_ref = rest[:-1], rest[-1]
            live_keys = lax.broadcasted_iota(jnp.int32, (1, slots), 1) < live_ref[0]

            def place_of(h, part):
                return pl.ds(pl.multiple_of(part * width + h * HEAD_DIM, 8), HEAD_DIM)

            def head(h):
                def place(part):
                    return place_of(h, part)

                query = turned_ref[place(0), :].astype(bf16)
                key_part = turned_ref[place(1), :].astype(bf16)
                value = turned_ref[place(2), :].astype(bf16)
                d_out = d_ref[place(0), :].astype(bf16)
                both_first = (((0,), (0,)), ((), ()))
                scores = lax.dot_general(
                    query, key_part, both_first, preferred_element_type=f32
                )
                scores = jnp.where(live_keys, scores * scale, masked_value)
                highest = jnp.max(scores, axis=-1, keepdims=True)
                total = jnp.sum(jnp.exp(scores - highest), axis=-1, keepdims=True)
                probs = jnp.exp(scores - (highest + jnp.log(total)))
                d_probs = lax.dot_general(
                    d_out, value, both_first, preferred_element_type=f32
                )
                inner = jnp.sum(probs * d_probs, axis=-1, keepdims=True)
                d_scores = (probs * (d_probs - inner)).astype(bf16)
                d_value = jnp.dot(d_out, probs.astype(bf16), preferred_element_type=f32)
                d_query = scale * lax.dot_general(
                    key_part, d_scores, (((1,), (1,)), ((), ())), preferred_element_type=f32
                )
                d_key = scale * jnp.dot(query, d_scores, preferred_element_type=f32)
                return d_query, d_key, d_value

            def some_heads(i, unused):
                outs = [head(i * heads_at_once + j) for j in range(heads_at_once)]
                for j, parts in enumerate(outs):
                    for part, out in enumerate(parts):
                        total_ref[place_of(i * heads_at_once + j, part), :] = out
                return unused

            lax.fori_loop(0, count // heads_at_once, some_heads, 0)
            out_ref[...] = total_ref[...].astype(bf16)
            for k, block in enumerate(block_refs):
                first = pl.multiple_of(chip_ref[k] * part, 16)
                block[...] = total_ref[pl.ds(first, part), :].astype(bf16)

        n_blocks = 4 if groups == 1 else 0
        return pl.pallas_call(
            kernel,
            out_shape=[jax.ShapeDtypeStruct((3 * width, slots), bf16)]
            + [jax.ShapeDtypeStruct((part, slots), bf16)] * n_blocks,
            in_specs=[smem, smem, vmem, vmem],
            out_specs=[vmem] * (1 + n_blocks),
            scratch_shapes=[pltpu.VMEM((3 * width, slots), f32)],
            cost_estimate=cost(12),
            compiler_params=params(60),
        )(live, where_chip, turned, d_turned)

    def middle_forward(where, attended, tokens_own, owns, sets, bias_out, bias_up, mods):
        slots, width = attended.shape
        owns = [in_blocks(own) for own in owns]
        hidden = owns[1].shape[-1]
        tile = hidden // fs
        quarter = tile // 4
        shapes = [(fs,) + own.shape for own in owns]
        n_pieces = len(sets[0])
        n_copies = 2 + 2 * 15 * (fs - 1)

        def kernel(where_ref, attended_ref, tokens_ref, bias_out_ref, bias_up_ref, mods_ref, *refs):
            own_refs = refs[:2]
            set_refs = (refs[2 : 2 + n_pieces], refs[2 + n_pieces : 2 + 2 * n_pieces])
            (
                attn_ref,
                normed_ref,
                pre_ref,
                act_ref,
                block0,
                block1,
                block2,
                block3,
                whole_out,
                whole_up,
                scratch_out,
                scratch_up,
                turned,
                sems,
                out_sems,
            ) = refs[2 + 2 * n_pieces :]
            step = pl.program_id(0)
            scratches, wholes = (scratch_out, scratch_up), (whole_out, whole_up)

            def outs():
                return [
                    pltpu.make_async_copy(scratch, whole, out_sems.at[i])
                    for i, (scratch, whole) in enumerate(zip(scratches, wholes))
                ]

            @pl.when(step == 0)
            def first():
                for core in range(2):

                    @pl.when(where_ref[fs] == core)
                    def gather(core=core):
                        copies = copy_all(
                            wide_copies(core, where_ref, own_refs, set_refs, scratches), sems
                        )
                        start_all(copies)
                        wait_all(copies)

                start_all(outs())
                attn_ref[...] = (
                    jnp.dot(
                        attended_ref[...],
                        scratch_out.reshape(width, width)[...],
                        preferred_element_type=f32,
                    )
                    + bias_out_ref[...]
                )

                def work(rows, unused):
                    middle = tokens_ref[rows, :].astype(f32) + mods_ref[2:3, :] * attn_ref[rows, :]
                    normal = norm_parts(middle)[0]
                    normed_ref[rows, :] = (
                        normal * (1.0 + mods_ref[4:5, :]) + mods_ref[3:4, :]
                    ).astype(bf16)

                chunks(slots, 32, work)

            cols = pl.ds(pl.multiple_of(step * tile, 128), tile)
            pre_ref[...] = (
                jnp.dot(
                    normed_ref[...],
                    scratch_up.reshape(width, hidden)[:, cols],
                    preferred_element_type=f32,
                )
                + bias_up_ref[0]
            )

            def work(rows, unused):
                act_ref[rows, :] = gelu_tanh(pre_ref[rows, :]).astype(bf16)

            chunks(slots, 32, work)
            turned[...] = act_ref[...].astype(f32).T
            for k, block in enumerate((block0, block1, block2, block3)):
                first = pl.multiple_of(where_ref[fs + 1 + k] * quarter, 16)
                block[...] = turned[pl.ds(first, quarter), :].astype(bf16)

            @pl.when(step == fs - 1)
            def last():
                wait_all(outs())

        def whole(shape):
            return pl.BlockSpec(shape, lambda j, where_ref: (0,) * len(shape))

        *results, whole_out, whole_up = pl.pallas_call(
            kernel,
            out_shape=[
                jax.ShapeDtypeStruct((slots, width), f32),
                jax.ShapeDtypeStruct((slots, width), bf16),
                jax.ShapeDtypeStruct((slots, hidden), f32),
                jax.ShapeDtypeStruct((slots, hidden), bf16),
            ]
            + [jax.ShapeDtypeStruct((fs * quarter, slots), bf16)] * 4
            + [jax.ShapeDtypeStruct(shape, bf16) for shape in shapes],
            grid_spec=pltpu.PrefetchScalarGridSpec(
                num_scalar_prefetch=1,
                grid=(fs,),
                in_specs=[
                    whole((slots, width)),
                    whole((slots, width)),
                    whole((1, width)),
                    pl.BlockSpec((1, 1, tile), lambda j, where_ref: (j, 0, 0)),
                    whole(mods.shape),
                ]
                + [any_spec] * (2 + 2 * n_pieces),
                out_specs=[
                    whole((slots, width)),
                    whole((slots, width)),
                    pl.BlockSpec((slots, tile), lambda j, where_ref: (0, j)),
                    pl.BlockSpec((slots, tile), lambda j, where_ref: (0, j)),
                ]
                + [pl.BlockSpec((quarter, slots), lambda j, where_ref: (j, 0))] * 4
                + [any_spec, any_spec],
                scratch_shapes=[pltpu.VMEM(shape, bf16) for shape in shapes]
                + [
                    pltpu.VMEM((tile, slots), f32),
                    pltpu.SemaphoreType.DMA((n_copies,)),
                    pltpu.SemaphoreType.DMA((2,)),
                ],
            ),
            cost_estimate=cost(20),
            compiler_params=params(60),
        )(
            where,
            attended,
            tokens_own,
            bias_out.reshape(1, width),
            bias_up.reshape(fs, 1, tile),
            mods,
            *owns,
            *sets[0],
            *sets[1],
        )
        return (
            *results,
            whole_out.reshape(width, width),
            whole_up.reshape(width, hidden),
        )

    def hidden_back(where, d_mlp, own, pieces, pre_act):
        slots, width = d_mlp.shape
        hidden = pre_act.shape[1]
        tile = hidden // fs
        if groups == 1:
            turned_shapes = [jax.ShapeDtypeStruct((tile, slots), bf16)] * 4
            turned_specs = [pl.BlockSpec((tile, slots), lambda j, where_ref: (0, 0))] * 4
        else:
            turned_shapes = [jax.ShapeDtypeStruct((hidden, slots), bf16)]
            turned_specs = [pl.BlockSpec((tile, slots), lambda j, where_ref: (j, 0))]
        arrays, plan = piece_plan(pieces)
        own = in_blocks(own)
        shape = (fs,) + own.shape

        def kernel(where_ref, d_mlp_ref, pre_ref, own_ref, *refs):
            array_refs = refs[: len(arrays)]
            d_pre_ref, *turned_refs, sum_ref, whole_ref = refs[len(arrays) : -4]
            d_act_ref, scratch, sems, out_sem = refs[-4:]
            step = pl.program_id(0)

            def out():
                return pltpu.make_async_copy(scratch, whole_ref, out_sem)

            @pl.when(step == 0)
            def first():
                copies = copy_all(
                    piece_copies(where_ref, own_ref, array_refs, plan, scratch), sems
                )
                start_all(copies)
                wait_all(copies)
                out().start()

            d_act_ref[...] = lax.dot_general(
                d_mlp_ref[...],
                scratch.at[step].reshape(tile, width)[...],
                (((1,), (1,)), ((), ())),
                preferred_element_type=f32,
            )

            def work(rows, unused):
                pre = pre_ref[rows, :]
                square = pre * pre
                bend = jnp.tanh(gelu_root * (pre + 0.044715 * square * pre))
                slope = 0.5 * (1.0 + bend) + 0.5 * pre * (1.0 - bend * bend) * gelu_root * (
                    1.0 + 3.0 * 0.044715 * square
                )
                d_pre = (d_act_ref[rows, :] * slope).astype(bf16)
                d_pre_ref[rows, :] = d_pre
                d_act_ref[rows, :] = d_pre.astype(f32)

            chunks(slots, 32, work)
            sum_ref[0] = jnp.sum(d_act_ref[...], axis=0, keepdims=True)
            if groups == 1:
                for k, turned_ref in enumerate(turned_refs):

                    @pl.when(step == where_ref[fs + 4 + k])
                    def block(turned_ref=turned_ref):
                        turned_ref[...] = d_act_ref[...].T.astype(bf16)
            else:
                turned_refs[0][...] = d_act_ref[...].T.astype(bf16)

            @pl.when(step == fs - 1)
            def last():
                out().wait()

        *results, whole = pl.pallas_call(
            kernel,
            out_shape=[
                jax.ShapeDtypeStruct((slots, hidden), bf16),
                *turned_shapes,
                jax.ShapeDtypeStruct((fs, 1, tile), f32),
                jax.ShapeDtypeStruct(shape, bf16),
            ],
            grid_spec=pltpu.PrefetchScalarGridSpec(
                num_scalar_prefetch=1,
                grid=(fs,),
                in_specs=[
                    pl.BlockSpec((slots, width), lambda j, where_ref: (0, 0)),
                    pl.BlockSpec((slots, tile), lambda j, where_ref: (0, j)),
                    any_spec,
                ]
                + [any_spec] * len(arrays),
                out_specs=[
                    pl.BlockSpec((slots, tile), lambda j, where_ref: (0, j)),
                    *turned_specs,
                    pl.BlockSpec((1, 1, tile), lambda j, where_ref: (j, 0, 0)),
                    any_spec,
                ],
                scratch_shapes=[
                    pltpu.VMEM((slots, tile), f32),
                    pltpu.VMEM(shape, bf16),
                    pltpu.SemaphoreType.DMA((1 + 4 * (fs - 1),)),
                    pltpu.SemaphoreType.DMA,
                ],
            ),
            cost_estimate=cost(15),
            compiler_params=params(60),
        )(where, d_mlp, pre_act, own, *arrays)
        return (*results, whole.reshape(hidden, width))

    def middle_back(d_pre, up_full, out_full, attn_out, tokens_own, cotangent_own, mods, live):
        slots, hidden = d_pre.shape
        width = attn_out.shape[1]
        tile = hidden // fs

        def kernel(
            live_ref,
            d_pre_ref,
            up_ref,
            out_ref,
            attn_ref,
            tokens_ref,
            cot_ref,
            mods_ref,
            d_middle_ref,
            d_attn_turned_ref,
            d_attended_turned_ref,
            sums_ref,
            total,
            d_attn_ref,
        ):
            step = pl.program_id(0)
            part = lax.dot_general(
                d_pre_ref[...],
                up_ref[...],
                (((1,), (1,)), ((), ())),
                preferred_element_type=f32,
            )

            @pl.when(step == 0)
            def start():
                total[...] = part

            @pl.when(step > 0)
            def add():
                total[...] += part

            @pl.when(step == fs - 1)
            def finish():
                sums_ref[...] = jnp.zeros_like(sums_ref)

                def work(rows, first):
                    grad = total[rows, :]
                    attn = attn_ref[rows, :]
                    middle = tokens_ref[rows, :].astype(f32) + mods_ref[2:3, :] * attn
                    normal, rate = norm_parts(middle)
                    alive = alive_rows(first, grad.shape[0], live_ref[0])
                    d_middle = alive * cot_ref[rows, :].astype(f32) + norm_back(
                        normal, rate, grad * (1.0 + mods_ref[4:5, :])
                    )
                    d_middle_ref[rows, :] = d_middle
                    d_attn = (mods_ref[2:3, :] * d_middle).astype(bf16)
                    d_attn_ref[rows, :] = d_attn
                    for i, each in enumerate(
                        (d_middle * attn, grad, grad * normal, d_attn.astype(f32))
                    ):
                        sums_ref[i : i + 1, :] += jnp.sum(each, axis=0, keepdims=True)

                chunks(slots, 32, work)
                d_attn_turned_ref[...] = d_attn_ref[...].astype(f32).T.astype(bf16)
                d_attended = lax.dot_general(
                    d_attn_ref[...],
                    out_ref[...],
                    (((1,), (1,)), ((), ())),
                    preferred_element_type=f32,
                )
                d_attended_turned_ref[...] = d_attended.astype(bf16).astype(f32).T

        def whole(shape):
            return pl.BlockSpec(shape, lambda j, live_ref: (0,) * len(shape))

        return pl.pallas_call(
            kernel,
            out_shape=[
                jax.ShapeDtypeStruct((slots, width), f32),
                jax.ShapeDtypeStruct((width, slots), bf16),
                jax.ShapeDtypeStruct((width, slots), f32),
                jax.ShapeDtypeStruct((8, width), f32),
            ],
            grid_spec=pltpu.PrefetchScalarGridSpec(
                num_scalar_prefetch=1,
                grid=(fs,),
                in_specs=[
                    pl.BlockSpec((slots, tile), lambda j, live_ref: (0, j)),
                    pl.BlockSpec((width, tile), lambda j, live_ref: (0, j)),
                    whole((width, width)),
                    whole((slots, width)),
                    whole((slots, width)),
                    whole((slots, width)),
                    whole(mods.shape),
                ],
                out_specs=[
                    whole((slots, width)),
                    whole((width, slots)),
                    whole((width, slots)),
                    whole((8, width)),
                ],
                scratch_shapes=[
                    pltpu.VMEM((slots, width), f32),
                    pltpu.VMEM((slots, width), bf16),
                ],
            ),
            cost_estimate=cost(12),
            compiler_params=params(60),
        )(live, d_pre, up_full, out_full, attn_out, tokens_own, cotangent_own, mods)

    def first_back(d_turned, qkv_full, tokens_own, d_middle, mods):
        slots, width = d_middle.shape

        def kernel(d_ref, w_ref, tokens_ref, d_middle_ref, mods_ref, grad_ref, sums_ref, total):
            sums_ref[...] = jnp.zeros_like(sums_ref)
            for part in range(3):
                cols = slice(part * width, (part + 1) * width)
                d_part = d_ref[cols, :].astype(f32).T
                if part != 1:
                    row = 2 + part // 2
                    sums_ref[row : row + 1, :] = jnp.sum(d_part, axis=0, keepdims=True)
                product = lax.dot_general(
                    d_part.astype(bf16),
                    w_ref[:, cols],
                    (((1,), (1,)), ((), ())),
                    preferred_element_type=f32,
                )
                if part == 0:
                    total[...] = product
                else:
                    total[...] += product

            def work(rows, unused):
                grad = total[rows, :]
                normal, rate = norm_parts(tokens_ref[rows, :].astype(f32))
                sums_ref[0:1, :] += jnp.sum(grad, axis=0, keepdims=True)
                sums_ref[1:2, :] += jnp.sum(grad * normal, axis=0, keepdims=True)
                grad_ref[rows, :] = (
                    d_middle_ref[rows, :]
                    + norm_back(normal, rate, grad * (1.0 + mods_ref[1:2, :]))
                ).astype(bf16)

            chunks(slots, 32, work)

        return pl.pallas_call(
            kernel,
            out_shape=[
                jax.ShapeDtypeStruct((slots, width), bf16),
                jax.ShapeDtypeStruct((8, width), f32),
            ],
            in_specs=[vmem] * 5,
            out_specs=[vmem] * 2,
            scratch_shapes=[pltpu.VMEM((slots, width), f32)],
            cost_estimate=cost(9),
            compiler_params=params(60),
        )(d_turned, qkv_full, tokens_own, d_middle, mods)

    def output_rows(
        activated, down_full, bias_down, tokens_own, attn_out, cotangent_own, d_mlp, mods, live
    ):
        slots, hidden = activated.shape
        width = attn_out.shape[1]
        tile = hidden // fs

        def kernel(
            live_ref,
            act_ref,
            down_ref,
            bias_ref,
            tokens_ref,
            attn_ref,
            cot_ref,
            d_mlp_ref,
            mods_ref,
            out_ref,
            sums_ref,
            total,
        ):
            step = pl.program_id(0)
            part = jnp.dot(act_ref[...], down_ref[...], preferred_element_type=f32)

            @pl.when(step == 0)
            def start():
                total[...] = part

            @pl.when(step > 0)
            def add():
                total[...] += part

            @pl.when(step == fs - 1)
            def finish():
                sums_ref[...] = jnp.zeros_like(sums_ref)

                def work(rows, first):
                    mlp_out = total[rows, :] + bias_ref[...]
                    middle = (
                        tokens_ref[rows, :].astype(f32) + mods_ref[2:3, :] * attn_ref[rows, :]
                    )
                    alive = alive_rows(first, mlp_out.shape[0], live_ref[0])
                    out_ref[rows, :] = (alive * (middle + mods_ref[5:6, :] * mlp_out)).astype(bf16)
                    d_gate = alive * cot_ref[rows, :].astype(f32) * mlp_out
                    sums_ref[0:1, :] += jnp.sum(d_gate, axis=0, keepdims=True)
                    sums_ref[1:2, :] += jnp.sum(
                        d_mlp_ref[rows, :].astype(f32), axis=0, keepdims=True
                    )

                chunks(slots, 32, work)

        def whole(shape):
            return pl.BlockSpec(shape, lambda j, live_ref: (0,) * len(shape))

        return pl.pallas_call(
            kernel,
            out_shape=[
                jax.ShapeDtypeStruct((slots, width), bf16),
                jax.ShapeDtypeStruct((8, width), f32),
            ],
            grid_spec=pltpu.PrefetchScalarGridSpec(
                num_scalar_prefetch=1,
                grid=(fs,),
                in_specs=[
                    pl.BlockSpec((slots, tile), lambda j, live_ref: (0, j)),
                    pl.BlockSpec((tile, width), lambda j, live_ref: (j, 0)),
                    whole((1, width)),
                    whole((slots, width)),
                    whole((slots, width)),
                    whole((slots, width)),
                    whole((slots, width)),
                    whole(mods.shape),
                ],
                out_specs=[whole((slots, width)), whole((8, width))],
                scratch_shapes=[pltpu.VMEM((slots, width), f32)],
            ),
            cost_estimate=cost(6),
            compiler_params=params(60),
        )(
            live,
            activated,
            down_full,
            bias_down.reshape(1, width),
            tokens_own,
            attn_out,
            cotangent_own,
            d_mlp,
            mods,
        )

    def column_grad(where, items, rights):
        slots = rights[0].shape[1]
        width = items[0][0][0].shape[1]
        tile = width // 3
        half = slots // 2
        counts = [(stop - start) // 2 for unused, start, stop in items]
        n_out = sum(counts)
        lefts = [left for box, unused, unused_stop in items for left in box]

        def kernel(where_ref, *refs):
            core = where_ref[0]
            y0, y1, y2, y3, keep_ref, send_ref = refs[len(lefts) :]
            for i, (unused, start, unused_stop) in enumerate(items):
                x0, x1, x2, x3, x4 = refs[5 * i : 5 * i + 5]
                n = counts[i]
                below = sum(counts[:i])
                for out_ref, first in ((keep_ref, core * n), (send_ref, (1 - core) * n)):
                    rows = pl.ds(pl.multiple_of(start + first, 16), n)
                    total = None
                    for x, y, cols in (
                        (x0, y0, slice(None)),
                        (x1, y1, slice(None)),
                        (x2, y2, slice(None)),
                        (x3, y3, slice(0, half)),
                        (x4, y3, slice(half, slots)),
                    ):
                        part = jnp.dot(y[rows, cols], x[...], preferred_element_type=f32)
                        total = part if total is None else total + part
                    out_ref[below : below + n, :] = total

        left_specs = [
            pl.BlockSpec((left.shape[0], tile), lambda i, where_ref: (0, i)) for left in lefts
        ]
        right_spec = pl.BlockSpec(rights[0].shape, lambda i, where_ref: (0, 0))
        out_spec = pl.BlockSpec((n_out, tile), lambda i, where_ref: (0, i))
        return pl.pallas_call(
            kernel,
            out_shape=[jax.ShapeDtypeStruct((n_out, width), f32)] * 2,
            grid_spec=pltpu.PrefetchScalarGridSpec(
                num_scalar_prefetch=1,
                grid=(width // tile,),
                in_specs=left_specs + [right_spec] * 4,
                out_specs=[out_spec] * 2,
            ),
            cost_estimate=cost(8),
            compiler_params=params(60),
        )(where, *lefts, *rights)

    def sums_message(first_sums, middle_sums, output_sums, d_pre_sums, cond_act):
        width = cond_act.shape[1]
        extra = d_pre_sums.shape[0]

        def kernel(first_ref, middle_ref, output_ref, d_pre_ref, cond_ref, out_ref):
            out_ref[0:2, :] = first_ref[0:2, :].astype(bf16).astype(f32)
            out_ref[2:5, :] = middle_ref[0:3, :].astype(bf16).astype(f32)
            out_ref[5:6, :] = output_ref[0:1, :].astype(bf16).astype(f32)
            for row in (6, 7):
                out_ref[row : row + 1, :] = cond_ref[...].astype(f32)
            out_ref[8:10, :] = first_ref[2:4, :]
            out_ref[10:11, :] = middle_ref[3:4, :]
            out_ref[11:12, :] = output_ref[1:2, :]
            out_ref[12:, :] = d_pre_ref[...]

        return pl.pallas_call(
            kernel,
            out_shape=jax.ShapeDtypeStruct((12 + extra, width), f32),
            in_specs=[vmem] * 5,
            out_specs=vmem,
            cost_estimate=cost(1),
            compiler_params=params(60),
        )(first_sums, middle_sums, output_sums, d_pre_sums, cond_act)

    def column_total(items):
        width = items[0][0].shape[1]
        n = sum(item[0].shape[0] for item in items)
        padded = -(-n // 128) * 128
        arrays = [array for item in items for array in item]

        def kernel(*refs):
            for first in range(0, width, 128):
                totals, used = [], 0
                for item in items:
                    parts = [ref[:, first : first + 128] for ref in refs[used : used + len(item)]]
                    totals.append(sum((part.astype(f32) for part in parts[1:]), parts[0]))
                    used += len(item)
                if padded > n:
                    totals.append(jnp.zeros((padded - n, 128), f32))
                total = jnp.concatenate(totals, axis=0) if len(totals) > 1 else totals[0]
                refs[-1][first : first + 128, :] = total.T.astype(bf16)

        return pl.pallas_call(
            kernel,
            out_shape=jax.ShapeDtypeStruct((width, padded), bf16),
            in_specs=[vmem] * len(arrays),
            out_specs=vmem,
            cost_estimate=cost(5),
            compiler_params=params(60),
        )(*arrays)

    def row_total(keep, got):
        def kernel(keep_ref, got_ref, out_ref):
            out_ref[...] = (keep_ref[...] + got_ref[...]).astype(bf16)

        total = pl.pallas_call(
            kernel,
            out_shape=jax.ShapeDtypeStruct(keep.shape, bf16),
            in_specs=[vmem] * 2,
            out_specs=vmem,
            cost_estimate=cost(3),
            compiler_params=params(60),
        )(keep, got)
        return total.reshape(-1, keep.shape[2])

    def fsdp_sum(x):
        return lax.psum_scatter(x, "fsdp", scatter_dimension=0, tiled=True)

    def out_grad(where, d_attn_turned, attended):
        width, slots = d_attn_turned.shape
        n = width // BOX

        def kernel(where_ref, d_ref, x_ref, keep_ref, send_ref):
            step = pl.program_id(0)
            core = where_ref[0]
            for out_ref, which in ((keep_ref, core), (send_ref, 1 - core)):
                first = (where_ref[step + 1] * 2 + which) * n
                rows = pl.ds(pl.multiple_of(first, 16), n)
                out_ref[0] = jnp.dot(d_ref[rows, :], x_ref[...], preferred_element_type=f32)

        out_spec = pl.BlockSpec((1, n, width), lambda i, where_ref: (i, 0, 0))
        return pl.pallas_call(
            kernel,
            out_shape=[jax.ShapeDtypeStruct((BOX // 2, n, width), f32)] * 2,
            grid_spec=pltpu.PrefetchScalarGridSpec(
                num_scalar_prefetch=1,
                grid=(BOX // 2,),
                in_specs=[
                    pl.BlockSpec((width, slots), lambda i, where_ref: (0, 0)),
                    pl.BlockSpec((slots, width), lambda i, where_ref: (0, 0)),
                ],
                out_specs=[out_spec] * 2,
            ),
            cost_estimate=cost(5),
            compiler_params=params(60),
        )(where, d_attn_turned, attended)

    def chip_split(keep, got):
        count, rows, width = keep.shape

        def kernel(keep_ref, got_ref, *outs):
            for k, out_ref in enumerate(outs):
                out_ref[...] = (keep_ref[k] + got_ref[k]).astype(out_ref.dtype)

        return pl.pallas_call(
            kernel,
            out_shape=[jax.ShapeDtypeStruct((rows, width), f32)]
            + [jax.ShapeDtypeStruct((rows, width), bf16)] * (count - 1),
            in_specs=[vmem] * 2,
            out_specs=[vmem] * count,
            cost_estimate=cost(3),
            compiler_params=params(60),
        )(keep, got)

    def row_grad(where, lefts, rights):
        rows = lefts[0].shape[0] // fs
        slots, n = lefts[0].shape[1], rows // 2
        width = rights[0].shape[1]
        half = slots // 2

        def kernel(where_ref, x0, x1, x2, x3, y0, y1, y2, y3, y4, keep_ref, send_ref):
            core = where_ref[0]
            for out_ref, first in ((keep_ref, core * n), (send_ref, (1 - core) * n)):
                lines = pl.ds(pl.multiple_of(first, 16), n)
                total = None
                for x, y, cols in (
                    (x0, y0, slice(None)),
                    (x1, y1, slice(None)),
                    (x2, y2, slice(None)),
                    (x3, y3, slice(0, half)),
                    (x3, y4, slice(half, slots)),
                ):
                    part = jnp.dot(x[lines, cols], y[...], preferred_element_type=f32)
                    total = part if total is None else total + part
                out_ref[0] = total

        left_spec = pl.BlockSpec((rows, slots), lambda i, where_ref: (i, 0))
        right_specs = [
            pl.BlockSpec((right.shape[0], width), lambda i, where_ref: (0, 0))
            for right in rights
        ]
        out_spec = pl.BlockSpec((1, n, width), lambda i, where_ref: (i, 0, 0))
        return pl.pallas_call(
            kernel,
            out_shape=[jax.ShapeDtypeStruct((fs, n, width), f32)] * 2,
            grid_spec=pltpu.PrefetchScalarGridSpec(
                num_scalar_prefetch=1,
                grid=(fs,),
                in_specs=[left_spec] * 4 + right_specs,
                out_specs=[out_spec] * 2,
            ),
            cost_estimate=cost(6),
            compiler_params=params(60),
        )(where, *lefts, *rights)

    def body(
        tokens,
        condition,
        grid_sizes,
        w_ada,
        w_qkv,
        w_out,
        w_up,
        w_down,
        b_ada,
        b_qv,
        b_out,
        b_up,
        b_down,
        cotangent,
    ):
        slots, width = tokens.shape[1:]
        heads = width // HEAD_DIM
        hidden = w_up.shape[1]
        rank = lax.axis_index("dp")
        z = lax.axis_index("fsdp")
        place = lax.rem(rank, BOX)
        group = lax.div(rank, BOX)
        core = place & 1
        chip = place >> 1
        side = (chip ^ (chip >> 1)) & 1
        near = 2 * side + core
        far = 2 * (1 - side) + core
        where = jnp.stack(
            [lax.rem(z - k + fs, fs) for k in range(fs)]
            + [near, far, near ^ 1, far ^ 1]
            + [chip ^ k for k in range(4)]
        ).astype(jnp.int32)
        where_core = core.reshape(1).astype(jnp.int32)
        where_wide = jnp.stack(
            [lax.rem(z - k + fs, fs) for k in range(fs)] + [core] + [chip ^ k for k in range(4)]
        ).astype(jnp.int32)

        cond_wide = condition.astype(f32)
        gate = jax.nn.sigmoid(cond_wide)
        cond_act = (cond_wide * gate).astype(bf16)

        def quarter_of(shard):
            return pick(in_blocks(shard), near)

        qkv_quarter = quarter_of(w_qkv)
        cond_rows = ring_gather(after(cond_act, qkv_quarter))
        raw = jnp.concatenate([tokens[0], cotangent[0]], axis=1)
        qkv_helds = [ring_send(qkv_quarter, 1)]
        mid_rows = jnp.concatenate(
            [pick(in_blocks(w_out), chip), pick(in_blocks(w_up), chip)], axis=-1
        )
        mid_width = mid_rows.shape[-1]
        mid_part = -(-mid_width // 256) * 128
        mid_start = jnp.where(core == 0, 0, mid_width - mid_part)
        mid_eighth = lax.dynamic_slice_in_dim(mid_rows, mid_start, mid_part, 2)
        down_quarter = quarter_of(w_down)
        ada_shard = b_ada.shape[0]
        bias_ada = lax.dynamic_update_slice_in_dim(
            jnp.zeros((fs * ada_shard,), f32), b_ada.astype(f32), z * ada_shard, 0
        ).reshape(6, width)
        small = jnp.concatenate([b_qv, b_out, b_down, b_up]).astype(f32).reshape(-1, width)
        cond_rows, qkv_helds, bias_ada, small, mid_eighth, down_quarter = gated(
            (cond_rows, qkv_helds, bias_ada, small, mid_eighth, down_quarter)
        )

        rows_z = width // fs
        conds = jnp.concatenate(cond_rows)
        conds_z = lax.dynamic_slice_in_dim(conds, z * rows_z, rows_z, 1)
        partials = modulation_parts(conds_z, w_ada, bias_ada, small)
        partials = [partials[0]] + [ring_send(partials[k], fs - k) for k in range(1, fs)]
        raw_near = chip_near(after(raw, conds_z))
        qkv_helds.append(ring_send(qkv_helds[-1], 1))
        partials, qkv_helds = gated((partials, qkv_helds))

        live = (grid_sizes[0, 0] * grid_sizes[0, 1]).reshape(1)
        mods, head = modulation_rows(partials, live)
        (normed,), (d_mlp,) = other_heads((raw,), (0,), (head,))
        qkv_helds.append(ring_send(qkv_helds[-1], 1))
        mods, head, normed, d_mlp, raw_near, qkv_helds = gated(
            (mods, head, normed, d_mlp, raw_near, qkv_helds)
        )

        qkv_mine = jnp.stack(qkv_helds)
        qkv_other = side_send(qkv_mine)
        qkv_mine_got = box_send(qkv_mine, 1)
        mid_helds = [ring_send(after(mid_eighth, qkv_mine), 1)]
        bias_rows = [each[6:].reshape(-1) for each in partials]
        bias_rows = jnp.stack(bias_rows + bias_rows)
        biases = lax.dynamic_slice_in_dim(bias_rows, lax.rem(fs - z, fs), fs, 0)
        ends = [0]
        for bias in (b_qv, b_out, b_down, b_up):
            ends.append(ends[-1] + bias.shape[0])
        biases = [biases[:, ends[i] : ends[i + 1]].reshape(-1) for i in range(4)]
        qkv_mine, qkv_other, qkv_mine_got, mid_helds, biases = gated(
            (qkv_mine, qkv_other, qkv_mine_got, mid_helds, biases)
        )
        bias_qv, bias_out, bias_down, bias_up = biases

        last = fs - 1

        def in_order(array):
            return [(array, k) for k in range(last)]

        qkv_other_got = box_send(qkv_other, 1)
        raw_far = chip_far([after(each, qkv_other) for each in raw_near])
        mid_helds.append(ring_send(mid_helds[-1], 1))
        turned, qkv_full = projection(
            where,
            normed,
            w_qkv,
            [in_order(each) for each in (qkv_mine, qkv_other, qkv_mine_got, qkv_other_got)],
            bias_qv.reshape(2, width),
        )
        turned, qkv_full, mid_helds, raw_far = gated((turned, qkv_full, mid_helds, raw_far))

        heads_got = [box_send(after(head, turned), bits) for bits in (2, 4, 6)]
        mid_helds.append(ring_send(mid_helds[-1], 1))
        attended = attention(turned, live)
        attended, mid_helds, heads_got = gated((attended, mid_helds, heads_got))

        mid_mine = jnp.concatenate(mid_helds)
        mid_near = chip_near(mid_mine)
        mid_got = [box_send(mid_mine, 1)]
        down_helds = [ring_send(after(down_quarter, mid_mine), 1)]
        down_helds.append(ring_send(down_helds[-1], 1))
        normed_box, d_mlp_box = other_heads(
            (*raw_near, *raw_far), (0, 0, 0, slots // 2), (*heads_got, heads_got[2])
        )
        normed_box, d_mlp_box = [normed, *normed_box], [d_mlp, *d_mlp_box]
        attended, mid_mine, mid_near, mid_got, down_helds, normed_box, d_mlp_box = gated(
            (attended, mid_mine, mid_near, mid_got, down_helds, normed_box, d_mlp_box)
        )

        mid_far = chip_far(mid_near)
        mid_got += [box_send(each, 1) for each in mid_near]
        down_helds.append(ring_send(down_helds[-1], 1))
        attended, mid_far, mid_got, down_helds = gated((attended, mid_far, mid_got, down_helds))

        mid_got += [box_send(each, 1) for each in mid_far]
        down_others = [side_send(each) for each in down_helds]
        attn_out, normed_two, pre_act, activated, *act_blocks, out_full, up_full = middle_forward(
            where_wide,
            attended,
            tokens[0],
            [w_out, w_up],
            ((mid_mine, *mid_near, *mid_far), mid_got),
            bias_out,
            bias_up,
            mods,
        )
        down_helds, down_others, act_blocks, normed_two = gated(
            (down_helds, down_others, act_blocks, normed_two)
        )

        down_got = [[box_send(each, 1) for each in kind] for kind in (down_helds, down_others)]
        act_blocks, down_got = gated((act_blocks, down_got))

        act_box = chip_exchange(act_blocks)
        d_pre, *d_pre_turned, d_pre_sums, down_full = hidden_back(
            where,
            d_mlp,
            w_down,
            [[(each, None) for each in kind] for kind in (down_helds, down_others, *down_got)],
            pre_act,
        )

        def column_blocks(grad_t):
            n = grad_t.shape[0] // dp
            blocks = grad_t.reshape(groups, BOX, n, slots).transpose(1, 0, 2, 3)
            blocks = blocks.reshape(BOX // 2, 2 * groups * n, slots)
            return [pick(blocks, chip ^ k) for k in range(BOX // 2)]

        d_pre_blocks = d_pre_turned if groups == 1 else column_blocks(d_pre_turned[0])
        output, output_sums = output_rows(
            activated,
            down_full,
            bias_down,
            tokens[0],
            attn_out,
            cotangent[0],
            d_mlp,
            mods,
            live,
        )
        d_pre, d_pre_blocks, act_box, normed_two, output_sums = gated(
            (d_pre, d_pre_blocks, act_box, normed_two, output_sums)
        )

        d_pre_box = chip_exchange(d_pre_blocks)
        keep_down, send_down = row_grad(where_core, act_box, d_mlp_box)
        d_middle, d_attn_turned, d_attended_turned, middle_sums = middle_back(
            d_pre, up_full, out_full, attn_out, tokens[0], cotangent[0], mods, live
        )
        d_attended_turned, d_attn_turned, d_pre_box, keep_down, send_down, normed_two = gated(
            (d_attended_turned, d_attn_turned, d_pre_box, keep_down, send_down, normed_two)
        )

        normed_two_near = chip_near(normed_two)
        total_down = row_total(keep_down, box_send(send_down, 1))
        grad_down = fsdp_sum(total_down)
        d_projected, *last_blocks = attention_back(
            turned, after(d_attended_turned, total_down), live, where[fs + 4 :]
        )
        if groups > 1:
            last_blocks = column_blocks(d_projected)
            d_attn_turned = d_attn_turned.reshape(groups, BOX, -1, slots)
            d_attn_turned = d_attn_turned.transpose(1, 0, 2, 3).reshape(width, slots)
        keep_out, send_out = out_grad(
            jnp.concatenate([where_core, where[fs + 4 :]]), d_attn_turned, attended
        )
        got_out = box_send(send_out, 1)
        normed_two_far = chip_far([after(each, d_projected) for each in normed_two_near])
        normed_two_box = [normed_two, *normed_two_near, *normed_two_far]
        d_projected, last_blocks, normed_two_box, grad_down, keep_out, got_out = gated(
            (d_projected, last_blocks, normed_two_box, grad_down, keep_out, got_out)
        )

        def over_groups(grad):
            rows, cols = grad.shape
            return group_sum(grad.reshape(rows, groups, -1).transpose(1, 0, 2), group)

        last_box = chip_exchange(last_blocks)
        grad_tokens, first_sums = first_back(d_projected, qkv_full, tokens[0], d_middle, mods)
        out_blocks = chip_split(keep_out, got_out)
        keep_up, send_up = column_grad(
            where_core, [(normed_two_box, 0, d_pre_box[0].shape[0])], d_pre_box
        )
        total_up = column_total([(keep_up, box_send(send_up, 1))])
        last_box, first_sums, total_up, out_blocks = gated(
            (last_box, first_sums, total_up, out_blocks)
        )

        grad_up = fsdp_sum(total_up)
        keep_qkv, send_qkv = column_grad(
            where_core, [(normed_box, 0, last_box[0].shape[0])], last_box
        )
        message = sums_message(
            first_sums, middle_sums, output_sums, d_pre_sums.reshape(-1, width), cond_act
        )
        out_parts = chip_exchange(out_blocks)
        messages = ring_gather(message)
        total_last = column_total([(keep_qkv, box_send(send_qkv, 1)), tuple(out_parts)])
        grad_down = after(grad_down, keep_qkv)
        if groups > 1:
            grad_down = over_groups(grad_down.astype(f32))
        down_rows = grad_down.shape[0]
        down_cols = grad_down.reshape(down_rows, BOX, -1).transpose(1, 0, 2)
        if groups == 1:
            parts = lax.all_to_all(down_cols, "dp", 0, 0, tiled=True)
        else:
            parts = [pick(down_cols, place)] + [
                box_send(pick(down_cols, place ^ k), k) for k in range(1, BOX)
            ]
            parts = jnp.stack(parts)
            parts = jnp.stack([pick(parts, place ^ k) for k in range(BOX)])
        total_last, messages, grad_up, parts = gated((total_last, messages, grad_up, parts))

        grad_last = fsdp_sum(total_last)
        images_near = jnp.stack([each[:8] for each in messages]).astype(bf16)
        totals = [each[8:] for each in messages]
        images, total = images_near, sum(totals[1:], totals[0])
        for bits in (1, 2, 4):
            images = jnp.concatenate([images, box_send(images, bits)])
            total = total + box_send(total, bits)
        images_box, total_box = images, total
        for k in range(1, groups):
            images = jnp.concatenate([images, group_send(images_box, k)])
            total = total + group_send(total_box, k)
        grad_w_down = parts.reshape(BOX * down_rows, width // dp).astype(f32)
        grad_w_up = over_groups(grad_up[:, : keep_up.shape[0]].astype(f32))
        cut_cols, last_cols = keep_qkv.shape[0], keep_qkv.shape[0] + keep_out.shape[1]
        grad_w_qkv = over_groups(grad_last[:, :cut_cols].astype(f32))
        grad_w_out = over_groups(grad_last[:, cut_cols:last_cols].astype(f32))
        conds_all = lax.dynamic_slice_in_dim(images[:, 6], z * rows_z, rows_z, 1)
        d_mod_all = images[:, :6]
        ada_cols = 6 * width // dp
        grad_w_ada = lax.dot_general(
            conds_all,
            lax.dynamic_slice_in_dim(
                d_mod_all.reshape(dp * fs, 6 * width), rank * ada_cols, ada_cols, 1
            ),
            (((0,), (0,)), ((), ())),
            preferred_element_type=f32,
        )
        d_conds = lax.dot_general(
            images_near[:, :6].reshape(fs, 6 * width),
            w_ada,
            (((1,), (1,)), ((), ())),
            preferred_element_type=f32,
        )
        cond_parts = [d_conds[0]] + [ring_send(d_conds[k], fs - k) for k in range(1, fs)]
        twice = jnp.stack(cond_parts + cond_parts)
        d_cond_act = lax.dynamic_slice_in_dim(twice, lax.rem(fs - z, fs), fs, 0).reshape(-1)
        grad_condition = d_cond_act[None] * gate * (1.0 + cond_wide * (1.0 - gate))

        def shard_of(rows):
            return pick(rows.reshape(fs, -1), z)

        grads_bias = [
            shard_of(jnp.sum(d_mod_all.astype(f32), axis=0)),
            shard_of(total[:2]),
            shard_of(total[2]),
            shard_of(total[4:]),
            shard_of(total[3]),
        ]
        return (
            output[None],
            grad_tokens[None],
            grad_condition,
            grad_w_ada,
            grad_w_qkv,
            grad_w_out,
            grad_w_up,
            grad_w_down,
            *grads_bias,
        )

    return body


def solution(mesh):
    return jax.shard_map(
        make_body(mesh.shape["dp"], mesh.shape["fsdp"]),
        mesh=mesh,
        in_specs=(
            P(("dp", "fsdp"), None, None),
            P(("dp", "fsdp"), None),
            P(("dp", "fsdp"), None),
            P("fsdp", None),
            P("fsdp", None),
            P("fsdp", None),
            P("fsdp", None),
            P("fsdp", None),
            P("fsdp"),
            P("fsdp"),
            P("fsdp"),
            P("fsdp"),
            P("fsdp"),
            P(("dp", "fsdp"), None, None),
        ),
        out_specs=(
            P(("dp", "fsdp"), None, None),
            P(("dp", "fsdp"), None, None),
            P(("dp", "fsdp"), None),
            P("fsdp", "dp"),
            P("fsdp", "dp"),
            P("fsdp", "dp"),
            P("fsdp", "dp"),
            P("fsdp", "dp"),
            P("fsdp"),
            P("fsdp"),
            P("fsdp"),
            P("fsdp"),
            P("fsdp"),
        ),
        check_vma=False,
    )
```

```python
import math

import jax
import jax.numpy as jnp
from jax import lax
from jax.experimental import pallas as pl
from jax.experimental.pallas import tpu as pltpu
from jax.sharding import PartitionSpec as P

HEAD_DIM = 72
BOX = 8

epsilon = 1e-06
masked_value = -1e30
gelu_root = math.sqrt(2.0 / math.pi)
f32 = jnp.float32
bf16 = jnp.bfloat16


def norm_parts(values_in):
    centred = values_in - jnp.mean(values_in, axis=-1, keepdims=True)
    spread = jnp.mean(centred * centred, axis=-1, keepdims=True)
    rate = lax.rsqrt(spread + epsilon)
    return centred * rate, rate


def norm_back(normal, rate, grad):
    mean_grad = jnp.mean(grad, axis=-1, keepdims=True)
    mean_both = jnp.mean(grad * normal, axis=-1, keepdims=True)
    return rate * (grad - mean_grad - normal * mean_both)


def gelu_tanh(pre_act):
    return (
        0.5
        * pre_act
        * (1.0 + jnp.tanh(gelu_root * (pre_act + 0.044715 * pre_act * pre_act * pre_act)))
    )


def after(value, other):
    return lax.optimization_barrier((value, other))[0]


def gated(values):
    return lax.optimization_barrier(values)


def pick(array, index, axis=0):
    return lax.dynamic_index_in_dim(array, index, axis, keepdims=False)


def make_body(dp, fs):
    groups = dp // BOX

    def box_send(x, bits):
        return lax.ppermute(x, "dp", [(i, i ^ bits) for i in range(dp)])

    def side_send(x):
        return lax.ppermute(x, "dp", [(i, i ^ (4 if i & 1 else 2)) for i in range(dp)])

    def ring_send(x, hops):
        return lax.ppermute(x, "fsdp", [(i, (i + hops) % fs) for i in range(fs)])

    def group_send(x, hops):
        return lax.ppermute(x, "dp", [(i, (i + hops * BOX) % dp) for i in range(dp)])

    def ring_gather(x):
        return [x] + [ring_send(x, k) for k in range(1, fs)]

    def ring_sorted(blocks, z):
        back = jnp.stack(blocks[::-1] + blocks[::-1])
        return lax.dynamic_slice_in_dim(back, fs - 1 - z, fs, 0)

    def chip_near(x):
        return box_send(x, 2), box_send(x, 4)

    def chip_far(near):
        half = near[0].shape[0] // 2
        return box_send(near[0][:half], 4), box_send(near[1][half:], 2)

    def chip_exchange(blocks):
        return [blocks[0]] + [box_send(blocks[k], 2 * k) for k in range(1, BOX // 2)]

    def ring_sum(x, z):
        total = pick(x, z)
        for k in range(1, fs):
            sent = pick(x, lax.rem(z + k, fs)).astype(bf16)
            total = total + ring_send(sent, k).astype(f32)
        return total

    def group_sum(x, group):
        total = pick(x, group)
        for k in range(1, groups):
            total = total + group_send(pick(x, lax.rem(group + k, groups)), k)
        return total

    def cost(microseconds):
        return pl.CostEstimate(
            flops=int(microseconds * 1e8),
            transcendentals=0,
            bytes_accessed=int(microseconds * 3.2e5),
        )

    vmem = pl.BlockSpec(memory_space=pltpu.VMEM)
    smem = pl.BlockSpec(memory_space=pltpu.SMEM)

    def params(mebibytes):
        return pltpu.CompilerParams(vmem_limit_bytes=mebibytes << 20)

    def chunks(rows, step, work):
        def one(i, unused):
            work(pl.ds(pl.multiple_of(i * step, step), step), i * step)
            return unused

        lax.fori_loop(0, rows // step, one, 0)

    def alive_rows(first, rows, live):
        return ((lax.broadcasted_iota(jnp.int32, (rows, 1), 0) + first) < live).astype(f32)

    def modulation_parts(conds, w_ada, bias_ada, extra):
        images = conds.shape[0]
        parts, width = bias_ada.shape

        def kernel(cond_ref, w_ref, bias_ref, extra_ref, *out_refs):
            for part in range(parts):
                cols = slice(part * width, (part + 1) * width)
                product = jnp.dot(cond_ref[...], w_ref[:, cols], preferred_element_type=f32)
                product = product + bias_ref[part : part + 1, :]
                for image, out_ref in enumerate(out_refs):
                    out_ref[part : part + 1, :] = product[image : image + 1, :]
            for out_ref in out_refs:
                out_ref[parts:, :] = extra_ref[...]

        rows = parts + extra.shape[0]
        return pl.pallas_call(
            kernel,
            out_shape=[jax.ShapeDtypeStruct((rows, width), f32)] * images,
            in_specs=[vmem] * 4,
            out_specs=[vmem] * images,
            cost_estimate=cost(4),
            compiler_params=params(60),
        )(conds, w_ada, bias_ada, extra)

    def modulation_rows(partials, live):
        rows, width = partials[0].shape

        def kernel(live_ref, *refs):
            mods_ref, head_ref = refs[-2:]
            total = refs[0][...]
            for ref in refs[1:-2]:
                total = total + ref[...]
            mods_ref[...] = total
            head_ref[...] = jnp.full(head_ref.shape, live_ref[0].astype(f32))
            head_ref[0:2, :] = total[0:2, :]
            head_ref[2:3, :] = total[5:6, :]

        return pl.pallas_call(
            kernel,
            out_shape=[jax.ShapeDtypeStruct((rows, width), f32)] * 2,
            in_specs=[smem] + [vmem] * len(partials),
            out_specs=[vmem] * 2,
            cost_estimate=cost(1),
            compiler_params=params(60),
        )(live, *partials)

    def other_heads(raws, firsts, heads):
        n = len(raws)
        width = raws[0].shape[1] // 2

        def kernel(*refs):
            raw_refs, head_refs = refs[:n], refs[n : 2 * n]
            normed_refs, d_mlp_refs = refs[2 * n : 3 * n], refs[3 * n :]
            for raw, head, normed, d_mlp, first in zip(
                raw_refs, head_refs, normed_refs, d_mlp_refs, firsts
            ):
                live = head[3, 0].astype(jnp.int32)

                def work(rows, start):
                    normal = norm_parts(raw[rows, :width].astype(f32))[0]
                    normed[rows, :] = (
                        normal * (1.0 + head[1:2, :]) + head[0:1, :]
                    ).astype(bf16)
                    count = normal.shape[0]
                    up_rows = alive_rows(start + first, count, live) * raw[
                        rows, width:
                    ].astype(f32)
                    d_mlp[rows, :] = (head[2:3, :] * up_rows).astype(bf16)

                chunks(raw.shape[0], 32, work)

        outs = pl.pallas_call(
            kernel,
            out_shape=[jax.ShapeDtypeStruct((raw.shape[0], width), bf16) for raw in raws] * 2,
            in_specs=[vmem] * (2 * n),
            out_specs=[vmem] * (2 * n),
            cost_estimate=cost(8),
            compiler_params=params(60),
        )(*raws, *heads)
        return outs[:n], outs[n:]

    def piece_plan(pieces):
        arrays = []
        for piece, unused in (each for kind in pieces for each in kind):
            if not any(piece is array for array in arrays):
                arrays.append(piece)
        position = {id(array): i for i, array in enumerate(arrays)}
        plan = [[(position[id(piece)], index) for piece, index in kind] for kind in pieces]
        return arrays, plan

    def piece_copies(where_ref, own_ref, array_refs, plan, whole_ref):
        copies = [(own_ref, whole_ref.at[where_ref[0]])]
        for kind, blocks in enumerate(plan):
            for k, (which, index) in enumerate(blocks):
                source = array_refs[which] if index is None else array_refs[which].at[index]
                copies.append((source, whole_ref.at[where_ref[k + 1], where_ref[fs + kind]]))
        return copies

    def wide_copies(core, where_ref, own_refs, sets, whole_refs):
        widths = [ref.shape[-1] for ref in own_refs]
        width, part = sum(widths), sets[0][0].shape[-1]
        lead, split = whole_refs[0].shape[2], sets[0][6].shape[0]
        copies = [(own, whole.at[where_ref[0]]) for own, whole in zip(own_refs, whole_refs)]
        for side, piece_refs in enumerate(sets):
            low, high = (0, part) if core ^ side == 0 else (part, width)
            offset = 0 if core ^ side == 0 else width - part
            for block in range(1, fs):
                base = (block - 1) * lead
                top = min(max(split - base, 0), lead)
                late = int(block == fs - 1)
                rows = [(2 * i + late, 0 if late else base, i, 0, lead) for i in range(3)]
                if top:
                    rows.append((6, base, 3, 0, top))
                if top < lead:
                    rows.append((7, base + top - split, 3, top, lead - top))
                for piece, first, slot, row, count in rows:
                    start = 0
                    for i, each in enumerate(widths):
                        left, right = max(low, start), min(high, start + each)
                        if left < right:
                            source = piece_refs[piece].at[
                                first : first + count, :, left - offset : right - offset
                            ]
                            target = whole_refs[i].at[
                                where_ref[block],
                                where_ref[fs + 1 + slot],
                                row : row + count,
                                :,
                                left - start : right - start,
                            ]
                            copies.append((source, target))
                        start += each
        return copies

    def copy_all(copies, sems):
        return [
            pltpu.make_async_copy(source, target, sems.at[j])
            for j, (source, target) in enumerate(copies)
        ]

    def start_all(copies):
        for copy in copies:
            copy.start()

    def wait_all(copies):
        for copy in copies:
            copy.wait()

    def in_blocks(shard):
        rows, cols = shard.shape
        return shard.reshape(4, rows // 32, 8, cols)

    any_spec = pl.BlockSpec(memory_space=pl.ANY)

    def projection(where, normed, own, pieces, biases):
        slots, width = normed.shape
        arrays, plan = piece_plan(pieces)
        own = in_blocks(own)
        shape = (fs,) + own.shape

        def kernel(where_ref, normed_ref, bias_ref, own_ref, *refs):
            array_refs = refs[: len(arrays)]
            turned_ref, whole_ref, scratch, sems, out_sem = refs[len(arrays) :]
            copies = copy_all(
                piece_copies(where_ref, own_ref, array_refs, plan, scratch), sems
            )
            start_all(copies)
            wait_all(copies)
            out = pltpu.make_async_copy(scratch, whole_ref, out_sem)
            out.start()
            w_ref = scratch.reshape(width, 3 * width)
            for part in range(3):
                cols = slice(part * width, (part + 1) * width)
                proj = jnp.dot(normed_ref[...], w_ref[:, cols], preferred_element_type=f32)
                if part != 1:
                    proj = proj + bias_ref[part // 2 : part // 2 + 1, :]
                turned_ref[cols, :] = proj.astype(bf16).astype(f32).T
            out.wait()

        turned, whole = pl.pallas_call(
            kernel,
            out_shape=[
                jax.ShapeDtypeStruct((3 * width, slots), f32),
                jax.ShapeDtypeStruct(shape, bf16),
            ],
            in_specs=[smem, vmem, vmem, any_spec] + [any_spec] * len(arrays),
            out_specs=[vmem, any_spec],
            scratch_shapes=[
                pltpu.VMEM(shape, bf16),
                pltpu.SemaphoreType.DMA((1 + 4 * (fs - 1),)),
                pltpu.SemaphoreType.DMA,
            ],
            cost_estimate=cost(11),
            compiler_params=params(60),
        )(where, normed, biases, own, *arrays)
        return turned, whole.reshape(width, 3 * width)

    def attention(turned, live):
        slots = turned.shape[1]
        width = turned.shape[0] // 3
        count = width // HEAD_DIM
        heads_at_once = 2 if count % 2 == 0 else 1
        scale = HEAD_DIM ** (-0.5)

        def kernel(live_ref, turned_ref, attended_ref, out_turned):
            live_keys = lax.broadcasted_iota(jnp.int32, (1, slots), 1) < live_ref[0]

            def head(h):
                def rows(part):
                    first = pl.multiple_of(part * width + h * HEAD_DIM, 8)
                    return turned_ref[pl.ds(first, HEAD_DIM), :].astype(bf16)

                scores = lax.dot_general(
                    rows(0), rows(1), (((0,), (0,)), ((), ())), preferred_element_type=f32
                )
                scores = jnp.where(live_keys, scores * scale, masked_value)
                highest = jnp.max(scores, axis=-1, keepdims=True)
                total = jnp.sum(jnp.exp(scores - highest), axis=-1, keepdims=True)
                probs = jnp.exp(scores - (highest + jnp.log(total)))
                return lax.dot_general(
                    rows(2),
                    probs.astype(bf16),
                    (((1,), (1,)), ((), ())),
                    preferred_element_type=f32,
                )

            def some_heads(i, unused):
                outs = [head(i * heads_at_once + j) for j in range(heads_at_once)]
                for j, out in enumerate(outs):
                    first = pl.multiple_of((i * heads_at_once + j) * HEAD_DIM, 8)
                    out_turned[pl.ds(first, HEAD_DIM), :] = out
                return unused

            lax.fori_loop(0, count // heads_at_once, some_heads, 0)
            attended_ref[...] = out_turned[...].T.astype(bf16)

        return pl.pallas_call(
            kernel,
            out_shape=jax.ShapeDtypeStruct((slots, width), bf16),
            in_specs=[smem, vmem],
            out_specs=vmem,
            scratch_shapes=[pltpu.VMEM((width, slots), f32)],
            cost_estimate=cost(11),
            compiler_params=params(60),
        )(live, turned)

    def attention_back(turned, d_turned, live, where_chip):
        width, slots = d_turned.shape
        part = 3 * width // 4
        count = width // HEAD_DIM
        heads_at_once = 1
        scale = HEAD_DIM ** (-0.5)

        def kernel(live_ref, chip_ref, turned_ref, d_ref, out_ref, *rest):
            block_refs, total_ref = rest[:-1], rest[-1]
            live_keys = lax.broadcasted_iota(jnp.int32, (1, slots), 1) < live_ref[0]

            def place_of(h, part):
                return pl.ds(pl.multiple_of(part * width + h * HEAD_DIM, 8), HEAD_DIM)

            def head(h):
                def place(part):
                    return place_of(h, part)

                query = turned_ref[place(0), :].astype(bf16)
                key_part = turned_ref[place(1), :].astype(bf16)
                value = turned_ref[place(2), :].astype(bf16)
                d_out = d_ref[place(0), :].astype(bf16)
                both_first = (((0,), (0,)), ((), ()))
                scores = lax.dot_general(
                    query, key_part, both_first, preferred_element_type=f32
                )
                scores = jnp.where(live_keys, scores * scale, masked_value)
                highest = jnp.max(scores, axis=-1, keepdims=True)
                total = jnp.sum(jnp.exp(scores - highest), axis=-1, keepdims=True)
                probs = jnp.exp(scores - (highest + jnp.log(total)))
                d_probs = lax.dot_general(
                    d_out, value, both_first, preferred_element_type=f32
                )
                inner = jnp.sum(probs * d_probs, axis=-1, keepdims=True)
                d_scores = (probs * (d_probs - inner)).astype(bf16)
                d_value = jnp.dot(d_out, probs.astype(bf16), preferred_element_type=f32)
                d_query = scale * lax.dot_general(
                    key_part, d_scores, (((1,), (1,)), ((), ())), preferred_element_type=f32
                )
                d_key = scale * jnp.dot(query, d_scores, preferred_element_type=f32)
                return d_query, d_key, d_value

            def some_heads(i, unused):
                outs = [head(i * heads_at_once + j) for j in range(heads_at_once)]
                for j, parts in enumerate(outs):
                    for part, out in enumerate(parts):
                        total_ref[place_of(i * heads_at_once + j, part), :] = out
                return unused

            lax.fori_loop(0, count // heads_at_once, some_heads, 0)
            out_ref[...] = total_ref[...].astype(bf16)
            for k, block in enumerate(block_refs):
                first = pl.multiple_of(chip_ref[k] * part, 16)
                block[...] = total_ref[pl.ds(first, part), :].astype(bf16)

        n_blocks = 4 if groups == 1 else 0
        return pl.pallas_call(
            kernel,
            out_shape=[jax.ShapeDtypeStruct((3 * width, slots), bf16)]
            + [jax.ShapeDtypeStruct((part, slots), bf16)] * n_blocks,
            in_specs=[smem, smem, vmem, vmem],
            out_specs=[vmem] * (1 + n_blocks),
            scratch_shapes=[pltpu.VMEM((3 * width, slots), f32)],
            cost_estimate=cost(12),
            compiler_params=params(60),
        )(live, where_chip, turned, d_turned)

    def middle_forward(where, attended, tokens_own, owns, sets, bias_out, bias_up, mods):
        slots, width = attended.shape
        owns = [in_blocks(own) for own in owns]
        hidden = owns[1].shape[-1]
        tile = hidden // fs
        quarter = tile // 4
        shapes = [(fs,) + own.shape for own in owns]
        n_pieces = len(sets[0])
        n_copies = 2 + 2 * 15 * (fs - 1)

        def kernel(where_ref, attended_ref, tokens_ref, bias_out_ref, bias_up_ref, mods_ref, *refs):
            own_refs = refs[:2]
            set_refs = (refs[2 : 2 + n_pieces], refs[2 + n_pieces : 2 + 2 * n_pieces])
            (
                attn_ref,
                normed_ref,
                pre_ref,
                act_ref,
                block0,
                block1,
                block2,
                block3,
                whole_out,
                whole_up,
                scratch_out,
                scratch_up,
                turned,
                sems,
                out_sems,
            ) = refs[2 + 2 * n_pieces :]
            step = pl.program_id(0)
            scratches, wholes = (scratch_out, scratch_up), (whole_out, whole_up)

            def outs():
                return [
                    pltpu.make_async_copy(scratch, whole, out_sems.at[i])
                    for i, (scratch, whole) in enumerate(zip(scratches, wholes))
                ]

            @pl.when(step == 0)
            def first():
                for core in range(2):

                    @pl.when(where_ref[fs] == core)
                    def gather(core=core):
                        copies = copy_all(
                            wide_copies(core, where_ref, own_refs, set_refs, scratches), sems
                        )
                        start_all(copies)
                        wait_all(copies)

                start_all(outs())
                attn_ref[...] = (
                    jnp.dot(
                        attended_ref[...],
                        scratch_out.reshape(width, width)[...],
                        preferred_element_type=f32,
                    )
                    + bias_out_ref[...]
                )

                def work(rows, unused):
                    middle = tokens_ref[rows, :].astype(f32) + mods_ref[2:3, :] * attn_ref[rows, :]
                    normal = norm_parts(middle)[0]
                    normed_ref[rows, :] = (
                        normal * (1.0 + mods_ref[4:5, :]) + mods_ref[3:4, :]
                    ).astype(bf16)

                chunks(slots, 32, work)

            cols = pl.ds(pl.multiple_of(step * tile, 128), tile)
            pre_ref[...] = (
                jnp.dot(
                    normed_ref[...],
                    scratch_up.reshape(width, hidden)[:, cols],
                    preferred_element_type=f32,
                )
                + bias_up_ref[0]
            )

            def work(rows, unused):
                act_ref[rows, :] = gelu_tanh(pre_ref[rows, :]).astype(bf16)

            chunks(slots, 32, work)
            turned[...] = act_ref[...].astype(f32).T
            for k, block in enumerate((block0, block1, block2, block3)):
                first = pl.multiple_of(where_ref[fs + 1 + k] * quarter, 16)
                block[...] = turned[pl.ds(first, quarter), :].astype(bf16)

            @pl.when(step == fs - 1)
            def last():
                wait_all(outs())

        def whole(shape):
            return pl.BlockSpec(shape, lambda j, where_ref: (0,) * len(shape))

        *results, whole_out, whole_up = pl.pallas_call(
            kernel,
            out_shape=[
                jax.ShapeDtypeStruct((slots, width), f32),
                jax.ShapeDtypeStruct((slots, width), bf16),
                jax.ShapeDtypeStruct((slots, hidden), f32),
                jax.ShapeDtypeStruct((slots, hidden), bf16),
            ]
            + [jax.ShapeDtypeStruct((fs * quarter, slots), bf16)] * 4
            + [jax.ShapeDtypeStruct(shape, bf16) for shape in shapes],
            grid_spec=pltpu.PrefetchScalarGridSpec(
                num_scalar_prefetch=1,
                grid=(fs,),
                in_specs=[
                    whole((slots, width)),
                    whole((slots, width)),
                    whole((1, width)),
                    pl.BlockSpec((1, 1, tile), lambda j, where_ref: (j, 0, 0)),
                    whole(mods.shape),
                ]
                + [any_spec] * (2 + 2 * n_pieces),
                out_specs=[
                    whole((slots, width)),
                    whole((slots, width)),
                    pl.BlockSpec((slots, tile), lambda j, where_ref: (0, j)),
                    pl.BlockSpec((slots, tile), lambda j, where_ref: (0, j)),
                ]
                + [pl.BlockSpec((quarter, slots), lambda j, where_ref: (j, 0))] * 4
                + [any_spec, any_spec],
                scratch_shapes=[pltpu.VMEM(shape, bf16) for shape in shapes]
                + [
                    pltpu.VMEM((tile, slots), f32),
                    pltpu.SemaphoreType.DMA((n_copies,)),
                    pltpu.SemaphoreType.DMA((2,)),
                ],
            ),
            cost_estimate=cost(20),
            compiler_params=params(60),
        )(
            where,
            attended,
            tokens_own,
            bias_out.reshape(1, width),
            bias_up.reshape(fs, 1, tile),
            mods,
            *owns,
            *sets[0],
            *sets[1],
        )
        return (
            *results,
            whole_out.reshape(width, width),
            whole_up.reshape(width, hidden),
        )

    def hidden_back(where, d_mlp, own, pieces, pre_act):
        slots, width = d_mlp.shape
        hidden = pre_act.shape[1]
        tile = hidden // fs
        if groups == 1:
            turned_shapes = [jax.ShapeDtypeStruct((tile, slots), bf16)] * 4
            turned_specs = [pl.BlockSpec((tile, slots), lambda j, where_ref: (0, 0))] * 4
        else:
            turned_shapes = [jax.ShapeDtypeStruct((hidden, slots), bf16)]
            turned_specs = [pl.BlockSpec((tile, slots), lambda j, where_ref: (j, 0))]
        arrays, plan = piece_plan(pieces)
        own = in_blocks(own)
        shape = (fs,) + own.shape

        def kernel(where_ref, d_mlp_ref, pre_ref, own_ref, *refs):
            array_refs = refs[: len(arrays)]
            d_pre_ref, *turned_refs, sum_ref, whole_ref = refs[len(arrays) : -4]
            d_act_ref, scratch, sems, out_sem = refs[-4:]
            step = pl.program_id(0)

            def out():
                return pltpu.make_async_copy(scratch, whole_ref, out_sem)

            @pl.when(step == 0)
            def first():
                copies = copy_all(
                    piece_copies(where_ref, own_ref, array_refs, plan, scratch), sems
                )
                start_all(copies)
                wait_all(copies)
                out().start()

            d_act_ref[...] = lax.dot_general(
                d_mlp_ref[...],
                scratch.at[step].reshape(tile, width)[...],
                (((1,), (1,)), ((), ())),
                preferred_element_type=f32,
            )

            def work(rows, unused):
                pre = pre_ref[rows, :]
                square = pre * pre
                bend = jnp.tanh(gelu_root * (pre + 0.044715 * square * pre))
                slope = 0.5 * (1.0 + bend) + 0.5 * pre * (1.0 - bend * bend) * gelu_root * (
                    1.0 + 3.0 * 0.044715 * square
                )
                d_pre = (d_act_ref[rows, :] * slope).astype(bf16)
                d_pre_ref[rows, :] = d_pre
                d_act_ref[rows, :] = d_pre.astype(f32)

            chunks(slots, 32, work)
            sum_ref[0] = jnp.sum(d_act_ref[...], axis=0, keepdims=True)
            if groups == 1:
                for k, turned_ref in enumerate(turned_refs):

                    @pl.when(step == where_ref[fs + 4 + k])
                    def block(turned_ref=turned_ref):
                        turned_ref[...] = d_act_ref[...].T.astype(bf16)
            else:
                turned_refs[0][...] = d_act_ref[...].T.astype(bf16)

            @pl.when(step == fs - 1)
            def last():
                out().wait()

        *results, whole = pl.pallas_call(
            kernel,
            out_shape=[
                jax.ShapeDtypeStruct((slots, hidden), bf16),
                *turned_shapes,
                jax.ShapeDtypeStruct((fs, 1, tile), f32),
                jax.ShapeDtypeStruct(shape, bf16),
            ],
            grid_spec=pltpu.PrefetchScalarGridSpec(
                num_scalar_prefetch=1,
                grid=(fs,),
                in_specs=[
                    pl.BlockSpec((slots, width), lambda j, where_ref: (0, 0)),
                    pl.BlockSpec((slots, tile), lambda j, where_ref: (0, j)),
                    any_spec,
                ]
                + [any_spec] * len(arrays),
                out_specs=[
                    pl.BlockSpec((slots, tile), lambda j, where_ref: (0, j)),
                    *turned_specs,
                    pl.BlockSpec((1, 1, tile), lambda j, where_ref: (j, 0, 0)),
                    any_spec,
                ],
                scratch_shapes=[
                    pltpu.VMEM((slots, tile), f32),
                    pltpu.VMEM(shape, bf16),
                    pltpu.SemaphoreType.DMA((1 + 4 * (fs - 1),)),
                    pltpu.SemaphoreType.DMA,
                ],
            ),
            cost_estimate=cost(15),
            compiler_params=params(60),
        )(where, d_mlp, pre_act, own, *arrays)
        return (*results, whole.reshape(hidden, width))

    def middle_back(d_pre, up_full, out_full, attn_out, tokens_own, cotangent_own, mods, live):
        slots, hidden = d_pre.shape
        width = attn_out.shape[1]
        tile = hidden // fs

        def kernel(
            live_ref,
            d_pre_ref,
            up_ref,
            out_ref,
            attn_ref,
            tokens_ref,
            cot_ref,
            mods_ref,
            d_middle_ref,
            d_attn_turned_ref,
            d_attended_turned_ref,
            sums_ref,
            total,
            d_attn_ref,
        ):
            step = pl.program_id(0)
            part = lax.dot_general(
                d_pre_ref[...],
                up_ref[...],
                (((1,), (1,)), ((), ())),
                preferred_element_type=f32,
            )

            @pl.when(step == 0)
            def start():
                total[...] = part

            @pl.when(step > 0)
            def add():
                total[...] += part

            @pl.when(step == fs - 1)
            def finish():
                sums_ref[...] = jnp.zeros_like(sums_ref)

                def work(rows, first):
                    grad = total[rows, :]
                    attn = attn_ref[rows, :]
                    middle = tokens_ref[rows, :].astype(f32) + mods_ref[2:3, :] * attn
                    normal, rate = norm_parts(middle)
                    alive = alive_rows(first, grad.shape[0], live_ref[0])
                    d_middle = alive * cot_ref[rows, :].astype(f32) + norm_back(
                        normal, rate, grad * (1.0 + mods_ref[4:5, :])
                    )
                    d_middle_ref[rows, :] = d_middle
                    d_attn = (mods_ref[2:3, :] * d_middle).astype(bf16)
                    d_attn_ref[rows, :] = d_attn
                    for i, each in enumerate(
                        (d_middle * attn, grad, grad * normal, d_attn.astype(f32))
                    ):
                        sums_ref[i : i + 1, :] += jnp.sum(each, axis=0, keepdims=True)

                chunks(slots, 32, work)
                d_attn_turned_ref[...] = d_attn_ref[...].astype(f32).T.astype(bf16)
                d_attended = lax.dot_general(
                    d_attn_ref[...],
                    out_ref[...],
                    (((1,), (1,)), ((), ())),
                    preferred_element_type=f32,
                )
                d_attended_turned_ref[...] = d_attended.astype(bf16).astype(f32).T

        def whole(shape):
            return pl.BlockSpec(shape, lambda j, live_ref: (0,) * len(shape))

        return pl.pallas_call(
            kernel,
            out_shape=[
                jax.ShapeDtypeStruct((slots, width), f32),
                jax.ShapeDtypeStruct((width, slots), bf16),
                jax.ShapeDtypeStruct((width, slots), f32),
                jax.ShapeDtypeStruct((8, width), f32),
            ],
            grid_spec=pltpu.PrefetchScalarGridSpec(
                num_scalar_prefetch=1,
                grid=(fs,),
                in_specs=[
                    pl.BlockSpec((slots, tile), lambda j, live_ref: (0, j)),
                    pl.BlockSpec((width, tile), lambda j, live_ref: (0, j)),
                    whole((width, width)),
                    whole((slots, width)),
                    whole((slots, width)),
                    whole((slots, width)),
                    whole(mods.shape),
                ],
                out_specs=[
                    whole((slots, width)),
                    whole((width, slots)),
                    whole((width, slots)),
                    whole((8, width)),
                ],
                scratch_shapes=[
                    pltpu.VMEM((slots, width), f32),
                    pltpu.VMEM((slots, width), bf16),
                ],
            ),
            cost_estimate=cost(12),
            compiler_params=params(60),
        )(live, d_pre, up_full, out_full, attn_out, tokens_own, cotangent_own, mods)

    def first_back(d_turned, qkv_full, tokens_own, d_middle, mods):
        slots, width = d_middle.shape

        def kernel(d_ref, w_ref, tokens_ref, d_middle_ref, mods_ref, grad_ref, sums_ref, total):
            sums_ref[...] = jnp.zeros_like(sums_ref)
            for part in range(3):
                cols = slice(part * width, (part + 1) * width)
                d_part = d_ref[cols, :].astype(f32).T
                if part != 1:
                    row = 2 + part // 2
                    sums_ref[row : row + 1, :] = jnp.sum(d_part, axis=0, keepdims=True)
                product = lax.dot_general(
                    d_part.astype(bf16),
                    w_ref[:, cols],
                    (((1,), (1,)), ((), ())),
                    preferred_element_type=f32,
                )
                if part == 0:
                    total[...] = product
                else:
                    total[...] += product

            def work(rows, unused):
                grad = total[rows, :]
                normal, rate = norm_parts(tokens_ref[rows, :].astype(f32))
                sums_ref[0:1, :] += jnp.sum(grad, axis=0, keepdims=True)
                sums_ref[1:2, :] += jnp.sum(grad * normal, axis=0, keepdims=True)
                grad_ref[rows, :] = (
                    d_middle_ref[rows, :]
                    + norm_back(normal, rate, grad * (1.0 + mods_ref[1:2, :]))
                ).astype(bf16)

            chunks(slots, 32, work)

        return pl.pallas_call(
            kernel,
            out_shape=[
                jax.ShapeDtypeStruct((slots, width), bf16),
                jax.ShapeDtypeStruct((8, width), f32),
            ],
            in_specs=[vmem] * 5,
            out_specs=[vmem] * 2,
            scratch_shapes=[pltpu.VMEM((slots, width), f32)],
            cost_estimate=cost(9),
            compiler_params=params(60),
        )(d_turned, qkv_full, tokens_own, d_middle, mods)

    def output_rows(
        activated, down_full, bias_down, tokens_own, attn_out, cotangent_own, d_mlp, mods, live
    ):
        slots, hidden = activated.shape
        width = attn_out.shape[1]
        tile = hidden // fs

        def kernel(
            live_ref,
            act_ref,
            down_ref,
            bias_ref,
            tokens_ref,
            attn_ref,
            cot_ref,
            d_mlp_ref,
            mods_ref,
            out_ref,
            sums_ref,
            total,
        ):
            step = pl.program_id(0)
            part = jnp.dot(act_ref[...], down_ref[...], preferred_element_type=f32)

            @pl.when(step == 0)
            def start():
                total[...] = part

            @pl.when(step > 0)
            def add():
                total[...] += part

            @pl.when(step == fs - 1)
            def finish():
                sums_ref[...] = jnp.zeros_like(sums_ref)

                def work(rows, first):
                    mlp_out = total[rows, :] + bias_ref[...]
                    middle = (
                        tokens_ref[rows, :].astype(f32) + mods_ref[2:3, :] * attn_ref[rows, :]
                    )
                    alive = alive_rows(first, mlp_out.shape[0], live_ref[0])
                    out_ref[rows, :] = (alive * (middle + mods_ref[5:6, :] * mlp_out)).astype(bf16)
                    d_gate = alive * cot_ref[rows, :].astype(f32) * mlp_out
                    sums_ref[0:1, :] += jnp.sum(d_gate, axis=0, keepdims=True)
                    sums_ref[1:2, :] += jnp.sum(
                        d_mlp_ref[rows, :].astype(f32), axis=0, keepdims=True
                    )

                chunks(slots, 32, work)

        def whole(shape):
            return pl.BlockSpec(shape, lambda j, live_ref: (0,) * len(shape))

        return pl.pallas_call(
            kernel,
            out_shape=[
                jax.ShapeDtypeStruct((slots, width), bf16),
                jax.ShapeDtypeStruct((8, width), f32),
            ],
            grid_spec=pltpu.PrefetchScalarGridSpec(
                num_scalar_prefetch=1,
                grid=(fs,),
                in_specs=[
                    pl.BlockSpec((slots, tile), lambda j, live_ref: (0, j)),
                    pl.BlockSpec((tile, width), lambda j, live_ref: (j, 0)),
                    whole((1, width)),
                    whole((slots, width)),
                    whole((slots, width)),
                    whole((slots, width)),
                    whole((slots, width)),
                    whole(mods.shape),
                ],
                out_specs=[whole((slots, width)), whole((8, width))],
                scratch_shapes=[pltpu.VMEM((slots, width), f32)],
            ),
            cost_estimate=cost(6),
            compiler_params=params(60),
        )(
            live,
            activated,
            down_full,
            bias_down.reshape(1, width),
            tokens_own,
            attn_out,
            cotangent_own,
            d_mlp,
            mods,
        )

    def column_grad(where, items, rights):
        slots = rights[0].shape[1]
        width = items[0][0][0].shape[1]
        tile = width // 3
        half = slots // 2
        counts = [(stop - start) // 2 for unused, start, stop in items]
        n_out = sum(counts)
        lefts = [left for box, unused, unused_stop in items for left in box]

        def kernel(where_ref, *refs):
            core = where_ref[0]
            y0, y1, y2, y3, keep_ref, send_ref = refs[len(lefts) :]
            for i, (unused, start, unused_stop) in enumerate(items):
                x0, x1, x2, x3, x4 = refs[5 * i : 5 * i + 5]
                n = counts[i]
                below = sum(counts[:i])
                for out_ref, first in ((keep_ref, core * n), (send_ref, (1 - core) * n)):
                    rows = pl.ds(pl.multiple_of(start + first, 16), n)
                    total = None
                    for x, y, cols in (
                        (x0, y0, slice(None)),
                        (x1, y1, slice(None)),
                        (x2, y2, slice(None)),
                        (x3, y3, slice(0, half)),
                        (x4, y3, slice(half, slots)),
                    ):
                        part = jnp.dot(y[rows, cols], x[...], preferred_element_type=f32)
                        total = part if total is None else total + part
                    out_ref[below : below + n, :] = total

        left_specs = [
            pl.BlockSpec((left.shape[0], tile), lambda i, where_ref: (0, i)) for left in lefts
        ]
        right_spec = pl.BlockSpec(rights[0].shape, lambda i, where_ref: (0, 0))
        out_spec = pl.BlockSpec((n_out, tile), lambda i, where_ref: (0, i))
        return pl.pallas_call(
            kernel,
            out_shape=[jax.ShapeDtypeStruct((n_out, width), f32)] * 2,
            grid_spec=pltpu.PrefetchScalarGridSpec(
                num_scalar_prefetch=1,
                grid=(width // tile,),
                in_specs=left_specs + [right_spec] * 4,
                out_specs=[out_spec] * 2,
            ),
            cost_estimate=cost(8),
            compiler_params=params(60),
        )(where, *lefts, *rights)

    def sums_message(first_sums, middle_sums, output_sums, d_pre_sums, cond_act):
        width = cond_act.shape[1]
        extra = d_pre_sums.shape[0]

        def kernel(first_ref, middle_ref, output_ref, d_pre_ref, cond_ref, out_ref):
            out_ref[0:2, :] = first_ref[0:2, :].astype(bf16).astype(f32)
            out_ref[2:5, :] = middle_ref[0:3, :].astype(bf16).astype(f32)
            out_ref[5:6, :] = output_ref[0:1, :].astype(bf16).astype(f32)
            for row in (6, 7):
                out_ref[row : row + 1, :] = cond_ref[...].astype(f32)
            out_ref[8:10, :] = first_ref[2:4, :]
            out_ref[10:11, :] = middle_ref[3:4, :]
            out_ref[11:12, :] = output_ref[1:2, :]
            out_ref[12:, :] = d_pre_ref[...]

        return pl.pallas_call(
            kernel,
            out_shape=jax.ShapeDtypeStruct((12 + extra, width), f32),
            in_specs=[vmem] * 5,
            out_specs=vmem,
            cost_estimate=cost(1),
            compiler_params=params(60),
        )(first_sums, middle_sums, output_sums, d_pre_sums, cond_act)

    def column_total(items):
        width = items[0][0].shape[1]
        n = sum(item[0].shape[0] for item in items)
        padded = -(-n // 128) * 128
        arrays = [array for item in items for array in item]

        def kernel(*refs):
            for first in range(0, width, 128):
                totals, used = [], 0
                for item in items:
                    parts = [ref[:, first : first + 128] for ref in refs[used : used + len(item)]]
                    totals.append(sum((part.astype(f32) for part in parts[1:]), parts[0]))
                    used += len(item)
                if padded > n:
                    totals.append(jnp.zeros((padded - n, 128), f32))
                total = jnp.concatenate(totals, axis=0) if len(totals) > 1 else totals[0]
                refs[-1][first : first + 128, :] = total.T.astype(bf16)

        return pl.pallas_call(
            kernel,
            out_shape=jax.ShapeDtypeStruct((width, padded), bf16),
            in_specs=[vmem] * len(arrays),
            out_specs=vmem,
            cost_estimate=cost(5),
            compiler_params=params(60),
        )(*arrays)

    def row_total(keep, got):
        def kernel(keep_ref, got_ref, out_ref):
            out_ref[...] = (keep_ref[...] + got_ref[...]).astype(bf16)

        total = pl.pallas_call(
            kernel,
            out_shape=jax.ShapeDtypeStruct(keep.shape, bf16),
            in_specs=[vmem] * 2,
            out_specs=vmem,
            cost_estimate=cost(3),
            compiler_params=params(60),
        )(keep, got)
        return total.reshape(-1, keep.shape[2])

    def fsdp_sum(x):
        return lax.psum_scatter(x, "fsdp", scatter_dimension=0, tiled=True)

    def out_grad(where, d_attn_turned, attended):
        width, slots = d_attn_turned.shape
        n = width // BOX

        def kernel(where_ref, d_ref, x_ref, keep_ref, send_ref):
            step = pl.program_id(0)
            core = where_ref[0]
            for out_ref, which in ((keep_ref, core), (send_ref, 1 - core)):
                first = (where_ref[step + 1] * 2 + which) * n
                rows = pl.ds(pl.multiple_of(first, 16), n)
                out_ref[0] = jnp.dot(d_ref[rows, :], x_ref[...], preferred_element_type=f32)

        out_spec = pl.BlockSpec((1, n, width), lambda i, where_ref: (i, 0, 0))
        return pl.pallas_call(
            kernel,
            out_shape=[jax.ShapeDtypeStruct((BOX // 2, n, width), f32)] * 2,
            grid_spec=pltpu.PrefetchScalarGridSpec(
                num_scalar_prefetch=1,
                grid=(BOX // 2,),
                in_specs=[
                    pl.BlockSpec((width, slots), lambda i, where_ref: (0, 0)),
                    pl.BlockSpec((slots, width), lambda i, where_ref: (0, 0)),
                ],
                out_specs=[out_spec] * 2,
            ),
            cost_estimate=cost(5),
            compiler_params=params(60),
        )(where, d_attn_turned, attended)

    def chip_split(keep, got):
        count, rows, width = keep.shape

        def kernel(keep_ref, got_ref, *outs):
            for k, out_ref in enumerate(outs):
                out_ref[...] = (keep_ref[k] + got_ref[k]).astype(out_ref.dtype)

        return pl.pallas_call(
            kernel,
            out_shape=[jax.ShapeDtypeStruct((rows, width), f32)]
            + [jax.ShapeDtypeStruct((rows, width), bf16)] * (count - 1),
            in_specs=[vmem] * 2,
            out_specs=[vmem] * count,
            cost_estimate=cost(3),
            compiler_params=params(60),
        )(keep, got)

    def row_grad(where, lefts, rights):
        rows = lefts[0].shape[0] // fs
        slots, n = lefts[0].shape[1], rows // 2
        width = rights[0].shape[1]
        half = slots // 2

        def kernel(where_ref, x0, x1, x2, x3, y0, y1, y2, y3, y4, keep_ref, send_ref):
            core = where_ref[0]
            for out_ref, first in ((keep_ref, core * n), (send_ref, (1 - core) * n)):
                lines = pl.ds(pl.multiple_of(first, 16), n)
                total = None
                for x, y, cols in (
                    (x0, y0, slice(None)),
                    (x1, y1, slice(None)),
                    (x2, y2, slice(None)),
                    (x3, y3, slice(0, half)),
                    (x3, y4, slice(half, slots)),
                ):
                    part = jnp.dot(x[lines, cols], y[...], preferred_element_type=f32)
                    total = part if total is None else total + part
                out_ref[0] = total

        left_spec = pl.BlockSpec((rows, slots), lambda i, where_ref: (i, 0))
        right_specs = [
            pl.BlockSpec((right.shape[0], width), lambda i, where_ref: (0, 0))
            for right in rights
        ]
        out_spec = pl.BlockSpec((1, n, width), lambda i, where_ref: (i, 0, 0))
        return pl.pallas_call(
            kernel,
            out_shape=[jax.ShapeDtypeStruct((fs, n, width), f32)] * 2,
            grid_spec=pltpu.PrefetchScalarGridSpec(
                num_scalar_prefetch=1,
                grid=(fs,),
                in_specs=[left_spec] * 4 + right_specs,
                out_specs=[out_spec] * 2,
            ),
            cost_estimate=cost(6),
            compiler_params=params(60),
        )(where, *lefts, *rights)

    def body(
        tokens,
        condition,
        grid_sizes,
        w_ada,
        w_qkv,
        w_out,
        w_up,
        w_down,
        b_ada,
        b_qv,
        b_out,
        b_up,
        b_down,
        cotangent,
    ):
        slots, width = tokens.shape[1:]
        heads = width // HEAD_DIM
        hidden = w_up.shape[1]
        rank = lax.axis_index("dp")
        z = lax.axis_index("fsdp")
        place = lax.rem(rank, BOX)
        group = lax.div(rank, BOX)
        core = place & 1
        chip = place >> 1
        side = (chip ^ (chip >> 1)) & 1
        near = 2 * side + core
        far = 2 * (1 - side) + core
        where = jnp.stack(
            [lax.rem(z - k + fs, fs) for k in range(fs)]
            + [near, far, near ^ 1, far ^ 1]
            + [chip ^ k for k in range(4)]
        ).astype(jnp.int32)
        where_core = core.reshape(1).astype(jnp.int32)
        where_wide = jnp.stack(
            [lax.rem(z - k + fs, fs) for k in range(fs)] + [core] + [chip ^ k for k in range(4)]
        ).astype(jnp.int32)

        cond_wide = condition.astype(f32)
        gate = jax.nn.sigmoid(cond_wide)
        cond_act = (cond_wide * gate).astype(bf16)

        def quarter_of(shard):
            return pick(in_blocks(shard), near)

        qkv_quarter = quarter_of(w_qkv)
        cond_rows = ring_gather(after(cond_act, qkv_quarter))
        raw = jnp.concatenate([tokens[0], cotangent[0]], axis=1)
        qkv_helds = [ring_send(qkv_quarter, 1)]
        mid_rows = jnp.concatenate(
            [pick(in_blocks(w_out), chip), pick(in_blocks(w_up), chip)], axis=-1
        )
        mid_width = mid_rows.shape[-1]
        mid_part = -(-mid_width // 256) * 128
        mid_start = jnp.where(core == 0, 0, mid_width - mid_part)
        mid_eighth = lax.dynamic_slice_in_dim(mid_rows, mid_start, mid_part, 2)
        down_quarter = quarter_of(w_down)
        ada_shard = b_ada.shape[0]
        bias_ada = lax.dynamic_update_slice_in_dim(
            jnp.zeros((fs * ada_shard,), f32), b_ada.astype(f32), z * ada_shard, 0
        ).reshape(6, width)
        small = jnp.concatenate([b_qv, b_out, b_down, b_up]).astype(f32).reshape(-1, width)
        cond_rows, qkv_helds, bias_ada, small, mid_eighth, down_quarter = gated(
            (cond_rows, qkv_helds, bias_ada, small, mid_eighth, down_quarter)
        )

        rows_z = width // fs
        conds = jnp.concatenate(cond_rows)
        conds_z = lax.dynamic_slice_in_dim(conds, z * rows_z, rows_z, 1)
        partials = modulation_parts(conds_z, w_ada, bias_ada, small)
        partials = [partials[0]] + [ring_send(partials[k], fs - k) for k in range(1, fs)]
        raw_near = chip_near(after(raw, conds_z))
        qkv_helds.append(ring_send(qkv_helds[-1], 1))
        partials, qkv_helds = gated((partials, qkv_helds))

        live = (grid_sizes[0, 0] * grid_sizes[0, 1]).reshape(1)
        mods, head = modulation_rows(partials, live)
        (normed,), (d_mlp,) = other_heads((raw,), (0,), (head,))
        qkv_helds.append(ring_send(qkv_helds[-1], 1))
        mods, head, normed, d_mlp, raw_near, qkv_helds = gated(
            (mods, head, normed, d_mlp, raw_near, qkv_helds)
        )

        qkv_mine = jnp.stack(qkv_helds)
        qkv_other = side_send(qkv_mine)
        qkv_mine_got = box_send(qkv_mine, 1)
        mid_helds = [ring_send(after(mid_eighth, qkv_mine), 1)]
        heads_got = [box_send(after(head, qkv_mine), bits) for bits in (2, 4)]
        bias_rows = [each[6:].reshape(-1) for each in partials]
        bias_rows = jnp.stack(bias_rows + bias_rows)
        biases = lax.dynamic_slice_in_dim(bias_rows, lax.rem(fs - z, fs), fs, 0)
        ends = [0]
        for bias in (b_qv, b_out, b_down, b_up):
            ends.append(ends[-1] + bias.shape[0])
        biases = [biases[:, ends[i] : ends[i + 1]].reshape(-1) for i in range(4)]
        qkv_mine, qkv_other, qkv_mine_got, mid_helds, biases, heads_got = gated(
            (qkv_mine, qkv_other, qkv_mine_got, mid_helds, biases, heads_got)
        )
        bias_qv, bias_out, bias_down, bias_up = biases

        last = fs - 1

        def in_order(array):
            return [(array, k) for k in range(last)]

        qkv_other_got = box_send(qkv_other, 1)
        heads_got.append(box_send(after(head, qkv_other), 6))
        raw_far = chip_far([after(each, qkv_other) for each in raw_near])
        mid_helds.append(ring_send(mid_helds[-1], 1))
        turned, qkv_full = projection(
            where,
            normed,
            w_qkv,
            [in_order(each) for each in (qkv_mine, qkv_other, qkv_mine_got, qkv_other_got)],
            bias_qv.reshape(2, width),
        )
        turned, qkv_full, mid_helds, raw_far, heads_got = gated(
            (turned, qkv_full, mid_helds, raw_far, heads_got)
        )

        mid_first = jnp.concatenate(mid_helds)
        first_near = chip_near(mid_first)
        mid_last = ring_send(mid_helds[-1], 1)
        down_helds = [ring_send(after(down_quarter, mid_first), 1)]
        attended = attention(turned, live)
        attended, mid_first, first_near, mid_last = gated(
            (attended, mid_first, first_near, mid_last)
        )

        last_near = chip_near(mid_last)
        first_got = [box_send(mid_first, 1)]
        normed_box, d_mlp_box = other_heads(
            (*raw_near, *raw_far), (0, 0, 0, slots // 2), (*heads_got, heads_got[2])
        )
        normed_box, d_mlp_box = [normed, *normed_box], [d_mlp, *d_mlp_box]
        first_near, last_near, first_got, down_helds, normed_box, d_mlp_box = gated(
            (first_near, last_near, first_got, down_helds, normed_box, d_mlp_box)
        )

        split = (mid_first.shape[0] + mid_last.shape[0]) // 2
        mid_far = (
            box_send(first_near[0][:split], 4),
            box_send(jnp.concatenate([first_near[1][split:], last_near[1]]), 2),
        )
        first_got += [box_send(each, 1) for each in first_near]
        down_helds.append(ring_send(down_helds[-1], 1))
        attended, mid_far, first_got, down_helds = gated(
            (attended, mid_far, first_got, down_helds)
        )

        last_got = [box_send(each, 1) for each in (mid_last, *last_near)]
        far_got = [box_send(each, 1) for each in mid_far]
        down_helds.append(ring_send(down_helds[-1], 1))
        down_others = [side_send(each) for each in down_helds[:-1]]

        def paired(first, last_ones, far):
            pairs = [each for pair in zip(first, last_ones) for each in pair]
            return [*pairs, *far]

        attn_out, normed_two, pre_act, activated, *act_blocks, out_full, up_full = middle_forward(
            where_wide,
            attended,
            tokens[0],
            [w_out, w_up],
            (
                paired((mid_first, *first_near), (mid_last, *last_near), mid_far),
                paired(first_got, last_got, far_got),
            ),
            bias_out,
            bias_up,
            mods,
        )
        down_helds, down_others, act_blocks, normed_two = gated(
            (down_helds, down_others, act_blocks, normed_two)
        )

        down_others.append(side_send(down_helds[-1]))
        down_got = [[box_send(each, 1) for each in kind] for kind in (down_helds, down_others)]
        act_blocks, down_others, down_got = gated((act_blocks, down_others, down_got))

        act_box = chip_exchange(act_blocks)
        d_pre, *d_pre_turned, d_pre_sums, down_full = hidden_back(
            where,
            d_mlp,
            w_down,
            [[(each, None) for each in kind] for kind in (down_helds, down_others, *down_got)],
            pre_act,
        )

        def column_blocks(grad_t):
            n = grad_t.shape[0] // dp
            blocks = grad_t.reshape(groups, BOX, n, slots).transpose(1, 0, 2, 3)
            blocks = blocks.reshape(BOX // 2, 2 * groups * n, slots)
            return [pick(blocks, chip ^ k) for k in range(BOX // 2)]

        d_pre_blocks = d_pre_turned if groups == 1 else column_blocks(d_pre_turned[0])
        output, output_sums = output_rows(
            activated,
            down_full,
            bias_down,
            tokens[0],
            attn_out,
            cotangent[0],
            d_mlp,
            mods,
            live,
        )
        d_pre, d_pre_blocks, act_box, normed_two, output_sums = gated(
            (d_pre, d_pre_blocks, act_box, normed_two, output_sums)
        )

        d_pre_box = chip_exchange(d_pre_blocks)
        keep_down, send_down = row_grad(where_core, act_box, d_mlp_box)
        d_middle, d_attn_turned, d_attended_turned, middle_sums = middle_back(
            d_pre, up_full, out_full, attn_out, tokens[0], cotangent[0], mods, live
        )
        d_attended_turned, d_attn_turned, d_pre_box, keep_down, send_down, normed_two = gated(
            (d_attended_turned, d_attn_turned, d_pre_box, keep_down, send_down, normed_two)
        )

        normed_two_near = chip_near(normed_two)
        total_down = row_total(keep_down, box_send(send_down, 1))
        grad_down = fsdp_sum(total_down)
        d_projected, *last_blocks = attention_back(
            turned, after(d_attended_turned, total_down), live, where[fs + 4 :]
        )
        if groups > 1:
            last_blocks = column_blocks(d_projected)
            d_attn_turned = d_attn_turned.reshape(groups, BOX, -1, slots)
            d_attn_turned = d_attn_turned.transpose(1, 0, 2, 3).reshape(width, slots)
        keep_out, send_out = out_grad(
            jnp.concatenate([where_core, where[fs + 4 :]]), d_attn_turned, attended
        )
        got_out = box_send(send_out, 1)
        normed_two_far = chip_far([after(each, d_projected) for each in normed_two_near])
        normed_two_box = [normed_two, *normed_two_near, *normed_two_far]
        d_projected, last_blocks, normed_two_box, grad_down, keep_out, got_out = gated(
            (d_projected, last_blocks, normed_two_box, grad_down, keep_out, got_out)
        )

        def over_groups(grad):
            rows, cols = grad.shape
            return group_sum(grad.reshape(rows, groups, -1).transpose(1, 0, 2), group)

        last_box = chip_exchange(last_blocks)
        grad_tokens, first_sums = first_back(d_projected, qkv_full, tokens[0], d_middle, mods)
        out_blocks = chip_split(keep_out, got_out)
        keep_up, send_up = column_grad(
            where_core, [(normed_two_box, 0, d_pre_box[0].shape[0])], d_pre_box
        )
        total_up = column_total([(keep_up, box_send(send_up, 1))])
        last_box, first_sums, total_up, out_blocks = gated(
            (last_box, first_sums, total_up, out_blocks)
        )

        grad_up = fsdp_sum(total_up)
        keep_qkv, send_qkv = column_grad(
            where_core, [(normed_box, 0, last_box[0].shape[0])], last_box
        )
        message = sums_message(
            first_sums, middle_sums, output_sums, d_pre_sums.reshape(-1, width), cond_act
        )
        out_parts = chip_exchange(out_blocks)
        messages = ring_gather(message)
        total_last = column_total([(keep_qkv, box_send(send_qkv, 1)), tuple(out_parts)])
        grad_down = after(grad_down, keep_qkv)
        if groups > 1:
            grad_down = over_groups(grad_down.astype(f32))
        down_rows = grad_down.shape[0]
        down_cols = grad_down.reshape(down_rows, BOX, -1).transpose(1, 0, 2)
        if groups == 1:
            parts = lax.all_to_all(down_cols, "dp", 0, 0, tiled=True)
        else:
            parts = [pick(down_cols, place)] + [
                box_send(pick(down_cols, place ^ k), k) for k in range(1, BOX)
            ]
            parts = jnp.stack(parts)
            parts = jnp.stack([pick(parts, place ^ k) for k in range(BOX)])
        total_last, messages, grad_up, parts = gated((total_last, messages, grad_up, parts))

        grad_last = fsdp_sum(total_last)
        images_near = jnp.stack([each[:8] for each in messages]).astype(bf16)
        totals = [each[8:] for each in messages]
        images, total = images_near, sum(totals[1:], totals[0])
        for bits in (1, 2, 4):
            images = jnp.concatenate([images, box_send(images, bits)])
            total = total + box_send(total, bits)
        images_box, total_box = images, total
        for k in range(1, groups):
            images = jnp.concatenate([images, group_send(images_box, k)])
            total = total + group_send(total_box, k)
        grad_w_down = parts.reshape(BOX * down_rows, width // dp).astype(f32)
        grad_w_up = over_groups(grad_up[:, : keep_up.shape[0]].astype(f32))
        cut_cols, last_cols = keep_qkv.shape[0], keep_qkv.shape[0] + keep_out.shape[1]
        grad_w_qkv = over_groups(grad_last[:, :cut_cols].astype(f32))
        grad_w_out = over_groups(grad_last[:, cut_cols:last_cols].astype(f32))
        conds_all = lax.dynamic_slice_in_dim(images[:, 6], z * rows_z, rows_z, 1)
        d_mod_all = images[:, :6]
        ada_cols = 6 * width // dp
        grad_w_ada = lax.dot_general(
            conds_all,
            lax.dynamic_slice_in_dim(
                d_mod_all.reshape(dp * fs, 6 * width), rank * ada_cols, ada_cols, 1
            ),
            (((0,), (0,)), ((), ())),
            preferred_element_type=f32,
        )
        d_conds = lax.dot_general(
            images_near[:, :6].reshape(fs, 6 * width),
            w_ada,
            (((1,), (1,)), ((), ())),
            preferred_element_type=f32,
        )
        cond_parts = [d_conds[0]] + [ring_send(d_conds[k], fs - k) for k in range(1, fs)]
        twice = jnp.stack(cond_parts + cond_parts)
        d_cond_act = lax.dynamic_slice_in_dim(twice, lax.rem(fs - z, fs), fs, 0).reshape(-1)
        grad_condition = d_cond_act[None] * gate * (1.0 + cond_wide * (1.0 - gate))

        def shard_of(rows):
            return pick(rows.reshape(fs, -1), z)

        grads_bias = [
            shard_of(jnp.sum(d_mod_all.astype(f32), axis=0)),
            shard_of(total[:2]),
            shard_of(total[2]),
            shard_of(total[4:]),
            shard_of(total[3]),
        ]
        return (
            output[None],
            grad_tokens[None],
            grad_condition,
            grad_w_ada,
            grad_w_qkv,
            grad_w_out,
            grad_w_up,
            grad_w_down,
            *grads_bias,
        )

    return body


def solution(mesh):
    return jax.shard_map(
        make_body(mesh.shape["dp"], mesh.shape["fsdp"]),
        mesh=mesh,
        in_specs=(
            P(("dp", "fsdp"), None, None),
            P(("dp", "fsdp"), None),
            P(("dp", "fsdp"), None),
            P("fsdp", None),
            P("fsdp", None),
            P("fsdp", None),
            P("fsdp", None),
            P("fsdp", None),
            P("fsdp"),
            P("fsdp"),
            P("fsdp"),
            P("fsdp"),
            P("fsdp"),
            P(("dp", "fsdp"), None, None),
        ),
        out_specs=(
            P(("dp", "fsdp"), None, None),
            P(("dp", "fsdp"), None, None),
            P(("dp", "fsdp"), None),
            P("fsdp", "dp"),
            P("fsdp", "dp"),
            P("fsdp", "dp"),
            P("fsdp", "dp"),
            P("fsdp", "dp"),
            P("fsdp"),
            P("fsdp"),
            P("fsdp"),
            P("fsdp"),
            P("fsdp"),
        ),
        check_vma=False,
    )
```

```python
import math

import jax
import jax.numpy as jnp
from jax import lax
from jax.experimental import pallas as pl
from jax.experimental.pallas import tpu as pltpu
from jax.sharding import PartitionSpec as P

HEAD_DIM = 72
BOX = 8

epsilon = 1e-06
masked_value = -1e30
gelu_root = math.sqrt(2.0 / math.pi)
f32 = jnp.float32
bf16 = jnp.bfloat16


def norm_parts(values_in):
    centred = values_in - jnp.mean(values_in, axis=-1, keepdims=True)
    spread = jnp.mean(centred * centred, axis=-1, keepdims=True)
    rate = lax.rsqrt(spread + epsilon)
    return centred * rate, rate


def norm_back(normal, rate, grad):
    mean_grad = jnp.mean(grad, axis=-1, keepdims=True)
    mean_both = jnp.mean(grad * normal, axis=-1, keepdims=True)
    return rate * (grad - mean_grad - normal * mean_both)


def gelu_tanh(pre_act):
    return (
        0.5
        * pre_act
        * (1.0 + jnp.tanh(gelu_root * (pre_act + 0.044715 * pre_act * pre_act * pre_act)))
    )


def after(value, other):
    return lax.optimization_barrier((value, other))[0]


def gated(values):
    return lax.optimization_barrier(values)


def pick(array, index, axis=0):
    return lax.dynamic_index_in_dim(array, index, axis, keepdims=False)


def make_body(dp, fs):
    groups = dp // BOX

    def box_send(x, bits):
        return lax.ppermute(x, "dp", [(i, i ^ bits) for i in range(dp)])

    def side_send(x):
        return lax.ppermute(x, "dp", [(i, i ^ (4 if i & 1 else 2)) for i in range(dp)])

    def ring_send(x, hops):
        return lax.ppermute(x, "fsdp", [(i, (i + hops) % fs) for i in range(fs)])

    def group_send(x, hops):
        return lax.ppermute(x, "dp", [(i, (i + hops * BOX) % dp) for i in range(dp)])

    def ring_gather(x):
        return [x] + [ring_send(x, k) for k in range(1, fs)]

    def ring_sorted(blocks, z):
        back = jnp.stack(blocks[::-1] + blocks[::-1])
        return lax.dynamic_slice_in_dim(back, fs - 1 - z, fs, 0)

    def chip_near(x):
        return box_send(x, 2), box_send(x, 4)

    def chip_far(near):
        half = near[0].shape[0] // 2
        return box_send(near[0][:half], 4), box_send(near[1][half:], 2)

    def chip_exchange(blocks):
        return [blocks[0]] + [box_send(blocks[k], 2 * k) for k in range(1, BOX // 2)]

    def ring_sum(x, z):
        total = pick(x, z)
        for k in range(1, fs):
            sent = pick(x, lax.rem(z + k, fs)).astype(bf16)
            total = total + ring_send(sent, k).astype(f32)
        return total

    def group_sum(x, group):
        total = pick(x, group)
        for k in range(1, groups):
            total = total + group_send(pick(x, lax.rem(group + k, groups)), k)
        return total

    def cost(microseconds):
        return pl.CostEstimate(
            flops=int(microseconds * 1e8),
            transcendentals=0,
            bytes_accessed=int(microseconds * 3.2e5),
        )

    vmem = pl.BlockSpec(memory_space=pltpu.VMEM)
    smem = pl.BlockSpec(memory_space=pltpu.SMEM)

    def params(mebibytes):
        return pltpu.CompilerParams(vmem_limit_bytes=mebibytes << 20)

    def chunks(rows, step, work):
        def one(i, unused):
            work(pl.ds(pl.multiple_of(i * step, step), step), i * step)
            return unused

        lax.fori_loop(0, rows // step, one, 0)

    def alive_rows(first, rows, live):
        return ((lax.broadcasted_iota(jnp.int32, (rows, 1), 0) + first) < live).astype(f32)

    def modulation_parts(conds, w_ada, bias_ada, extra):
        images = conds.shape[0]
        parts, width = bias_ada.shape

        def kernel(cond_ref, w_ref, bias_ref, extra_ref, *out_refs):
            for part in range(parts):
                cols = slice(part * width, (part + 1) * width)
                product = jnp.dot(cond_ref[...], w_ref[:, cols], preferred_element_type=f32)
                product = product + bias_ref[part : part + 1, :]
                for image, out_ref in enumerate(out_refs):
                    out_ref[part : part + 1, :] = product[image : image + 1, :]
            for out_ref in out_refs:
                out_ref[parts:, :] = extra_ref[...]

        rows = parts + extra.shape[0]
        return pl.pallas_call(
            kernel,
            out_shape=[jax.ShapeDtypeStruct((rows, width), f32)] * images,
            in_specs=[vmem] * 4,
            out_specs=[vmem] * images,
            cost_estimate=cost(4),
            compiler_params=params(60),
        )(conds, w_ada, bias_ada, extra)

    def modulation_rows(partials, live):
        rows, width = partials[0].shape

        def kernel(live_ref, *refs):
            mods_ref, head_ref = refs[-2:]
            total = refs[0][...]
            for ref in refs[1:-2]:
                total = total + ref[...]
            mods_ref[...] = total
            head_ref[...] = jnp.full(head_ref.shape, live_ref[0].astype(f32))
            head_ref[0:2, :] = total[0:2, :]
            head_ref[2:3, :] = total[5:6, :]

        return pl.pallas_call(
            kernel,
            out_shape=[jax.ShapeDtypeStruct((rows, width), f32)] * 2,
            in_specs=[smem] + [vmem] * len(partials),
            out_specs=[vmem] * 2,
            cost_estimate=cost(1),
            compiler_params=params(60),
        )(live, *partials)

    def other_heads(raws, firsts, heads):
        n = len(raws)
        width = raws[0].shape[1] // 2

        def kernel(*refs):
            raw_refs, head_refs = refs[:n], refs[n : 2 * n]
            normed_refs, d_mlp_refs = refs[2 * n : 3 * n], refs[3 * n :]
            for raw, head, normed, d_mlp, first in zip(
                raw_refs, head_refs, normed_refs, d_mlp_refs, firsts
            ):
                live = head[3, 0].astype(jnp.int32)

                def work(rows, start):
                    normal = norm_parts(raw[rows, :width].astype(f32))[0]
                    normed[rows, :] = (
                        normal * (1.0 + head[1:2, :]) + head[0:1, :]
                    ).astype(bf16)
                    count = normal.shape[0]
                    up_rows = alive_rows(start + first, count, live) * raw[
                        rows, width:
                    ].astype(f32)
                    d_mlp[rows, :] = (head[2:3, :] * up_rows).astype(bf16)

                chunks(raw.shape[0], 32, work)

        outs = pl.pallas_call(
            kernel,
            out_shape=[jax.ShapeDtypeStruct((raw.shape[0], width), bf16) for raw in raws] * 2,
            in_specs=[vmem] * (2 * n),
            out_specs=[vmem] * (2 * n),
            cost_estimate=cost(8),
            compiler_params=params(60),
        )(*raws, *heads)
        return outs[:n], outs[n:]

    def piece_plan(pieces):
        arrays = []
        for piece, unused in (each for kind in pieces for each in kind):
            if not any(piece is array for array in arrays):
                arrays.append(piece)
        position = {id(array): i for i, array in enumerate(arrays)}
        plan = [[(position[id(piece)], index) for piece, index in kind] for kind in pieces]
        return arrays, plan

    def piece_copies(where_ref, own_ref, array_refs, plan, whole_ref):
        copies = [(own_ref, whole_ref.at[where_ref[0]])]
        for kind, blocks in enumerate(plan):
            for k, (which, index) in enumerate(blocks):
                source = array_refs[which] if index is None else array_refs[which].at[index]
                copies.append((source, whole_ref.at[where_ref[k + 1], where_ref[fs + kind]]))
        return copies

    def wide_copies(core, where_ref, own_refs, sets, whole_refs):
        widths = [ref.shape[-1] for ref in own_refs]
        width, part = sum(widths), sets[0][0].shape[-1]
        lead, split = whole_refs[0].shape[2], sets[0][6].shape[0]
        copies = [(own, whole.at[where_ref[0]]) for own, whole in zip(own_refs, whole_refs)]
        for side, piece_refs in enumerate(sets):
            low, high = (0, part) if core ^ side == 0 else (part, width)
            offset = 0 if core ^ side == 0 else width - part
            for block in range(1, fs):
                base = (block - 1) * lead
                top = min(max(split - base, 0), lead)
                late = int(block == fs - 1)
                rows = [(2 * i + late, 0 if late else base, i, 0, lead) for i in range(3)]
                if top:
                    rows.append((6, base, 3, 0, top))
                if top < lead:
                    rows.append((7, base + top - split, 3, top, lead - top))
                for piece, first, slot, row, count in rows:
                    start = 0
                    for i, each in enumerate(widths):
                        left, right = max(low, start), min(high, start + each)
                        if left < right:
                            source = piece_refs[piece].at[
                                first : first + count, :, left - offset : right - offset
                            ]
                            target = whole_refs[i].at[
                                where_ref[block],
                                where_ref[fs + 1 + slot],
                                row : row + count,
                                :,
                                left - start : right - start,
                            ]
                            copies.append((source, target))
                        start += each
        return copies

    def copy_all(copies, sems):
        return [
            pltpu.make_async_copy(source, target, sems.at[j])
            for j, (source, target) in enumerate(copies)
        ]

    def start_all(copies):
        for copy in copies:
            copy.start()

    def wait_all(copies):
        for copy in copies:
            copy.wait()

    def in_blocks(shard):
        rows, cols = shard.shape
        return shard.reshape(4, rows // 32, 8, cols)

    any_spec = pl.BlockSpec(memory_space=pl.ANY)

    def projection(where, normed, own, pieces, biases):
        slots, width = normed.shape
        arrays, plan = piece_plan(pieces)
        own = in_blocks(own)
        shape = (fs,) + own.shape

        def kernel(where_ref, normed_ref, bias_ref, own_ref, *refs):
            array_refs = refs[: len(arrays)]
            turned_ref, whole_ref, scratch, sems, out_sem = refs[len(arrays) :]
            copies = copy_all(
                piece_copies(where_ref, own_ref, array_refs, plan, scratch), sems
            )
            start_all(copies)
            wait_all(copies)
            out = pltpu.make_async_copy(scratch, whole_ref, out_sem)
            out.start()
            w_ref = scratch.reshape(width, 3 * width)
            for part in range(3):
                cols = slice(part * width, (part + 1) * width)
                proj = jnp.dot(normed_ref[...], w_ref[:, cols], preferred_element_type=f32)
                if part != 1:
                    proj = proj + bias_ref[part // 2 : part // 2 + 1, :]
                turned_ref[cols, :] = proj.astype(bf16).astype(f32).T
            out.wait()

        turned, whole = pl.pallas_call(
            kernel,
            out_shape=[
                jax.ShapeDtypeStruct((3 * width, slots), f32),
                jax.ShapeDtypeStruct(shape, bf16),
            ],
            in_specs=[smem, vmem, vmem, any_spec] + [any_spec] * len(arrays),
            out_specs=[vmem, any_spec],
            scratch_shapes=[
                pltpu.VMEM(shape, bf16),
                pltpu.SemaphoreType.DMA((1 + 4 * (fs - 1),)),
                pltpu.SemaphoreType.DMA,
            ],
            cost_estimate=cost(11),
            compiler_params=params(60),
        )(where, normed, biases, own, *arrays)
        return turned, whole.reshape(width, 3 * width)

    def attention(turned, live):
        slots = turned.shape[1]
        width = turned.shape[0] // 3
        count = width // HEAD_DIM
        heads_at_once = 2 if count % 2 == 0 else 1
        scale = HEAD_DIM ** (-0.5)

        def kernel(live_ref, turned_ref, attended_ref, out_turned):
            live_keys = lax.broadcasted_iota(jnp.int32, (1, slots), 1) < live_ref[0]

            def head(h):
                def rows(part):
                    first = pl.multiple_of(part * width + h * HEAD_DIM, 8)
                    return turned_ref[pl.ds(first, HEAD_DIM), :].astype(bf16)

                scores = lax.dot_general(
                    rows(0), rows(1), (((0,), (0,)), ((), ())), preferred_element_type=f32
                )
                scores = jnp.where(live_keys, scores * scale, masked_value)
                highest = jnp.max(scores, axis=-1, keepdims=True)
                total = jnp.sum(jnp.exp(scores - highest), axis=-1, keepdims=True)
                probs = jnp.exp(scores - (highest + jnp.log(total)))
                return lax.dot_general(
                    rows(2),
                    probs.astype(bf16),
                    (((1,), (1,)), ((), ())),
                    preferred_element_type=f32,
                )

            def some_heads(i, unused):
                outs = [head(i * heads_at_once + j) for j in range(heads_at_once)]
                for j, out in enumerate(outs):
                    first = pl.multiple_of((i * heads_at_once + j) * HEAD_DIM, 8)
                    out_turned[pl.ds(first, HEAD_DIM), :] = out
                return unused

            lax.fori_loop(0, count // heads_at_once, some_heads, 0)
            attended_ref[...] = out_turned[...].T.astype(bf16)

        return pl.pallas_call(
            kernel,
            out_shape=jax.ShapeDtypeStruct((slots, width), bf16),
            in_specs=[smem, vmem],
            out_specs=vmem,
            scratch_shapes=[pltpu.VMEM((width, slots), f32)],
            cost_estimate=cost(11),
            compiler_params=params(60),
        )(live, turned)

    def attention_back(turned, d_turned, live, where_chip):
        width, slots = d_turned.shape
        part = 3 * width // 4
        count = width // HEAD_DIM
        heads_at_once = 1
        scale = HEAD_DIM ** (-0.5)

        def kernel(live_ref, chip_ref, turned_ref, d_ref, out_ref, *rest):
            block_refs, total_ref = rest[:-1], rest[-1]
            live_keys = lax.broadcasted_iota(jnp.int32, (1, slots), 1) < live_ref[0]

            def place_of(h, part):
                return pl.ds(pl.multiple_of(part * width + h * HEAD_DIM, 8), HEAD_DIM)

            def head(h):
                def place(part):
                    return place_of(h, part)

                query = turned_ref[place(0), :].astype(bf16)
                key_part = turned_ref[place(1), :].astype(bf16)
                value = turned_ref[place(2), :].astype(bf16)
                d_out = d_ref[place(0), :].astype(bf16)
                both_first = (((0,), (0,)), ((), ()))
                scores = lax.dot_general(
                    query, key_part, both_first, preferred_element_type=f32
                )
                scores = jnp.where(live_keys, scores * scale, masked_value)
                highest = jnp.max(scores, axis=-1, keepdims=True)
                total = jnp.sum(jnp.exp(scores - highest), axis=-1, keepdims=True)
                probs = jnp.exp(scores - (highest + jnp.log(total)))
                d_probs = lax.dot_general(
                    d_out, value, both_first, preferred_element_type=f32
                )
                inner = jnp.sum(probs * d_probs, axis=-1, keepdims=True)
                d_scores = (probs * (d_probs - inner)).astype(bf16)
                d_value = jnp.dot(d_out, probs.astype(bf16), preferred_element_type=f32)
                d_query = scale * lax.dot_general(
                    key_part, d_scores, (((1,), (1,)), ((), ())), preferred_element_type=f32
                )
                d_key = scale * jnp.dot(query, d_scores, preferred_element_type=f32)
                return d_query, d_key, d_value

            def some_heads(i, unused):
                outs = [head(i * heads_at_once + j) for j in range(heads_at_once)]
                for j, parts in enumerate(outs):
                    for part, out in enumerate(parts):
                        total_ref[place_of(i * heads_at_once + j, part), :] = out
                return unused

            lax.fori_loop(0, count // heads_at_once, some_heads, 0)
            out_ref[...] = total_ref[...].astype(bf16)
            for k, block in enumerate(block_refs):
                first = pl.multiple_of(chip_ref[k] * part, 16)
                block[...] = total_ref[pl.ds(first, part), :].astype(bf16)

        n_blocks = 4 if groups == 1 else 0
        return pl.pallas_call(
            kernel,
            out_shape=[jax.ShapeDtypeStruct((3 * width, slots), bf16)]
            + [jax.ShapeDtypeStruct((part, slots), bf16)] * n_blocks,
            in_specs=[smem, smem, vmem, vmem],
            out_specs=[vmem] * (1 + n_blocks),
            scratch_shapes=[pltpu.VMEM((3 * width, slots), f32)],
            cost_estimate=cost(12),
            compiler_params=params(60),
        )(live, where_chip, turned, d_turned)

    def middle_forward(where, attended, tokens_own, owns, sets, bias_out, bias_up, mods):
        slots, width = attended.shape
        owns = [in_blocks(own) for own in owns]
        hidden = owns[1].shape[-1]
        tile = hidden // fs
        quarter = tile // 4
        shapes = [(fs,) + own.shape for own in owns]
        n_pieces = len(sets[0])
        n_copies = 2 + 2 * 15 * (fs - 1)

        def kernel(where_ref, attended_ref, tokens_ref, bias_out_ref, bias_up_ref, mods_ref, *refs):
            own_refs = refs[:2]
            set_refs = (refs[2 : 2 + n_pieces], refs[2 + n_pieces : 2 + 2 * n_pieces])
            (
                attn_ref,
                normed_ref,
                pre_ref,
                act_ref,
                block0,
                block1,
                block2,
                block3,
                whole_out,
                whole_up,
                scratch_out,
                scratch_up,
                turned,
                sems,
                out_sems,
            ) = refs[2 + 2 * n_pieces :]
            step = pl.program_id(0)
            scratches, wholes = (scratch_out, scratch_up), (whole_out, whole_up)

            def outs():
                return [
                    pltpu.make_async_copy(scratch, whole, out_sems.at[i])
                    for i, (scratch, whole) in enumerate(zip(scratches, wholes))
                ]

            @pl.when(step == 0)
            def first():
                for core in range(2):

                    @pl.when(where_ref[fs] == core)
                    def gather(core=core):
                        copies = copy_all(
                            wide_copies(core, where_ref, own_refs, set_refs, scratches), sems
                        )
                        start_all(copies)
                        wait_all(copies)

                start_all(outs())
                attn_ref[...] = (
                    jnp.dot(
                        attended_ref[...],
                        scratch_out.reshape(width, width)[...],
                        preferred_element_type=f32,
                    )
                    + bias_out_ref[...]
                )

                def work(rows, unused):
                    middle = tokens_ref[rows, :].astype(f32) + mods_ref[2:3, :] * attn_ref[rows, :]
                    normal = norm_parts(middle)[0]
                    normed_ref[rows, :] = (
                        normal * (1.0 + mods_ref[4:5, :]) + mods_ref[3:4, :]
                    ).astype(bf16)

                chunks(slots, 32, work)

            cols = pl.ds(pl.multiple_of(step * tile, 128), tile)
            pre_ref[...] = (
                jnp.dot(
                    normed_ref[...],
                    scratch_up.reshape(width, hidden)[:, cols],
                    preferred_element_type=f32,
                )
                + bias_up_ref[0]
            )

            def work(rows, unused):
                act_ref[rows, :] = gelu_tanh(pre_ref[rows, :]).astype(bf16)

            chunks(slots, 32, work)
            turned[...] = act_ref[...].astype(f32).T
            for k, block in enumerate((block0, block1, block2, block3)):
                first = pl.multiple_of(where_ref[fs + 1 + k] * quarter, 16)
                block[...] = turned[pl.ds(first, quarter), :].astype(bf16)

            @pl.when(step == fs - 1)
            def last():
                wait_all(outs())

        def whole(shape):
            return pl.BlockSpec(shape, lambda j, where_ref: (0,) * len(shape))

        *results, whole_out, whole_up = pl.pallas_call(
            kernel,
            out_shape=[
                jax.ShapeDtypeStruct((slots, width), f32),
                jax.ShapeDtypeStruct((slots, width), bf16),
                jax.ShapeDtypeStruct((slots, hidden), f32),
                jax.ShapeDtypeStruct((slots, hidden), bf16),
            ]
            + [jax.ShapeDtypeStruct((fs * quarter, slots), bf16)] * 4
            + [jax.ShapeDtypeStruct(shape, bf16) for shape in shapes],
            grid_spec=pltpu.PrefetchScalarGridSpec(
                num_scalar_prefetch=1,
                grid=(fs,),
                in_specs=[
                    whole((slots, width)),
                    whole((slots, width)),
                    whole((1, width)),
                    pl.BlockSpec((1, 1, tile), lambda j, where_ref: (j, 0, 0)),
                    whole(mods.shape),
                ]
                + [any_spec] * (2 + 2 * n_pieces),
                out_specs=[
                    whole((slots, width)),
                    whole((slots, width)),
                    pl.BlockSpec((slots, tile), lambda j, where_ref: (0, j)),
                    pl.BlockSpec((slots, tile), lambda j, where_ref: (0, j)),
                ]
                + [pl.BlockSpec((quarter, slots), lambda j, where_ref: (j, 0))] * 4
                + [any_spec, any_spec],
                scratch_shapes=[pltpu.VMEM(shape, bf16) for shape in shapes]
                + [
                    pltpu.VMEM((tile, slots), f32),
                    pltpu.SemaphoreType.DMA((n_copies,)),
                    pltpu.SemaphoreType.DMA((2,)),
                ],
            ),
            cost_estimate=cost(20),
            compiler_params=params(60),
        )(
            where,
            attended,
            tokens_own,
            bias_out.reshape(1, width),
            bias_up.reshape(fs, 1, tile),
            mods,
            *owns,
            *sets[0],
            *sets[1],
        )
        return (
            *results,
            whole_out.reshape(width, width),
            whole_up.reshape(width, hidden),
        )

    def hidden_back(where, d_mlp, own, pieces, pre_act):
        slots, width = d_mlp.shape
        hidden = pre_act.shape[1]
        tile = hidden // fs
        if groups == 1:
            turned_shapes = [jax.ShapeDtypeStruct((tile, slots), bf16)] * 4
            turned_specs = [pl.BlockSpec((tile, slots), lambda j, where_ref: (0, 0))] * 4
        else:
            turned_shapes = [jax.ShapeDtypeStruct((hidden, slots), bf16)]
            turned_specs = [pl.BlockSpec((tile, slots), lambda j, where_ref: (j, 0))]
        arrays, plan = piece_plan(pieces)
        own = in_blocks(own)
        shape = (fs,) + own.shape

        def kernel(where_ref, d_mlp_ref, pre_ref, own_ref, *refs):
            array_refs = refs[: len(arrays)]
            d_pre_ref, *turned_refs, sum_ref, whole_ref = refs[len(arrays) : -4]
            d_act_ref, scratch, sems, out_sem = refs[-4:]
            step = pl.program_id(0)

            def out():
                return pltpu.make_async_copy(scratch, whole_ref, out_sem)

            @pl.when(step == 0)
            def first():
                copies = copy_all(
                    piece_copies(where_ref, own_ref, array_refs, plan, scratch), sems
                )
                start_all(copies)
                wait_all(copies)
                out().start()

            d_act_ref[...] = lax.dot_general(
                d_mlp_ref[...],
                scratch.at[step].reshape(tile, width)[...],
                (((1,), (1,)), ((), ())),
                preferred_element_type=f32,
            )

            def work(rows, unused):
                pre = pre_ref[rows, :]
                square = pre * pre
                bend = jnp.tanh(gelu_root * (pre + 0.044715 * square * pre))
                slope = 0.5 * (1.0 + bend) + 0.5 * pre * (1.0 - bend * bend) * gelu_root * (
                    1.0 + 3.0 * 0.044715 * square
                )
                d_pre = (d_act_ref[rows, :] * slope).astype(bf16)
                d_pre_ref[rows, :] = d_pre
                d_act_ref[rows, :] = d_pre.astype(f32)

            chunks(slots, 32, work)
            sum_ref[0] = jnp.sum(d_act_ref[...], axis=0, keepdims=True)
            if groups == 1:
                for k, turned_ref in enumerate(turned_refs):

                    @pl.when(step == where_ref[fs + 4 + k])
                    def block(turned_ref=turned_ref):
                        turned_ref[...] = d_act_ref[...].T.astype(bf16)
            else:
                turned_refs[0][...] = d_act_ref[...].T.astype(bf16)

            @pl.when(step == fs - 1)
            def last():
                out().wait()

        *results, whole = pl.pallas_call(
            kernel,
            out_shape=[
                jax.ShapeDtypeStruct((slots, hidden), bf16),
                *turned_shapes,
                jax.ShapeDtypeStruct((fs, 1, tile), f32),
                jax.ShapeDtypeStruct(shape, bf16),
            ],
            grid_spec=pltpu.PrefetchScalarGridSpec(
                num_scalar_prefetch=1,
                grid=(fs,),
                in_specs=[
                    pl.BlockSpec((slots, width), lambda j, where_ref: (0, 0)),
                    pl.BlockSpec((slots, tile), lambda j, where_ref: (0, j)),
                    any_spec,
                ]
                + [any_spec] * len(arrays),
                out_specs=[
                    pl.BlockSpec((slots, tile), lambda j, where_ref: (0, j)),
                    *turned_specs,
                    pl.BlockSpec((1, 1, tile), lambda j, where_ref: (j, 0, 0)),
                    any_spec,
                ],
                scratch_shapes=[
                    pltpu.VMEM((slots, tile), f32),
                    pltpu.VMEM(shape, bf16),
                    pltpu.SemaphoreType.DMA((1 + 4 * (fs - 1),)),
                    pltpu.SemaphoreType.DMA,
                ],
            ),
            cost_estimate=cost(15),
            compiler_params=params(60),
        )(where, d_mlp, pre_act, own, *arrays)
        return (*results, whole.reshape(hidden, width))

    def middle_back(d_pre, up_full, out_full, attn_out, tokens_own, cotangent_own, mods, live):
        slots, hidden = d_pre.shape
        width = attn_out.shape[1]
        tile = hidden // fs

        def kernel(
            live_ref,
            d_pre_ref,
            up_ref,
            out_ref,
            attn_ref,
            tokens_ref,
            cot_ref,
            mods_ref,
            d_middle_ref,
            d_attn_turned_ref,
            d_attended_turned_ref,
            sums_ref,
            total,
            d_attn_ref,
        ):
            step = pl.program_id(0)
            part = lax.dot_general(
                d_pre_ref[...],
                up_ref[...],
                (((1,), (1,)), ((), ())),
                preferred_element_type=f32,
            )

            @pl.when(step == 0)
            def start():
                total[...] = part

            @pl.when(step > 0)
            def add():
                total[...] += part

            @pl.when(step == fs - 1)
            def finish():
                sums_ref[...] = jnp.zeros_like(sums_ref)

                def work(rows, first):
                    grad = total[rows, :]
                    attn = attn_ref[rows, :]
                    middle = tokens_ref[rows, :].astype(f32) + mods_ref[2:3, :] * attn
                    normal, rate = norm_parts(middle)
                    alive = alive_rows(first, grad.shape[0], live_ref[0])
                    d_middle = alive * cot_ref[rows, :].astype(f32) + norm_back(
                        normal, rate, grad * (1.0 + mods_ref[4:5, :])
                    )
                    d_middle_ref[rows, :] = d_middle
                    d_attn = (mods_ref[2:3, :] * d_middle).astype(bf16)
                    d_attn_ref[rows, :] = d_attn
                    for i, each in enumerate(
                        (d_middle * attn, grad, grad * normal, d_attn.astype(f32))
                    ):
                        sums_ref[i : i + 1, :] += jnp.sum(each, axis=0, keepdims=True)

                chunks(slots, 32, work)
                d_attn_turned_ref[...] = d_attn_ref[...].astype(f32).T.astype(bf16)
                d_attended = lax.dot_general(
                    d_attn_ref[...],
                    out_ref[...],
                    (((1,), (1,)), ((), ())),
                    preferred_element_type=f32,
                )
                d_attended_turned_ref[...] = d_attended.astype(bf16).astype(f32).T

        def whole(shape):
            return pl.BlockSpec(shape, lambda j, live_ref: (0,) * len(shape))

        return pl.pallas_call(
            kernel,
            out_shape=[
                jax.ShapeDtypeStruct((slots, width), f32),
                jax.ShapeDtypeStruct((width, slots), bf16),
                jax.ShapeDtypeStruct((width, slots), f32),
                jax.ShapeDtypeStruct((8, width), f32),
            ],
            grid_spec=pltpu.PrefetchScalarGridSpec(
                num_scalar_prefetch=1,
                grid=(fs,),
                in_specs=[
                    pl.BlockSpec((slots, tile), lambda j, live_ref: (0, j)),
                    pl.BlockSpec((width, tile), lambda j, live_ref: (0, j)),
                    whole((width, width)),
                    whole((slots, width)),
                    whole((slots, width)),
                    whole((slots, width)),
                    whole(mods.shape),
                ],
                out_specs=[
                    whole((slots, width)),
                    whole((width, slots)),
                    whole((width, slots)),
                    whole((8, width)),
                ],
                scratch_shapes=[
                    pltpu.VMEM((slots, width), f32),
                    pltpu.VMEM((slots, width), bf16),
                ],
            ),
            cost_estimate=cost(12),
            compiler_params=params(60),
        )(live, d_pre, up_full, out_full, attn_out, tokens_own, cotangent_own, mods)

    def first_back(d_turned, qkv_full, tokens_own, d_middle, mods):
        slots, width = d_middle.shape

        def kernel(d_ref, w_ref, tokens_ref, d_middle_ref, mods_ref, grad_ref, sums_ref, total):
            sums_ref[...] = jnp.zeros_like(sums_ref)
            for part in range(3):
                cols = slice(part * width, (part + 1) * width)
                d_part = d_ref[cols, :].astype(f32).T
                if part != 1:
                    row = 2 + part // 2
                    sums_ref[row : row + 1, :] = jnp.sum(d_part, axis=0, keepdims=True)
                product = lax.dot_general(
                    d_part.astype(bf16),
                    w_ref[:, cols],
                    (((1,), (1,)), ((), ())),
                    preferred_element_type=f32,
                )
                if part == 0:
                    total[...] = product
                else:
                    total[...] += product

            def work(rows, unused):
                grad = total[rows, :]
                normal, rate = norm_parts(tokens_ref[rows, :].astype(f32))
                sums_ref[0:1, :] += jnp.sum(grad, axis=0, keepdims=True)
                sums_ref[1:2, :] += jnp.sum(grad * normal, axis=0, keepdims=True)
                grad_ref[rows, :] = (
                    d_middle_ref[rows, :]
                    + norm_back(normal, rate, grad * (1.0 + mods_ref[1:2, :]))
                ).astype(bf16)

            chunks(slots, 32, work)

        return pl.pallas_call(
            kernel,
            out_shape=[
                jax.ShapeDtypeStruct((slots, width), bf16),
                jax.ShapeDtypeStruct((8, width), f32),
            ],
            in_specs=[vmem] * 5,
            out_specs=[vmem] * 2,
            scratch_shapes=[pltpu.VMEM((slots, width), f32)],
            cost_estimate=cost(9),
            compiler_params=params(60),
        )(d_turned, qkv_full, tokens_own, d_middle, mods)

    def output_rows(
        activated, down_full, bias_down, tokens_own, attn_out, cotangent_own, d_mlp, mods, live
    ):
        slots, hidden = activated.shape
        width = attn_out.shape[1]
        tile = hidden // fs

        def kernel(
            live_ref,
            act_ref,
            down_ref,
            bias_ref,
            tokens_ref,
            attn_ref,
            cot_ref,
            d_mlp_ref,
            mods_ref,
            out_ref,
            sums_ref,
            total,
        ):
            step = pl.program_id(0)
            part = jnp.dot(act_ref[...], down_ref[...], preferred_element_type=f32)

            @pl.when(step == 0)
            def start():
                total[...] = part

            @pl.when(step > 0)
            def add():
                total[...] += part

            @pl.when(step == fs - 1)
            def finish():
                sums_ref[...] = jnp.zeros_like(sums_ref)

                def work(rows, first):
                    mlp_out = total[rows, :] + bias_ref[...]
                    middle = (
                        tokens_ref[rows, :].astype(f32) + mods_ref[2:3, :] * attn_ref[rows, :]
                    )
                    alive = alive_rows(first, mlp_out.shape[0], live_ref[0])
                    out_ref[rows, :] = (alive * (middle + mods_ref[5:6, :] * mlp_out)).astype(bf16)
                    d_gate = alive * cot_ref[rows, :].astype(f32) * mlp_out
                    sums_ref[0:1, :] += jnp.sum(d_gate, axis=0, keepdims=True)
                    sums_ref[1:2, :] += jnp.sum(
                        d_mlp_ref[rows, :].astype(f32), axis=0, keepdims=True
                    )

                chunks(slots, 32, work)

        def whole(shape):
            return pl.BlockSpec(shape, lambda j, live_ref: (0,) * len(shape))

        return pl.pallas_call(
            kernel,
            out_shape=[
                jax.ShapeDtypeStruct((slots, width), bf16),
                jax.ShapeDtypeStruct((8, width), f32),
            ],
            grid_spec=pltpu.PrefetchScalarGridSpec(
                num_scalar_prefetch=1,
                grid=(fs,),
                in_specs=[
                    pl.BlockSpec((slots, tile), lambda j, live_ref: (0, j)),
                    pl.BlockSpec((tile, width), lambda j, live_ref: (j, 0)),
                    whole((1, width)),
                    whole((slots, width)),
                    whole((slots, width)),
                    whole((slots, width)),
                    whole((slots, width)),
                    whole(mods.shape),
                ],
                out_specs=[whole((slots, width)), whole((8, width))],
                scratch_shapes=[pltpu.VMEM((slots, width), f32)],
            ),
            cost_estimate=cost(6),
            compiler_params=params(60),
        )(
            live,
            activated,
            down_full,
            bias_down.reshape(1, width),
            tokens_own,
            attn_out,
            cotangent_own,
            d_mlp,
            mods,
        )

    def column_grad(where, items, rights):
        slots = rights[0].shape[1]
        width = items[0][0][0].shape[1]
        tile = width // 3
        half = slots // 2
        counts = [(stop - start) // 2 for unused, start, stop in items]
        n_out = sum(counts)
        lefts = [left for box, unused, unused_stop in items for left in box]

        def kernel(where_ref, *refs):
            core = where_ref[0]
            y0, y1, y2, y3, keep_ref, send_ref = refs[len(lefts) :]
            for i, (unused, start, unused_stop) in enumerate(items):
                x0, x1, x2, x3, x4 = refs[5 * i : 5 * i + 5]
                n = counts[i]
                below = sum(counts[:i])
                for out_ref, first in ((keep_ref, core * n), (send_ref, (1 - core) * n)):
                    rows = pl.ds(pl.multiple_of(start + first, 16), n)
                    total = None
                    for x, y, cols in (
                        (x0, y0, slice(None)),
                        (x1, y1, slice(None)),
                        (x2, y2, slice(None)),
                        (x3, y3, slice(0, half)),
                        (x4, y3, slice(half, slots)),
                    ):
                        part = jnp.dot(y[rows, cols], x[...], preferred_element_type=f32)
                        total = part if total is None else total + part
                    out_ref[below : below + n, :] = total

        left_specs = [
            pl.BlockSpec((left.shape[0], tile), lambda i, where_ref: (0, i)) for left in lefts
        ]
        right_spec = pl.BlockSpec(rights[0].shape, lambda i, where_ref: (0, 0))
        out_spec = pl.BlockSpec((n_out, tile), lambda i, where_ref: (0, i))
        return pl.pallas_call(
            kernel,
            out_shape=[jax.ShapeDtypeStruct((n_out, width), f32)] * 2,
            grid_spec=pltpu.PrefetchScalarGridSpec(
                num_scalar_prefetch=1,
                grid=(width // tile,),
                in_specs=left_specs + [right_spec] * 4,
                out_specs=[out_spec] * 2,
            ),
            cost_estimate=cost(8),
            compiler_params=params(60),
        )(where, *lefts, *rights)

    def sums_message(first_sums, middle_sums, output_sums, d_pre_sums, cond_act):
        width = cond_act.shape[1]
        extra = d_pre_sums.shape[0]

        def kernel(first_ref, middle_ref, output_ref, d_pre_ref, cond_ref, out_ref):
            out_ref[0:2, :] = first_ref[0:2, :].astype(bf16).astype(f32)
            out_ref[2:5, :] = middle_ref[0:3, :].astype(bf16).astype(f32)
            out_ref[5:6, :] = output_ref[0:1, :].astype(bf16).astype(f32)
            for row in (6, 7):
                out_ref[row : row + 1, :] = cond_ref[...].astype(f32)
            out_ref[8:10, :] = first_ref[2:4, :]
            out_ref[10:11, :] = middle_ref[3:4, :]
            out_ref[11:12, :] = output_ref[1:2, :]
            out_ref[12:, :] = d_pre_ref[...]

        return pl.pallas_call(
            kernel,
            out_shape=jax.ShapeDtypeStruct((12 + extra, width), f32),
            in_specs=[vmem] * 5,
            out_specs=vmem,
            cost_estimate=cost(1),
            compiler_params=params(60),
        )(first_sums, middle_sums, output_sums, d_pre_sums, cond_act)

    def column_total(items):
        width = items[0][0].shape[1]
        n = sum(item[0].shape[0] for item in items)
        padded = -(-n // 128) * 128
        half = width // fs // 2
        arrays = [array for item in items for array in item]

        def kernel(*refs):
            out_ref, turned = refs[-2:]
            for first in range(0, width, 128):
                totals, used = [], 0
                for item in items:
                    parts = [ref[:, first : first + 128] for ref in refs[used : used + len(item)]]
                    totals.append(sum((part.astype(f32) for part in parts[1:]), parts[0]))
                    used += len(item)
                if padded > n:
                    totals.append(jnp.zeros((padded - n, 128), f32))
                total = jnp.concatenate(totals, axis=0) if len(totals) > 1 else totals[0]
                turned[first : first + 128, :] = total.T[:, :n]
            for block in range(fs):
                rows = slice(block * half, (block + 1) * half)
                upper = 2 * block * half
                out_ref[rows, :n] = turned[upper : upper + half, :].astype(bf16)
                out_ref[rows, n:] = turned[upper + half : upper + 2 * half, :].astype(bf16)

        return pl.pallas_call(
            kernel,
            out_shape=jax.ShapeDtypeStruct((fs * half, 2 * n), bf16),
            in_specs=[vmem] * len(arrays),
            out_specs=vmem,
            scratch_shapes=[pltpu.VMEM((width, n), f32)],
            cost_estimate=cost(5),
            compiler_params=params(60),
        )(*arrays)

    def unfolded(x, start, stop):
        n = x.shape[1] // 2
        return jnp.concatenate([x[:, start:stop], x[:, n + start : n + stop]]).astype(f32)

    def row_total(keep, got):
        def kernel(keep_ref, got_ref, out_ref):
            out_ref[...] = (keep_ref[...] + got_ref[...]).astype(bf16)

        total = pl.pallas_call(
            kernel,
            out_shape=jax.ShapeDtypeStruct(keep.shape, bf16),
            in_specs=[vmem] * 2,
            out_specs=vmem,
            cost_estimate=cost(3),
            compiler_params=params(60),
        )(keep, got)
        return total.reshape(-1, keep.shape[2])

    def fsdp_sum(x):
        return lax.psum_scatter(x, "fsdp", scatter_dimension=0, tiled=True)

    def out_grad(where, d_attn_turned, attended):
        width, slots = d_attn_turned.shape
        n = width // BOX

        def kernel(where_ref, d_ref, x_ref, keep_ref, send_ref):
            step = pl.program_id(0)
            core = where_ref[0]
            for out_ref, which in ((keep_ref, core), (send_ref, 1 - core)):
                first = (where_ref[step + 1] * 2 + which) * n
                rows = pl.ds(pl.multiple_of(first, 16), n)
                out_ref[0] = jnp.dot(d_ref[rows, :], x_ref[...], preferred_element_type=f32)

        out_spec = pl.BlockSpec((1, n, width), lambda i, where_ref: (i, 0, 0))
        return pl.pallas_call(
            kernel,
            out_shape=[jax.ShapeDtypeStruct((BOX // 2, n, width), f32)] * 2,
            grid_spec=pltpu.PrefetchScalarGridSpec(
                num_scalar_prefetch=1,
                grid=(BOX // 2,),
                in_specs=[
                    pl.BlockSpec((width, slots), lambda i, where_ref: (0, 0)),
                    pl.BlockSpec((slots, width), lambda i, where_ref: (0, 0)),
                ],
                out_specs=[out_spec] * 2,
            ),
            cost_estimate=cost(5),
            compiler_params=params(60),
        )(where, d_attn_turned, attended)

    def chip_split(keep, got):
        count, rows, width = keep.shape

        def kernel(keep_ref, got_ref, *outs):
            for k, out_ref in enumerate(outs):
                out_ref[...] = (keep_ref[k] + got_ref[k]).astype(out_ref.dtype)

        return pl.pallas_call(
            kernel,
            out_shape=[jax.ShapeDtypeStruct((rows, width), f32)]
            + [jax.ShapeDtypeStruct((rows, width), bf16)] * (count - 1),
            in_specs=[vmem] * 2,
            out_specs=[vmem] * count,
            cost_estimate=cost(3),
            compiler_params=params(60),
        )(keep, got)

    def row_grad(where, lefts, rights):
        rows = lefts[0].shape[0] // fs
        slots, n = lefts[0].shape[1], rows // 2
        width = rights[0].shape[1]
        half = slots // 2

        def kernel(where_ref, x0, x1, x2, x3, y0, y1, y2, y3, y4, keep_ref, send_ref):
            core = where_ref[0]
            for out_ref, first in ((keep_ref, core * n), (send_ref, (1 - core) * n)):
                lines = pl.ds(pl.multiple_of(first, 16), n)
                total = None
                for x, y, cols in (
                    (x0, y0, slice(None)),
                    (x1, y1, slice(None)),
                    (x2, y2, slice(None)),
                    (x3, y3, slice(0, half)),
                    (x3, y4, slice(half, slots)),
                ):
                    part = jnp.dot(x[lines, cols], y[...], preferred_element_type=f32)
                    total = part if total is None else total + part
                out_ref[0] = total

        left_spec = pl.BlockSpec((rows, slots), lambda i, where_ref: (i, 0))
        right_specs = [
            pl.BlockSpec((right.shape[0], width), lambda i, where_ref: (0, 0))
            for right in rights
        ]
        out_spec = pl.BlockSpec((1, n, width), lambda i, where_ref: (i, 0, 0))
        return pl.pallas_call(
            kernel,
            out_shape=[jax.ShapeDtypeStruct((fs, n, width), f32)] * 2,
            grid_spec=pltpu.PrefetchScalarGridSpec(
                num_scalar_prefetch=1,
                grid=(fs,),
                in_specs=[left_spec] * 4 + right_specs,
                out_specs=[out_spec] * 2,
            ),
            cost_estimate=cost(6),
            compiler_params=params(60),
        )(where, *lefts, *rights)

    def body(
        tokens,
        condition,
        grid_sizes,
        w_ada,
        w_qkv,
        w_out,
        w_up,
        w_down,
        b_ada,
        b_qv,
        b_out,
        b_up,
        b_down,
        cotangent,
    ):
        slots, width = tokens.shape[1:]
        heads = width // HEAD_DIM
        hidden = w_up.shape[1]
        rank = lax.axis_index("dp")
        z = lax.axis_index("fsdp")
        place = lax.rem(rank, BOX)
        group = lax.div(rank, BOX)
        core = place & 1
        chip = place >> 1
        side = (chip ^ (chip >> 1)) & 1
        near = 2 * side + core
        far = 2 * (1 - side) + core
        where = jnp.stack(
            [lax.rem(z - k + fs, fs) for k in range(fs)]
            + [near, far, near ^ 1, far ^ 1]
            + [chip ^ k for k in range(4)]
        ).astype(jnp.int32)
        where_core = core.reshape(1).astype(jnp.int32)
        where_wide = jnp.stack(
            [lax.rem(z - k + fs, fs) for k in range(fs)] + [core] + [chip ^ k for k in range(4)]
        ).astype(jnp.int32)

        cond_wide = condition.astype(f32)
        gate = jax.nn.sigmoid(cond_wide)
        cond_act = (cond_wide * gate).astype(bf16)

        def quarter_of(shard):
            return pick(in_blocks(shard), near)

        qkv_quarter = quarter_of(w_qkv)
        cond_rows = ring_gather(after(cond_act, qkv_quarter))
        raw = jnp.concatenate([tokens[0], cotangent[0]], axis=1)
        qkv_helds = [ring_send(qkv_quarter, 1)]
        mid_rows = jnp.concatenate(
            [pick(in_blocks(w_out), chip), pick(in_blocks(w_up), chip)], axis=-1
        )
        mid_width = mid_rows.shape[-1]
        mid_part = -(-mid_width // 256) * 128
        mid_start = jnp.where(core == 0, 0, mid_width - mid_part)
        mid_eighth = lax.dynamic_slice_in_dim(mid_rows, mid_start, mid_part, 2)
        down_quarter = quarter_of(w_down)
        ada_shard = b_ada.shape[0]
        bias_ada = lax.dynamic_update_slice_in_dim(
            jnp.zeros((fs * ada_shard,), f32), b_ada.astype(f32), z * ada_shard, 0
        ).reshape(6, width)
        small = jnp.concatenate([b_qv, b_out, b_down, b_up]).astype(f32).reshape(-1, width)
        cond_rows, qkv_helds, bias_ada, small, mid_eighth, down_quarter = gated(
            (cond_rows, qkv_helds, bias_ada, small, mid_eighth, down_quarter)
        )

        rows_z = width // fs
        conds = jnp.concatenate(cond_rows)
        conds_z = lax.dynamic_slice_in_dim(conds, z * rows_z, rows_z, 1)
        partials = modulation_parts(conds_z, w_ada, bias_ada, small)
        partials = [partials[0]] + [ring_send(partials[k], fs - k) for k in range(1, fs)]
        raw_near = chip_near(after(raw, conds_z))
        qkv_helds.append(ring_send(qkv_helds[-1], 1))
        partials, qkv_helds = gated((partials, qkv_helds))

        live = (grid_sizes[0, 0] * grid_sizes[0, 1]).reshape(1)
        mods, head = modulation_rows(partials, live)
        (normed,), (d_mlp,) = other_heads((raw,), (0,), (head,))
        qkv_helds.append(ring_send(qkv_helds[-1], 1))
        mods, head, normed, d_mlp, raw_near, qkv_helds = gated(
            (mods, head, normed, d_mlp, raw_near, qkv_helds)
        )

        qkv_mine = jnp.stack(qkv_helds)
        qkv_other = side_send(qkv_mine)
        qkv_mine_got = box_send(qkv_mine, 1)
        mid_helds = [ring_send(after(mid_eighth, qkv_mine), 1)]
        heads_got = [box_send(after(head, qkv_mine), bits) for bits in (2, 4)]
        bias_rows = [each[6:].reshape(-1) for each in partials]
        bias_rows = jnp.stack(bias_rows + bias_rows)
        biases = lax.dynamic_slice_in_dim(bias_rows, lax.rem(fs - z, fs), fs, 0)
        ends = [0]
        for bias in (b_qv, b_out, b_down, b_up):
            ends.append(ends[-1] + bias.shape[0])
        biases = [biases[:, ends[i] : ends[i + 1]].reshape(-1) for i in range(4)]
        qkv_mine, qkv_other, qkv_mine_got, mid_helds, biases, heads_got = gated(
            (qkv_mine, qkv_other, qkv_mine_got, mid_helds, biases, heads_got)
        )
        bias_qv, bias_out, bias_down, bias_up = biases

        last = fs - 1

        def in_order(array):
            return [(array, k) for k in range(last)]

        qkv_other_got = box_send(qkv_other, 1)
        heads_got.append(box_send(after(head, qkv_other), 6))
        raw_far = chip_far([after(each, qkv_other) for each in raw_near])
        mid_helds.append(ring_send(mid_helds[-1], 1))
        turned, qkv_full = projection(
            where,
            normed,
            w_qkv,
            [in_order(each) for each in (qkv_mine, qkv_other, qkv_mine_got, qkv_other_got)],
            bias_qv.reshape(2, width),
        )
        turned, qkv_full, mid_helds, raw_far, heads_got = gated(
            (turned, qkv_full, mid_helds, raw_far, heads_got)
        )

        mid_first = jnp.concatenate(mid_helds)
        first_near = chip_near(mid_first)
        mid_last = ring_send(mid_helds[-1], 1)
        down_helds = [ring_send(after(down_quarter, mid_first), 1)]
        attended = attention(turned, live)
        attended, mid_first, first_near, mid_last = gated(
            (attended, mid_first, first_near, mid_last)
        )

        last_near = chip_near(mid_last)
        first_got = [box_send(mid_first, 1)]
        normed_box, d_mlp_box = other_heads(
            (*raw_near, *raw_far), (0, 0, 0, slots // 2), (*heads_got, heads_got[2])
        )
        normed_box, d_mlp_box = [normed, *normed_box], [d_mlp, *d_mlp_box]
        first_near, last_near, first_got, down_helds, normed_box, d_mlp_box = gated(
            (first_near, last_near, first_got, down_helds, normed_box, d_mlp_box)
        )

        split = (mid_first.shape[0] + mid_last.shape[0]) // 2
        mid_far = (
            box_send(first_near[0][:split], 4),
            box_send(jnp.concatenate([first_near[1][split:], last_near[1]]), 2),
        )
        first_got += [box_send(each, 1) for each in first_near]
        down_helds.append(ring_send(down_helds[-1], 1))
        attended, mid_far, first_got, down_helds = gated(
            (attended, mid_far, first_got, down_helds)
        )

        last_got = [box_send(each, 1) for each in (mid_last, *last_near)]
        far_got = [box_send(each, 1) for each in mid_far]
        down_helds.append(ring_send(down_helds[-1], 1))
        down_others = [side_send(each) for each in down_helds[:-1]]

        def paired(first, last_ones, far):
            pairs = [each for pair in zip(first, last_ones) for each in pair]
            return [*pairs, *far]

        attn_out, normed_two, pre_act, activated, *act_blocks, out_full, up_full = middle_forward(
            where_wide,
            attended,
            tokens[0],
            [w_out, w_up],
            (
                paired((mid_first, *first_near), (mid_last, *last_near), mid_far),
                paired(first_got, last_got, far_got),
            ),
            bias_out,
            bias_up,
            mods,
        )
        down_helds, down_others, act_blocks, normed_two = gated(
            (down_helds, down_others, act_blocks, normed_two)
        )

        down_others.append(side_send(down_helds[-1]))
        down_got = [[box_send(each, 1) for each in kind] for kind in (down_helds, down_others)]
        act_blocks, down_others, down_got = gated((act_blocks, down_others, down_got))

        act_box = chip_exchange(act_blocks)
        d_pre, *d_pre_turned, d_pre_sums, down_full = hidden_back(
            where,
            d_mlp,
            w_down,
            [[(each, None) for each in kind] for kind in (down_helds, down_others, *down_got)],
            pre_act,
        )

        def column_blocks(grad_t):
            n = grad_t.shape[0] // dp
            blocks = grad_t.reshape(groups, BOX, n, slots).transpose(1, 0, 2, 3)
            blocks = blocks.reshape(BOX // 2, 2 * groups * n, slots)
            return [pick(blocks, chip ^ k) for k in range(BOX // 2)]

        d_pre_blocks = d_pre_turned if groups == 1 else column_blocks(d_pre_turned[0])
        output, output_sums = output_rows(
            activated,
            down_full,
            bias_down,
            tokens[0],
            attn_out,
            cotangent[0],
            d_mlp,
            mods,
            live,
        )
        d_pre, d_pre_blocks, act_box, normed_two, output_sums = gated(
            (d_pre, d_pre_blocks, act_box, normed_two, output_sums)
        )

        d_pre_box = chip_exchange(d_pre_blocks)
        keep_down, send_down = row_grad(where_core, act_box, d_mlp_box)
        d_middle, d_attn_turned, d_attended_turned, middle_sums = middle_back(
            d_pre, up_full, out_full, attn_out, tokens[0], cotangent[0], mods, live
        )
        d_attended_turned, d_attn_turned, d_pre_box, keep_down, send_down, normed_two = gated(
            (d_attended_turned, d_attn_turned, d_pre_box, keep_down, send_down, normed_two)
        )

        normed_two_near = chip_near(normed_two)
        total_down = row_total(keep_down, box_send(send_down, 1))
        grad_down = fsdp_sum(total_down)
        d_projected, *last_blocks = attention_back(
            turned, after(d_attended_turned, total_down), live, where[fs + 4 :]
        )
        if groups > 1:
            last_blocks = column_blocks(d_projected)
            d_attn_turned = d_attn_turned.reshape(groups, BOX, -1, slots)
            d_attn_turned = d_attn_turned.transpose(1, 0, 2, 3).reshape(width, slots)
        keep_out, send_out = out_grad(
            jnp.concatenate([where_core, where[fs + 4 :]]), d_attn_turned, attended
        )
        got_out = box_send(send_out, 1)
        normed_two_far = chip_far([after(each, d_projected) for each in normed_two_near])
        normed_two_box = [normed_two, *normed_two_near, *normed_two_far]
        d_projected, last_blocks, normed_two_box, grad_down, keep_out, got_out = gated(
            (d_projected, last_blocks, normed_two_box, grad_down, keep_out, got_out)
        )

        def over_groups(grad):
            rows, cols = grad.shape
            return group_sum(grad.reshape(rows, groups, -1).transpose(1, 0, 2), group)

        last_box = chip_exchange(last_blocks)
        grad_tokens, first_sums = first_back(d_projected, qkv_full, tokens[0], d_middle, mods)
        out_blocks = chip_split(keep_out, got_out)
        keep_up, send_up = column_grad(
            where_core, [(normed_two_box, 0, d_pre_box[0].shape[0])], d_pre_box
        )
        total_up = column_total([(keep_up, box_send(send_up, 1))])
        last_box, first_sums, total_up, out_blocks = gated(
            (last_box, first_sums, total_up, out_blocks)
        )

        grad_up = fsdp_sum(total_up)
        keep_qkv, send_qkv = column_grad(
            where_core, [(normed_box, 0, last_box[0].shape[0])], last_box
        )
        message = sums_message(
            first_sums, middle_sums, output_sums, d_pre_sums.reshape(-1, width), cond_act
        )
        out_parts = chip_exchange(out_blocks)
        messages = ring_gather(message)
        total_last = column_total([(keep_qkv, box_send(send_qkv, 1)), tuple(out_parts)])
        grad_down = after(grad_down, keep_qkv)
        if groups > 1:
            grad_down = over_groups(grad_down.astype(f32))
        down_rows = grad_down.shape[0]
        down_cols = grad_down.reshape(down_rows, BOX, -1).transpose(1, 0, 2)
        if groups == 1:
            parts = lax.all_to_all(down_cols, "dp", 0, 0, tiled=True)
        else:
            parts = [pick(down_cols, place)] + [
                box_send(pick(down_cols, place ^ k), k) for k in range(1, BOX)
            ]
            parts = jnp.stack(parts)
            parts = jnp.stack([pick(parts, place ^ k) for k in range(BOX)])
        total_last, messages, grad_up, parts = gated((total_last, messages, grad_up, parts))

        grad_last = fsdp_sum(total_last)
        images_near = jnp.stack([each[:8] for each in messages]).astype(bf16)
        totals = [each[8:] for each in messages]
        images, total = images_near, sum(totals[1:], totals[0])
        for bits in (1, 2, 4):
            images = jnp.concatenate([images, box_send(images, bits)])
            total = total + box_send(total, bits)
        images_box, total_box = images, total
        for k in range(1, groups):
            images = jnp.concatenate([images, group_send(images_box, k)])
            total = total + group_send(total_box, k)
        grad_w_down = parts.reshape(BOX * down_rows, width // dp).astype(f32)
        grad_w_up = over_groups(unfolded(grad_up, 0, keep_up.shape[0]))
        cut_cols, last_cols = keep_qkv.shape[0], keep_qkv.shape[0] + keep_out.shape[1]
        grad_w_qkv = over_groups(unfolded(grad_last, 0, cut_cols))
        grad_w_out = over_groups(unfolded(grad_last, cut_cols, last_cols))
        conds_all = lax.dynamic_slice_in_dim(images[:, 6], z * rows_z, rows_z, 1)
        d_mod_all = images[:, :6]
        ada_cols = 6 * width // dp
        grad_w_ada = lax.dot_general(
            conds_all,
            lax.dynamic_slice_in_dim(
                d_mod_all.reshape(dp * fs, 6 * width), rank * ada_cols, ada_cols, 1
            ),
            (((0,), (0,)), ((), ())),
            preferred_element_type=f32,
        )
        d_conds = lax.dot_general(
            images_near[:, :6].reshape(fs, 6 * width),
            w_ada,
            (((1,), (1,)), ((), ())),
            preferred_element_type=f32,
        )
        cond_parts = [d_conds[0]] + [ring_send(d_conds[k], fs - k) for k in range(1, fs)]
        twice = jnp.stack(cond_parts + cond_parts)
        d_cond_act = lax.dynamic_slice_in_dim(twice, lax.rem(fs - z, fs), fs, 0).reshape(-1)
        grad_condition = d_cond_act[None] * gate * (1.0 + cond_wide * (1.0 - gate))

        def shard_of(rows):
            return pick(rows.reshape(fs, -1), z)

        grads_bias = [
            shard_of(jnp.sum(d_mod_all.astype(f32), axis=0)),
            shard_of(total[:2]),
            shard_of(total[2]),
            shard_of(total[4:]),
            shard_of(total[3]),
        ]
        return (
            output[None],
            grad_tokens[None],
            grad_condition,
            grad_w_ada,
            grad_w_qkv,
            grad_w_out,
            grad_w_up,
            grad_w_down,
            *grads_bias,
        )

    return body


def solution(mesh):
    return jax.shard_map(
        make_body(mesh.shape["dp"], mesh.shape["fsdp"]),
        mesh=mesh,
        in_specs=(
            P(("dp", "fsdp"), None, None),
            P(("dp", "fsdp"), None),
            P(("dp", "fsdp"), None),
            P("fsdp", None),
            P("fsdp", None),
            P("fsdp", None),
            P("fsdp", None),
            P("fsdp", None),
            P("fsdp"),
            P("fsdp"),
            P("fsdp"),
            P("fsdp"),
            P("fsdp"),
            P(("dp", "fsdp"), None, None),
        ),
        out_specs=(
            P(("dp", "fsdp"), None, None),
            P(("dp", "fsdp"), None, None),
            P(("dp", "fsdp"), None),
            P("fsdp", "dp"),
            P("fsdp", "dp"),
            P("fsdp", "dp"),
            P("fsdp", "dp"),
            P("fsdp", "dp"),
            P("fsdp"),
            P("fsdp"),
            P("fsdp"),
            P("fsdp"),
            P("fsdp"),
        ),
        check_vma=False,
    )
```

```python
import math

import jax
import jax.numpy as jnp
from jax import lax
from jax.experimental import pallas as pl
from jax.experimental.pallas import tpu as pltpu
from jax.sharding import PartitionSpec as P

HEAD_DIM = 72
BOX = 8

epsilon = 1e-06
masked_value = -1e30
gelu_root = math.sqrt(2.0 / math.pi)
f32 = jnp.float32
bf16 = jnp.bfloat16


def norm_parts(values_in):
    centred = values_in - jnp.mean(values_in, axis=-1, keepdims=True)
    spread = jnp.mean(centred * centred, axis=-1, keepdims=True)
    rate = lax.rsqrt(spread + epsilon)
    return centred * rate, rate


def norm_back(normal, rate, grad):
    mean_grad = jnp.mean(grad, axis=-1, keepdims=True)
    mean_both = jnp.mean(grad * normal, axis=-1, keepdims=True)
    return rate * (grad - mean_grad - normal * mean_both)


def gelu_tanh(pre_act):
    return (
        0.5
        * pre_act
        * (1.0 + jnp.tanh(gelu_root * (pre_act + 0.044715 * pre_act * pre_act * pre_act)))
    )


def after(value, other):
    return lax.optimization_barrier((value, other))[0]


def gated(values):
    return lax.optimization_barrier(values)


def pick(array, index, axis=0):
    return lax.dynamic_index_in_dim(array, index, axis, keepdims=False)


def make_body(dp, fs):
    groups = dp // BOX

    def box_send(x, bits):
        return lax.ppermute(x, "dp", [(i, i ^ bits) for i in range(dp)])

    def side_send(x):
        return lax.ppermute(x, "dp", [(i, i ^ (4 if i & 1 else 2)) for i in range(dp)])

    def ring_send(x, hops):
        return lax.ppermute(x, "fsdp", [(i, (i + hops) % fs) for i in range(fs)])

    def group_send(x, hops):
        return lax.ppermute(x, "dp", [(i, (i + hops * BOX) % dp) for i in range(dp)])

    def ring_gather(x):
        return [x] + [ring_send(x, k) for k in range(1, fs)]

    def ring_sorted(blocks, z):
        back = jnp.stack(blocks[::-1] + blocks[::-1])
        return lax.dynamic_slice_in_dim(back, fs - 1 - z, fs, 0)

    def chip_near(x):
        return box_send(x, 2), box_send(x, 4)

    def chip_far(near):
        half = near[0].shape[0] // 2
        return box_send(near[0][:half], 4), box_send(near[1][half:], 2)

    def chip_exchange(blocks):
        return [blocks[0]] + [box_send(blocks[k], 2 * k) for k in range(1, BOX // 2)]

    def ring_sum(x, z):
        total = pick(x, z)
        for k in range(1, fs):
            sent = pick(x, lax.rem(z + k, fs)).astype(bf16)
            total = total + ring_send(sent, k).astype(f32)
        return total

    def group_sum(x, group):
        total = pick(x, group)
        for k in range(1, groups):
            total = total + group_send(pick(x, lax.rem(group + k, groups)), k)
        return total

    def cost(microseconds):
        return pl.CostEstimate(
            flops=int(microseconds * 1e8),
            transcendentals=0,
            bytes_accessed=int(microseconds * 3.2e5),
        )

    vmem = pl.BlockSpec(memory_space=pltpu.VMEM)
    smem = pl.BlockSpec(memory_space=pltpu.SMEM)

    def params(mebibytes):
        return pltpu.CompilerParams(vmem_limit_bytes=mebibytes << 20)

    def chunks(rows, step, work):
        def one(i, unused):
            work(pl.ds(pl.multiple_of(i * step, step), step), i * step)
            return unused

        lax.fori_loop(0, rows // step, one, 0)

    def alive_rows(first, rows, live):
        return ((lax.broadcasted_iota(jnp.int32, (rows, 1), 0) + first) < live).astype(f32)

    def modulation_parts(conds, w_ada, bias_ada, extra):
        images = conds.shape[0]
        parts, width = bias_ada.shape

        def kernel(cond_ref, w_ref, bias_ref, extra_ref, *out_refs):
            for part in range(parts):
                cols = slice(part * width, (part + 1) * width)
                product = jnp.dot(cond_ref[...], w_ref[:, cols], preferred_element_type=f32)
                product = product + bias_ref[part : part + 1, :]
                for image, out_ref in enumerate(out_refs):
                    out_ref[part : part + 1, :] = product[image : image + 1, :]
            for out_ref in out_refs:
                out_ref[parts:, :] = extra_ref[...]

        rows = parts + extra.shape[0]
        return pl.pallas_call(
            kernel,
            out_shape=[jax.ShapeDtypeStruct((rows, width), f32)] * images,
            in_specs=[vmem] * 4,
            out_specs=[vmem] * images,
            cost_estimate=cost(4),
            compiler_params=params(60),
        )(conds, w_ada, bias_ada, extra)

    def modulation_rows(partials, live):
        rows, width = partials[0].shape

        def kernel(live_ref, *refs):
            mods_ref, head_ref = refs[-2:]
            total = refs[0][...]
            for ref in refs[1:-2]:
                total = total + ref[...]
            mods_ref[...] = total
            head_ref[...] = jnp.full(head_ref.shape, live_ref[0].astype(f32))
            head_ref[0:2, :] = total[0:2, :]
            head_ref[2:3, :] = total[5:6, :]

        return pl.pallas_call(
            kernel,
            out_shape=[jax.ShapeDtypeStruct((rows, width), f32)] * 2,
            in_specs=[smem] + [vmem] * len(partials),
            out_specs=[vmem] * 2,
            cost_estimate=cost(1),
            compiler_params=params(60),
        )(live, *partials)

    def other_heads(raws, firsts, heads):
        n = len(raws)
        width = raws[0].shape[1] // 2

        def kernel(*refs):
            raw_refs, head_refs = refs[:n], refs[n : 2 * n]
            normed_refs, d_mlp_refs = refs[2 * n : 3 * n], refs[3 * n :]
            for raw, head, normed, d_mlp, first in zip(
                raw_refs, head_refs, normed_refs, d_mlp_refs, firsts
            ):
                live = head[3, 0].astype(jnp.int32)

                def work(rows, start):
                    normal = norm_parts(raw[rows, :width].astype(f32))[0]
                    normed[rows, :] = (
                        normal * (1.0 + head[1:2, :]) + head[0:1, :]
                    ).astype(bf16)
                    count = normal.shape[0]
                    up_rows = alive_rows(start + first, count, live) * raw[
                        rows, width:
                    ].astype(f32)
                    d_mlp[rows, :] = (head[2:3, :] * up_rows).astype(bf16)

                chunks(raw.shape[0], 32, work)

        outs = pl.pallas_call(
            kernel,
            out_shape=[jax.ShapeDtypeStruct((raw.shape[0], width), bf16) for raw in raws] * 2,
            in_specs=[vmem] * (2 * n),
            out_specs=[vmem] * (2 * n),
            cost_estimate=cost(8),
            compiler_params=params(60),
        )(*raws, *heads)
        return outs[:n], outs[n:]

    def piece_plan(pieces):
        arrays = []
        for piece, unused in (each for kind in pieces for each in kind):
            if not any(piece is array for array in arrays):
                arrays.append(piece)
        position = {id(array): i for i, array in enumerate(arrays)}
        plan = [[(position[id(piece)], index) for piece, index in kind] for kind in pieces]
        return arrays, plan

    def piece_copies(where_ref, own_ref, array_refs, plan, whole_ref):
        copies = [(own_ref, whole_ref.at[where_ref[0]])]
        for kind, blocks in enumerate(plan):
            for k, (which, index) in enumerate(blocks):
                source = array_refs[which] if index is None else array_refs[which].at[index]
                copies.append((source, whole_ref.at[where_ref[k + 1], where_ref[fs + kind]]))
        return copies

    def wide_copies(core, where_ref, own_refs, sets, whole_refs):
        widths = [ref.shape[-1] for ref in own_refs]
        width, part = sum(widths), sets[0][0].shape[-1]
        lead, split = whole_refs[0].shape[2], sets[0][6].shape[0]
        copies = [(own, whole.at[where_ref[0]]) for own, whole in zip(own_refs, whole_refs)]
        for side, piece_refs in enumerate(sets):
            low, high = (0, part) if core ^ side == 0 else (part, width)
            offset = 0 if core ^ side == 0 else width - part
            for block in range(1, fs):
                base = (block - 1) * lead
                top = min(max(split - base, 0), lead)
                late = int(block == fs - 1)
                rows = [(2 * i + late, 0 if late else base, i, 0, lead) for i in range(3)]
                if top:
                    rows.append((6, base, 3, 0, top))
                if top < lead:
                    rows.append((7, base + top - split, 3, top, lead - top))
                for piece, first, slot, row, count in rows:
                    start = 0
                    for i, each in enumerate(widths):
                        left, right = max(low, start), min(high, start + each)
                        if left < right:
                            source = piece_refs[piece].at[
                                first : first + count, :, left - offset : right - offset
                            ]
                            target = whole_refs[i].at[
                                where_ref[block],
                                where_ref[fs + 1 + slot],
                                row : row + count,
                                :,
                                left - start : right - start,
                            ]
                            copies.append((source, target))
                        start += each
        return copies

    def copy_all(copies, sems):
        return [
            pltpu.make_async_copy(source, target, sems.at[j])
            for j, (source, target) in enumerate(copies)
        ]

    def start_all(copies):
        for copy in copies:
            copy.start()

    def wait_all(copies):
        for copy in copies:
            copy.wait()

    def in_blocks(shard):
        rows, cols = shard.shape
        return shard.reshape(4, rows // 32, 8, cols)

    any_spec = pl.BlockSpec(memory_space=pl.ANY)

    def projection(where, normed, own, pieces, biases):
        slots, width = normed.shape
        arrays, plan = piece_plan(pieces)
        own = in_blocks(own)
        shape = (fs,) + own.shape

        def kernel(where_ref, normed_ref, bias_ref, own_ref, *refs):
            array_refs = refs[: len(arrays)]
            turned_ref, whole_ref, scratch, sems, out_sem = refs[len(arrays) :]
            copies = copy_all(
                piece_copies(where_ref, own_ref, array_refs, plan, scratch), sems
            )
            start_all(copies)
            wait_all(copies)
            out = pltpu.make_async_copy(scratch, whole_ref, out_sem)
            out.start()
            w_ref = scratch.reshape(width, 3 * width)
            for part in range(3):
                cols = slice(part * width, (part + 1) * width)
                proj = jnp.dot(normed_ref[...], w_ref[:, cols], preferred_element_type=f32)
                if part != 1:
                    proj = proj + bias_ref[part // 2 : part // 2 + 1, :]
                turned_ref[cols, :] = proj.astype(bf16).astype(f32).T
            out.wait()

        turned, whole = pl.pallas_call(
            kernel,
            out_shape=[
                jax.ShapeDtypeStruct((3 * width, slots), f32),
                jax.ShapeDtypeStruct(shape, bf16),
            ],
            in_specs=[smem, vmem, vmem, any_spec] + [any_spec] * len(arrays),
            out_specs=[vmem, any_spec],
            scratch_shapes=[
                pltpu.VMEM(shape, bf16),
                pltpu.SemaphoreType.DMA((1 + 4 * (fs - 1),)),
                pltpu.SemaphoreType.DMA,
            ],
            cost_estimate=cost(11),
            compiler_params=params(60),
        )(where, normed, biases, own, *arrays)
        return turned, whole.reshape(width, 3 * width)

    def attention(turned, live):
        slots = turned.shape[1]
        width = turned.shape[0] // 3
        count = width // HEAD_DIM
        heads_at_once = 1
        scale = HEAD_DIM ** (-0.5)

        def kernel(live_ref, turned_ref, attended_ref, out_turned):
            live_keys = lax.broadcasted_iota(jnp.int32, (1, slots), 1) < live_ref[0]

            def head(h):
                def rows(part):
                    first = pl.multiple_of(part * width + h * HEAD_DIM, 8)
                    return turned_ref[pl.ds(first, HEAD_DIM), :].astype(bf16)

                scores = lax.dot_general(
                    rows(0), rows(1), (((0,), (0,)), ((), ())), preferred_element_type=f32
                )
                scores = jnp.where(live_keys, scores * scale, masked_value)
                highest = jnp.max(scores, axis=-1, keepdims=True)
                total = jnp.sum(jnp.exp(scores - highest), axis=-1, keepdims=True)
                probs = jnp.exp(scores - (highest + jnp.log(total)))
                return lax.dot_general(
                    rows(2),
                    probs.astype(bf16),
                    (((1,), (1,)), ((), ())),
                    preferred_element_type=f32,
                )

            def some_heads(i, unused):
                outs = [head(i * heads_at_once + j) for j in range(heads_at_once)]
                for j, out in enumerate(outs):
                    first = pl.multiple_of((i * heads_at_once + j) * HEAD_DIM, 8)
                    out_turned[pl.ds(first, HEAD_DIM), :] = out
                return unused

            lax.fori_loop(0, count // heads_at_once, some_heads, 0)
            attended_ref[...] = out_turned[...].T.astype(bf16)

        return pl.pallas_call(
            kernel,
            out_shape=jax.ShapeDtypeStruct((slots, width), bf16),
            in_specs=[smem, vmem],
            out_specs=vmem,
            scratch_shapes=[pltpu.VMEM((width, slots), f32)],
            cost_estimate=cost(11),
            compiler_params=params(60),
        )(live, turned)

    def attention_back(turned, d_turned, live, where_chip):
        width, slots = d_turned.shape
        part = 3 * width // 4
        count = width // HEAD_DIM
        heads_at_once = 1
        scale = HEAD_DIM ** (-0.5)

        def kernel(live_ref, chip_ref, turned_ref, d_ref, out_ref, *rest):
            block_refs, total_ref = rest[:-1], rest[-1]
            live_keys = lax.broadcasted_iota(jnp.int32, (1, slots), 1) < live_ref[0]

            def place_of(h, part):
                return pl.ds(pl.multiple_of(part * width + h * HEAD_DIM, 8), HEAD_DIM)

            def head(h):
                def place(part):
                    return place_of(h, part)

                query = turned_ref[place(0), :].astype(bf16)
                key_part = turned_ref[place(1), :].astype(bf16)
                value = turned_ref[place(2), :].astype(bf16)
                d_out = d_ref[place(0), :].astype(bf16)
                both_first = (((0,), (0,)), ((), ()))
                scores = lax.dot_general(
                    query, key_part, both_first, preferred_element_type=f32
                )
                scores = jnp.where(live_keys, scores * scale, masked_value)
                highest = jnp.max(scores, axis=-1, keepdims=True)
                total = jnp.sum(jnp.exp(scores - highest), axis=-1, keepdims=True)
                probs = jnp.exp(scores - (highest + jnp.log(total)))
                d_probs = lax.dot_general(
                    d_out, value, both_first, preferred_element_type=f32
                )
                inner = jnp.sum(probs * d_probs, axis=-1, keepdims=True)
                d_scores = (probs * (d_probs - inner)).astype(bf16)
                d_value = jnp.dot(d_out, probs.astype(bf16), preferred_element_type=f32)
                d_query = scale * lax.dot_general(
                    key_part, d_scores, (((1,), (1,)), ((), ())), preferred_element_type=f32
                )
                d_key = scale * jnp.dot(query, d_scores, preferred_element_type=f32)
                return d_query, d_key, d_value

            def some_heads(i, unused):
                outs = [head(i * heads_at_once + j) for j in range(heads_at_once)]
                for j, parts in enumerate(outs):
                    for part, out in enumerate(parts):
                        total_ref[place_of(i * heads_at_once + j, part), :] = out
                return unused

            lax.fori_loop(0, count // heads_at_once, some_heads, 0)
            out_ref[...] = total_ref[...].astype(bf16)
            for k, block in enumerate(block_refs):
                first = pl.multiple_of(chip_ref[k] * part, 16)
                block[...] = total_ref[pl.ds(first, part), :].astype(bf16)

        n_blocks = 4 if groups == 1 else 0
        return pl.pallas_call(
            kernel,
            out_shape=[jax.ShapeDtypeStruct((3 * width, slots), bf16)]
            + [jax.ShapeDtypeStruct((part, slots), bf16)] * n_blocks,
            in_specs=[smem, smem, vmem, vmem],
            out_specs=[vmem] * (1 + n_blocks),
            scratch_shapes=[pltpu.VMEM((3 * width, slots), f32)],
            cost_estimate=cost(12),
            compiler_params=params(60),
        )(live, where_chip, turned, d_turned)

    def middle_forward(where, attended, tokens_own, owns, sets, bias_out, bias_up, mods):
        slots, width = attended.shape
        owns = [in_blocks(own) for own in owns]
        hidden = owns[1].shape[-1]
        tile = hidden // fs
        quarter = tile // 4
        shapes = [(fs,) + own.shape for own in owns]
        n_pieces = len(sets[0])
        n_copies = 2 + 2 * 15 * (fs - 1)

        def kernel(where_ref, attended_ref, tokens_ref, bias_out_ref, bias_up_ref, mods_ref, *refs):
            own_refs = refs[:2]
            set_refs = (refs[2 : 2 + n_pieces], refs[2 + n_pieces : 2 + 2 * n_pieces])
            (
                attn_ref,
                normed_ref,
                pre_ref,
                act_ref,
                block0,
                block1,
                block2,
                block3,
                whole_out,
                whole_up,
                scratch_out,
                scratch_up,
                turned,
                sems,
                out_sems,
            ) = refs[2 + 2 * n_pieces :]
            step = pl.program_id(0)
            scratches, wholes = (scratch_out, scratch_up), (whole_out, whole_up)

            def outs():
                return [
                    pltpu.make_async_copy(scratch, whole, out_sems.at[i])
                    for i, (scratch, whole) in enumerate(zip(scratches, wholes))
                ]

            @pl.when(step == 0)
            def first():
                for core in range(2):

                    @pl.when(where_ref[fs] == core)
                    def gather(core=core):
                        copies = copy_all(
                            wide_copies(core, where_ref, own_refs, set_refs, scratches), sems
                        )
                        start_all(copies)
                        wait_all(copies)

                start_all(outs())
                attn_ref[...] = (
                    jnp.dot(
                        attended_ref[...],
                        scratch_out.reshape(width, width)[...],
                        preferred_element_type=f32,
                    )
                    + bias_out_ref[...]
                )

                def work(rows, unused):
                    middle = tokens_ref[rows, :].astype(f32) + mods_ref[2:3, :] * attn_ref[rows, :]
                    normal = norm_parts(middle)[0]
                    normed_ref[rows, :] = (
                        normal * (1.0 + mods_ref[4:5, :]) + mods_ref[3:4, :]
                    ).astype(bf16)

                chunks(slots, 32, work)

            cols = pl.ds(pl.multiple_of(step * tile, 128), tile)
            pre_ref[...] = (
                jnp.dot(
                    normed_ref[...],
                    scratch_up.reshape(width, hidden)[:, cols],
                    preferred_element_type=f32,
                )
                + bias_up_ref[0]
            )

            def work(rows, unused):
                act_ref[rows, :] = gelu_tanh(pre_ref[rows, :]).astype(bf16)

            chunks(slots, 32, work)
            turned[...] = act_ref[...].astype(f32).T
            for k, block in enumerate((block0, block1, block2, block3)):
                first = pl.multiple_of(where_ref[fs + 1 + k] * quarter, 16)
                block[...] = turned[pl.ds(first, quarter), :].astype(bf16)

            @pl.when(step == fs - 1)
            def last():
                wait_all(outs())

        def whole(shape):
            return pl.BlockSpec(shape, lambda j, where_ref: (0,) * len(shape))

        *results, whole_out, whole_up = pl.pallas_call(
            kernel,
            out_shape=[
                jax.ShapeDtypeStruct((slots, width), f32),
                jax.ShapeDtypeStruct((slots, width), bf16),
                jax.ShapeDtypeStruct((slots, hidden), f32),
                jax.ShapeDtypeStruct((slots, hidden), bf16),
            ]
            + [jax.ShapeDtypeStruct((fs * quarter, slots), bf16)] * 4
            + [jax.ShapeDtypeStruct(shape, bf16) for shape in shapes],
            grid_spec=pltpu.PrefetchScalarGridSpec(
                num_scalar_prefetch=1,
                grid=(fs,),
                in_specs=[
                    whole((slots, width)),
                    whole((slots, width)),
                    whole((1, width)),
                    pl.BlockSpec((1, 1, tile), lambda j, where_ref: (j, 0, 0)),
                    whole(mods.shape),
                ]
                + [any_spec] * (2 + 2 * n_pieces),
                out_specs=[
                    whole((slots, width)),
                    whole((slots, width)),
                    pl.BlockSpec((slots, tile), lambda j, where_ref: (0, j)),
                    pl.BlockSpec((slots, tile), lambda j, where_ref: (0, j)),
                ]
                + [pl.BlockSpec((quarter, slots), lambda j, where_ref: (j, 0))] * 4
                + [any_spec, any_spec],
                scratch_shapes=[pltpu.VMEM(shape, bf16) for shape in shapes]
                + [
                    pltpu.VMEM((tile, slots), f32),
                    pltpu.SemaphoreType.DMA((n_copies,)),
                    pltpu.SemaphoreType.DMA((2,)),
                ],
            ),
            cost_estimate=cost(20),
            compiler_params=params(60),
        )(
            where,
            attended,
            tokens_own,
            bias_out.reshape(1, width),
            bias_up.reshape(fs, 1, tile),
            mods,
            *owns,
            *sets[0],
            *sets[1],
        )
        return (
            *results,
            whole_out.reshape(width, width),
            whole_up.reshape(width, hidden),
        )

    def hidden_back(where, d_mlp, own, pieces, pre_act):
        slots, width = d_mlp.shape
        hidden = pre_act.shape[1]
        tile = hidden // fs
        if groups == 1:
            turned_shapes = [jax.ShapeDtypeStruct((tile, slots), bf16)] * 4
            turned_specs = [pl.BlockSpec((tile, slots), lambda j, where_ref: (0, 0))] * 4
        else:
            turned_shapes = [jax.ShapeDtypeStruct((hidden, slots), bf16)]
            turned_specs = [pl.BlockSpec((tile, slots), lambda j, where_ref: (j, 0))]
        arrays, plan = piece_plan(pieces)
        own = in_blocks(own)
        shape = (fs,) + own.shape

        def kernel(where_ref, d_mlp_ref, pre_ref, own_ref, *refs):
            array_refs = refs[: len(arrays)]
            d_pre_ref, *turned_refs, sum_ref, whole_ref = refs[len(arrays) : -4]
            d_act_ref, scratch, sems, out_sem = refs[-4:]
            step = pl.program_id(0)

            def out():
                return pltpu.make_async_copy(scratch, whole_ref, out_sem)

            @pl.when(step == 0)
            def first():
                copies = copy_all(
                    piece_copies(where_ref, own_ref, array_refs, plan, scratch), sems
                )
                start_all(copies)
                wait_all(copies)
                out().start()

            d_act_ref[...] = lax.dot_general(
                d_mlp_ref[...],
                scratch.at[step].reshape(tile, width)[...],
                (((1,), (1,)), ((), ())),
                preferred_element_type=f32,
            )

            def work(rows, unused):
                pre = pre_ref[rows, :]
                square = pre * pre
                bend = jnp.tanh(gelu_root * (pre + 0.044715 * square * pre))
                slope = 0.5 * (1.0 + bend) + 0.5 * pre * (1.0 - bend * bend) * gelu_root * (
                    1.0 + 3.0 * 0.044715 * square
                )
                d_pre = (d_act_ref[rows, :] * slope).astype(bf16)
                d_pre_ref[rows, :] = d_pre
                d_act_ref[rows, :] = d_pre.astype(f32)

            chunks(slots, 32, work)
            sum_ref[0] = jnp.sum(d_act_ref[...], axis=0, keepdims=True)
            if groups == 1:
                for k, turned_ref in enumerate(turned_refs):

                    @pl.when(step == where_ref[fs + 4 + k])
                    def block(turned_ref=turned_ref):
                        turned_ref[...] = d_act_ref[...].T.astype(bf16)
            else:
                turned_refs[0][...] = d_act_ref[...].T.astype(bf16)

            @pl.when(step == fs - 1)
            def last():
                out().wait()

        *results, whole = pl.pallas_call(
            kernel,
            out_shape=[
                jax.ShapeDtypeStruct((slots, hidden), bf16),
                *turned_shapes,
                jax.ShapeDtypeStruct((fs, 1, tile), f32),
                jax.ShapeDtypeStruct(shape, bf16),
            ],
            grid_spec=pltpu.PrefetchScalarGridSpec(
                num_scalar_prefetch=1,
                grid=(fs,),
                in_specs=[
                    pl.BlockSpec((slots, width), lambda j, where_ref: (0, 0)),
                    pl.BlockSpec((slots, tile), lambda j, where_ref: (0, j)),
                    any_spec,
                ]
                + [any_spec] * len(arrays),
                out_specs=[
                    pl.BlockSpec((slots, tile), lambda j, where_ref: (0, j)),
                    *turned_specs,
                    pl.BlockSpec((1, 1, tile), lambda j, where_ref: (j, 0, 0)),
                    any_spec,
                ],
                scratch_shapes=[
                    pltpu.VMEM((slots, tile), f32),
                    pltpu.VMEM(shape, bf16),
                    pltpu.SemaphoreType.DMA((1 + 4 * (fs - 1),)),
                    pltpu.SemaphoreType.DMA,
                ],
            ),
            cost_estimate=cost(15),
            compiler_params=params(60),
        )(where, d_mlp, pre_act, own, *arrays)
        return (*results, whole.reshape(hidden, width))

    def middle_back(d_pre, up_full, out_full, attn_out, tokens_own, cotangent_own, mods, live):
        slots, hidden = d_pre.shape
        width = attn_out.shape[1]
        tile = hidden // fs

        def kernel(
            live_ref,
            d_pre_ref,
            up_ref,
            out_ref,
            attn_ref,
            tokens_ref,
            cot_ref,
            mods_ref,
            d_middle_ref,
            d_attn_turned_ref,
            d_attended_turned_ref,
            sums_ref,
            total,
            d_attn_ref,
        ):
            step = pl.program_id(0)
            part = lax.dot_general(
                d_pre_ref[...],
                up_ref[...],
                (((1,), (1,)), ((), ())),
                preferred_element_type=f32,
            )

            @pl.when(step == 0)
            def start():
                total[...] = part

            @pl.when(step > 0)
            def add():
                total[...] += part

            @pl.when(step == fs - 1)
            def finish():
                sums_ref[...] = jnp.zeros_like(sums_ref)

                def work(rows, first):
                    grad = total[rows, :]
                    attn = attn_ref[rows, :]
                    middle = tokens_ref[rows, :].astype(f32) + mods_ref[2:3, :] * attn
                    normal, rate = norm_parts(middle)
                    alive = alive_rows(first, grad.shape[0], live_ref[0])
                    d_middle = alive * cot_ref[rows, :].astype(f32) + norm_back(
                        normal, rate, grad * (1.0 + mods_ref[4:5, :])
                    )
                    d_middle_ref[rows, :] = d_middle
                    d_attn = (mods_ref[2:3, :] * d_middle).astype(bf16)
                    d_attn_ref[rows, :] = d_attn
                    for i, each in enumerate(
                        (d_middle * attn, grad, grad * normal, d_attn.astype(f32))
                    ):
                        sums_ref[i : i + 1, :] += jnp.sum(each, axis=0, keepdims=True)

                chunks(slots, 32, work)
                d_attn_turned_ref[...] = d_attn_ref[...].astype(f32).T.astype(bf16)
                d_attended = lax.dot_general(
                    d_attn_ref[...],
                    out_ref[...],
                    (((1,), (1,)), ((), ())),
                    preferred_element_type=f32,
                )
                d_attended_turned_ref[...] = d_attended.astype(bf16).astype(f32).T

        def whole(shape):
            return pl.BlockSpec(shape, lambda j, live_ref: (0,) * len(shape))

        return pl.pallas_call(
            kernel,
            out_shape=[
                jax.ShapeDtypeStruct((slots, width), f32),
                jax.ShapeDtypeStruct((width, slots), bf16),
                jax.ShapeDtypeStruct((width, slots), f32),
                jax.ShapeDtypeStruct((8, width), f32),
            ],
            grid_spec=pltpu.PrefetchScalarGridSpec(
                num_scalar_prefetch=1,
                grid=(fs,),
                in_specs=[
                    pl.BlockSpec((slots, tile), lambda j, live_ref: (0, j)),
                    pl.BlockSpec((width, tile), lambda j, live_ref: (0, j)),
                    whole((width, width)),
                    whole((slots, width)),
                    whole((slots, width)),
                    whole((slots, width)),
                    whole(mods.shape),
                ],
                out_specs=[
                    whole((slots, width)),
                    whole((width, slots)),
                    whole((width, slots)),
                    whole((8, width)),
                ],
                scratch_shapes=[
                    pltpu.VMEM((slots, width), f32),
                    pltpu.VMEM((slots, width), bf16),
                ],
            ),
            cost_estimate=cost(12),
            compiler_params=params(60),
        )(live, d_pre, up_full, out_full, attn_out, tokens_own, cotangent_own, mods)

    def first_back(d_turned, qkv_full, tokens_own, d_middle, mods):
        slots, width = d_middle.shape

        def kernel(d_ref, w_ref, tokens_ref, d_middle_ref, mods_ref, grad_ref, sums_ref, total):
            sums_ref[...] = jnp.zeros_like(sums_ref)
            for part in range(3):
                cols = slice(part * width, (part + 1) * width)
                d_part = d_ref[cols, :].astype(f32).T
                if part != 1:
                    row = 2 + part // 2
                    sums_ref[row : row + 1, :] = jnp.sum(d_part, axis=0, keepdims=True)
                product = lax.dot_general(
                    d_part.astype(bf16),
                    w_ref[:, cols],
                    (((1,), (1,)), ((), ())),
                    preferred_element_type=f32,
                )
                if part == 0:
                    total[...] = product
                else:
                    total[...] += product

            def work(rows, unused):
                grad = total[rows, :]
                normal, rate = norm_parts(tokens_ref[rows, :].astype(f32))
                sums_ref[0:1, :] += jnp.sum(grad, axis=0, keepdims=True)
                sums_ref[1:2, :] += jnp.sum(grad * normal, axis=0, keepdims=True)
                grad_ref[rows, :] = (
                    d_middle_ref[rows, :]
                    + norm_back(normal, rate, grad * (1.0 + mods_ref[1:2, :]))
                ).astype(bf16)

            chunks(slots, 32, work)

        return pl.pallas_call(
            kernel,
            out_shape=[
                jax.ShapeDtypeStruct((slots, width), bf16),
                jax.ShapeDtypeStruct((8, width), f32),
            ],
            in_specs=[vmem] * 5,
            out_specs=[vmem] * 2,
            scratch_shapes=[pltpu.VMEM((slots, width), f32)],
            cost_estimate=cost(9),
            compiler_params=params(60),
        )(d_turned, qkv_full, tokens_own, d_middle, mods)

    def output_rows(
        activated, down_full, bias_down, tokens_own, attn_out, cotangent_own, d_mlp, mods, live
    ):
        slots, hidden = activated.shape
        width = attn_out.shape[1]
        tile = hidden // fs

        def kernel(
            live_ref,
            act_ref,
            down_ref,
            bias_ref,
            tokens_ref,
            attn_ref,
            cot_ref,
            d_mlp_ref,
            mods_ref,
            out_ref,
            sums_ref,
            total,
        ):
            step = pl.program_id(0)
            part = jnp.dot(act_ref[...], down_ref[...], preferred_element_type=f32)

            @pl.when(step == 0)
            def start():
                total[...] = part

            @pl.when(step > 0)
            def add():
                total[...] += part

            @pl.when(step == fs - 1)
            def finish():
                sums_ref[...] = jnp.zeros_like(sums_ref)

                def work(rows, first):
                    mlp_out = total[rows, :] + bias_ref[...]
                    middle = (
                        tokens_ref[rows, :].astype(f32) + mods_ref[2:3, :] * attn_ref[rows, :]
                    )
                    alive = alive_rows(first, mlp_out.shape[0], live_ref[0])
                    out_ref[rows, :] = (alive * (middle + mods_ref[5:6, :] * mlp_out)).astype(bf16)
                    d_gate = alive * cot_ref[rows, :].astype(f32) * mlp_out
                    sums_ref[0:1, :] += jnp.sum(d_gate, axis=0, keepdims=True)
                    sums_ref[1:2, :] += jnp.sum(
                        d_mlp_ref[rows, :].astype(f32), axis=0, keepdims=True
                    )

                chunks(slots, 32, work)

        def whole(shape):
            return pl.BlockSpec(shape, lambda j, live_ref: (0,) * len(shape))

        return pl.pallas_call(
            kernel,
            out_shape=[
                jax.ShapeDtypeStruct((slots, width), bf16),
                jax.ShapeDtypeStruct((8, width), f32),
            ],
            grid_spec=pltpu.PrefetchScalarGridSpec(
                num_scalar_prefetch=1,
                grid=(fs,),
                in_specs=[
                    pl.BlockSpec((slots, tile), lambda j, live_ref: (0, j)),
                    pl.BlockSpec((tile, width), lambda j, live_ref: (j, 0)),
                    whole((1, width)),
                    whole((slots, width)),
                    whole((slots, width)),
                    whole((slots, width)),
                    whole((slots, width)),
                    whole(mods.shape),
                ],
                out_specs=[whole((slots, width)), whole((8, width))],
                scratch_shapes=[pltpu.VMEM((slots, width), f32)],
            ),
            cost_estimate=cost(6),
            compiler_params=params(60),
        )(
            live,
            activated,
            down_full,
            bias_down.reshape(1, width),
            tokens_own,
            attn_out,
            cotangent_own,
            d_mlp,
            mods,
        )

    def column_grad(where, items, rights):
        slots = rights[0].shape[1]
        width = items[0][0][0].shape[1]
        tile = width // 3
        half = slots // 2
        counts = [(stop - start) // 2 for unused, start, stop in items]
        n_out = sum(counts)
        lefts = [left for box, unused, unused_stop in items for left in box]

        def kernel(where_ref, *refs):
            core = where_ref[0]
            y0, y1, y2, y3, keep_ref, send_ref = refs[len(lefts) :]
            for i, (unused, start, unused_stop) in enumerate(items):
                x0, x1, x2, x3, x4 = refs[5 * i : 5 * i + 5]
                n = counts[i]
                below = sum(counts[:i])
                for out_ref, first in ((keep_ref, core * n), (send_ref, (1 - core) * n)):
                    rows = pl.ds(pl.multiple_of(start + first, 16), n)
                    total = None
                    for x, y, cols in (
                        (x0, y0, slice(None)),
                        (x1, y1, slice(None)),
                        (x2, y2, slice(None)),
                        (x3, y3, slice(0, half)),
                        (x4, y3, slice(half, slots)),
                    ):
                        part = jnp.dot(y[rows, cols], x[...], preferred_element_type=f32)
                        total = part if total is None else total + part
                    out_ref[below : below + n, :] = total

        left_specs = [
            pl.BlockSpec((left.shape[0], tile), lambda i, where_ref: (0, i)) for left in lefts
        ]
        right_spec = pl.BlockSpec(rights[0].shape, lambda i, where_ref: (0, 0))
        out_spec = pl.BlockSpec((n_out, tile), lambda i, where_ref: (0, i))
        return pl.pallas_call(
            kernel,
            out_shape=[jax.ShapeDtypeStruct((n_out, width), f32)] * 2,
            grid_spec=pltpu.PrefetchScalarGridSpec(
                num_scalar_prefetch=1,
                grid=(width // tile,),
                in_specs=left_specs + [right_spec] * 4,
                out_specs=[out_spec] * 2,
            ),
            cost_estimate=cost(8),
            compiler_params=params(60),
        )(where, *lefts, *rights)

    def sums_message(first_sums, middle_sums, output_sums, d_pre_sums, cond_act):
        width = cond_act.shape[1]
        extra = d_pre_sums.shape[0]

        def kernel(first_ref, middle_ref, output_ref, d_pre_ref, cond_ref, out_ref):
            out_ref[0:2, :] = first_ref[0:2, :].astype(bf16).astype(f32)
            out_ref[2:5, :] = middle_ref[0:3, :].astype(bf16).astype(f32)
            out_ref[5:6, :] = output_ref[0:1, :].astype(bf16).astype(f32)
            for row in (6, 7):
                out_ref[row : row + 1, :] = cond_ref[...].astype(f32)
            out_ref[8:10, :] = first_ref[2:4, :]
            out_ref[10:11, :] = middle_ref[3:4, :]
            out_ref[11:12, :] = output_ref[1:2, :]
            out_ref[12:, :] = d_pre_ref[...]

        return pl.pallas_call(
            kernel,
            out_shape=jax.ShapeDtypeStruct((12 + extra, width), f32),
            in_specs=[vmem] * 5,
            out_specs=vmem,
            cost_estimate=cost(1),
            compiler_params=params(60),
        )(first_sums, middle_sums, output_sums, d_pre_sums, cond_act)

    def column_total(items):
        width = items[0][0].shape[1]
        n = sum(item[0].shape[0] for item in items)
        padded = -(-n // 128) * 128
        half = width // fs // 2
        arrays = [array for item in items for array in item]

        def kernel(*refs):
            out_ref, turned = refs[-2:]
            for first in range(0, width, 128):
                totals, used = [], 0
                for item in items:
                    parts = [ref[:, first : first + 128] for ref in refs[used : used + len(item)]]
                    totals.append(sum((part.astype(f32) for part in parts[1:]), parts[0]))
                    used += len(item)
                if padded > n:
                    totals.append(jnp.zeros((padded - n, 128), f32))
                total = jnp.concatenate(totals, axis=0) if len(totals) > 1 else totals[0]
                turned[first : first + 128, :] = total.T[:, :n]
            for block in range(fs):
                rows = slice(block * half, (block + 1) * half)
                upper = 2 * block * half
                out_ref[rows, :n] = turned[upper : upper + half, :].astype(bf16)
                out_ref[rows, n:] = turned[upper + half : upper + 2 * half, :].astype(bf16)

        return pl.pallas_call(
            kernel,
            out_shape=jax.ShapeDtypeStruct((fs * half, 2 * n), bf16),
            in_specs=[vmem] * len(arrays),
            out_specs=vmem,
            scratch_shapes=[pltpu.VMEM((width, n), f32)],
            cost_estimate=cost(5),
            compiler_params=params(60),
        )(*arrays)

    def unfolded(x, start, stop):
        n = x.shape[1] // 2
        return jnp.concatenate([x[:, start:stop], x[:, n + start : n + stop]]).astype(f32)

    def row_total(keep, got):
        def kernel(keep_ref, got_ref, out_ref):
            out_ref[...] = (keep_ref[...] + got_ref[...]).astype(bf16)

        total = pl.pallas_call(
            kernel,
            out_shape=jax.ShapeDtypeStruct(keep.shape, bf16),
            in_specs=[vmem] * 2,
            out_specs=vmem,
            cost_estimate=cost(3),
            compiler_params=params(60),
        )(keep, got)
        return total.reshape(-1, keep.shape[2])

    def fsdp_sum(x):
        return lax.psum_scatter(x, "fsdp", scatter_dimension=0, tiled=True)

    def out_grad(where, d_attn_turned, attended):
        width, slots = d_attn_turned.shape
        n = width // BOX

        def kernel(where_ref, d_ref, x_ref, keep_ref, send_ref):
            step = pl.program_id(0)
            core = where_ref[0]
            for out_ref, which in ((keep_ref, core), (send_ref, 1 - core)):
                first = (where_ref[step + 1] * 2 + which) * n
                rows = pl.ds(pl.multiple_of(first, 16), n)
                out_ref[0] = jnp.dot(d_ref[rows, :], x_ref[...], preferred_element_type=f32)

        out_spec = pl.BlockSpec((1, n, width), lambda i, where_ref: (i, 0, 0))
        return pl.pallas_call(
            kernel,
            out_shape=[jax.ShapeDtypeStruct((BOX // 2, n, width), f32)] * 2,
            grid_spec=pltpu.PrefetchScalarGridSpec(
                num_scalar_prefetch=1,
                grid=(BOX // 2,),
                in_specs=[
                    pl.BlockSpec((width, slots), lambda i, where_ref: (0, 0)),
                    pl.BlockSpec((slots, width), lambda i, where_ref: (0, 0)),
                ],
                out_specs=[out_spec] * 2,
            ),
            cost_estimate=cost(5),
            compiler_params=params(60),
        )(where, d_attn_turned, attended)

    def chip_split(keep, got):
        count, rows, width = keep.shape

        def kernel(keep_ref, got_ref, *outs):
            for k, out_ref in enumerate(outs):
                out_ref[...] = (keep_ref[k] + got_ref[k]).astype(out_ref.dtype)

        return pl.pallas_call(
            kernel,
            out_shape=[jax.ShapeDtypeStruct((rows, width), f32)]
            + [jax.ShapeDtypeStruct((rows, width), bf16)] * (count - 1),
            in_specs=[vmem] * 2,
            out_specs=[vmem] * count,
            cost_estimate=cost(3),
            compiler_params=params(60),
        )(keep, got)

    def row_grad(where, lefts, rights):
        rows = lefts[0].shape[0] // fs
        slots, n = lefts[0].shape[1], rows // 2
        width = rights[0].shape[1]
        half = slots // 2

        def kernel(where_ref, x0, x1, x2, x3, y0, y1, y2, y3, y4, keep_ref, send_ref):
            core = where_ref[0]
            for out_ref, first in ((keep_ref, core * n), (send_ref, (1 - core) * n)):
                lines = pl.ds(pl.multiple_of(first, 16), n)
                total = None
                for x, y, cols in (
                    (x0, y0, slice(None)),
                    (x1, y1, slice(None)),
                    (x2, y2, slice(None)),
                    (x3, y3, slice(0, half)),
                    (x3, y4, slice(half, slots)),
                ):
                    part = jnp.dot(x[lines, cols], y[...], preferred_element_type=f32)
                    total = part if total is None else total + part
                out_ref[0] = total

        left_spec = pl.BlockSpec((rows, slots), lambda i, where_ref: (i, 0))
        right_specs = [
            pl.BlockSpec((right.shape[0], width), lambda i, where_ref: (0, 0))
            for right in rights
        ]
        out_spec = pl.BlockSpec((1, n, width), lambda i, where_ref: (i, 0, 0))
        return pl.pallas_call(
            kernel,
            out_shape=[jax.ShapeDtypeStruct((fs, n, width), f32)] * 2,
            grid_spec=pltpu.PrefetchScalarGridSpec(
                num_scalar_prefetch=1,
                grid=(fs,),
                in_specs=[left_spec] * 4 + right_specs,
                out_specs=[out_spec] * 2,
            ),
            cost_estimate=cost(6),
            compiler_params=params(60),
        )(where, *lefts, *rights)

    def body(
        tokens,
        condition,
        grid_sizes,
        w_ada,
        w_qkv,
        w_out,
        w_up,
        w_down,
        b_ada,
        b_qv,
        b_out,
        b_up,
        b_down,
        cotangent,
    ):
        slots, width = tokens.shape[1:]
        heads = width // HEAD_DIM
        hidden = w_up.shape[1]
        rank = lax.axis_index("dp")
        z = lax.axis_index("fsdp")
        place = lax.rem(rank, BOX)
        group = lax.div(rank, BOX)
        core = place & 1
        chip = place >> 1
        side = (chip ^ (chip >> 1)) & 1
        near = 2 * side + core
        far = 2 * (1 - side) + core
        where = jnp.stack(
            [lax.rem(z - k + fs, fs) for k in range(fs)]
            + [near, far, near ^ 1, far ^ 1]
            + [chip ^ k for k in range(4)]
        ).astype(jnp.int32)
        where_core = core.reshape(1).astype(jnp.int32)
        where_wide = jnp.stack(
            [lax.rem(z - k + fs, fs) for k in range(fs)] + [core] + [chip ^ k for k in range(4)]
        ).astype(jnp.int32)

        cond_wide = condition.astype(f32)
        gate = jax.nn.sigmoid(cond_wide)
        cond_act = (cond_wide * gate).astype(bf16)

        def quarter_of(shard):
            return pick(in_blocks(shard), near)

        qkv_quarter = quarter_of(w_qkv)
        cond_rows = ring_gather(after(cond_act, qkv_quarter))
        raw = jnp.concatenate([tokens[0], cotangent[0]], axis=1)
        qkv_helds = [ring_send(qkv_quarter, 1)]
        mid_rows = jnp.concatenate(
            [pick(in_blocks(w_out), chip), pick(in_blocks(w_up), chip)], axis=-1
        )
        mid_width = mid_rows.shape[-1]
        mid_part = -(-mid_width // 256) * 128
        mid_start = jnp.where(core == 0, 0, mid_width - mid_part)
        mid_eighth = lax.dynamic_slice_in_dim(mid_rows, mid_start, mid_part, 2)
        down_quarter = quarter_of(w_down)
        ada_shard = b_ada.shape[0]
        bias_ada = lax.dynamic_update_slice_in_dim(
            jnp.zeros((fs * ada_shard,), f32), b_ada.astype(f32), z * ada_shard, 0
        ).reshape(6, width)
        small = jnp.concatenate([b_qv, b_out, b_down, b_up]).astype(f32).reshape(-1, width)
        cond_rows, qkv_helds, bias_ada, small, mid_eighth, down_quarter = gated(
            (cond_rows, qkv_helds, bias_ada, small, mid_eighth, down_quarter)
        )

        rows_z = width // fs
        conds = jnp.concatenate(cond_rows)
        conds_z = lax.dynamic_slice_in_dim(conds, z * rows_z, rows_z, 1)
        partials = modulation_parts(conds_z, w_ada, bias_ada, small)
        partials = [partials[0]] + [ring_send(partials[k], fs - k) for k in range(1, fs)]
        raw_near = chip_near(after(raw, conds_z))
        qkv_helds.append(ring_send(qkv_helds[-1], 1))
        partials, qkv_helds = gated((partials, qkv_helds))

        live = (grid_sizes[0, 0] * grid_sizes[0, 1]).reshape(1)
        mods, head = modulation_rows(partials, live)
        (normed,), (d_mlp,) = other_heads((raw,), (0,), (head,))
        qkv_helds.append(ring_send(qkv_helds[-1], 1))
        mods, head, normed, d_mlp, raw_near, qkv_helds = gated(
            (mods, head, normed, d_mlp, raw_near, qkv_helds)
        )

        qkv_mine = jnp.stack(qkv_helds)
        qkv_other = side_send(qkv_mine)
        qkv_mine_got = box_send(qkv_mine, 1)
        mid_helds = [ring_send(after(mid_eighth, qkv_mine), 1)]
        heads_got = [box_send(after(head, qkv_mine), bits) for bits in (2, 4)]
        bias_rows = [each[6:].reshape(-1) for each in partials]
        bias_rows = jnp.stack(bias_rows + bias_rows)
        biases = lax.dynamic_slice_in_dim(bias_rows, lax.rem(fs - z, fs), fs, 0)
        ends = [0]
        for bias in (b_qv, b_out, b_down, b_up):
            ends.append(ends[-1] + bias.shape[0])
        biases = [biases[:, ends[i] : ends[i + 1]].reshape(-1) for i in range(4)]
        qkv_mine, qkv_other, qkv_mine_got, mid_helds, biases, heads_got = gated(
            (qkv_mine, qkv_other, qkv_mine_got, mid_helds, biases, heads_got)
        )
        bias_qv, bias_out, bias_down, bias_up = biases

        last = fs - 1

        def in_order(array):
            return [(array, k) for k in range(last)]

        qkv_other_got = box_send(qkv_other, 1)
        heads_got.append(box_send(after(head, qkv_other), 6))
        raw_far = chip_far([after(each, qkv_other) for each in raw_near])
        mid_helds.append(ring_send(mid_helds[-1], 1))
        turned, qkv_full = projection(
            where,
            normed,
            w_qkv,
            [in_order(each) for each in (qkv_mine, qkv_other, qkv_mine_got, qkv_other_got)],
            bias_qv.reshape(2, width),
        )
        turned, qkv_full, mid_helds, raw_far, heads_got = gated(
            (turned, qkv_full, mid_helds, raw_far, heads_got)
        )

        mid_first = jnp.concatenate(mid_helds)
        first_near = chip_near(mid_first)
        mid_last = ring_send(mid_helds[-1], 1)
        down_helds = [ring_send(after(down_quarter, mid_first), 1)]
        attended = attention(turned, live)
        attended, mid_first, first_near, mid_last = gated(
            (attended, mid_first, first_near, mid_last)
        )

        last_near = chip_near(mid_last)
        first_got = [box_send(mid_first, 1)]
        normed_box, d_mlp_box = other_heads(
            (*raw_near, *raw_far), (0, 0, 0, slots // 2), (*heads_got, heads_got[2])
        )
        normed_box, d_mlp_box = [normed, *normed_box], [d_mlp, *d_mlp_box]
        first_near, last_near, first_got, down_helds, normed_box, d_mlp_box = gated(
            (first_near, last_near, first_got, down_helds, normed_box, d_mlp_box)
        )

        split = (mid_first.shape[0] + mid_last.shape[0]) // 2
        mid_far = (
            box_send(first_near[0][:split], 4),
            box_send(jnp.concatenate([first_near[1][split:], last_near[1]]), 2),
        )
        first_got += [box_send(each, 1) for each in first_near]
        down_helds.append(ring_send(down_helds[-1], 1))
        attended, mid_far, first_got, down_helds = gated(
            (attended, mid_far, first_got, down_helds)
        )

        last_got = [box_send(each, 1) for each in (mid_last, *last_near)]
        far_got = [box_send(each, 1) for each in mid_far]
        down_helds.append(ring_send(down_helds[-1], 1))
        down_others = [side_send(each) for each in down_helds[:-1]]

        def paired(first, last_ones, far):
            pairs = [each for pair in zip(first, last_ones) for each in pair]
            return [*pairs, *far]

        attn_out, normed_two, pre_act, activated, *act_blocks, out_full, up_full = middle_forward(
            where_wide,
            attended,
            tokens[0],
            [w_out, w_up],
            (
                paired((mid_first, *first_near), (mid_last, *last_near), mid_far),
                paired(first_got, last_got, far_got),
            ),
            bias_out,
            bias_up,
            mods,
        )
        down_helds, down_others, act_blocks, normed_two = gated(
            (down_helds, down_others, act_blocks, normed_two)
        )

        down_others.append(side_send(down_helds[-1]))
        down_got = [[box_send(each, 1) for each in kind] for kind in (down_helds, down_others)]
        act_blocks, down_others, down_got = gated((act_blocks, down_others, down_got))

        act_box = chip_exchange(act_blocks)
        d_pre, *d_pre_turned, d_pre_sums, down_full = hidden_back(
            where,
            d_mlp,
            w_down,
            [[(each, None) for each in kind] for kind in (down_helds, down_others, *down_got)],
            pre_act,
        )

        def column_blocks(grad_t):
            n = grad_t.shape[0] // dp
            blocks = grad_t.reshape(groups, BOX, n, slots).transpose(1, 0, 2, 3)
            blocks = blocks.reshape(BOX // 2, 2 * groups * n, slots)
            return [pick(blocks, chip ^ k) for k in range(BOX // 2)]

        d_pre_blocks = d_pre_turned if groups == 1 else column_blocks(d_pre_turned[0])
        output, output_sums = output_rows(
            activated,
            down_full,
            bias_down,
            tokens[0],
            attn_out,
            cotangent[0],
            d_mlp,
            mods,
            live,
        )
        d_pre, d_pre_blocks, act_box, normed_two, output_sums = gated(
            (d_pre, d_pre_blocks, act_box, normed_two, output_sums)
        )

        d_pre_box = chip_exchange(d_pre_blocks)
        keep_down, send_down = row_grad(where_core, act_box, d_mlp_box)
        d_middle, d_attn_turned, d_attended_turned, middle_sums = middle_back(
            d_pre, up_full, out_full, attn_out, tokens[0], cotangent[0], mods, live
        )
        d_attended_turned, d_attn_turned, d_pre_box, keep_down, send_down, normed_two = gated(
            (d_attended_turned, d_attn_turned, d_pre_box, keep_down, send_down, normed_two)
        )

        normed_two_near = chip_near(normed_two)
        total_down = row_total(keep_down, box_send(send_down, 1))
        grad_down = fsdp_sum(total_down)
        d_projected, *last_blocks = attention_back(
            turned, after(d_attended_turned, total_down), live, where[fs + 4 :]
        )
        if groups > 1:
            last_blocks = column_blocks(d_projected)
            d_attn_turned = d_attn_turned.reshape(groups, BOX, -1, slots)
            d_attn_turned = d_attn_turned.transpose(1, 0, 2, 3).reshape(width, slots)
        keep_out, send_out = out_grad(
            jnp.concatenate([where_core, where[fs + 4 :]]), d_attn_turned, attended
        )
        got_out = box_send(send_out, 1)
        normed_two_far = chip_far([after(each, d_projected) for each in normed_two_near])
        normed_two_box = [normed_two, *normed_two_near, *normed_two_far]
        d_projected, last_blocks, normed_two_box, grad_down, keep_out, got_out = gated(
            (d_projected, last_blocks, normed_two_box, grad_down, keep_out, got_out)
        )

        def over_groups(grad):
            rows, cols = grad.shape
            return group_sum(grad.reshape(rows, groups, -1).transpose(1, 0, 2), group)

        last_box = chip_exchange(last_blocks)
        grad_tokens, first_sums = first_back(d_projected, qkv_full, tokens[0], d_middle, mods)
        out_blocks = chip_split(keep_out, got_out)
        keep_up, send_up = column_grad(
            where_core, [(normed_two_box, 0, d_pre_box[0].shape[0])], d_pre_box
        )
        total_up = column_total([(keep_up, box_send(send_up, 1))])
        last_box, first_sums, total_up, out_blocks = gated(
            (last_box, first_sums, total_up, out_blocks)
        )

        grad_up = fsdp_sum(total_up)
        keep_qkv, send_qkv = column_grad(
            where_core, [(normed_box, 0, last_box[0].shape[0])], last_box
        )
        message = sums_message(
            first_sums, middle_sums, output_sums, d_pre_sums.reshape(-1, width), cond_act
        )
        out_parts = chip_exchange(out_blocks)
        messages = ring_gather(message)
        total_last = column_total([(keep_qkv, box_send(send_qkv, 1)), tuple(out_parts)])
        grad_down = after(grad_down, keep_qkv)
        if groups > 1:
            grad_down = over_groups(grad_down.astype(f32))
        down_rows = grad_down.shape[0]
        down_cols = grad_down.reshape(down_rows, BOX, -1).transpose(1, 0, 2)
        if groups == 1:
            parts = lax.all_to_all(down_cols, "dp", 0, 0, tiled=True)
        else:
            parts = [pick(down_cols, place)] + [
                box_send(pick(down_cols, place ^ k), k) for k in range(1, BOX)
            ]
            parts = jnp.stack(parts)
            parts = jnp.stack([pick(parts, place ^ k) for k in range(BOX)])
        total_last, messages, grad_up, parts = gated((total_last, messages, grad_up, parts))

        grad_last = fsdp_sum(total_last)
        images_near = jnp.stack([each[:8] for each in messages]).astype(bf16)
        totals = [each[8:] for each in messages]
        images, total = images_near, sum(totals[1:], totals[0])
        for bits in (1, 2, 4):
            images = jnp.concatenate([images, box_send(images, bits)])
            total = total + box_send(total, bits)
        images_box, total_box = images, total
        for k in range(1, groups):
            images = jnp.concatenate([images, group_send(images_box, k)])
            total = total + group_send(total_box, k)
        grad_w_down = parts.reshape(BOX * down_rows, width // dp).astype(f32)
        grad_w_up = over_groups(unfolded(grad_up, 0, keep_up.shape[0]))
        cut_cols, last_cols = keep_qkv.shape[0], keep_qkv.shape[0] + keep_out.shape[1]
        grad_w_qkv = over_groups(unfolded(grad_last, 0, cut_cols))
        grad_w_out = over_groups(unfolded(grad_last, cut_cols, last_cols))
        conds_all = lax.dynamic_slice_in_dim(images[:, 6], z * rows_z, rows_z, 1)
        d_mod_all = images[:, :6]
        ada_cols = 6 * width // dp
        grad_w_ada = lax.dot_general(
            conds_all,
            lax.dynamic_slice_in_dim(
                d_mod_all.reshape(dp * fs, 6 * width), rank * ada_cols, ada_cols, 1
            ),
            (((0,), (0,)), ((), ())),
            preferred_element_type=f32,
        )
        d_conds = lax.dot_general(
            images_near[:, :6].reshape(fs, 6 * width),
            w_ada,
            (((1,), (1,)), ((), ())),
            preferred_element_type=f32,
        )
        cond_parts = [d_conds[0]] + [ring_send(d_conds[k], fs - k) for k in range(1, fs)]
        twice = jnp.stack(cond_parts + cond_parts)
        d_cond_act = lax.dynamic_slice_in_dim(twice, lax.rem(fs - z, fs), fs, 0).reshape(-1)
        grad_condition = d_cond_act[None] * gate * (1.0 + cond_wide * (1.0 - gate))

        def shard_of(rows):
            return pick(rows.reshape(fs, -1), z)

        grads_bias = [
            shard_of(jnp.sum(d_mod_all.astype(f32), axis=0)),
            shard_of(total[:2]),
            shard_of(total[2]),
            shard_of(total[4:]),
            shard_of(total[3]),
        ]
        return (
            output[None],
            grad_tokens[None],
            grad_condition,
            grad_w_ada,
            grad_w_qkv,
            grad_w_out,
            grad_w_up,
            grad_w_down,
            *grads_bias,
        )

    return body


def solution(mesh):
    return jax.shard_map(
        make_body(mesh.shape["dp"], mesh.shape["fsdp"]),
        mesh=mesh,
        in_specs=(
            P(("dp", "fsdp"), None, None),
            P(("dp", "fsdp"), None),
            P(("dp", "fsdp"), None),
            P("fsdp", None),
            P("fsdp", None),
            P("fsdp", None),
            P("fsdp", None),
            P("fsdp", None),
            P("fsdp"),
            P("fsdp"),
            P("fsdp"),
            P("fsdp"),
            P("fsdp"),
            P(("dp", "fsdp"), None, None),
        ),
        out_specs=(
            P(("dp", "fsdp"), None, None),
            P(("dp", "fsdp"), None, None),
            P(("dp", "fsdp"), None),
            P("fsdp", "dp"),
            P("fsdp", "dp"),
            P("fsdp", "dp"),
            P("fsdp", "dp"),
            P("fsdp", "dp"),
            P("fsdp"),
            P("fsdp"),
            P("fsdp"),
            P("fsdp"),
            P("fsdp"),
        ),
        check_vma=False,
    )
```
